32 devices in a mesh: groups: 2 (over x), ctx: 16 (over z, y, core).
Axes of the slice: x: 2, y: 2, z: 4, core: 2. Of those that a mesh axis runs over, the one named last changes fastest.
Arguments:
- queries: bfloat16 [4096, 4096], P(('groups', 'ctx')), parts along dimension 0, may hold values from -6 to 6
- key_input: bfloat16 [4096, 4096], P(('groups', 'ctx')), parts along dimension 0, may hold values from -6 to 6
- value_input: bfloat16 [4096, 4096], P(('groups', 'ctx')), parts along dimension 0, may hold values from -6 to 6
- log_decay: float32 [4096, 32], P(('groups', 'ctx')), parts along dimension 0, may hold values from -2.5 to 0
- conv_weight: float32 [4, 4096], replicated, may hold values from -3 to 3
- norm_gain: float32 [4096], replicated, may hold values from 0.1 to 1.9
Outputs:
- mixed_out: bfloat16 [4096, 4096], P(('groups', 'ctx')), parts along dimension 0
The draws below stay inside these ranges and needn't reach their ends.
There are 2 independent parts, one for each index of `groups`. The reference program is written for one: setup_inputs(seed, part) draws one part's arguments, and reference() takes and returns one part's arrays. A program takes and returns all parts, laid end to end along the dimension named above; an argument that names none is the same for every part. Nothing has to cross between parts.
All inputs are finite; a program needn't handle non-finite values.
Results may differ from the reference program's by a relative error of at most 0.0066.
Values may be sent and summed in bfloat16 or wider, within the bound.
No kernel may reach another device: no remote copies, remote signals or barrier semaphores. Data moves between devices by JAX's collectives and lax.ppermute only.
A program may use at most 320 MiB of HBM per device.

```python
import math
import jax
import jax.numpy as jnp
from jax import lax

SHARD_HEADS = 32
HEAD_DIM = 128
KERNEL = 4
TOK_DEV = 128
WIDTH = 4096
SEQUENCE_TOKENS = 2048


def draw_log_decay(key, part):
    complete_keys = jax.random.split(jax.random.fold_in(key, 17), 10)
    rapid_fraction = 0.375
    surge_ratio = 0.375
    head_selection = jax.random.uniform(complete_keys[0], (SHARD_HEADS,))
    is_fast = head_selection < rapid_fraction
    surge_flag = jnp.logical_and(head_selection >= rapid_fraction, head_selection < rapid_fraction + surge_ratio)
    fast_rate = jnp.exp(jax.random.uniform(complete_keys[1], (SHARD_HEADS,), jnp.float32, math.log(1.0 / 50.0), math.log(1.0 / 30.0)))
    slow_rate = -math.log(0.95) / SEQUENCE_TOKENS * jnp.exp(jax.random.uniform(complete_keys[2], (SHARD_HEADS,), jnp.float32, math.log(0.3), 0.0))
    head_rate = jnp.where(is_fast, fast_rate, slow_rate)
    factor = jnp.exp(jax.random.uniform(complete_keys[3], (SEQUENCE_TOKENS, SHARD_HEADS), jnp.float32, math.log(0.5), math.log(2.0)))
    baseline_fraction = -head_rate[None, :] * factor
    spike_position = jax.random.randint(complete_keys[4], (3, SHARD_HEADS), 0, SEQUENCE_TOKENS)
    spike_loss = jax.random.uniform(complete_keys[5], (3, SHARD_HEADS), jnp.float32, 0.2, 0.5)
    token_location = jnp.arange(SEQUENCE_TOKENS)[:, None, None]
    marked_tokens = token_location == spike_position[None]
    peak_fraction = jnp.sum(jnp.where(marked_tokens, jnp.log1p(-spike_loss)[None], 0.0), axis=1)
    block_ordinal = SEQUENCE_TOKENS // TOK_DEV
    surge_count = max(block_ordinal // 8, 2)
    surge_interval = SEQUENCE_TOKENS // surge_count
    surge_offset = jax.random.randint(complete_keys[6], (surge_count, SHARD_HEADS), 0, surge_interval - 2)
    surge_begin = jnp.arange(surge_count)[:, None] * surge_interval + surge_offset
    heavy_selection = jax.random.uniform(complete_keys[7], (surge_count, SHARD_HEADS)) < 0.5
    heavy_total = jax.random.uniform(complete_keys[8], (surge_count, SHARD_HEADS), jnp.float32, -5.0, -4.7)
    gentle_total = jax.random.uniform(complete_keys[9], (surge_count, SHARD_HEADS), jnp.float32, -3.5, -1.2)
    surge_tokens_total = jnp.where(heavy_selection, heavy_total, gentle_total)
    within_surge = jnp.logical_and(token_location >= surge_begin[None], token_location < surge_begin[None] + 3)
    surge_fraction = jnp.sum(jnp.where(within_surge, (surge_tokens_total / 3.0)[None], 0.0), axis=1)
    surge_fraction = jnp.where(surge_flag[None, :], surge_fraction, 0.0)
    merged_result = baseline_fraction + peak_fraction + surge_fraction
    return jnp.maximum(merged_result, -2.5).astype(jnp.float32)


def block_levels(rng, shape, shards, low, largest):
    loudness = 1.0
    for axis_at, parts in shards:
        steps = jax.random.uniform(jax.random.fold_in(jax.random.fold_in(rng, 6), axis_at), (parts,), jnp.float32, low / len(shards), largest / len(shards))
        loudness = loudness * jnp.repeat(jnp.exp(steps), shape[axis_at] // parts).reshape((-1,) + (1,) * (len(shape) - 1 - axis_at))
    return loudness


def gaussian(rng, extent, scale, reach, pieces=(), kind=jnp.bfloat16):
    array = jax.random.normal(rng, extent, jnp.float32) * scale
    if len(pieces) > 0:
        array = block_levels(rng, extent, pieces, -0.22, 0.18) * array
    return jnp.clip(array, min=-reach, max=reach).astype(kind)


def setup_inputs(seed: int = 0, part: int = 0) -> dict:
    seeds = jax.random.split(jax.random.key(seed), 7)
    part_keys = jax.random.split(jax.random.fold_in(seeds[6], part), 7)
    queries = gaussian(part_keys[0], (SEQUENCE_TOKENS, WIDTH), 1.0, 6.0, ((0, 16),))
    key_input = gaussian(part_keys[1], (SEQUENCE_TOKENS, WIDTH), 1.0, 6.0, ((0, 16),))
    value_input = gaussian(part_keys[2], (SEQUENCE_TOKENS, WIDTH), 1.0, 6.0, ((0, 16),))
    log_decay = draw_log_decay(jax.random.fold_in(jax.random.fold_in(seeds[6], part), 71), part)
    conv_weight = gaussian(seeds[4], (KERNEL, WIDTH), 0.6, 3.0, (), jnp.float32)
    norm_gain = jnp.clip(1.0 + 0.18 * jax.random.normal(seeds[5], (WIDTH,), jnp.float32), 0.1, 1.9)
    return dict(queries=queries, key_input=key_input, value_input=value_input, log_decay=log_decay, conv_weight=conv_weight, norm_gain=norm_gain)


def reference(queries, key_input, value_input, log_decay, conv_weight, norm_gain):
    block_count = SEQUENCE_TOKENS // TOK_DEV
    taps = KERNEL
    query_blocks = queries.reshape(block_count, TOK_DEV, SHARD_HEADS, HEAD_DIM)
    key_blocks = key_input.reshape(block_count, TOK_DEV, WIDTH)
    value_blocks = value_input.reshape(block_count, TOK_DEV, SHARD_HEADS, HEAD_DIM)
    decay_blocks = log_decay.reshape(block_count, TOK_DEV, SHARD_HEADS)
    gain_heads = norm_gain.reshape(SHARD_HEADS, HEAD_DIM)
    causal = jnp.arange(TOK_DEV)[:, None] >= jnp.arange(TOK_DEV)[None, :]

    def one_block(carry, inputs):
        prefix, key_tail = carry
        query_blk, key_raw, value_blk, decay_blk = inputs
        extended = jnp.concatenate([key_tail, key_raw], 0)
        conv_sum = jnp.zeros((TOK_DEV, WIDTH), jnp.float32)
        for offset in range(taps):
            start = taps - 1 - offset
            conv_sum = conv_sum + conv_weight[offset][None, :] * extended[start:start + TOK_DEV].astype(jnp.float32)
        key_conv = conv_sum.astype(jnp.bfloat16).reshape(TOK_DEV, SHARD_HEADS, HEAD_DIM)
        cum = jnp.cumsum(decay_blk, axis=0)
        total = cum[-1]
        cum_heads = cum.T
        scores = jnp.einsum('thd,shd->hts', query_blk.astype(jnp.float32), key_conv.astype(jnp.float32))
        spread = cum_heads[:, :, None] - cum_heads[:, None, :]
        weights = jnp.where(causal[None], scores * jnp.exp(jnp.where(causal[None], spread, 0.0)), 0.0).astype(jnp.bfloat16)
        intra = jnp.einsum('hts,shd->thd', weights.astype(jnp.float32), value_blk.astype(jnp.float32))
        weighted_keys = (key_conv.astype(jnp.float32) * jnp.exp(total[None, :] - cum)[:, :, None]).astype(jnp.bfloat16)
        block_state = jnp.einsum('shd,she->hde', weighted_keys.astype(jnp.float32), value_blk.astype(jnp.float32))
        prefix_low = prefix.astype(jnp.bfloat16)
        inter = jnp.einsum('thd,hde->the', query_blk.astype(jnp.float32), prefix_low.astype(jnp.float32)) * jnp.exp(cum)[:, :, None]
        mixed = intra + inter
        scale_inv = lax.rsqrt(lax.optimization_barrier(jnp.mean(mixed * mixed, axis=2, keepdims=True)) + 1e-05)
        result = (mixed * scale_inv * gain_heads[None]).astype(jnp.bfloat16)
        new_prefix = jnp.exp(total)[:, None, None] * prefix + block_state
        return ((new_prefix, key_raw[TOK_DEV - (taps - 1):]), result.reshape(TOK_DEV, WIDTH))
    start_prefix = jnp.zeros((SHARD_HEADS, HEAD_DIM, HEAD_DIM), jnp.float32)
    start_tail = jnp.zeros((KERNEL - 1, WIDTH), jnp.bfloat16)
    carry_end, outputs = lax.scan(one_block, (start_prefix, start_tail), (query_blocks, key_blocks, value_blocks, decay_blocks))
    return outputs.reshape(SEQUENCE_TOKENS, WIDTH)
```

```python
import functools

import jax
import jax.numpy as jnp
from jax import lax
from jax.experimental import pallas as pl
from jax.experimental.pallas import tpu as pltpu
from jax.sharding import PartitionSpec as P

F32 = jnp.float32
BF16 = jnp.bfloat16
CHIPS = 4
SPAN = 2 * CHIPS
HALO = 8


def three_parts(x):
    hi = x.astype(BF16)
    rest = x - hi.astype(F32)
    mid = rest.astype(BF16)
    low = (rest - mid.astype(F32)).astype(BF16)
    return hi, mid, low


def conv_keys(k_ref, halo_ref, w_ref, ext_ref):
    rows = k_ref.shape[0]
    ext_ref[0:HALO, :] = halo_ref[...].astype(F32)
    ext_ref[HALO : HALO + rows, :] = k_ref[...].astype(F32)
    total = None
    for j in range(w_ref.shape[0]):
        term = w_ref[j : j + 1, :] * ext_ref[HALO - j : HALO - j + rows, :]
        total = term if total is None else total + term
    return total.astype(BF16)


def put_decay(out, heads, size, decays):
    base = heads * size
    zero = jnp.zeros((16 - 3 * heads, 128), BF16)
    rows = jnp.concatenate(decays, 0)
    parts = [p.astype(F32) for p in three_parts(rows)]
    out[base : base + 16, :] = jnp.concatenate(parts + [zero.astype(F32)], 0).astype(BF16)


def get_decay(packet, heads, size):
    base = heads * size
    tail = packet[base : base + 16, :].astype(F32)
    return tail[0:heads] + tail[heads : 2 * heads] + tail[2 * heads : 3 * heads]


def state_kernel(heads, size, idx, k_ref, halo_ref, v_ref, w_ref, cum_ref, out_ref, ext_ref):
    del idx
    key_conv = conv_keys(k_ref, halo_ref, w_ref, ext_ref)
    cum = cum_ref[0, 0:heads, :]
    total = cum_ref[0, heads : 2 * heads, :]
    ending = jnp.exp(total - cum).T
    for j in range(heads):
        cols = slice(j * size, (j + 1) * size)
        weighted = (key_conv[:, cols].astype(F32) * ending[:, j : j + 1]).astype(BF16)
        state = lax.dot_general(
            weighted, v_ref[:, cols], (((0,), (0,)), ((), ())), preferred_element_type=F32
        )
        out_ref[0, j * size : (j + 1) * size, :] = state.astype(BF16)
    decay = jnp.exp(total)
    put_decay(out_ref.at[0], heads, size, [decay[j : j + 1] for j in range(heads)])


def intra_kernel(heads, size, q_ref, k_ref, halo_ref, v_ref, w_ref, cum_ref, out_ref, ext_ref):
    rows = q_ref.shape[0]
    key_conv = conv_keys(k_ref, halo_ref, w_ref, ext_ref)
    cum = cum_ref[0, 0:heads, :]
    cum_col = cum.T
    causal = lax.broadcasted_iota(jnp.int32, (rows, rows), 0) >= lax.broadcasted_iota(
        jnp.int32, (rows, rows), 1
    )
    for j in range(heads):
        cols = slice(j * size, (j + 1) * size)
        scores = lax.dot_general(
            q_ref[:, cols],
            key_conv[:, cols],
            (((1,), (1,)), ((), ())),
            preferred_element_type=F32,
        )
        spread = cum_col[:, j : j + 1] - cum[j : j + 1, :]
        weights = jnp.where(causal, scores * jnp.exp(jnp.where(causal, spread, 0.0)), 0.0)
        out_ref[:, cols] = jnp.dot(
            weights.astype(BF16), v_ref[:, cols], preferred_element_type=F32
        )


def chip_kernel(heads, size, idx, own_ref, got_ref, *out_refs):
    first = idx[0] == 0
    for g in range(CHIPS):
        own_decay = get_decay(own_ref.at[g], heads, size)
        got_decay = get_decay(got_ref.at[g], heads, size)
        own_by = jnp.where(first, got_decay, 1.0)
        got_by = jnp.where(first, 1.0, own_decay)
        for j in range(heads):
            rows = slice(j * size, (j + 1) * size)
            out_refs[g][rows, :] = (
                own_ref[g, rows, :].astype(F32) * own_by[j : j + 1]
                + got_ref[g, rows, :].astype(F32) * got_by[j : j + 1]
            ).astype(BF16)
        both = own_decay * got_decay
        put_decay(out_refs[g], heads, size, [both[j : j + 1] for j in range(heads)])


def span_kernel(heads, size, idx, *refs):
    packets, out_ref, held = refs[:CHIPS], refs[CHIPS], refs[CHIPS + 1]
    for g in range(CHIPS):
        held[idx[1] ^ g] = packets[g][...]
    decays = [get_decay(held.at[b], heads, size) for b in range(CHIPS)]
    for j in range(heads):
        rows = slice(j * size, (j + 1) * size)
        acc = held[0, rows, :].astype(F32)
        for b in range(1, CHIPS):
            acc = acc * decays[b][j : j + 1] + held[b, rows, :].astype(F32)
        out_ref[rows, :] = acc.astype(BF16)
    whole = decays[0]
    for b in range(1, CHIPS):
        whole = whole * decays[b]
    put_decay(out_ref, heads, size, [whole[j : j + 1] for j in range(heads)])


def spread_kernel(heads, size, idx, *refs):
    packets, before = refs[:CHIPS], refs[CHIPS]
    outs, held, made = refs[CHIPS + 1 : 2 * CHIPS + 1], refs[2 * CHIPS + 1], refs[2 * CHIPS + 2]
    for g in range(CHIPS):
        held[idx[1] ^ g] = packets[g][...]
    decays = [get_decay(held.at[b], heads, size) for b in range(CHIPS)]
    for j in range(heads):
        rows = slice(j * size, (j + 1) * size)
        acc = before[rows, :].astype(F32)
        made[0, rows, :] = before[rows, :]
        for b in range(1, CHIPS):
            acc = acc * decays[b - 1][j : j + 1] + held[b - 1, rows, :].astype(F32)
            made[b, rows, :] = acc.astype(BF16)
    for g in range(CHIPS):
        outs[g][...] = made[idx[1] ^ g]


def out_kernel(heads, size, idx, q_ref, intra_ref, cum_ref, gain_ref, *refs):
    prefixes, sib_ref, out_ref, held = refs[:CHIPS], refs[CHIPS], refs[-2], refs[-1]
    g = pl.program_id(0)
    for i in range(CHIPS):

        @pl.when(g == i)
        def _():
            held[...] = prefixes[i][...]

    second = idx[0] == 1
    sib_decay = get_decay(sib_ref.at[0], heads, size)
    started = jnp.exp(cum_ref[0, 0:heads, :]).T
    for j in range(heads):
        cols = slice(j * size, (j + 1) * size)
        chip_prefix = held[cols, :].astype(F32)
        prefix = jnp.where(
            second,
            chip_prefix * sib_decay[j : j + 1] + sib_ref[0, cols, :].astype(F32),
            chip_prefix,
        ).astype(BF16)
        inter = jnp.dot(q_ref[:, cols], prefix, preferred_element_type=F32)
        mixed = intra_ref[:, cols] + inter * started[:, j : j + 1]
        scale = lax.rsqrt(jnp.mean(mixed * mixed, axis=1, keepdims=True) + 1e-05)
        out_ref[:, cols] = (mixed * scale * gain_ref[0:1, cols]).astype(BF16)


def join_spans(earlier, later, heads, size):
    base = heads * size

    def decay(x):
        tail = x[base:].astype(F32)
        return tail[0:heads] + tail[heads : 2 * heads] + tail[2 * heads : 3 * heads]

    by = decay(later)
    state = (
        by[:, None, :] * earlier[:base].astype(F32).reshape(heads, size, -1)
        + later[:base].astype(F32).reshape(heads, size, -1)
    ).reshape(base, -1)
    parts = three_parts(by * decay(earlier))
    return jnp.concatenate([state.astype(BF16), *parts, later[base + 3 * heads :]], 0)


def on_device(queries, key_input, value_input, log_decay, conv_weight, norm_gain):
    rows, width = queries.shape
    head_count = log_decay.shape[1]
    size = width // head_count
    taps = conv_weight.shape[0]
    heads = head_count // SPAN
    wide = heads * size
    packet = wide + 16
    n = lax.axis_size("ctx")
    me = lax.axis_index("ctx")
    core, chip = me % 2, (me // 2) % CHIPS
    idx = jnp.stack([core, chip]).astype(jnp.int32)

    def swap(x, mask):
        return lax.ppermute(x, "ctx", [(i, i ^ mask) for i in range(n)])

    def shift(x, by):
        return lax.ppermute(x, "ctx", [(i, i + by) for i in range(n - by)])

    halo = shift(key_input[rows - HALO :], 1)
    cum = jnp.cumsum(log_decay, axis=0).T.reshape(SPAN, heads, rows)
    cum = jnp.concatenate([cum, jnp.broadcast_to(cum[:, :, -1:], cum.shape)], 1)
    gain = norm_gain.reshape(1, width)

    def states(mine):
        def at(g, s):
            half = s[0] if mine else 1 - s[0]
            return half * CHIPS + (s[1] ^ g)

        col = lambda g, s: (0, at(g, s))
        return pl.pallas_call(
            functools.partial(state_kernel, heads, size),
            out_shape=jax.ShapeDtypeStruct((CHIPS, packet, size), BF16),
            grid_spec=pltpu.PrefetchScalarGridSpec(
                num_scalar_prefetch=1,
                grid=(CHIPS,),
                in_specs=[
                    pl.BlockSpec((rows, wide), col),
                    pl.BlockSpec((HALO, wide), col),
                    pl.BlockSpec((rows, wide), col),
                    pl.BlockSpec((taps, wide), col),
                    pl.BlockSpec((1, 2 * heads, rows), lambda g, s: (at(g, s), 0, 0)),
                ],
                out_specs=pl.BlockSpec((1, packet, size), lambda g, s: (g, 0, 0)),
                scratch_shapes=[pltpu.VMEM((rows + HALO, wide), F32)],
            ),
            name="states_mine" if mine else "states_other",
        )(idx, key_input, halo, value_input, conv_weight, cum)

    theirs = states(False)
    got = swap(theirs, 1)
    mine = states(True)
    got_late = swap(mine, 1)

    whole = lambda shape: pl.BlockSpec(shape, lambda i, s: (0,) * len(shape))
    flat = jax.ShapeDtypeStruct((packet, size), BF16)
    chip_states = pl.pallas_call(
        functools.partial(chip_kernel, heads, size),
        out_shape=[flat] * CHIPS,
        grid_spec=pltpu.PrefetchScalarGridSpec(
            num_scalar_prefetch=1,
            grid=(1,),
            in_specs=[whole((CHIPS, packet, size))] * 2,
            out_specs=[whole((packet, size))] * CHIPS,
        ),
        name="chip_states",
    )(idx, mine, got)
    packets = [chip_states[0]] + [swap(chip_states[g], 2 * g) for g in range(1, CHIPS)]

    blk = lambda g: (0, g)
    intra = pl.pallas_call(
        functools.partial(intra_kernel, heads, size),
        out_shape=jax.ShapeDtypeStruct((rows, width), F32),
        grid=(SPAN,),
        in_specs=[
            pl.BlockSpec((rows, wide), blk),
            pl.BlockSpec((rows, wide), blk),
            pl.BlockSpec((HALO, wide), blk),
            pl.BlockSpec((rows, wide), blk),
            pl.BlockSpec((taps, wide), blk),
            pl.BlockSpec((1, 2 * heads, rows), lambda g: (g, 0, 0)),
        ],
        out_specs=pl.BlockSpec((rows, wide), blk),
        scratch_shapes=[pltpu.VMEM((rows + HALO, wide), F32)],
        name="intra",
    )(queries, key_input, halo, value_input, conv_weight, cum)

    span = pl.pallas_call(
        functools.partial(span_kernel, heads, size),
        out_shape=flat,
        grid_spec=pltpu.PrefetchScalarGridSpec(
            num_scalar_prefetch=1,
            grid=(1,),
            in_specs=[whole((packet, size))] * CHIPS,
            out_specs=whole((packet, size)),
            scratch_shapes=[pltpu.VMEM((CHIPS, packet, size), BF16)],
        ),
        name="span_state",
    )(idx, *packets)
    before = shift(span, SPAN)
    reach = 1
    while reach < n // SPAN - 1:
        before = join_spans(shift(before, SPAN * reach), before, heads, size)
        reach *= 2

    low = jax.ShapeDtypeStruct((wide, size), BF16)
    chip_prefix = pl.pallas_call(
        functools.partial(spread_kernel, heads, size),
        out_shape=[low] * CHIPS,
        grid_spec=pltpu.PrefetchScalarGridSpec(
            num_scalar_prefetch=1,
            grid=(1,),
            in_specs=[whole((packet, size))] * (CHIPS + 1),
            out_specs=[whole((wide, size))] * CHIPS,
            scratch_shapes=[
                pltpu.VMEM((CHIPS, packet, size), BF16),
                pltpu.VMEM((CHIPS, wide, size), BF16),
            ],
        ),
        name="chip_prefix",
    )(idx, *packets, before)
    own = [chip_prefix[0]] + [swap(chip_prefix[g], 2 * g) for g in range(1, CHIPS)]
    other = [swap(x, 1) for x in own]

    def output(mine, prefixes, sibling, result):
        def at(g, s):
            half = s[0] if mine else 1 - s[0]
            return half * CHIPS + (s[1] ^ g)

        col = lambda g, s: (0, at(g, s))
        extra = [] if result is None else [result]
        return pl.pallas_call(
            functools.partial(out_kernel, heads, size),
            out_shape=jax.ShapeDtypeStruct((rows, width), BF16),
            grid_spec=pltpu.PrefetchScalarGridSpec(
                num_scalar_prefetch=1,
                grid=(CHIPS,),
                in_specs=[
                    pl.BlockSpec((rows, wide), col),
                    pl.BlockSpec((rows, wide), col),
                    pl.BlockSpec((1, 2 * heads, rows), lambda g, s: (at(g, s), 0, 0)),
                    pl.BlockSpec((1, wide), col),
                ]
                + [pl.BlockSpec((wide, size), lambda g, s: (0, 0))] * CHIPS
                + [pl.BlockSpec((1, packet, size), lambda g, s: (g, 0, 0))]
                + [pl.BlockSpec(memory_space=pl.ANY)] * len(extra),
                out_specs=pl.BlockSpec((rows, wide), col),
                scratch_shapes=[pltpu.VMEM((wide, size), BF16)],
            ),
            input_output_aliases={} if result is None else {6 + CHIPS: 0},
            name="out_mine" if mine else "out_other",
        )(idx, queries, intra, cum, gain, *prefixes, sibling, *extra)

    result = output(True, own, got, None)
    return output(False, other, got_late, result)


def solution(mesh):
    rows = P(("groups", "ctx"), None)
    return jax.shard_map(
        on_device,
        mesh=mesh,
        in_specs=(rows, rows, rows, rows, P(), P()),
        out_specs=rows,
        check_vma=False,
    )
```

```python
import functools

import jax
import jax.numpy as jnp
from jax import lax
from jax.experimental import pallas as pl
from jax.experimental.pallas import tpu as pltpu
from jax.sharding import PartitionSpec as P

F32 = jnp.float32
BF16 = jnp.bfloat16
CHIPS = 4
SPAN = 2 * CHIPS
HALO = 8
PARTS = 16
VMEM = pl.BlockSpec(memory_space=pltpu.VMEM)
ANY = pl.BlockSpec(memory_space=pl.ANY)


def position():
    me = lax.axis_index("ctx")
    return me & 1, (me >> 1) & (CHIPS - 1)


def head_group(mine, g):
    core, chip = position()
    return (core if mine else 1 - core) * CHIPS + (chip ^ g)


def columns(block, offset, size):
    return pl.ds(pl.multiple_of(block + offset, size), size)


def call(kernel, name, out_shape, *args, scratch=(), in_specs=None, out_specs=VMEM, **options):
    if in_specs is None:
        in_specs = [VMEM] * len(args)
    args = [
        pltpu.with_memory_space_constraint(x, pltpu.VMEM) if s is VMEM else x
        for x, s in zip(args, in_specs)
    ]
    return pl.pallas_call(
        kernel,
        out_shape=out_shape,
        in_specs=in_specs,
        out_specs=out_specs,
        scratch_shapes=list(scratch),
        name=name,
        compiler_params=pltpu.CompilerParams(vmem_limit_bytes=6 << 20),
        **options,
    )(*args)


def tail_kernel(k_ref, out_ref, sem):
    rows = k_ref.shape[0]
    copy = pltpu.make_async_copy(k_ref.at[rows - HALO : rows, :], out_ref, sem)
    copy.start()
    copy.wait()


def cum_kernel(heads, decay_ref, out_ref):
    x = decay_ref[...]
    rows = x.shape[1]
    lane = lax.broadcasted_iota(jnp.int32, x.shape, 1)
    step = 1
    while step < rows:
        x = x + jnp.where(lane >= step, pltpu.roll(x, step, 1), 0.0)
        step *= 2
    total = jnp.broadcast_to(x[:, rows - 1 : rows], x.shape)
    for b in range(out_ref.shape[0]):
        these = slice(b * heads, (b + 1) * heads)
        out_ref[b, 0:heads, :] = x[these]
        out_ref[b, heads : 2 * heads, :] = total[these]


def three_parts(x):
    hi = x.astype(BF16)
    rest = x - hi.astype(F32)
    mid = rest.astype(BF16)
    low = (rest - mid.astype(F32)).astype(BF16)
    return hi, mid, low


def put_decay(out, decays, heads, size):
    base = heads * size
    parts = [p.astype(F32) for p in three_parts(decays)]
    spare = jnp.zeros((PARTS - 3 * heads, decays.shape[1]), F32)
    out[base : base + PARTS, :] = jnp.concatenate(parts + [spare], 0).astype(BF16)


def get_decay(packet, heads, size):
    base = heads * size
    tail = packet[base : base + PARTS, :].astype(F32)
    return tail[0:heads] + tail[heads : 2 * heads] + tail[2 * heads : 3 * heads]


def conv_keys(k_ref, halo_ref, w_ref, ext, cols):
    rows = k_ref.shape[0]
    ext[0:HALO, :] = halo_ref[:, cols].astype(F32)
    ext[HALO : HALO + rows, :] = k_ref[:, cols].astype(F32)
    total = None
    for j in range(w_ref.shape[0]):
        term = w_ref[j : j + 1, cols] * ext[HALO - j : HALO - j + rows, :]
        total = term if total is None else total + term
    return total.astype(BF16)


def state_kernel(mine, heads, size, k_ref, halo_ref, v_ref, w_ref, cum_ref, out_ref, ext, held):
    for g in range(CHIPS):
        b = head_group(mine, g)
        cum = cum_ref[b]
        ending = jnp.exp(cum[heads : 2 * heads] - cum[0:heads]).T
        for j in range(heads):
            cols = columns(b * heads * size, j * size, size)
            key_conv = conv_keys(k_ref, halo_ref, w_ref, ext.at[j], cols)
            held[g * heads + j] = (key_conv.astype(F32) * ending[:, j : j + 1]).astype(BF16)
    for g in range(CHIPS):
        b = head_group(mine, g)
        for j in range(heads):
            cols = columns(b * heads * size, j * size, size)
            state = lax.dot_general(
                v_ref[:, cols], held[g * heads + j], (((0,), (0,)), ((), ())),
                preferred_element_type=F32,
            )
            out_ref[g, j * size : (j + 1) * size, :] = state.astype(BF16)
        put_decay(out_ref.at[g], jnp.exp(cum_ref[b][heads : 2 * heads]), heads, size)


def intra_kernel(
    mine, heads, size, q_ref, k_ref, halo_ref, v_ref, w_ref, cum_ref, out_ref, ext, held
):
    rows = q_ref.shape[0]
    causal = lax.broadcasted_iota(jnp.int32, (rows, rows), 0) >= lax.broadcasted_iota(
        jnp.int32, (rows, rows), 1
    )
    for g in range(CHIPS):
        b = head_group(mine, g)
        cum = cum_ref[b][0:heads]
        cum_col = cum.T
        for j in range(heads):
            cols = columns(b * heads * size, j * size, size)
            key_conv = conv_keys(k_ref, halo_ref, w_ref, ext.at[j], cols)
            scores = lax.dot_general(
                q_ref[:, cols], key_conv, (((1,), (1,)), ((), ())), preferred_element_type=F32
            )
            spread = cum_col[:, j : j + 1] - cum[j : j + 1]
            weights = jnp.where(causal, scores * jnp.exp(jnp.where(causal, spread, 0.0)), 0.0)
            held[g * heads + j] = weights.astype(BF16)
    for g in range(CHIPS):
        b = head_group(mine, g)
        for j in range(heads):
            cols = columns(b * heads * size, j * size, size)
            out_ref[g * heads + j] = jnp.dot(
                held[g * heads + j], v_ref[:, cols], preferred_element_type=F32
            )


def chip_kernel(heads, size, own_ref, got_ref, out_ref):
    core, _ = position()
    first = core == 0
    for g in range(CHIPS):
        own_decay = get_decay(own_ref.at[g], heads, size)
        got_decay = get_decay(got_ref.at[g], heads, size)
        own_by = jnp.where(first, got_decay, 1.0)
        got_by = jnp.where(first, 1.0, own_decay)
        for j in range(heads):
            rows = slice(j * size, (j + 1) * size)
            out_ref[g, rows, :] = (
                own_ref[g, rows, :].astype(F32) * own_by[j : j + 1]
                + got_ref[g, rows, :].astype(F32) * got_by[j : j + 1]
            ).astype(BF16)
        put_decay(out_ref.at[g], own_decay * got_decay, heads, size)


def in_order(packets, held):
    _, chip = position()
    for g in range(CHIPS):
        held[chip ^ g] = packets[g][...]


def span_kernel(heads, size, *refs):
    packets, out_ref, held = refs[:CHIPS], refs[CHIPS], refs[CHIPS + 1]
    in_order(packets, held)
    decays = [get_decay(held.at[b], heads, size) for b in range(CHIPS)]
    for j in range(heads):
        rows = slice(j * size, (j + 1) * size)
        acc = held[0, rows, :].astype(F32)
        for b in range(1, CHIPS):
            acc = acc * decays[b][j : j + 1] + held[b, rows, :].astype(F32)
        out_ref[rows, :] = acc.astype(BF16)
    whole = decays[0]
    for b in range(1, CHIPS):
        whole = whole * decays[b]
    put_decay(out_ref, whole, heads, size)


def spread_kernel(heads, size, *refs):
    packets, before, out_ref, held = refs[:CHIPS], refs[CHIPS], refs[CHIPS + 1], refs[CHIPS + 2]
    _, chip = position()
    in_order(packets, held)
    decays = [get_decay(held.at[b], heads, size) for b in range(CHIPS)]
    for j in range(heads):
        rows = slice(j * size, (j + 1) * size)
        acc = before[rows, :].astype(F32)
        out_ref[chip, rows, :] = before[rows, :]
        for b in range(1, CHIPS):
            acc = acc * decays[b - 1][j : j + 1] + held[b - 1, rows, :].astype(F32)
            out_ref[chip ^ b, rows, :] = acc.astype(BF16)


def out_kernel(mine, heads, size, q_ref, intra_ref, cum_ref, gain_ref, sib_ref, *refs):
    prefixes, (out_ref, mixed_ref, done_ref, sems) = refs[:CHIPS], refs[-4:]
    core, _ = position()
    second = core == 1
    for g in range(CHIPS):
        b = head_group(mine, g)
        started = jnp.exp(cum_ref[b][0:heads]).T
        sib_decay = get_decay(sib_ref.at[g], heads, size)
        by = jnp.where(second, sib_decay, 1.0)
        for j in range(heads):
            cols = columns(b * heads * size, j * size, size)
            rows = slice(j * size, (j + 1) * size)
            sib = jnp.where(second, sib_ref[g, rows, :].astype(F32), 0.0)
            prefix = prefixes[g][rows, :].astype(F32) * by[j : j + 1] + sib
            inter = lax.dot_general(
                q_ref[:, cols], prefix.astype(BF16), (((1,), (1,)), ((), ())),
                preferred_element_type=F32,
            )
            mixed_ref[g * heads + j] = intra_ref[g * heads + j] + inter * started[:, j : j + 1]
    copies = []
    for g in range(CHIPS):
        b = head_group(mine, g)
        for j in range(heads):
            cols = columns(b * heads * size, j * size, size)
            mixed = mixed_ref[g * heads + j]
            scale = lax.rsqrt(jnp.mean(mixed * mixed, axis=1, keepdims=True) + 1e-05)
            done_ref[g, :, j * size : (j + 1) * size] = (
                mixed * scale * gain_ref[:, cols]
            ).astype(BF16)
        wide = columns(b * heads * size, 0, heads * size)
        copies.append(pltpu.make_async_copy(done_ref.at[g], out_ref.at[:, wide], sems.at[g]))
        copies[-1].start()
    for copy in copies:
        copy.wait()


def join_spans(earlier, later, heads, size):
    base = heads * size

    def decay(x):
        tail = x[base:].astype(F32)
        return tail[0:heads] + tail[heads : 2 * heads] + tail[2 * heads : 3 * heads]

    by = decay(later)
    state = (
        by[:, None, :] * earlier[:base].astype(F32).reshape(heads, size, -1)
        + later[:base].astype(F32).reshape(heads, size, -1)
    ).reshape(base, -1)
    parts = three_parts(by * decay(earlier))
    return jnp.concatenate([state.astype(BF16), *parts, later[base + 3 * heads :]], 0)


def on_device(queries, key_input, value_input, log_decay, conv_weight, norm_gain):
    rows, width = queries.shape
    head_count = log_decay.shape[1]
    size = width // head_count
    heads = head_count // SPAN
    half = CHIPS * heads
    packet = heads * size + PARTS
    n = lax.axis_size("ctx")

    def swap(x, mask):
        return lax.ppermute(x, "ctx", [(i, i ^ mask) for i in range(n)])

    def shift(x, by):
        return lax.ppermute(x, "ctx", [(i, i + by) for i in range(n - by)])

    tail = call(
        tail_kernel,
        "tail",
        pltpu.VMEM((HALO, width), BF16),
        key_input,
        in_specs=[ANY],
        scratch=[pltpu.SemaphoreType.DMA(())],
    )
    halo = shift(tail, 1)
    cum = call(
        functools.partial(cum_kernel, heads),
        "cum",
        pltpu.VMEM((SPAN, 2 * heads, rows), F32),
        log_decay.T,
    )
    gain = norm_gain.reshape(1, width)
    ext = pltpu.VMEM((heads, rows + HALO, size), F32)
    held = pltpu.VMEM((half, rows, size), BF16)

    def states(mine):
        return call(
            functools.partial(state_kernel, mine, heads, size),
            "states_mine" if mine else "states_other",
            pltpu.VMEM((CHIPS, packet, size), BF16),
            key_input, halo, value_input, conv_weight, cum,
            scratch=[ext, pltpu.VMEM((half, rows, size), BF16)],
        )

    def intra_part(mine, q):
        return call(
            functools.partial(intra_kernel, mine, heads, size),
            "intra_mine" if mine else "intra_other",
            pltpu.VMEM((half, rows, size), F32),
            q, key_input, halo, value_input, conv_weight, cum,
            scratch=[ext, held],
        )

    theirs = states(False)
    got = swap(theirs, 1)
    mine = states(True)
    got_late = swap(mine, 1)

    chip_states = call(
        functools.partial(chip_kernel, heads, size),
        "chip_states",
        pltpu.VMEM((CHIPS, packet, size), BF16),
        mine, got,
    )
    packets = [chip_states[0]] + [swap(chip_states[g], 2 * g) for g in range(1, CHIPS)]
    q_after, chip_states = lax.optimization_barrier((queries, chip_states))
    intra_mine = intra_part(True, q_after)
    *packets, intra_mine = lax.optimization_barrier((*packets, intra_mine))

    order = pltpu.VMEM((CHIPS, packet, size), BF16)
    span = call(
        functools.partial(span_kernel, heads, size),
        "span_state",
        pltpu.VMEM((packet, size), BF16),
        *packets,
        scratch=[order],
    )
    before = shift(span, SPAN)
    reach = 1
    while reach < n // SPAN - 1:
        before = join_spans(shift(before, SPAN * reach), before, heads, size)
        reach *= 2
    q_after, span = lax.optimization_barrier((queries, span))
    intra_other = intra_part(False, q_after)
    before, intra_other = lax.optimization_barrier((before, intra_other))

    chip_prefix = call(
        functools.partial(spread_kernel, heads, size),
        "chip_prefix",
        pltpu.VMEM((CHIPS, heads * size, size), BF16),
        *packets, before,
        scratch=[order],
    )
    own = [chip_prefix[0]] + [swap(chip_prefix[g], 2 * g) for g in range(1, CHIPS)]
    other = [swap(x, 1) for x in own]

    def output(mine, intra, sibling, prefixes, result):
        extra = [] if result is None else [result]
        return call(
            functools.partial(out_kernel, mine, heads, size),
            "out_mine" if mine else "out_other",
            jax.ShapeDtypeStruct((rows, width), BF16),
            queries, intra, cum, gain, sibling, *prefixes, *extra,
            in_specs=[VMEM] * (5 + CHIPS) + [ANY] * len(extra),
            out_specs=ANY,
            input_output_aliases={5 + CHIPS: 0} if extra else {},
            scratch=[
                pltpu.VMEM((half, rows, size), F32),
                pltpu.VMEM((CHIPS, rows, heads * size), BF16),
                pltpu.SemaphoreType.DMA((CHIPS,)),
            ],
        )

    result = output(True, intra_mine, got, own, None)
    return output(False, intra_other, got_late, other, result)


def solution(mesh):
    rows = P(("groups", "ctx"), None)
    return jax.shard_map(
        on_device,
        mesh=mesh,
        in_specs=(rows, rows, rows, rows, P(), P()),
        out_specs=rows,
        check_vma=False,
    )
```

```python
import functools

import jax
import jax.numpy as jnp
from jax import lax
from jax.experimental import pallas as pl
from jax.experimental.pallas import tpu as pltpu
from jax.sharding import PartitionSpec as P

F32 = jnp.float32
BF16 = jnp.bfloat16
CHIPS = 4
SPAN = 2 * CHIPS
HALO = 8
EXCHANGE = (1, 3, 2)
PARTS = 16
VMEM = pl.BlockSpec(memory_space=pltpu.VMEM)
HBM = pl.BlockSpec(memory_space=pltpu.HBM)


def position():
    me = lax.axis_index("ctx")
    return me & 1, (me >> 1) & (CHIPS - 1)


def head_group(mine, g):
    core, chip = position()
    return (core if mine else 1 - core) * CHIPS + (chip ^ g)


def columns(block, offset, size):
    return pl.ds(pl.multiple_of(block + offset, size), size)


def call(kernel, name, out_shape, *args, scratch=(), in_specs=None, out_specs=VMEM, **options):
    if in_specs is None:
        in_specs = [VMEM] * len(args)
    args = [
        pltpu.with_memory_space_constraint(x, pltpu.VMEM if s is VMEM else pltpu.HBM)
        for x, s in zip(args, in_specs)
    ]
    return pl.pallas_call(
        kernel,
        out_shape=out_shape,
        in_specs=in_specs,
        out_specs=out_specs,
        scratch_shapes=list(scratch),
        name=name,
        compiler_params=pltpu.CompilerParams(vmem_limit_bytes=6 << 20),
        **options,
    )(*args)


def tail_kernel(k_ref, out_ref, sem):
    rows = k_ref.shape[0]
    copy = pltpu.make_async_copy(k_ref.at[rows - HALO : rows, :], out_ref, sem)
    copy.start()
    copy.wait()


def cum_kernel(heads, decay_ref, early_ref, out_ref):
    del early_ref
    x = decay_ref[...]
    rows = x.shape[1]
    lane = lax.broadcasted_iota(jnp.int32, x.shape, 1)
    step = 1
    while step < rows:
        x = x + jnp.where(lane >= step, pltpu.roll(x, step, 1), 0.0)
        step *= 2
    total = jnp.broadcast_to(x[:, rows - 1 : rows], x.shape)
    for b in range(out_ref.shape[0]):
        these = slice(b * heads, (b + 1) * heads)
        out_ref[b, 0:heads, :] = x[these]
        out_ref[b, heads : 2 * heads, :] = total[these]


def three_parts(x):
    hi = x.astype(BF16)
    rest = x - hi.astype(F32)
    mid = rest.astype(BF16)
    low = (rest - mid.astype(F32)).astype(BF16)
    return hi, mid, low


def put_decay(out, decays, heads, size):
    base = heads * size
    parts = [p.astype(F32) for p in three_parts(decays)]
    spare = jnp.zeros((PARTS - 3 * heads, decays.shape[1]), F32)
    out[base : base + PARTS, :] = jnp.concatenate(parts + [spare], 0).astype(BF16)


def get_decay(packet, heads, size):
    base = heads * size
    tail = packet[base : base + PARTS, :].astype(F32)
    return tail[0:heads] + tail[heads : 2 * heads] + tail[2 * heads : 3 * heads]


def conv_keys(k_ref, halo_ref, w_ref, ext, cols):
    rows = k_ref.shape[0]
    ext[0:HALO, :] = halo_ref[:, cols].astype(F32)
    ext[HALO : HALO + rows, :] = k_ref[:, cols].astype(F32)
    total = None
    for j in range(w_ref.shape[0]):
        term = w_ref[j : j + 1, cols] * ext[HALO - j : HALO - j + rows, :]
        total = term if total is None else total + term
    return total.astype(BF16)


def state_kernel(mine, heads, size, k_ref, halo_ref, v_ref, w_ref, cum_ref, out_ref, ext, held):
    for g in range(CHIPS):
        b = head_group(mine, g)
        cum = cum_ref[b]
        ending = jnp.exp(cum[heads : 2 * heads] - cum[0:heads]).T
        for j in range(heads):
            cols = columns(b * heads * size, j * size, size)
            key_conv = conv_keys(k_ref, halo_ref, w_ref, ext.at[j], cols)
            held[g * heads + j] = (key_conv.astype(F32) * ending[:, j : j + 1]).astype(BF16)
    for g in range(CHIPS):
        b = head_group(mine, g)
        for j in range(heads):
            cols = columns(b * heads * size, j * size, size)
            state = lax.dot_general(
                v_ref[:, cols], held[g * heads + j], (((0,), (0,)), ((), ())),
                preferred_element_type=F32,
            )
            out_ref[g, j * size : (j + 1) * size, :] = state.astype(BF16)
        put_decay(out_ref.at[g], jnp.exp(cum_ref[b][heads : 2 * heads]), heads, size)


def intra_kernel(
    mine, heads, size, q_ref, k_ref, halo_ref, v_ref, w_ref, cum_ref, out_ref, ext, held
):
    rows = q_ref.shape[0]
    causal = lax.broadcasted_iota(jnp.int32, (rows, rows), 0) >= lax.broadcasted_iota(
        jnp.int32, (rows, rows), 1
    )
    for g in range(CHIPS):
        b = head_group(mine, g)
        cum = cum_ref[b][0:heads]
        cum_col = cum.T
        for j in range(heads):
            cols = columns(b * heads * size, j * size, size)
            key_conv = conv_keys(k_ref, halo_ref, w_ref, ext.at[j], cols)
            scores = lax.dot_general(
                q_ref[:, cols], key_conv, (((1,), (1,)), ((), ())), preferred_element_type=F32
            )
            spread = cum_col[:, j : j + 1] - cum[j : j + 1]
            weights = jnp.where(causal, scores * jnp.exp(jnp.where(causal, spread, 0.0)), 0.0)
            held[g * heads + j] = weights.astype(BF16)
    for g in range(CHIPS):
        b = head_group(mine, g)
        for j in range(heads):
            cols = columns(b * heads * size, j * size, size)
            out_ref[g * heads + j] = jnp.dot(
                held[g * heads + j], v_ref[:, cols], preferred_element_type=F32
            )


def chip_kernel(heads, size, own_ref, got_ref, out_ref):
    core, _ = position()
    first = core == 0
    for g in range(CHIPS):
        own_decay = get_decay(own_ref.at[g], heads, size)
        got_decay = get_decay(got_ref.at[g], heads, size)
        own_by = jnp.where(first, got_decay, 1.0)
        got_by = jnp.where(first, 1.0, own_decay)
        for j in range(heads):
            rows = slice(j * size, (j + 1) * size)
            out_ref[g, rows, :] = (
                own_ref[g, rows, :].astype(F32) * own_by[j : j + 1]
                + got_ref[g, rows, :].astype(F32) * got_by[j : j + 1]
            ).astype(BF16)
        put_decay(out_ref.at[g], own_decay * got_decay, heads, size)


def in_order(packets, held):
    _, chip = position()
    for g in range(CHIPS):
        held[chip ^ g] = packets[g][...]


def span_kernel(heads, size, *refs):
    packets, out_ref, held = refs[:CHIPS], refs[CHIPS], refs[CHIPS + 1]
    in_order(packets, held)
    decays = [get_decay(held.at[b], heads, size) for b in range(CHIPS)]
    for j in range(heads):
        rows = slice(j * size, (j + 1) * size)
        acc = held[0, rows, :].astype(F32)
        for b in range(1, CHIPS):
            acc = acc * decays[b][j : j + 1] + held[b, rows, :].astype(F32)
        out_ref[rows, :] = acc.astype(BF16)
    whole = decays[0]
    for b in range(1, CHIPS):
        whole = whole * decays[b]
    put_decay(out_ref, whole, heads, size)


def spread_kernel(heads, size, *refs):
    packets, before, out_ref, held = refs[:CHIPS], refs[CHIPS], refs[CHIPS + 1], refs[CHIPS + 2]
    _, chip = position()
    later = lax.axis_index("ctx") >= SPAN
    in_order(packets, held)
    decays = [get_decay(held.at[b], heads, size) for b in range(CHIPS)]
    for j in range(heads):
        rows = slice(j * size, (j + 1) * size)
        acc = jnp.where(later, before[rows, :].astype(F32), 0.0)
        out_ref[chip, rows, :] = acc.astype(BF16)
        for b in range(1, CHIPS):
            acc = acc * decays[b - 1][j : j + 1] + held[b - 1, rows, :].astype(F32)
            out_ref[chip ^ b, rows, :] = acc.astype(BF16)


def out_kernel(items, heads, size, *refs):
    q_ref, cum_ref, gain_ref = refs[:3]
    per_item = [refs[3 + 3 * i : 6 + 3 * i] for i in range(len(items))]
    out_ref, mixed_ref, done_ref, sems = refs[-4:]
    core, _ = position()
    second = core == 1
    for i, (mine, g) in enumerate(items):
        prefix_ref, intra_ref, sib_ref = per_item[i]
        b = head_group(mine, g)
        started = jnp.exp(cum_ref[b][0:heads]).T
        by = jnp.where(second, get_decay(sib_ref.at[g], heads, size), 1.0)
        for j in range(heads):
            cols = columns(b * heads * size, j * size, size)
            rows = slice(j * size, (j + 1) * size)
            sib = jnp.where(second, sib_ref[g, rows, :].astype(F32), 0.0)
            prefix = prefix_ref[rows, :].astype(F32) * by[j : j + 1] + sib
            inter = lax.dot_general(
                q_ref[:, cols], prefix.astype(BF16), (((1,), (1,)), ((), ())),
                preferred_element_type=F32,
            )
            mixed_ref[i * heads + j] = intra_ref[g * heads + j] + inter * started[:, j : j + 1]
    copies = []
    for i, (mine, g) in enumerate(items):
        b = head_group(mine, g)
        for j in range(heads):
            cols = columns(b * heads * size, j * size, size)
            mixed = mixed_ref[i * heads + j]
            scale = lax.rsqrt(jnp.mean(mixed * mixed, axis=1, keepdims=True) + 1e-05)
            done_ref[i, :, j * size : (j + 1) * size] = (
                mixed * scale * gain_ref[:, cols]
            ).astype(BF16)
        wide = columns(b * heads * size, 0, heads * size)
        copies.append(pltpu.make_async_copy(done_ref.at[i], out_ref.at[:, wide], sems.at[i]))
        copies[-1].start()
    for copy in copies:
        copy.wait()


def join_spans(earlier, later, heads, size):
    base = heads * size

    def decay(x):
        tail = x[base:].astype(F32)
        return tail[0:heads] + tail[heads : 2 * heads] + tail[2 * heads : 3 * heads]

    by = decay(later)
    state = (
        by[:, None, :] * earlier[:base].astype(F32).reshape(heads, size, -1)
        + later[:base].astype(F32).reshape(heads, size, -1)
    ).reshape(base, -1)
    parts = three_parts(by * decay(earlier))
    return jnp.concatenate([state.astype(BF16), *parts, later[base + 3 * heads :]], 0)


def on_device(queries, key_input, value_input, log_decay, conv_weight, norm_gain):
    rows, width = queries.shape
    head_count = log_decay.shape[1]
    size = width // head_count
    heads = head_count // SPAN
    half = CHIPS * heads
    packet = heads * size + PARTS
    n = lax.axis_size("ctx")

    def swap(x, mask):
        return lax.ppermute(x, "ctx", [(i, i ^ mask) for i in range(n)])

    def shift(x, by):
        return lax.ppermute(x, "ctx", [(i, i + by) for i in range(n - by)])

    tail = call(
        tail_kernel,
        "tail",
        pltpu.VMEM((HALO, width), BF16),
        key_input,
        in_specs=[HBM],
        scratch=[pltpu.SemaphoreType.DMA(())],
    )
    halo = shift(tail, 1)
    cum = call(
        functools.partial(cum_kernel, heads),
        "cum",
        pltpu.VMEM((SPAN, 2 * heads, rows), F32),
        log_decay.T, value_input,
    )
    gain = norm_gain.reshape(1, width)
    ext = pltpu.VMEM((heads, rows + HALO, size), F32)
    held = pltpu.VMEM((half, rows, size), BF16)

    def states(mine):
        return call(
            functools.partial(state_kernel, mine, heads, size),
            "states_mine" if mine else "states_other",
            pltpu.VMEM((CHIPS, packet, size), BF16),
            key_input, halo, value_input, conv_weight, cum,
            scratch=[ext, pltpu.VMEM((half, rows, size), BF16)],
        )

    def intra_part(mine, q):
        return call(
            functools.partial(intra_kernel, mine, heads, size),
            "intra_mine" if mine else "intra_other",
            pltpu.VMEM((half, rows, size), F32),
            q, key_input, halo, value_input, conv_weight, cum,
            scratch=[ext, held],
        )

    theirs = states(False)
    got = swap(theirs, 1)
    mine = states(True)
    got_late = swap(mine, 1)

    chip_states = call(
        functools.partial(chip_kernel, heads, size),
        "chip_states",
        pltpu.VMEM((CHIPS, packet, size), BF16),
        mine, got,
    )
    packets = {0: chip_states[0]}
    for g in EXCHANGE:
        packets[g] = swap(chip_states[g], 2 * g)
    q_after, chip_states = lax.optimization_barrier((queries, chip_states))
    intra_mine = intra_part(True, q_after)
    *late, intra_mine = lax.optimization_barrier((*[packets[g] for g in EXCHANGE], intra_mine))
    packets.update(zip(EXCHANGE, late))
    packets = [packets[g] for g in range(CHIPS)]

    order = pltpu.VMEM((CHIPS, packet, size), BF16)
    span = call(
        functools.partial(span_kernel, heads, size),
        "span_state",
        pltpu.VMEM((packet, size), BF16),
        *packets,
        scratch=[order],
    )
    before = swap(span, SPAN) if n == 2 * SPAN else shift(span, SPAN)
    reach = 1
    while reach < n // SPAN - 1:
        before = join_spans(shift(before, SPAN * reach), before, heads, size)
        reach *= 2
    q_after, span = lax.optimization_barrier((queries, span))
    intra_other = intra_part(False, q_after)
    before, intra_other = lax.optimization_barrier((before, intra_other))

    chip_prefix = call(
        functools.partial(spread_kernel, heads, size),
        "chip_prefix",
        pltpu.VMEM((CHIPS, heads * size, size), BF16),
        *packets, before,
        scratch=[order],
    )
    own = {0: chip_prefix[0]}
    for g in EXCHANGE:
        own[g] = swap(chip_prefix[g], 2 * g)
    other = {0: swap(own[0], 1)}

    def output(items, result):
        args = [queries, cum, gain]
        for mine, g in items:
            args += [own[g], intra_mine, got] if mine else [other[g], intra_other, got_late]
        count = len(args)
        extra = [] if result is None else [result]
        return call(
            functools.partial(out_kernel, items, heads, size),
            "out_" + "_".join(("m" if mine else "o") + str(g) for mine, g in items),
            jax.ShapeDtypeStruct((rows, width), BF16),
            *args, *extra,
            in_specs=[VMEM] * count + [HBM] * len(extra),
            out_specs=HBM,
            input_output_aliases={count: 0} if extra else {},
            scratch=[
                pltpu.VMEM((len(items) * heads, rows, size), F32),
                pltpu.VMEM((len(items), rows, heads * size), BF16),
                pltpu.SemaphoreType.DMA((len(items),)),
            ],
        )

    first, *last = EXCHANGE[:1] + EXCHANGE[:0:-1]
    result = output([(True, 0), (False, 0)], None)
    other[first] = swap(own[first], 1)
    *late, result = lax.optimization_barrier((*[own[g] for g in last], result))
    own.update(zip(last, late))
    other.update({g: swap(own[g], 1) for g in last})
    result = output([(True, first), (False, first)], result)
    result = output([(True, g) for g in last], result)
    return output([(False, g) for g in last], result)


def solution(mesh):
    rows = P(("groups", "ctx"), None)
    return jax.shard_map(
        on_device,
        mesh=mesh,
        in_specs=(rows, rows, rows, rows, P(), P()),
        out_specs=rows,
        check_vma=False,
    )
```

```python
import functools

import jax
import jax.numpy as jnp
from jax import lax
from jax.experimental import pallas as pl
from jax.experimental.pallas import tpu as pltpu
from jax.sharding import PartitionSpec as P

F32 = jnp.float32
BF16 = jnp.bfloat16
CHIPS = 4
SPAN = 2 * CHIPS
HALO = 8
EXCHANGE = (1, 3, 2)
PARTS = 16
VMEM = pl.BlockSpec(memory_space=pltpu.VMEM)
HBM = pl.BlockSpec(memory_space=pltpu.HBM)


def position():
    me = lax.axis_index("ctx")
    return me & 1, (me >> 1) & (CHIPS - 1)


def head_group(mine, g):
    core, chip = position()
    return (core if mine else 1 - core) * CHIPS + (chip ^ g)


def columns(block, offset, size):
    return pl.ds(pl.multiple_of(block + offset, size), size)


def call(kernel, name, out_shape, *args, scratch=(), in_specs=None, out_specs=VMEM, **options):
    if in_specs is None:
        in_specs = [VMEM] * len(args)
    args = [
        pltpu.with_memory_space_constraint(x, pltpu.VMEM if s is VMEM else pltpu.HBM)
        for x, s in zip(args, in_specs)
    ]
    return pl.pallas_call(
        kernel,
        out_shape=out_shape,
        in_specs=in_specs,
        out_specs=out_specs,
        scratch_shapes=list(scratch),
        name=name,
        compiler_params=pltpu.CompilerParams(vmem_limit_bytes=6 << 20),
        **options,
    )(*args)


def tail_kernel(k_ref, out_ref, sem):
    rows = k_ref.shape[0]
    copy = pltpu.make_async_copy(k_ref.at[rows - HALO : rows, :], out_ref, sem)
    copy.start()
    copy.wait()


def cum_kernel(heads, decay_ref, out_ref):
    x = decay_ref[...]
    count, rows = x.shape
    upto = lax.broadcasted_iota(jnp.int32, (rows, rows), 0) <= lax.broadcasted_iota(
        jnp.int32, (rows, rows), 1
    )
    parts = jnp.concatenate([p.astype(F32) for p in three_parts(x)], 0).astype(BF16)
    sums = jnp.dot(parts, upto.astype(F32).astype(BF16), preferred_element_type=F32)
    sums = sums[0:count] + (sums[count : 2 * count] + sums[2 * count :])
    total = jnp.broadcast_to(sums[:, rows - 1 : rows], sums.shape)
    for b in range(out_ref.shape[0]):
        these = slice(b * heads, (b + 1) * heads)
        out_ref[b, 0:heads, :] = sums[these]
        out_ref[b, heads : 2 * heads, :] = total[these]


def three_parts(x):
    hi = x.astype(BF16)
    rest = x - hi.astype(F32)
    mid = rest.astype(BF16)
    low = (rest - mid.astype(F32)).astype(BF16)
    return hi, mid, low


def put_decay(out, decays, heads, size):
    base = heads * size
    parts = [p.astype(F32) for p in three_parts(decays)]
    spare = jnp.zeros((PARTS - 3 * heads, decays.shape[1]), F32)
    out[base : base + PARTS, :] = jnp.concatenate(parts + [spare], 0).astype(BF16)


def get_decay(packet, heads, size):
    base = heads * size
    tail = packet[base : base + PARTS, :].astype(F32)
    return tail[0:heads] + tail[heads : 2 * heads] + tail[2 * heads : 3 * heads]


def conv_keys(k_ref, chip_halo_ref, core_halo_ref, w_ref, ext, cols):
    rows = k_ref.shape[0]
    core, _ = position()
    ext[0:HALO, :] = jnp.where(
        core == 0, chip_halo_ref[:, cols].astype(F32), core_halo_ref[:, cols].astype(F32)
    )
    ext[HALO : HALO + rows, :] = k_ref[:, cols].astype(F32)
    total = None
    for j in range(w_ref.shape[0]):
        term = w_ref[j : j + 1, cols] * ext[HALO - j : HALO - j + rows, :]
        total = term if total is None else total + term
    return total.astype(BF16)


def state_kernel(mine, heads, size, k_ref, chip_halo_ref, core_halo_ref, v_ref, w_ref, cum_ref, out_ref,
    ext, held):
    for g in range(CHIPS):
        b = head_group(mine, g)
        cum = cum_ref[b]
        ending = jnp.exp(cum[heads : 2 * heads] - cum[0:heads]).T
        for j in range(heads):
            cols = columns(b * heads * size, j * size, size)
            key_conv = conv_keys(k_ref, chip_halo_ref, core_halo_ref, w_ref, ext.at[j], cols)
            held[g * heads + j] = (key_conv.astype(F32) * ending[:, j : j + 1]).astype(BF16)
    for g in range(CHIPS):
        b = head_group(mine, g)
        for j in range(heads):
            cols = columns(b * heads * size, j * size, size)
            state = lax.dot_general(
                v_ref[:, cols], held[g * heads + j], (((0,), (0,)), ((), ())),
                preferred_element_type=F32,
            )
            out_ref[g, j * size : (j + 1) * size, :] = state.astype(BF16)
        put_decay(out_ref.at[g], jnp.exp(cum_ref[b][heads : 2 * heads]), heads, size)


def intra_kernel(
    mine, heads, size, q_ref, k_ref, chip_halo_ref, core_halo_ref, v_ref, w_ref, cum_ref, out_ref,
    ext, held
):
    rows = q_ref.shape[0]
    causal = lax.broadcasted_iota(jnp.int32, (rows, rows), 0) >= lax.broadcasted_iota(
        jnp.int32, (rows, rows), 1
    )
    for g in range(CHIPS):
        b = head_group(mine, g)
        cum = cum_ref[b][0:heads]
        cum_col = cum.T
        for j in range(heads):
            cols = columns(b * heads * size, j * size, size)
            key_conv = conv_keys(k_ref, chip_halo_ref, core_halo_ref, w_ref, ext.at[j], cols)
            scores = lax.dot_general(
                q_ref[:, cols], key_conv, (((1,), (1,)), ((), ())), preferred_element_type=F32
            )
            spread = cum_col[:, j : j + 1] - cum[j : j + 1]
            weights = jnp.where(causal, scores * jnp.exp(jnp.where(causal, spread, 0.0)), 0.0)
            held[g * heads + j] = weights.astype(BF16)
    for g in range(CHIPS):
        b = head_group(mine, g)
        for j in range(heads):
            cols = columns(b * heads * size, j * size, size)
            out_ref[g * heads + j] = jnp.dot(
                held[g * heads + j], v_ref[:, cols], preferred_element_type=F32
            )


def chip_kernel(heads, size, own_ref, got_ref, out_ref):
    core, _ = position()
    first = core == 0
    for g in range(CHIPS):
        own_decay = get_decay(own_ref.at[g], heads, size)
        got_decay = get_decay(got_ref.at[g], heads, size)
        own_by = jnp.where(first, got_decay, 1.0)
        got_by = jnp.where(first, 1.0, own_decay)
        for j in range(heads):
            rows = slice(j * size, (j + 1) * size)
            out_ref[g, rows, :] = (
                own_ref[g, rows, :].astype(F32) * own_by[j : j + 1]
                + got_ref[g, rows, :].astype(F32) * got_by[j : j + 1]
            ).astype(BF16)
        put_decay(out_ref.at[g], own_decay * got_decay, heads, size)


def in_order(packets, held):
    _, chip = position()
    for g in range(CHIPS):
        held[chip ^ g] = packets[g][...]


def span_kernel(heads, size, *refs):
    packets, out_ref, held = refs[:CHIPS], refs[CHIPS], refs[CHIPS + 1]
    in_order(packets, held)
    decays = [get_decay(held.at[b], heads, size) for b in range(CHIPS)]
    for j in range(heads):
        rows = slice(j * size, (j + 1) * size)
        acc = held[0, rows, :].astype(F32)
        for b in range(1, CHIPS):
            acc = acc * decays[b][j : j + 1] + held[b, rows, :].astype(F32)
        out_ref[rows, :] = acc.astype(BF16)
    whole = decays[0]
    for b in range(1, CHIPS):
        whole = whole * decays[b]
    put_decay(out_ref, whole, heads, size)


def spread_kernel(heads, size, *refs):
    packets, before, out_ref, held = refs[:CHIPS], refs[CHIPS], refs[CHIPS + 1], refs[CHIPS + 2]
    _, chip = position()
    later = lax.axis_index("ctx") >= SPAN
    in_order(packets, held)
    decays = [get_decay(held.at[b], heads, size) for b in range(CHIPS)]
    for j in range(heads):
        rows = slice(j * size, (j + 1) * size)
        acc = jnp.where(later, before[rows, :].astype(F32), 0.0)
        out_ref[chip, rows, :] = acc.astype(BF16)
        for b in range(1, CHIPS):
            acc = acc * decays[b - 1][j : j + 1] + held[b - 1, rows, :].astype(F32)
            out_ref[chip ^ b, rows, :] = acc.astype(BF16)


def out_kernel(items, heads, size, *refs):
    q_ref, cum_ref, gain_ref = refs[:3]
    per_item = [refs[3 + 3 * i : 6 + 3 * i] for i in range(len(items))]
    out_ref, mixed_ref, done_ref, sems = refs[-4:]
    core, _ = position()
    second = core == 1
    for i, (mine, g) in enumerate(items):
        prefix_ref, intra_ref, sib_ref = per_item[i]
        b = head_group(mine, g)
        started = jnp.exp(cum_ref[b][0:heads]).T
        by = jnp.where(second, get_decay(sib_ref.at[g], heads, size), 1.0)
        for j in range(heads):
            cols = columns(b * heads * size, j * size, size)
            rows = slice(j * size, (j + 1) * size)
            sib = jnp.where(second, sib_ref[g, rows, :].astype(F32), 0.0)
            prefix = prefix_ref[rows, :].astype(F32) * by[j : j + 1] + sib
            inter = lax.dot_general(
                q_ref[:, cols], prefix.astype(BF16), (((1,), (1,)), ((), ())),
                preferred_element_type=F32,
            )
            mixed_ref[i * heads + j] = intra_ref[g * heads + j] + inter * started[:, j : j + 1]
    copies = []
    for i, (mine, g) in enumerate(items):
        b = head_group(mine, g)
        for j in range(heads):
            cols = columns(b * heads * size, j * size, size)
            mixed = mixed_ref[i * heads + j]
            scale = lax.rsqrt(jnp.mean(mixed * mixed, axis=1, keepdims=True) + 1e-05)
            done_ref[i, :, j * size : (j + 1) * size] = (
                mixed * scale * gain_ref[:, cols]
            ).astype(BF16)
        wide = columns(b * heads * size, 0, heads * size)
        copies.append(pltpu.make_async_copy(done_ref.at[i], out_ref.at[:, wide], sems.at[i]))
        copies[-1].start()
    for copy in copies:
        copy.wait()


def join_spans(earlier, later, heads, size):
    base = heads * size

    def decay(x):
        tail = x[base:].astype(F32)
        return tail[0:heads] + tail[heads : 2 * heads] + tail[2 * heads : 3 * heads]

    by = decay(later)
    state = (
        by[:, None, :] * earlier[:base].astype(F32).reshape(heads, size, -1)
        + later[:base].astype(F32).reshape(heads, size, -1)
    ).reshape(base, -1)
    parts = three_parts(by * decay(earlier))
    return jnp.concatenate([state.astype(BF16), *parts, later[base + 3 * heads :]], 0)


def on_device(queries, key_input, value_input, log_decay, conv_weight, norm_gain):
    rows, width = queries.shape
    head_count = log_decay.shape[1]
    size = width // head_count
    heads = head_count // SPAN
    half = CHIPS * heads
    packet = heads * size + PARTS
    n = lax.axis_size("ctx")

    def swap(x, mask):
        return lax.ppermute(x, "ctx", [(i, i ^ mask) for i in range(n)])

    def shift(x, by):
        return lax.ppermute(x, "ctx", [(i, i + by) for i in range(n - by)])

    tail = call(
        tail_kernel,
        "tail",
        pltpu.VMEM((HALO, width), BF16),
        key_input,
        in_specs=[HBM],
        scratch=[pltpu.SemaphoreType.DMA(())],
    )
    cum = call(
        functools.partial(cum_kernel, heads),
        "cum",
        pltpu.VMEM((SPAN, 2 * heads, rows), F32),
        log_decay.T,
    )
    tail, cum, keys, values = lax.optimization_barrier((tail, cum, key_input, value_input))
    next_pairs = [(i, i + 1) for i in range(1, n - 1, 2)]
    chip_halo = lax.ppermute(tail, "ctx", next_pairs + [(j, i) for i, j in next_pairs])
    core_halo = swap(tail, 1)
    gain = norm_gain.reshape(1, width)
    ext = pltpu.VMEM((heads, rows + HALO, size), F32)
    held = pltpu.VMEM((half, rows, size), BF16)

    def states(mine):
        return call(
            functools.partial(state_kernel, mine, heads, size),
            "states_mine" if mine else "states_other",
            pltpu.VMEM((CHIPS, packet, size), BF16),
            keys, chip_halo, core_halo, values, conv_weight, cum,
            scratch=[ext, pltpu.VMEM((half, rows, size), BF16)],
        )

    def intra_part(mine, q):
        return call(
            functools.partial(intra_kernel, mine, heads, size),
            "intra_mine" if mine else "intra_other",
            pltpu.VMEM((half, rows, size), F32),
            q, keys, chip_halo, core_halo, values, conv_weight, cum,
            scratch=[ext, held],
        )

    theirs = states(False)
    got = swap(theirs, 1)
    mine = states(True)
    got_late = swap(mine, 1)

    chip_states = call(
        functools.partial(chip_kernel, heads, size),
        "chip_states",
        pltpu.VMEM((CHIPS, packet, size), BF16),
        mine, got,
    )
    packets = {0: chip_states[0]}
    for g in EXCHANGE:
        packets[g] = swap(chip_states[g], 2 * g)
    q_after, chip_states = lax.optimization_barrier((queries, chip_states))
    intra_mine = intra_part(True, q_after)
    *late, intra_mine = lax.optimization_barrier((*[packets[g] for g in EXCHANGE], intra_mine))
    packets.update(zip(EXCHANGE, late))
    packets = [packets[g] for g in range(CHIPS)]

    order = pltpu.VMEM((CHIPS, packet, size), BF16)
    span = call(
        functools.partial(span_kernel, heads, size),
        "span_state",
        pltpu.VMEM((packet, size), BF16),
        *packets,
        scratch=[order],
    )
    before = swap(span, SPAN) if n == 2 * SPAN else shift(span, SPAN)
    reach = 1
    while reach < n // SPAN - 1:
        before = join_spans(shift(before, SPAN * reach), before, heads, size)
        reach *= 2
    q_after, span = lax.optimization_barrier((queries, span))
    intra_other = intra_part(False, q_after)
    before, intra_other = lax.optimization_barrier((before, intra_other))

    chip_prefix = call(
        functools.partial(spread_kernel, heads, size),
        "chip_prefix",
        pltpu.VMEM((CHIPS, heads * size, size), BF16),
        *packets, before,
        scratch=[order],
    )
    own = {0: chip_prefix[0]}
    for g in EXCHANGE:
        own[g] = swap(chip_prefix[g], 2 * g)
    other = {0: swap(own[0], 1)}

    def output(items, result):
        args = [queries, cum, gain]
        for mine, g in items:
            args += [own[g], intra_mine, got] if mine else [other[g], intra_other, got_late]
        count = len(args)
        extra = [] if result is None else [result]
        return call(
            functools.partial(out_kernel, items, heads, size),
            "out_" + "_".join(("m" if mine else "o") + str(g) for mine, g in items),
            jax.ShapeDtypeStruct((rows, width), BF16),
            *args, *extra,
            in_specs=[VMEM] * count + [HBM] * len(extra),
            out_specs=HBM,
            input_output_aliases={count: 0} if extra else {},
            cost_estimate=pl.CostEstimate(flops=1, transcendentals=0, bytes_accessed=1),
            scratch=[
                pltpu.VMEM((len(items) * heads, rows, size), F32),
                pltpu.VMEM((len(items), rows, heads * size), BF16),
                pltpu.SemaphoreType.DMA((len(items),)),
            ],
        )

    first, *last = EXCHANGE
    result = output([(True, 0), (False, 0)], None)
    own[first], result = lax.optimization_barrier((own[first], result))
    other[first] = swap(own[first], 1)
    result = output([(True, first)], result)
    *late, result = lax.optimization_barrier((*[own[g] for g in last], result))
    own.update(zip(last, late))
    other.update({g: swap(own[g], 1) for g in last})
    result = output([(False, first)] + [(True, g) for g in last], result)
    return output([(False, g) for g in last], result)


def solution(mesh):
    rows = P(("groups", "ctx"), None)
    return jax.shard_map(
        on_device,
        mesh=mesh,
        in_specs=(rows, rows, rows, rows, P(), P()),
        out_specs=rows,
        check_vma=False,
    )
```

```python
import functools

import jax
import jax.numpy as jnp
from jax import lax
from jax.experimental import pallas as pl
from jax.experimental.pallas import tpu as pltpu
from jax.sharding import PartitionSpec as P

F32 = jnp.float32
BF16 = jnp.bfloat16
CHIPS = 4
SPAN = 2 * CHIPS
HALO = 8
EXCHANGE = (1, 3, 2)
PARTS = 16
VMEM = pl.BlockSpec(memory_space=pltpu.VMEM)
HBM = pl.BlockSpec(memory_space=pltpu.HBM)


def position():
    me = lax.axis_index("ctx")
    return me & 1, (me >> 1) & (CHIPS - 1)


def head_group(mine, g):
    core, chip = position()
    return (core if mine else 1 - core) * CHIPS + (chip ^ g)


def columns(block, offset, size):
    return pl.ds(pl.multiple_of(block + offset, size), size)


def call(kernel, name, out_shape, *args, scratch=(), in_specs=None, out_specs=VMEM, **options):
    if in_specs is None:
        in_specs = [VMEM] * len(args)
    args = [
        pltpu.with_memory_space_constraint(x, pltpu.VMEM if s is VMEM else pltpu.HBM)
        for x, s in zip(args, in_specs)
    ]
    return pl.pallas_call(
        kernel,
        out_shape=out_shape,
        in_specs=in_specs,
        out_specs=out_specs,
        scratch_shapes=list(scratch),
        name=name,
        compiler_params=pltpu.CompilerParams(vmem_limit_bytes=6 << 20),
        **options,
    )(*args)


def tail_kernel(k_ref, out_ref):
    rows = k_ref.shape[0]
    out_ref[...] = k_ref[rows - HALO : rows, :]


def cum_kernel(heads, decay_ref, out_ref):
    x = decay_ref[...]
    count, rows = x.shape
    upto = lax.broadcasted_iota(jnp.int32, (rows, rows), 0) <= lax.broadcasted_iota(
        jnp.int32, (rows, rows), 1
    )
    parts = jnp.concatenate([p.astype(F32) for p in three_parts(x)], 0).astype(BF16)
    sums = jnp.dot(parts, upto.astype(F32).astype(BF16), preferred_element_type=F32)
    sums = sums[0:count] + (sums[count : 2 * count] + sums[2 * count :])
    total = jnp.broadcast_to(sums[:, rows - 1 : rows], sums.shape)
    for b in range(out_ref.shape[0]):
        these = slice(b * heads, (b + 1) * heads)
        out_ref[b, 0:heads, :] = sums[these]
        out_ref[b, heads : 2 * heads, :] = total[these]


def three_parts(x):
    hi = x.astype(BF16)
    rest = x - hi.astype(F32)
    mid = rest.astype(BF16)
    low = (rest - mid.astype(F32)).astype(BF16)
    return hi, mid, low


def side(part, heads, size):
    base = heads * size + part * PARTS
    return slice(base, base + PARTS)


def padded(rows):
    rows = jnp.concatenate(rows, 0)
    spare = jnp.zeros((PARTS - rows.shape[0], rows.shape[1]), F32)
    return jnp.concatenate([rows, spare], 0).astype(BF16)


def put_decay(out, decays, heads, size):
    out[side(0, heads, size), :] = padded([p.astype(F32) for p in three_parts(decays)])


def get_decay(packet, heads, size):
    tail = packet[side(0, heads, size), :].astype(F32)
    return tail[0:heads] + tail[heads : 2 * heads] + tail[2 * heads : 3 * heads]


def edge_states(values, edges, heads):
    row = lax.broadcasted_iota(jnp.int32, values.shape, 0)
    out = []
    for j in range(heads):
        picked = jnp.where(lax.rem(row, heads) == j, values.astype(F32), 0.0).astype(BF16)
        out.append(
            lax.dot_general(picked, edges, (((0,), (0,)), ((), ())), preferred_element_type=F32)
        )
    return out


def conv_keys(k_ref, halo, w_ref, ext, cols):
    rows = k_ref.shape[0]
    ext[0:HALO, :] = halo
    ext[HALO : HALO + rows, :] = k_ref[:, cols].astype(F32)
    total = None
    for j in range(w_ref.shape[0]):
        term = w_ref[j : j + 1, cols] * ext[HALO - j : HALO - j + rows, :]
        total = term if total is None else total + term
    return total.astype(BF16)


def state_kernel(
    mine, heads, size, k_hbm, v_hbm, w_hbm, decay_hbm, out_ref,
    k_buf, v_buf, w_buf, decay_buf, cum_ref, ext, held, sems,
):
    rows, wide = k_buf.shape[1:]
    taps = w_buf.shape[1]
    copies = [pltpu.make_async_copy(decay_hbm, decay_buf, sems.at[3 * CHIPS])]
    copies[0].start()
    for g in range(CHIPS):
        cols = columns(head_group(mine, g) * wide, 0, wide)
        for i, (source, buf) in enumerate(((k_hbm, k_buf), (w_hbm, w_buf), (v_hbm, v_buf))):
            copies.append(
                pltpu.make_async_copy(source.at[:, cols], buf.at[g], sems.at[3 * g + i])
            )
            copies[-1].start()
    copies[0].wait()
    cum_kernel(heads, decay_buf, cum_ref)
    none = jnp.zeros((HALO, size), F32)
    for g in range(CHIPS):
        for copy in copies[1 + 3 * g : 4 + 3 * g]:
            copy.wait()
        cum = cum_ref[head_group(mine, g)]
        ending = jnp.exp(cum[heads : 2 * heads] - cum[0:heads]).T
        edges, values = [], []
        for j in range(heads):
            cols = slice(j * size, (j + 1) * size)
            key_conv = conv_keys(k_buf.at[g], none, w_buf.at[g], ext.at[j], cols)
            held[g * heads + j] = (key_conv.astype(F32) * ending[:, j : j + 1]).astype(BF16)
            last = k_buf[g, rows - HALO : rows, cols].astype(F32)
            head_edges = []
            for t in range(taps - 1):
                terms = [
                    w_buf[g, i : i + 1, cols] * last[HALO + t - i : HALO + t - i + 1]
                    for i in range(t + 1, taps)
                ]
                head_edges.append(sum(terms[1:], terms[0]))
            edges.append(head_edges)
            values.append(v_buf[g, 0:HALO, cols].astype(F32) * ending[0:HALO, j : j + 1])
        put_decay(out_ref.at[g], jnp.exp(cum[heads : 2 * heads]), heads, size)
        out_ref[g, side(1, heads, size), :] = padded(
            [edges[j][t] for t in range(taps - 1) for j in range(heads)]
        )
        out_ref[g, side(2, heads, size), :] = padded(
            [values[j][t : t + 1] for t in range(taps - 1) for j in range(heads)]
        )
    for g in range(CHIPS):
        for j in range(heads):
            cols = slice(j * size, (j + 1) * size)
            state = lax.dot_general(
                v_buf[g, :, cols], held[g * heads + j], (((0,), (0,)), ((), ())),
                preferred_element_type=F32,
            )
            out_ref[g, cols, :] = state.astype(BF16)


def intra_kernel(
    mine, heads, size, q_ref, k_ref, chip_halo_ref, core_halo_ref, v_ref, w_ref, cum_ref, out_ref,
    ext, held,
):
    rows = q_ref.shape[0]
    core, _ = position()
    causal = lax.broadcasted_iota(jnp.int32, (rows, rows), 0) >= lax.broadcasted_iota(
        jnp.int32, (rows, rows), 1
    )
    for g in range(CHIPS):
        b = head_group(mine, g)
        cum = cum_ref[b][0:heads]
        cum_col = cum.T
        for j in range(heads):
            cols = columns(b * heads * size, j * size, size)
            halo = jnp.where(
                core == 0, chip_halo_ref[:, cols].astype(F32), core_halo_ref[:, cols].astype(F32)
            )
            key_conv = conv_keys(k_ref, halo, w_ref, ext.at[j], cols)
            scores = lax.dot_general(
                q_ref[:, cols], key_conv, (((1,), (1,)), ((), ())), preferred_element_type=F32
            )
            spread = cum_col[:, j : j + 1] - cum[j : j + 1]
            weights = jnp.where(causal, scores * jnp.exp(jnp.where(causal, spread, 0.0)), 0.0)
            held[g * heads + j] = weights.astype(BF16)
    for g in range(CHIPS):
        b = head_group(mine, g)
        for j in range(heads):
            cols = columns(b * heads * size, j * size, size)
            out_ref[g * heads + j] = jnp.dot(
                held[g * heads + j], v_ref[:, cols], preferred_element_type=F32
            )


def chip_kernel(heads, size, own_ref, got_ref, out_ref):
    core, _ = position()
    first = core == 0
    for g in range(CHIPS):
        own_decay = get_decay(own_ref.at[g], heads, size)
        got_decay = get_decay(got_ref.at[g], heads, size)
        own_by = jnp.where(first, got_decay, 1.0)
        got_by = jnp.where(first, 1.0, own_decay)

        def earlier_later(part):
            own = own_ref[g, side(part, heads, size), :].astype(F32)
            got = got_ref[g, side(part, heads, size), :].astype(F32)
            return jnp.where(first, own, got), jnp.where(first, got, own)

        edges, out_edges = earlier_later(1)
        out_values, values = earlier_later(2)
        fixes = edge_states(values.astype(BF16), edges.astype(BF16), heads)
        for j in range(heads):
            rows = slice(j * size, (j + 1) * size)
            out_ref[g, rows, :] = (
                own_ref[g, rows, :].astype(F32) * own_by[j : j + 1]
                + got_ref[g, rows, :].astype(F32) * got_by[j : j + 1]
                + fixes[j]
            ).astype(BF16)
        put_decay(out_ref.at[g], own_decay * got_decay, heads, size)
        later_by = jnp.where(first, got_decay, own_decay)
        out_ref[g, side(1, heads, size), :] = out_edges.astype(BF16)
        out_ref[g, side(2, heads, size), :] = padded(
            [out_values[t * heads : (t + 1) * heads] * later_by for t in range(3)]
        )


def in_order(packets, held):
    _, chip = position()
    for g in range(CHIPS):
        held[chip ^ g] = packets[g][...]


def chip_fixes(held, b, edges, heads, size):
    return edge_states(held[b, side(2, heads, size), :], edges, heads)


def last_edge_kernel(heads, size, *refs):
    packets, out_ref, held = refs[:CHIPS], refs[CHIPS], refs[CHIPS + 1]
    in_order(packets, held)
    out_ref[...] = held[CHIPS - 1, side(1, heads, size), :]


def span_kernel(heads, size, *refs):
    packets, before, (out_ref, held) = refs[:CHIPS], refs[CHIPS:-2], refs[-2:]
    in_order(packets, held)
    decays = [get_decay(held.at[b], heads, size) for b in range(CHIPS)]
    fixes = [
        chip_fixes(held, b, held[b - 1, side(1, heads, size), :], heads, size)
        for b in range(1, CHIPS)
    ]
    fixes.insert(0, chip_fixes(held, 0, before[0][...], heads, size) if before else None)
    for j in range(heads):
        rows = slice(j * size, (j + 1) * size)
        acc = held[0, rows, :].astype(F32)
        if before:
            acc = acc + fixes[0][j]
        for b in range(1, CHIPS):
            acc = acc * decays[b][j : j + 1] + (held[b, rows, :].astype(F32) + fixes[b][j])
        out_ref[rows, :] = acc.astype(BF16)
    whole = decays[0]
    for b in range(1, CHIPS):
        whole = whole * decays[b]
    put_decay(out_ref, whole, heads, size)
    out_ref[side(1, heads, size), :] = held[CHIPS - 1, side(1, heads, size), :]
    out_ref[side(2, heads, size), :] = held[0, side(2, heads, size), :]


def spread_kernel(heads, size, *refs):
    packets, before, known, (out_ref, held) = refs[:CHIPS], refs[CHIPS], refs[CHIPS + 1 : -2], refs[-2:]
    _, chip = position()
    later = lax.axis_index("ctx") >= SPAN
    in_order(packets, held)
    decays = [get_decay(held.at[b], heads, size) for b in range(CHIPS)]
    edges = known[0][...] if known else before[side(1, heads, size), :]
    edges = [jnp.where(later, edges.astype(F32), 0.0).astype(BF16)]
    edges += [held[b, side(1, heads, size), :] for b in range(CHIPS - 1)]
    fixes = [chip_fixes(held, b, edges[b], heads, size) for b in range(CHIPS - 1)]
    for j in range(heads):
        rows = slice(j * size, (j + 1) * size)
        acc = jnp.where(later, before[rows, :].astype(F32), 0.0)
        out_ref[chip, rows, :] = acc.astype(BF16)
        for b in range(1, CHIPS):
            acc = acc * decays[b - 1][j : j + 1] + (
                held[b - 1, rows, :].astype(F32) + fixes[b - 1][j]
            )
            out_ref[chip ^ b, rows, :] = acc.astype(BF16)
    for b in range(CHIPS):
        out_ref[chip ^ b, heads * size : heads * size + PARTS, :] = edges[b]


def out_kernel(items, heads, size, *refs):
    q_ref, cum_ref, gain_ref = refs[:3]
    per_item = [refs[3 + 3 * i : 6 + 3 * i] for i in range(len(items))]
    out_ref, mixed_ref, done_ref, sems = refs[-4:]
    core, _ = position()
    second = core == 1
    for i, (mine, g) in enumerate(items):
        prefix_ref, intra_ref, sib_ref = per_item[i]
        b = head_group(mine, g)
        started = jnp.exp(cum_ref[b][0:heads]).T
        by = jnp.where(second, get_decay(sib_ref.at[g], heads, size), 1.0)
        fixes = edge_states(
            sib_ref[g, side(2, heads, size), :],
            prefix_ref[heads * size : heads * size + PARTS, :],
            heads,
        )
        for j in range(heads):
            cols = columns(b * heads * size, j * size, size)
            rows = slice(j * size, (j + 1) * size)
            sib = jnp.where(second, sib_ref[g, rows, :].astype(F32) + fixes[j], 0.0)
            prefix = prefix_ref[rows, :].astype(F32) * by[j : j + 1] + sib
            inter = lax.dot_general(
                q_ref[:, cols], prefix.astype(BF16), (((1,), (1,)), ((), ())),
                preferred_element_type=F32,
            )
            mixed_ref[i * heads + j] = intra_ref[g * heads + j] + inter * started[:, j : j + 1]
    copies = []
    for i, (mine, g) in enumerate(items):
        b = head_group(mine, g)
        for j in range(heads):
            cols = columns(b * heads * size, j * size, size)
            mixed = mixed_ref[i * heads + j]
            scale = lax.rsqrt(jnp.mean(mixed * mixed, axis=1, keepdims=True) + 1e-05)
            done_ref[i, :, j * size : (j + 1) * size] = (
                mixed * scale * gain_ref[:, cols]
            ).astype(BF16)
        wide = columns(b * heads * size, 0, heads * size)
        copies.append(pltpu.make_async_copy(done_ref.at[i], out_ref.at[:, wide], sems.at[i]))
        copies[-1].start()
    for copy in copies:
        copy.wait()


def join_spans(earlier, later, heads, size):
    base = heads * size
    own = side(0, heads, size)

    def decay(x):
        tail = x[own].astype(F32)
        return tail[0:heads] + tail[heads : 2 * heads] + tail[2 * heads : 3 * heads]

    by = decay(later)
    state = (
        by[:, None, :] * earlier[:base].astype(F32).reshape(heads, size, -1)
        + later[:base].astype(F32).reshape(heads, size, -1)
    ).reshape(base, -1)
    parts = three_parts(by * decay(earlier))
    return jnp.concatenate([state.astype(BF16), *parts, later[base + 3 * heads :]], 0)


def on_device(queries, key_input, value_input, log_decay, conv_weight, norm_gain):
    rows, width = queries.shape
    head_count = log_decay.shape[1]
    size = width // head_count
    heads = head_count // SPAN
    taps = conv_weight.shape[0]
    half = CHIPS * heads
    packet = heads * size + 3 * PARTS
    n = lax.axis_size("ctx")

    def swap(x, mask):
        return lax.ppermute(x, "ctx", [(i, i ^ mask) for i in range(n)])

    def shift(x, by):
        return lax.ppermute(x, "ctx", [(i, i + by) for i in range(n - by)])

    gain = norm_gain.reshape(1, width)
    ext = pltpu.VMEM((heads, rows + HALO, size), F32)
    held = pltpu.VMEM((half, rows, size), BF16)

    def states(mine):
        return call(
            functools.partial(state_kernel, mine, heads, size),
            "states_mine" if mine else "states_other",
            pltpu.VMEM((CHIPS, packet, size), BF16),
            key_input, value_input, conv_weight, log_decay.T,
            in_specs=[HBM] * 4,
            scratch=[
                pltpu.VMEM((CHIPS, rows, heads * size), BF16),
                pltpu.VMEM((CHIPS, rows, heads * size), BF16),
                pltpu.VMEM((CHIPS, taps, heads * size), F32),
                pltpu.VMEM((head_count, rows), F32),
                pltpu.VMEM((SPAN, 2 * heads, rows), F32),
                ext,
                held,
                pltpu.SemaphoreType.DMA((3 * CHIPS + 1,)),
            ],
        )

    def intra_part(mine, q):
        return call(
            functools.partial(intra_kernel, mine, heads, size),
            "intra_mine" if mine else "intra_other",
            pltpu.VMEM((half, rows, size), F32),
            q, key_input, chip_halo, core_halo, value_input, conv_weight, cum,
            scratch=[ext, held],
        )

    theirs = states(False)
    got = swap(theirs, 1)
    mine = states(True)
    got_late = swap(mine, 1)

    chip_states = call(
        functools.partial(chip_kernel, heads, size),
        "chip_states",
        pltpu.VMEM((CHIPS, packet, size), BF16),
        mine, got,
    )
    packets = {0: chip_states[0]}
    for g in EXCHANGE:
        packets[g] = swap(chip_states[g], 2 * g)
    keys_after, decay_after, chip_states = lax.optimization_barrier(
        (key_input, log_decay, chip_states)
    )
    cum = call(
        functools.partial(cum_kernel, heads),
        "cum",
        pltpu.VMEM((SPAN, 2 * heads, rows), F32),
        decay_after.T,
    )
    tail = call(tail_kernel, "tail", pltpu.VMEM((HALO, width), BF16), keys_after)
    next_pairs = [(i, i + 1) for i in range(1, n - 1, 2)]
    chip_halo = lax.ppermute(tail, "ctx", next_pairs + [(j, i) for i, j in next_pairs])
    core_halo = swap(tail, 1)
    *late, chip_halo, core_halo = lax.optimization_barrier(
        (*[packets[g] for g in EXCHANGE], chip_halo, core_halo)
    )
    packets.update(zip(EXCHANGE, late))
    packets = [packets[g] for g in range(CHIPS)]

    order = pltpu.VMEM((CHIPS, packet, size), BF16)
    known = []
    if n > 2 * SPAN:
        edge = call(
            functools.partial(last_edge_kernel, heads, size),
            "last_edge",
            pltpu.VMEM((PARTS, size), BF16),
            *packets,
            scratch=[order],
        )
        known = [shift(edge, SPAN)]
    span = call(
        functools.partial(span_kernel, heads, size),
        "span_state",
        pltpu.VMEM((packet, size), BF16),
        *packets, *known,
        scratch=[order],
    )
    before = swap(span, SPAN) if n == 2 * SPAN else shift(span, SPAN)
    reach = 1
    while reach < n // SPAN - 1:
        before = join_spans(shift(before, SPAN * reach), before, heads, size)
        reach *= 2
    q_after, span = lax.optimization_barrier((queries, span))
    intra_mine = intra_part(True, q_after)
    intra_other = intra_part(False, q_after)
    before, intra_mine, intra_other = lax.optimization_barrier((before, intra_mine, intra_other))

    chip_prefix = call(
        functools.partial(spread_kernel, heads, size),
        "chip_prefix",
        pltpu.VMEM((CHIPS, heads * size + PARTS, size), BF16),
        *packets, before, *known,
        scratch=[order],
    )
    own = {0: chip_prefix[0]}
    for g in EXCHANGE:
        own[g] = swap(chip_prefix[g], 2 * g)
    other = {0: swap(own[0], 1)}

    def output(items, result):
        args = [queries, cum, gain]
        for mine, g in items:
            args += [own[g], intra_mine, got] if mine else [other[g], intra_other, got_late]
        count = len(args)
        extra = [] if result is None else [result]
        return call(
            functools.partial(out_kernel, items, heads, size),
            "out_" + "_".join(("m" if mine else "o") + str(g) for mine, g in items),
            jax.ShapeDtypeStruct((rows, width), BF16),
            *args, *extra,
            in_specs=[VMEM] * count + [HBM] * len(extra),
            out_specs=HBM,
            input_output_aliases={count: 0} if extra else {},
            cost_estimate=pl.CostEstimate(flops=1, transcendentals=0, bytes_accessed=1),
            scratch=[
                pltpu.VMEM((len(items) * heads, rows, size), F32),
                pltpu.VMEM((len(items), rows, heads * size), BF16),
                pltpu.SemaphoreType.DMA((len(items),)),
            ],
        )

    result = output([(True, 0), (False, 0)], None)
    *late, result = lax.optimization_barrier((*[own[g] for g in EXCHANGE], result))
    own.update(zip(EXCHANGE, late))
    other.update({g: swap(own[g], 1) for g in EXCHANGE})
    result = output([(True, g) for g in EXCHANGE], result)
    return output([(False, g) for g in EXCHANGE], result)


def solution(mesh):
    rows = P(("groups", "ctx"), None)
    return jax.shard_map(
        on_device,
        mesh=mesh,
        in_specs=(rows, rows, rows, rows, P(), P()),
        out_specs=rows,
        check_vma=False,
    )
```

```python
import functools

import jax
import jax.numpy as jnp
from jax import lax
from jax.experimental import pallas as pl
from jax.experimental.pallas import tpu as pltpu
from jax.sharding import PartitionSpec as P

F32 = jnp.float32
BF16 = jnp.bfloat16
CHIPS = 4
SPAN = 2 * CHIPS
HALO = 8
EXCHANGE = (1, 3, 2)
PARTS = 16
VMEM = pl.BlockSpec(memory_space=pltpu.VMEM)
HBM = pl.BlockSpec(memory_space=pltpu.HBM)


def position():
    me = lax.axis_index("ctx")
    return me & 1, (me >> 1) & (CHIPS - 1)


def head_group(mine, g):
    core, chip = position()
    return (core if mine else 1 - core) * CHIPS + (chip ^ g)


def columns(block, offset, size):
    return pl.ds(pl.multiple_of(block + offset, size), size)


def call(kernel, name, out_shape, *args, scratch=(), in_specs=None, out_specs=VMEM, **options):
    if in_specs is None:
        in_specs = [VMEM] * len(args)
    args = [
        pltpu.with_memory_space_constraint(x, pltpu.VMEM if s is VMEM else pltpu.HBM)
        for x, s in zip(args, in_specs)
    ]
    return pl.pallas_call(
        kernel,
        out_shape=out_shape,
        in_specs=in_specs,
        out_specs=out_specs,
        scratch_shapes=list(scratch),
        name=name,
        compiler_params=pltpu.CompilerParams(vmem_limit_bytes=6 << 20),
        **options,
    )(*args)


def cum_kernel(heads, decay_ref, out_ref):
    x = decay_ref[...]
    count, rows = x.shape
    upto = lax.broadcasted_iota(jnp.int32, (rows, rows), 0) <= lax.broadcasted_iota(
        jnp.int32, (rows, rows), 1
    )
    parts = jnp.concatenate([p.astype(F32) for p in three_parts(x)], 0).astype(BF16)
    sums = jnp.dot(parts, upto.astype(F32).astype(BF16), preferred_element_type=F32)
    sums = sums[0:count] + (sums[count : 2 * count] + sums[2 * count :])
    total = jnp.broadcast_to(sums[:, rows - 1 : rows], sums.shape)
    for b in range(out_ref.shape[0]):
        these = slice(b * heads, (b + 1) * heads)
        out_ref[b, 0:heads, :] = sums[these]
        out_ref[b, heads : 2 * heads, :] = total[these]


def three_parts(x):
    hi = x.astype(BF16)
    rest = x - hi.astype(F32)
    mid = rest.astype(BF16)
    low = (rest - mid.astype(F32)).astype(BF16)
    return hi, mid, low


def side(part, heads, size):
    base = heads * size + part * PARTS
    return slice(base, base + PARTS)


def padded(rows):
    rows = jnp.concatenate(rows, 0)
    spare = jnp.zeros((PARTS - rows.shape[0], rows.shape[1]), F32)
    return jnp.concatenate([rows, spare], 0).astype(BF16)


def put_decay(out, decays, heads, size):
    out[side(0, heads, size), :] = padded([p.astype(F32) for p in three_parts(decays)])


def get_decay(packet, heads, size):
    tail = packet[side(0, heads, size), :].astype(F32)
    return tail[0:heads] + tail[heads : 2 * heads] + tail[2 * heads : 3 * heads]


def edge_states(values, edges, heads):
    row = lax.broadcasted_iota(jnp.int32, values.shape, 0)
    out = []
    for j in range(heads):
        picked = jnp.where(lax.rem(row, heads) == j, values.astype(F32), 0.0).astype(BF16)
        out.append(
            lax.dot_general(picked, edges, (((0,), (0,)), ((), ())), preferred_element_type=F32)
        )
    return out


def conv_keys(k_ref, halo, w_ref, ext, cols):
    rows = k_ref.shape[0]
    ext[0:HALO, :] = halo
    ext[HALO : HALO + rows, :] = k_ref[:, cols].astype(F32)
    total = None
    for j in range(w_ref.shape[0]):
        term = w_ref[j : j + 1, cols] * ext[HALO - j : HALO - j + rows, :]
        total = term if total is None else total + term
    return total.astype(BF16)


def state_kernel(
    mine, heads, size, k_hbm, v_hbm, w_hbm, decay_hbm, out_ref,
    k_buf, v_buf, w_buf, decay_buf, cum_ref, ext, held, sems,
):
    rows, wide = k_buf.shape[1:]
    taps = w_buf.shape[1]
    copies = [pltpu.make_async_copy(decay_hbm, decay_buf, sems.at[3 * CHIPS])]
    copies[0].start()
    for g in range(CHIPS):
        cols = columns(head_group(mine, g) * wide, 0, wide)
        for i, (source, buf) in enumerate(((k_hbm, k_buf), (w_hbm, w_buf), (v_hbm, v_buf))):
            copies.append(
                pltpu.make_async_copy(source.at[:, cols], buf.at[g], sems.at[3 * g + i])
            )
            copies[-1].start()
    copies[0].wait()
    cum_kernel(heads, decay_buf, cum_ref)
    none = jnp.zeros((HALO, size), F32)
    for g in range(CHIPS):
        for copy in copies[1 + 3 * g : 4 + 3 * g]:
            copy.wait()
        cum = cum_ref[head_group(mine, g)]
        ending = jnp.exp(cum[heads : 2 * heads] - cum[0:heads]).T
        edges, values = [], []
        for j in range(heads):
            cols = slice(j * size, (j + 1) * size)
            key_conv = conv_keys(k_buf.at[g], none, w_buf.at[g], ext.at[j], cols)
            held[g * heads + j] = (key_conv.astype(F32) * ending[:, j : j + 1]).astype(BF16)
            last = k_buf[g, rows - HALO : rows, cols].astype(F32)
            head_edges = []
            for t in range(taps - 1):
                terms = [
                    w_buf[g, i : i + 1, cols] * last[HALO + t - i : HALO + t - i + 1]
                    for i in range(t + 1, taps)
                ]
                head_edges.append(sum(terms[1:], terms[0]))
            edges.append(head_edges)
            values.append(v_buf[g, 0:HALO, cols].astype(F32) * ending[0:HALO, j : j + 1])
        put_decay(out_ref.at[g], jnp.exp(cum[heads : 2 * heads]), heads, size)
        out_ref[g, side(1, heads, size), :] = padded(
            [edges[j][t] for t in range(taps - 1) for j in range(heads)]
        )
        out_ref[g, side(2, heads, size), :] = padded(
            [values[j][t : t + 1] for t in range(taps - 1) for j in range(heads)]
        )
    for g in range(CHIPS):
        for j in range(heads):
            cols = slice(j * size, (j + 1) * size)
            state = lax.dot_general(
                v_buf[g, :, cols], held[g * heads + j], (((0,), (0,)), ((), ())),
                preferred_element_type=F32,
            )
            out_ref[g, cols, :] = state.astype(BF16)


def intra_kernel(mine, heads, size, q_ref, k_ref, v_ref, w_ref, cum_ref, out_ref, ext, held):
    rows = q_ref.shape[0]
    causal = lax.broadcasted_iota(jnp.int32, (rows, rows), 0) >= lax.broadcasted_iota(
        jnp.int32, (rows, rows), 1
    )
    none = jnp.zeros((HALO, size), F32)
    for g in range(CHIPS):
        b = head_group(mine, g)
        cum = cum_ref[b][0:heads]
        cum_col = cum.T
        growth = jnp.exp(-cum_col[0:HALO])
        values = []
        for j in range(heads):
            cols = columns(b * heads * size, j * size, size)
            key_conv = conv_keys(k_ref, none, w_ref, ext.at[j], cols)
            scores = lax.dot_general(
                q_ref[:, cols], key_conv, (((1,), (1,)), ((), ())), preferred_element_type=F32
            )
            spread = cum_col[:, j : j + 1] - cum[j : j + 1]
            weights = jnp.where(causal, scores * jnp.exp(jnp.where(causal, spread, 0.0)), 0.0)
            held[g * heads + j] = weights.astype(BF16)
            values.append(v_ref[0:HALO, cols].astype(F32) * growth[:, j : j + 1])
        out_ref[CHIPS * heads, g * PARTS : (g + 1) * PARTS, :] = padded(
            [values[j][t : t + 1] for t in range(3) for j in range(heads)]
        ).astype(F32)
    for g in range(CHIPS):
        b = head_group(mine, g)
        for j in range(heads):
            cols = columns(b * heads * size, j * size, size)
            out_ref[g * heads + j] = jnp.dot(
                held[g * heads + j], v_ref[:, cols], preferred_element_type=F32
            )


def chip_kernel(heads, size, own_ref, got_ref, out_ref):
    core, _ = position()
    first = core == 0
    for g in range(CHIPS):
        own_decay = get_decay(own_ref.at[g], heads, size)
        got_decay = get_decay(got_ref.at[g], heads, size)
        own_by = jnp.where(first, got_decay, 1.0)
        got_by = jnp.where(first, 1.0, own_decay)

        def earlier_later(part):
            own = own_ref[g, side(part, heads, size), :].astype(F32)
            got = got_ref[g, side(part, heads, size), :].astype(F32)
            return jnp.where(first, own, got), jnp.where(first, got, own)

        edges, out_edges = earlier_later(1)
        out_values, values = earlier_later(2)
        fixes = edge_states(values.astype(BF16), edges.astype(BF16), heads)
        for j in range(heads):
            rows = slice(j * size, (j + 1) * size)
            out_ref[g, rows, :] = (
                own_ref[g, rows, :].astype(F32) * own_by[j : j + 1]
                + got_ref[g, rows, :].astype(F32) * got_by[j : j + 1]
                + fixes[j]
            ).astype(BF16)
        put_decay(out_ref.at[g], own_decay * got_decay, heads, size)
        later_by = jnp.where(first, got_decay, own_decay)
        out_ref[g, side(1, heads, size), :] = out_edges.astype(BF16)
        out_ref[g, side(2, heads, size), :] = padded(
            [out_values[t * heads : (t + 1) * heads] * later_by for t in range(3)]
        )


def in_order(packets, held):
    _, chip = position()
    for g in range(CHIPS):
        held[chip ^ g] = packets[g][...]


def chip_fixes(held, b, edges, heads, size):
    return edge_states(held[b, side(2, heads, size), :], edges, heads)


def last_edge_kernel(heads, size, *refs):
    packets, out_ref, held = refs[:CHIPS], refs[CHIPS], refs[CHIPS + 1]
    in_order(packets, held)
    out_ref[...] = held[CHIPS - 1, side(1, heads, size), :]


def span_kernel(heads, size, *refs):
    packets, before, (out_ref, held) = refs[:CHIPS], refs[CHIPS:-2], refs[-2:]
    in_order(packets, held)
    decays = [get_decay(held.at[b], heads, size) for b in range(CHIPS)]
    fixes = [
        chip_fixes(held, b, held[b - 1, side(1, heads, size), :], heads, size)
        for b in range(1, CHIPS)
    ]
    fixes.insert(0, chip_fixes(held, 0, before[0][...], heads, size) if before else None)
    for j in range(heads):
        rows = slice(j * size, (j + 1) * size)
        acc = held[0, rows, :].astype(F32)
        if before:
            acc = acc + fixes[0][j]
        for b in range(1, CHIPS):
            acc = acc * decays[b][j : j + 1] + (held[b, rows, :].astype(F32) + fixes[b][j])
        out_ref[rows, :] = acc.astype(BF16)
    whole = decays[0]
    for b in range(1, CHIPS):
        whole = whole * decays[b]
    put_decay(out_ref, whole, heads, size)
    out_ref[side(1, heads, size), :] = held[CHIPS - 1, side(1, heads, size), :]
    out_ref[side(2, heads, size), :] = held[0, side(2, heads, size), :]


def spread_kernel(heads, size, *refs):
    packets, before, known, (out_ref, held) = refs[:CHIPS], refs[CHIPS], refs[CHIPS + 1 : -2], refs[-2:]
    _, chip = position()
    later = lax.axis_index("ctx") >= SPAN
    in_order(packets, held)
    decays = [get_decay(held.at[b], heads, size) for b in range(CHIPS)]
    edges = known[0][...] if known else before[side(1, heads, size), :]
    edges = [jnp.where(later, edges.astype(F32), 0.0).astype(BF16)]
    edges += [held[b, side(1, heads, size), :] for b in range(CHIPS - 1)]
    fixes = [chip_fixes(held, b, edges[b], heads, size) for b in range(CHIPS - 1)]
    for j in range(heads):
        rows = slice(j * size, (j + 1) * size)
        acc = jnp.where(later, before[rows, :].astype(F32), 0.0)
        out_ref[chip, rows, :] = acc.astype(BF16)
        for b in range(1, CHIPS):
            acc = acc * decays[b - 1][j : j + 1] + (
                held[b - 1, rows, :].astype(F32) + fixes[b - 1][j]
            )
            out_ref[chip ^ b, rows, :] = acc.astype(BF16)
    for b in range(CHIPS):
        out_ref[chip ^ b, heads * size : heads * size + PARTS, :] = edges[b]


def out_kernel(items, heads, size, *refs):
    q_ref, cum_ref, gain_ref = refs[:3]
    per_item = [refs[3 + 3 * i : 6 + 3 * i] for i in range(len(items))]
    out_ref, inter_ref, score_ref, done_ref, sems = refs[-5:]
    rows = q_ref.shape[0]
    core, _ = position()
    second = core == 1
    row = lax.broadcasted_iota(jnp.int32, (rows, PARTS), 0)
    edge = lax.broadcasted_iota(jnp.int32, (rows, PARTS), 1)
    seen = [
        (lax.rem(edge, heads) == j) & (lax.div(edge, heads) <= row) & (edge < 3 * heads)
        for j in range(heads)
    ]
    for i, (mine, g) in enumerate(items):
        prefix_ref, intra_ref, sib_ref = per_item[i]
        b = head_group(mine, g)
        by = jnp.where(second, get_decay(sib_ref.at[g], heads, size), 1.0)
        before_chip = prefix_ref[heads * size : heads * size + PARTS, :]
        fixes = edge_states(sib_ref[g, side(2, heads, size), :], before_chip, heads)
        edges = jnp.where(
            second,
            sib_ref[g, side(1, heads, size), :].astype(F32),
            before_chip.astype(F32),
        )
        for j in range(heads):
            cols = columns(b * heads * size, j * size, size)
            these = slice(j * size, (j + 1) * size)
            sib = jnp.where(second, sib_ref[g, these, :].astype(F32) + fixes[j], 0.0)
            prefix = prefix_ref[these, :].astype(F32) * by[j : j + 1] + sib
            both = lax.dot_general(
                q_ref[:, cols],
                jnp.concatenate([prefix, edges], 0).astype(BF16),
                (((1,), (1,)), ((), ())),
                preferred_element_type=F32,
            )
            inter_ref[i * heads + j] = both[:, 0:size]
            score_ref[i * heads + j] = jnp.where(seen[j], both[:, size : size + PARTS], 0.0).astype(
                BF16
            )
    copies = []
    for i, (mine, g) in enumerate(items):
        _, intra_ref, _ = per_item[i]
        b = head_group(mine, g)
        started = jnp.exp(cum_ref[b][0:heads]).T
        values = intra_ref[CHIPS * heads, g * PARTS : (g + 1) * PARTS, :].astype(BF16)
        for j in range(heads):
            cols = columns(b * heads * size, j * size, size)
            edge_part = jnp.dot(
                score_ref[i * heads + j], values, preferred_element_type=F32
            )
            mixed = intra_ref[g * heads + j] + (
                inter_ref[i * heads + j] + edge_part
            ) * started[:, j : j + 1]
            scale = lax.rsqrt(jnp.mean(mixed * mixed, axis=1, keepdims=True) + 1e-05)
            done_ref[i, :, j * size : (j + 1) * size] = (
                mixed * scale * gain_ref[:, cols]
            ).astype(BF16)
        wide = columns(b * heads * size, 0, heads * size)
        copies.append(pltpu.make_async_copy(done_ref.at[i], out_ref.at[:, wide], sems.at[i]))
        copies[-1].start()
    for copy in copies:
        copy.wait()


def join_spans(earlier, later, heads, size):
    base = heads * size
    own = side(0, heads, size)

    def decay(x):
        tail = x[own].astype(F32)
        return tail[0:heads] + tail[heads : 2 * heads] + tail[2 * heads : 3 * heads]

    by = decay(later)
    state = (
        by[:, None, :] * earlier[:base].astype(F32).reshape(heads, size, -1)
        + later[:base].astype(F32).reshape(heads, size, -1)
    ).reshape(base, -1)
    parts = three_parts(by * decay(earlier))
    return jnp.concatenate([state.astype(BF16), *parts, later[base + 3 * heads :]], 0)


def on_device(queries, key_input, value_input, log_decay, conv_weight, norm_gain):
    rows, width = queries.shape
    head_count = log_decay.shape[1]
    size = width // head_count
    heads = head_count // SPAN
    taps = conv_weight.shape[0]
    half = CHIPS * heads
    packet = heads * size + 3 * PARTS
    n = lax.axis_size("ctx")

    def swap(x, mask):
        return lax.ppermute(x, "ctx", [(i, i ^ mask) for i in range(n)])

    def shift(x, by):
        return lax.ppermute(x, "ctx", [(i, i + by) for i in range(n - by)])

    gain = norm_gain.reshape(1, width)
    ext = pltpu.VMEM((heads, rows + HALO, size), F32)
    held = pltpu.VMEM((half, rows, size), BF16)

    def states(mine):
        return call(
            functools.partial(state_kernel, mine, heads, size),
            "states_mine" if mine else "states_other",
            pltpu.VMEM((CHIPS, packet, size), BF16),
            key_input, value_input, conv_weight, log_decay.T,
            in_specs=[HBM] * 4,
            scratch=[
                pltpu.VMEM((CHIPS, rows, heads * size), BF16),
                pltpu.VMEM((CHIPS, rows, heads * size), BF16),
                pltpu.VMEM((CHIPS, taps, heads * size), F32),
                pltpu.VMEM((head_count, rows), F32),
                pltpu.VMEM((SPAN, 2 * heads, rows), F32),
                ext,
                held,
                pltpu.SemaphoreType.DMA((3 * CHIPS + 1,)),
            ],
        )

    def intra_part(mine, q):
        return call(
            functools.partial(intra_kernel, mine, heads, size),
            "intra_mine" if mine else "intra_other",
            pltpu.VMEM((half + 1, rows, size), F32),
            q, key_input, value_input, conv_weight, cum,
            scratch=[ext, held],
        )

    theirs = states(False)
    got = swap(theirs, 1)
    mine = states(True)
    got_late = swap(mine, 1)

    chip_states = call(
        functools.partial(chip_kernel, heads, size),
        "chip_states",
        pltpu.VMEM((CHIPS, packet, size), BF16),
        mine, got,
    )
    packets = {0: chip_states[0]}
    for g in EXCHANGE:
        packets[g] = swap(chip_states[g], 2 * g)
    q_after, decay_after, chip_states = lax.optimization_barrier(
        (queries, log_decay, chip_states)
    )
    cum = call(
        functools.partial(cum_kernel, heads),
        "cum",
        pltpu.VMEM((SPAN, 2 * heads, rows), F32),
        decay_after.T,
    )
    intra_mine = intra_part(True, q_after)
    *late, intra_mine = lax.optimization_barrier((*[packets[g] for g in EXCHANGE], intra_mine))
    packets.update(zip(EXCHANGE, late))
    packets = [packets[g] for g in range(CHIPS)]

    order = pltpu.VMEM((CHIPS, packet, size), BF16)
    known = []
    if n > 2 * SPAN:
        edge = call(
            functools.partial(last_edge_kernel, heads, size),
            "last_edge",
            pltpu.VMEM((PARTS, size), BF16),
            *packets,
            scratch=[order],
        )
        known = [shift(edge, SPAN)]
    span = call(
        functools.partial(span_kernel, heads, size),
        "span_state",
        pltpu.VMEM((packet, size), BF16),
        *packets, *known,
        scratch=[order],
    )
    before = swap(span, SPAN) if n == 2 * SPAN else shift(span, SPAN)
    reach = 1
    while reach < n // SPAN - 1:
        before = join_spans(shift(before, SPAN * reach), before, heads, size)
        reach *= 2
    q_after, span = lax.optimization_barrier((queries, span))
    intra_other = intra_part(False, q_after)
    before, intra_other = lax.optimization_barrier((before, intra_other))

    chip_prefix = call(
        functools.partial(spread_kernel, heads, size),
        "chip_prefix",
        pltpu.VMEM((CHIPS, heads * size + PARTS, size), BF16),
        *packets, before, *known,
        scratch=[order],
    )
    own = {0: chip_prefix[0]}
    for g in EXCHANGE:
        own[g] = swap(chip_prefix[g], 2 * g)
    other = {0: swap(own[0], 1)}

    def output(items, result):
        args = [queries, cum, gain]
        for mine, g in items:
            args += [own[g], intra_mine, got] if mine else [other[g], intra_other, got_late]
        count = len(args)
        extra = [] if result is None else [result]
        return call(
            functools.partial(out_kernel, items, heads, size),
            "out_" + "_".join(("m" if mine else "o") + str(g) for mine, g in items),
            jax.ShapeDtypeStruct((rows, width), BF16),
            *args, *extra,
            in_specs=[VMEM] * count + [HBM] * len(extra),
            out_specs=HBM,
            input_output_aliases={count: 0} if extra else {},
            cost_estimate=pl.CostEstimate(flops=1, transcendentals=0, bytes_accessed=1),
            scratch=[
                pltpu.VMEM((len(items) * heads, rows, size), F32),
                pltpu.VMEM((len(items) * heads, rows, PARTS), BF16),
                pltpu.VMEM((len(items), rows, heads * size), BF16),
                pltpu.SemaphoreType.DMA((len(items),)),
            ],
        )

    result = output([(True, 0), (False, 0)], None)
    *late, result = lax.optimization_barrier((*[own[g] for g in EXCHANGE], result))
    own.update(zip(EXCHANGE, late))
    other.update({g: swap(own[g], 1) for g in EXCHANGE})
    result = output([(True, g) for g in EXCHANGE], result)
    return output([(False, g) for g in EXCHANGE], result)


def solution(mesh):
    rows = P(("groups", "ctx"), None)
    return jax.shard_map(
        on_device,
        mesh=mesh,
        in_specs=(rows, rows, rows, rows, P(), P()),
        out_specs=rows,
        check_vma=False,
    )
```

```python
import functools

import jax
import jax.numpy as jnp
from jax import lax
from jax.experimental import pallas as pl
from jax.experimental.pallas import tpu as pltpu
from jax.sharding import PartitionSpec as P

F32 = jnp.float32
BF16 = jnp.bfloat16
CHIPS = 4
SPAN = 2 * CHIPS
HALO = 8
EXCHANGE = (2, 3, 1)
PARTS = 16
VMEM = pl.BlockSpec(memory_space=pltpu.VMEM)
HBM = pl.BlockSpec(memory_space=pltpu.HBM)


def position():
    me = lax.axis_index("ctx")
    return me & 1, (me >> 1) & (CHIPS - 1)


def head_group(mine, g):
    core, chip = position()
    return (core if mine else 1 - core) * CHIPS + (chip ^ g)


def columns(block, offset, size):
    return pl.ds(pl.multiple_of(block + offset, size), size)


def call(kernel, name, out_shape, *args, scratch=(), in_specs=None, out_specs=VMEM, **options):
    if in_specs is None:
        in_specs = [VMEM] * len(args)
    args = [
        pltpu.with_memory_space_constraint(x, pltpu.VMEM if s is VMEM else pltpu.HBM)
        for x, s in zip(args, in_specs)
    ]
    return pl.pallas_call(
        kernel,
        out_shape=out_shape,
        in_specs=in_specs,
        out_specs=out_specs,
        scratch_shapes=list(scratch),
        name=name,
        compiler_params=pltpu.CompilerParams(vmem_limit_bytes=6 << 20),
        **options,
    )(*args)


def cum_kernel(heads, decay_ref, out_ref):
    x = decay_ref[...]
    count, rows = x.shape
    upto = lax.broadcasted_iota(jnp.int32, (rows, rows), 0) <= lax.broadcasted_iota(
        jnp.int32, (rows, rows), 1
    )
    parts = jnp.concatenate([p.astype(F32) for p in three_parts(x)], 0).astype(BF16)
    sums = jnp.dot(parts, upto.astype(F32).astype(BF16), preferred_element_type=F32)
    sums = sums[0:count] + (sums[count : 2 * count] + sums[2 * count :])
    total = jnp.broadcast_to(sums[:, rows - 1 : rows], sums.shape)
    for b in range(out_ref.shape[0]):
        these = slice(b * heads, (b + 1) * heads)
        out_ref[b, 0:heads, :] = sums[these]
        out_ref[b, heads : 2 * heads, :] = total[these]


def three_parts(x):
    hi = x.astype(BF16)
    rest = x - hi.astype(F32)
    mid = rest.astype(BF16)
    low = (rest - mid.astype(F32)).astype(BF16)
    return hi, mid, low


def side(part, heads, size):
    base = heads * size + part * PARTS
    return slice(base, base + PARTS)


def padded(rows):
    rows = jnp.concatenate(rows, 0)
    spare = jnp.zeros((PARTS - rows.shape[0], rows.shape[1]), F32)
    return jnp.concatenate([rows, spare], 0).astype(BF16)


def put_decay(out, decays, heads, size):
    out[side(1, heads, size), :] = padded([p.astype(F32) for p in three_parts(decays)])


def get_decay(packet, heads, size):
    tail = packet[side(1, heads, size), :].astype(F32)
    return tail[0:heads] + tail[heads : 2 * heads] + tail[2 * heads : 3 * heads]


def edge_states(values, edges, heads):
    row = lax.broadcasted_iota(jnp.int32, values.shape, 0)
    out = []
    for j in range(heads):
        picked = jnp.where(lax.rem(row, heads) == j, values.astype(F32), 0.0).astype(BF16)
        out.append(
            lax.dot_general(picked, edges, (((0,), (0,)), ((), ())), preferred_element_type=F32)
        )
    return out


def conv_keys(k_ref, halo, w_ref, ext, cols):
    rows = k_ref.shape[0]
    ext[0:HALO, :] = halo
    ext[HALO : HALO + rows, :] = k_ref[:, cols].astype(F32)
    total = None
    for j in range(w_ref.shape[0]):
        term = w_ref[j : j + 1, cols] * ext[HALO - j : HALO - j + rows, :]
        total = term if total is None else total + term
    return total.astype(BF16)


def state_kernel(
    mine, heads, size, k_hbm, v_hbm, w_hbm, decay_hbm, out_ref,
    k_buf, v_buf, w_buf, decay_buf, cum_ref, ext, held, sems,
):
    rows, wide = k_buf.shape[1:]
    taps = w_buf.shape[1]
    copies = [pltpu.make_async_copy(decay_hbm, decay_buf, sems.at[3 * CHIPS])]
    copies[0].start()
    for g in range(CHIPS):
        cols = columns(head_group(mine, g) * wide, 0, wide)
        for i, (source, buf) in enumerate(((k_hbm, k_buf), (w_hbm, w_buf), (v_hbm, v_buf))):
            copies.append(
                pltpu.make_async_copy(source.at[:, cols], buf.at[g], sems.at[3 * g + i])
            )
            copies[-1].start()
    copies[0].wait()
    cum_kernel(heads, decay_buf, cum_ref)
    none = jnp.zeros((HALO, size), F32)
    for g in range(CHIPS):
        for copy in copies[1 + 3 * g : 4 + 3 * g]:
            copy.wait()
        cum = cum_ref[head_group(mine, g)]
        ending = jnp.exp(cum[heads : 2 * heads] - cum[0:heads]).T
        edges, values = [], []
        for j in range(heads):
            cols = slice(j * size, (j + 1) * size)
            key_conv = conv_keys(k_buf.at[g], none, w_buf.at[g], ext.at[j], cols)
            held[g * heads + j] = (key_conv.astype(F32) * ending[:, j : j + 1]).astype(BF16)
            last = k_buf[g, rows - HALO : rows, cols].astype(F32)
            head_edges = []
            for t in range(taps - 1):
                terms = [
                    w_buf[g, i : i + 1, cols] * last[HALO + t - i : HALO + t - i + 1]
                    for i in range(t + 1, taps)
                ]
                head_edges.append(sum(terms[1:], terms[0]))
            edges.append(head_edges)
            values.append(v_buf[g, 0:HALO, cols].astype(F32) * ending[0:HALO, j : j + 1])
        put_decay(out_ref.at[g], jnp.exp(cum[heads : 2 * heads]), heads, size)
        out_ref[g, side(0, heads, size), :] = padded(
            [edges[j][t] for t in range(taps - 1) for j in range(heads)]
        )
        out_ref[g, side(2, heads, size), :] = padded(
            [values[j][t : t + 1] for t in range(taps - 1) for j in range(heads)]
        )
    for g in range(CHIPS):
        for j in range(heads):
            cols = slice(j * size, (j + 1) * size)
            state = lax.dot_general(
                v_buf[g, :, cols], held[g * heads + j], (((0,), (0,)), ((), ())),
                preferred_element_type=F32,
            )
            out_ref[g, cols, :] = state.astype(BF16)


def intra_kernel(mine, heads, size, q_ref, k_ref, v_ref, w_ref, cum_ref, out_ref, ext, held):
    rows = q_ref.shape[0]
    causal = lax.broadcasted_iota(jnp.int32, (rows, rows), 0) >= lax.broadcasted_iota(
        jnp.int32, (rows, rows), 1
    )
    none = jnp.zeros((HALO, size), F32)
    for g in range(CHIPS):
        b = head_group(mine, g)
        cum = cum_ref[b][0:heads]
        cum_col = cum.T
        growth = jnp.exp(-cum_col[0:HALO])
        values = []
        for j in range(heads):
            cols = columns(b * heads * size, j * size, size)
            key_conv = conv_keys(k_ref, none, w_ref, ext.at[j], cols)
            scores = lax.dot_general(
                q_ref[:, cols], key_conv, (((1,), (1,)), ((), ())), preferred_element_type=F32
            )
            spread = cum_col[:, j : j + 1] - cum[j : j + 1]
            weights = jnp.where(causal, scores * jnp.exp(jnp.where(causal, spread, 0.0)), 0.0)
            held[g * heads + j] = weights.astype(BF16)
            values.append(v_ref[0:HALO, cols].astype(F32) * growth[:, j : j + 1])
        out_ref[CHIPS * heads, g * PARTS : (g + 1) * PARTS, :] = padded(
            [values[j][t : t + 1] for t in range(3) for j in range(heads)]
        ).astype(F32)
    for g in range(CHIPS):
        b = head_group(mine, g)
        for j in range(heads):
            cols = columns(b * heads * size, j * size, size)
            out_ref[g * heads + j] = jnp.dot(
                held[g * heads + j], v_ref[:, cols], preferred_element_type=F32
            )


def chip_kernel(heads, size, own_ref, got_ref, out_ref):
    core, _ = position()
    first = core == 0
    for g in range(CHIPS):
        own_decay = get_decay(own_ref.at[g], heads, size)
        got_decay = get_decay(got_ref.at[g], heads, size)
        own_by = jnp.where(first, got_decay, 1.0)
        got_by = jnp.where(first, 1.0, own_decay)

        def earlier_later(part):
            own = own_ref[g, side(part, heads, size), :].astype(F32)
            got = got_ref[g, side(part, heads, size), :].astype(F32)
            return jnp.where(first, own, got), jnp.where(first, got, own)

        edges, out_edges = earlier_later(0)
        out_values, values = earlier_later(2)
        fixes = edge_states(values.astype(BF16), edges.astype(BF16), heads)
        for j in range(heads):
            rows = slice(j * size, (j + 1) * size)
            out_ref[g, rows, :] = (
                own_ref[g, rows, :].astype(F32) * own_by[j : j + 1]
                + got_ref[g, rows, :].astype(F32) * got_by[j : j + 1]
                + fixes[j]
            ).astype(BF16)
        put_decay(out_ref.at[g], own_decay * got_decay, heads, size)
        later_by = jnp.where(first, got_decay, own_decay)
        out_ref[g, side(0, heads, size), :] = out_edges.astype(BF16)
        out_ref[g, side(2, heads, size), :] = padded(
            [out_values[t * heads : (t + 1) * heads] * later_by for t in range(3)]
        )


def in_order(packets, held):
    _, chip = position()
    for g in range(CHIPS):
        held[chip ^ g] = packets[g][...]


def chip_fixes(held, b, edges, heads, size):
    return edge_states(held[b, side(2, heads, size), :], edges, heads)


def last_edge_kernel(heads, size, *refs):
    packets, out_ref, held = refs[:CHIPS], refs[CHIPS], refs[CHIPS + 1]
    in_order(packets, held)
    out_ref[...] = held[CHIPS - 1, side(0, heads, size), :]


def span_kernel(heads, size, *refs):
    packets, before, (out_ref, held) = refs[:CHIPS], refs[CHIPS:-2], refs[-2:]
    in_order(packets, held)
    decays = [get_decay(held.at[b], heads, size) for b in range(CHIPS)]
    fixes = [
        chip_fixes(held, b, held[b - 1, side(0, heads, size), :], heads, size)
        for b in range(1, CHIPS)
    ]
    fixes.insert(0, chip_fixes(held, 0, before[0][...], heads, size) if before else None)
    for j in range(heads):
        rows = slice(j * size, (j + 1) * size)
        acc = held[0, rows, :].astype(F32)
        if before:
            acc = acc + fixes[0][j]
        for b in range(1, CHIPS):
            acc = acc * decays[b][j : j + 1] + (held[b, rows, :].astype(F32) + fixes[b][j])
        out_ref[rows, :] = acc.astype(BF16)
    whole = decays[0]
    for b in range(1, CHIPS):
        whole = whole * decays[b]
    out_ref[side(0, heads, size), :] = held[CHIPS - 1, side(0, heads, size), :]
    if before:
        put_decay(out_ref, whole, heads, size)


def spread_kernel(heads, size, *refs):
    packets, before, known, (out_ref, held) = refs[:CHIPS], refs[CHIPS], refs[CHIPS + 1 : -2], refs[-2:]
    _, chip = position()
    later = lax.axis_index("ctx") >= SPAN
    in_order(packets, held)
    decays = [get_decay(held.at[b], heads, size) for b in range(CHIPS)]
    edges = known[0][...] if known else before[side(0, heads, size), :]
    edges = [jnp.where(later, edges.astype(F32), 0.0).astype(BF16)]
    edges += [held[b, side(0, heads, size), :] for b in range(CHIPS - 1)]
    fixes = [chip_fixes(held, b, edges[b], heads, size) for b in range(CHIPS - 1)]
    for j in range(heads):
        rows = slice(j * size, (j + 1) * size)
        acc = jnp.where(later, before[rows, :].astype(F32), 0.0)
        out_ref[chip, rows, :] = acc.astype(BF16)
        for b in range(1, CHIPS):
            acc = acc * decays[b - 1][j : j + 1] + (
                held[b - 1, rows, :].astype(F32) + fixes[b - 1][j]
            )
            out_ref[chip ^ b, rows, :] = acc.astype(BF16)
    for b in range(CHIPS):
        out_ref[chip ^ b, heads * size : heads * size + PARTS, :] = edges[b]


def out_kernel(items, heads, size, *refs):
    q_ref, cum_ref, gain_ref = refs[:3]
    per_item = [refs[3 + 3 * i : 6 + 3 * i] for i in range(len(items))]
    out_ref, inter_ref, score_ref, done_ref, sems = refs[-5:]
    rows = q_ref.shape[0]
    core, _ = position()
    second = core == 1
    row = lax.broadcasted_iota(jnp.int32, (rows, 2 * PARTS), 0)
    column = lax.broadcasted_iota(jnp.int32, (rows, 2 * PARTS), 1)
    edge = lax.rem(column, PARTS)
    causal = (lax.div(edge, heads) <= row) & (edge < 3 * heads)
    ahead = column < PARTS
    kept = ((ahead & (core == 1)) | causal) & (ahead | (core == 1))
    kept = [kept & (lax.rem(edge, heads) == j) for j in range(heads)]
    for i, (mine, g) in enumerate(items):
        prefix_ref, _, sib_ref = per_item[i]
        b = head_group(mine, g)
        by = jnp.where(second, get_decay(sib_ref.at[g], heads, size), 1.0)
        edges = jnp.concatenate(
            [
                prefix_ref[heads * size : heads * size + PARTS, :].astype(F32),
                sib_ref[g, side(0, heads, size), :].astype(F32),
            ],
            0,
        ).astype(BF16)
        for j in range(heads):
            cols = columns(b * heads * size, j * size, size)
            these = slice(j * size, (j + 1) * size)
            sib = jnp.where(second, sib_ref[g, these, :].astype(F32), 0.0)
            prefix = (prefix_ref[these, :].astype(F32) * by[j : j + 1] + sib).astype(BF16)
            both = lax.dot_general(
                q_ref[:, cols],
                jnp.concatenate([prefix, edges], 0),
                (((1,), (1,)), ((), ())),
                preferred_element_type=F32,
            )
            inter_ref[i * heads + j] = both[:, 0:size]
            score_ref[i * heads + j] = jnp.where(kept[j], both[:, size:], 0.0).astype(BF16)
    copies = []
    for i, (mine, g) in enumerate(items):
        _, intra_ref, sib_ref = per_item[i]
        b = head_group(mine, g)
        started = jnp.exp(cum_ref[b][0:heads]).T
        values = intra_ref[CHIPS * heads, g * PARTS : (g + 1) * PARTS, :]
        ahead_values = jnp.where(second, sib_ref[g, side(2, heads, size), :].astype(F32), values)
        values = jnp.concatenate([ahead_values, values], 0).astype(BF16)
        for j in range(heads):
            cols = columns(b * heads * size, j * size, size)
            edge_part = jnp.dot(score_ref[i * heads + j], values, preferred_element_type=F32)
            mixed = intra_ref[g * heads + j] + (
                inter_ref[i * heads + j] + edge_part
            ) * started[:, j : j + 1]
            scale = lax.rsqrt(jnp.mean(mixed * mixed, axis=1, keepdims=True) + 1e-05)
            done_ref[i, :, j * size : (j + 1) * size] = (
                mixed * scale * gain_ref[:, cols]
            ).astype(BF16)
        wide = columns(b * heads * size, 0, heads * size)
        copies.append(pltpu.make_async_copy(done_ref.at[i], out_ref.at[:, wide], sems.at[i]))
        copies[-1].start()
    for copy in copies:
        copy.wait()


def join_spans(earlier, later, heads, size):
    base = heads * size
    own = side(1, heads, size)

    def decay(x):
        tail = x[own].astype(F32)
        return tail[0:heads] + tail[heads : 2 * heads] + tail[2 * heads : 3 * heads]

    by = decay(later)
    state = (
        by[:, None, :] * earlier[:base].astype(F32).reshape(heads, size, -1)
        + later[:base].astype(F32).reshape(heads, size, -1)
    ).reshape(base, -1)
    parts = three_parts(by * decay(earlier))
    return jnp.concatenate([state.astype(BF16), later[base : own.start], *parts, later[own.start + 3 * heads :]], 0)


def on_device(queries, key_input, value_input, log_decay, conv_weight, norm_gain):
    rows, width = queries.shape
    head_count = log_decay.shape[1]
    size = width // head_count
    heads = head_count // SPAN
    taps = conv_weight.shape[0]
    half = CHIPS * heads
    packet = heads * size + 3 * PARTS
    n = lax.axis_size("ctx")

    def swap(x, mask):
        return lax.ppermute(x, "ctx", [(i, i ^ mask) for i in range(n)])

    def shift(x, by):
        return lax.ppermute(x, "ctx", [(i, i + by) for i in range(n - by)])

    gain = norm_gain.reshape(1, width)
    ext = pltpu.VMEM((heads, rows + HALO, size), F32)
    held = pltpu.VMEM((half, rows, size), BF16)

    def states(mine):
        return call(
            functools.partial(state_kernel, mine, heads, size),
            "states_mine" if mine else "states_other",
            pltpu.VMEM((CHIPS, packet, size), BF16),
            key_input, value_input, conv_weight, log_decay.T,
            in_specs=[HBM] * 4,
            scratch=[
                pltpu.VMEM((CHIPS, rows, heads * size), BF16),
                pltpu.VMEM((CHIPS, rows, heads * size), BF16),
                pltpu.VMEM((CHIPS, taps, heads * size), F32),
                pltpu.VMEM((head_count, rows), F32),
                pltpu.VMEM((SPAN, 2 * heads, rows), F32),
                ext,
                held,
                pltpu.SemaphoreType.DMA((3 * CHIPS + 1,)),
            ],
        )

    def intra_part(mine, q):
        return call(
            functools.partial(intra_kernel, mine, heads, size),
            "intra_mine" if mine else "intra_other",
            pltpu.VMEM((half + 1, rows, size), F32),
            q, key_input, value_input, conv_weight, cum,
            scratch=[ext, held],
        )

    theirs = states(False)
    got = swap(theirs, 1)
    mine = states(True)
    got_late = swap(mine, 1)

    chip_states = call(
        functools.partial(chip_kernel, heads, size),
        "chip_states",
        pltpu.VMEM((CHIPS, packet, size), BF16),
        mine, got,
    )
    packets = {0: chip_states[0]}
    for g in EXCHANGE:
        packets[g] = swap(chip_states[g], 2 * g)
    q_after, decay_after, chip_states = lax.optimization_barrier(
        (queries, log_decay, chip_states)
    )
    cum = call(
        functools.partial(cum_kernel, heads),
        "cum",
        pltpu.VMEM((SPAN, 2 * heads, rows), F32),
        decay_after.T,
    )
    intra_mine = intra_part(True, q_after)
    *late, intra_mine = lax.optimization_barrier((*[packets[g] for g in EXCHANGE], intra_mine))
    packets.update(zip(EXCHANGE, late))
    packets = [packets[g] for g in range(CHIPS)]

    order = pltpu.VMEM((CHIPS, packet, size), BF16)
    known = []
    if n > 2 * SPAN:
        edge = call(
            functools.partial(last_edge_kernel, heads, size),
            "last_edge",
            pltpu.VMEM((PARTS, size), BF16),
            *packets,
            scratch=[order],
        )
        known = [shift(edge, SPAN)]
    span = call(
        functools.partial(span_kernel, heads, size),
        "span_state",
        pltpu.VMEM((heads * size + (2 if known else 1) * PARTS, size), BF16),
        *packets, *known,
        scratch=[order],
    )
    before = swap(span, SPAN) if n == 2 * SPAN else shift(span, SPAN)
    reach = 1
    while reach < n // SPAN - 1:
        before = join_spans(shift(before, SPAN * reach), before, heads, size)
        reach *= 2
    q_after, span = lax.optimization_barrier((queries, span))
    intra_other = intra_part(False, q_after)
    before, intra_other = lax.optimization_barrier((before, intra_other))

    chip_prefix = call(
        functools.partial(spread_kernel, heads, size),
        "chip_prefix",
        pltpu.VMEM((CHIPS, heads * size + PARTS, size), BF16),
        *packets, before, *known,
        scratch=[order],
    )
    own = {0: chip_prefix[0]}
    for g in EXCHANGE:
        own[g] = swap(chip_prefix[g], 2 * g)
    other = {0: swap(own[0], 1)}

    def output(items, result):
        args = [queries, cum, gain]
        for mine, g in items:
            args += [own[g], intra_mine, got] if mine else [other[g], intra_other, got_late]
        count = len(args)
        extra = [] if result is None else [result]
        return call(
            functools.partial(out_kernel, items, heads, size),
            "out_" + "_".join(("m" if mine else "o") + str(g) for mine, g in items),
            jax.ShapeDtypeStruct((rows, width), BF16),
            *args, *extra,
            in_specs=[VMEM] * count + [HBM] * len(extra),
            out_specs=HBM,
            input_output_aliases={count: 0} if extra else {},
            cost_estimate=pl.CostEstimate(flops=1, transcendentals=0, bytes_accessed=1),
            scratch=[
                pltpu.VMEM((len(items) * heads, rows, size), F32),
                pltpu.VMEM((len(items) * heads, rows, 2 * PARTS), BF16),
                pltpu.VMEM((len(items), rows, heads * size), BF16),
                pltpu.SemaphoreType.DMA((len(items),)),
            ],
        )

    result = output([(True, 0), (False, 0)], None)
    *late, result = lax.optimization_barrier((*[own[g] for g in EXCHANGE], result))
    own.update(zip(EXCHANGE, late))
    other.update({g: swap(own[g], 1) for g in EXCHANGE})
    result = output([(True, g) for g in EXCHANGE], result)
    return output([(False, g) for g in EXCHANGE], result)


def solution(mesh):
    rows = P(("groups", "ctx"), None)
    return jax.shard_map(
        on_device,
        mesh=mesh,
        in_specs=(rows, rows, rows, rows, P(), P()),
        out_specs=rows,
        check_vma=False,
    )
```

```python
import functools

import jax
import jax.numpy as jnp
from jax import lax
from jax.experimental import pallas as pl
from jax.experimental.pallas import tpu as pltpu
from jax.sharding import PartitionSpec as P

F32 = jnp.float32
BF16 = jnp.bfloat16
CHIPS = 4
SPAN = 2 * CHIPS
HALO = 8
EXCHANGE = (2, 3, 1)
PARTS = 16
VMEM = pl.BlockSpec(memory_space=pltpu.VMEM)
HBM = pl.BlockSpec(memory_space=pltpu.HBM)


def position():
    me = lax.axis_index("ctx")
    return me & 1, (me >> 1) & (CHIPS - 1)


def head_group(mine, g):
    core, chip = position()
    return (core if mine else 1 - core) * CHIPS + (chip ^ g)


def columns(block, offset, size):
    return pl.ds(pl.multiple_of(block + offset, size), size)


def call(kernel, name, out_shape, *args, scratch=(), in_specs=None, out_specs=VMEM, **options):
    if in_specs is None:
        in_specs = [VMEM] * len(args)
    args = [
        pltpu.with_memory_space_constraint(x, pltpu.VMEM if s is VMEM else pltpu.HBM)
        for x, s in zip(args, in_specs)
    ]
    return pl.pallas_call(
        kernel,
        out_shape=out_shape,
        in_specs=in_specs,
        out_specs=out_specs,
        scratch_shapes=list(scratch),
        name=name,
        compiler_params=pltpu.CompilerParams(vmem_limit_bytes=6 << 20),
        **options,
    )(*args)


def cum_kernel(heads, decay_ref, out_ref):
    x = decay_ref[...]
    count, rows = x.shape
    upto = lax.broadcasted_iota(jnp.int32, (rows, rows), 0) <= lax.broadcasted_iota(
        jnp.int32, (rows, rows), 1
    )
    parts = jnp.concatenate([p.astype(F32) for p in three_parts(x)], 0).astype(BF16)
    sums = jnp.dot(parts, upto.astype(F32).astype(BF16), preferred_element_type=F32)
    sums = sums[0:count] + (sums[count : 2 * count] + sums[2 * count :])
    total = jnp.broadcast_to(sums[:, rows - 1 : rows], sums.shape)
    for b in range(out_ref.shape[0]):
        these = slice(b * heads, (b + 1) * heads)
        out_ref[b, 0:heads, :] = sums[these]
        out_ref[b, heads : 2 * heads, :] = total[these]


def three_parts(x):
    hi = x.astype(BF16)
    rest = x - hi.astype(F32)
    mid = rest.astype(BF16)
    low = (rest - mid.astype(F32)).astype(BF16)
    return hi, mid, low


def side(part, heads, size):
    base = heads * size + part * PARTS
    return slice(base, base + PARTS)


def padded(rows):
    rows = jnp.concatenate(rows, 0)
    spare = jnp.zeros((PARTS - rows.shape[0], rows.shape[1]), F32)
    return jnp.concatenate([rows, spare], 0).astype(BF16)


def put_decay(out, decays, heads, size):
    out[side(1, heads, size), :] = padded([p.astype(F32) for p in three_parts(decays)])


def get_decay(packet, heads, size):
    tail = packet[side(1, heads, size), :].astype(F32)
    return tail[0:heads] + tail[heads : 2 * heads] + tail[2 * heads : 3 * heads]


def edge_states(values, edges, heads):
    row = lax.broadcasted_iota(jnp.int32, values.shape, 0)
    out = []
    for j in range(heads):
        picked = jnp.where(lax.rem(row, heads) == j, values.astype(F32), 0.0).astype(BF16)
        out.append(
            lax.dot_general(picked, edges, (((0,), (0,)), ((), ())), preferred_element_type=F32)
        )
    return out


def conv_keys(k_ref, halo, w_ref, ext, cols):
    rows = k_ref.shape[0]
    ext[0:HALO, :] = halo
    ext[HALO : HALO + rows, :] = k_ref[:, cols].astype(F32)
    total = None
    for j in range(w_ref.shape[0]):
        term = w_ref[j : j + 1, cols] * ext[HALO - j : HALO - j + rows, :]
        total = term if total is None else total + term
    return total.astype(BF16)


def state_kernel(
    mine, heads, size, k_hbm, v_hbm, w_hbm, decay_hbm, out_ref,
    k_buf, v_buf, w_buf, decay_buf, cum_ref, ext, held, sems,
):
    rows, wide = k_buf.shape[1:]
    taps = w_buf.shape[1]
    copies = [pltpu.make_async_copy(decay_hbm, decay_buf, sems.at[3 * CHIPS])]
    copies[0].start()
    for g in range(CHIPS):
        cols = columns(head_group(mine, g) * wide, 0, wide)
        for i, (source, buf) in enumerate(((k_hbm, k_buf), (w_hbm, w_buf), (v_hbm, v_buf))):
            copies.append(
                pltpu.make_async_copy(source.at[:, cols], buf.at[g], sems.at[3 * g + i])
            )
            copies[-1].start()
    copies[0].wait()
    cum_kernel(heads, decay_buf, cum_ref)
    none = jnp.zeros((HALO, size), F32)
    for g in range(CHIPS):
        for copy in copies[1 + 3 * g : 4 + 3 * g]:
            copy.wait()
        cum = cum_ref[head_group(mine, g)]
        ending = jnp.exp(cum[heads : 2 * heads] - cum[0:heads]).T
        edges, values = [], []
        for j in range(heads):
            cols = slice(j * size, (j + 1) * size)
            key_conv = conv_keys(k_buf.at[g], none, w_buf.at[g], ext.at[j], cols)
            held[g * heads + j] = (key_conv.astype(F32) * ending[:, j : j + 1]).astype(BF16)
            last = k_buf[g, rows - HALO : rows, cols].astype(F32)
            head_edges = []
            for t in range(taps - 1):
                terms = [
                    w_buf[g, i : i + 1, cols] * last[HALO + t - i : HALO + t - i + 1]
                    for i in range(t + 1, taps)
                ]
                head_edges.append(sum(terms[1:], terms[0]))
            edges.append(head_edges)
            values.append(v_buf[g, 0:HALO, cols].astype(F32) * ending[0:HALO, j : j + 1])
        put_decay(out_ref.at[g], jnp.exp(cum[heads : 2 * heads]), heads, size)
        out_ref[g, side(0, heads, size), :] = padded(
            [edges[j][t] for t in range(taps - 1) for j in range(heads)]
        )
        out_ref[g, side(2, heads, size), :] = padded(
            [values[j][t : t + 1] for t in range(taps - 1) for j in range(heads)]
        )
    for g in range(CHIPS):
        for j in range(heads):
            cols = slice(j * size, (j + 1) * size)
            state = lax.dot_general(
                v_buf[g, :, cols], held[g * heads + j], (((0,), (0,)), ((), ())),
                preferred_element_type=F32,
            )
            out_ref[g, cols, :] = state.astype(BF16)


def intra_kernel(mine, heads, size, q_ref, k_ref, v_ref, w_ref, cum_ref, out_ref, ext, held):
    rows = q_ref.shape[0]
    causal = lax.broadcasted_iota(jnp.int32, (rows, rows), 0) >= lax.broadcasted_iota(
        jnp.int32, (rows, rows), 1
    )
    none = jnp.zeros((HALO, size), F32)
    for g in range(CHIPS):
        b = head_group(mine, g)
        cum = cum_ref[b][0:heads]
        cum_col = cum.T
        growth = jnp.exp(-cum_col[0:HALO])
        values = []
        for j in range(heads):
            cols = columns(b * heads * size, j * size, size)
            key_conv = conv_keys(k_ref, none, w_ref, ext.at[j], cols)
            scores = lax.dot_general(
                q_ref[:, cols], key_conv, (((1,), (1,)), ((), ())), preferred_element_type=F32
            )
            spread = cum_col[:, j : j + 1] - cum[j : j + 1]
            weights = jnp.where(causal, scores * jnp.exp(jnp.where(causal, spread, 0.0)), 0.0)
            held[g * heads + j] = weights.astype(BF16)
            values.append(v_ref[0:HALO, cols].astype(F32) * growth[:, j : j + 1])
        out_ref[CHIPS * heads, g * PARTS : (g + 1) * PARTS, :] = padded(
            [values[j][t : t + 1] for t in range(3) for j in range(heads)]
        ).astype(F32)
    for g in range(CHIPS):
        b = head_group(mine, g)
        for j in range(heads):
            cols = columns(b * heads * size, j * size, size)
            out_ref[g * heads + j] = jnp.dot(
                held[g * heads + j], v_ref[:, cols], preferred_element_type=F32
            )


def chip_kernel(heads, size, own_ref, got_ref, out_ref):
    core, _ = position()
    first = core == 0
    for g in range(CHIPS):
        own_decay = get_decay(own_ref.at[g], heads, size)
        got_decay = get_decay(got_ref.at[g], heads, size)
        own_by = jnp.where(first, got_decay, 1.0)
        got_by = jnp.where(first, 1.0, own_decay)

        def earlier_later(part):
            own = own_ref[g, side(part, heads, size), :].astype(F32)
            got = got_ref[g, side(part, heads, size), :].astype(F32)
            return jnp.where(first, own, got), jnp.where(first, got, own)

        edges, out_edges = earlier_later(0)
        out_values, values = earlier_later(2)
        fixes = edge_states(values.astype(BF16), edges.astype(BF16), heads)
        for j in range(heads):
            rows = slice(j * size, (j + 1) * size)
            out_ref[g, rows, :] = (
                own_ref[g, rows, :].astype(F32) * own_by[j : j + 1]
                + got_ref[g, rows, :].astype(F32) * got_by[j : j + 1]
                + fixes[j]
            ).astype(BF16)
        put_decay(out_ref.at[g], own_decay * got_decay, heads, size)
        later_by = jnp.where(first, got_decay, own_decay)
        out_ref[g, side(0, heads, size), :] = out_edges.astype(BF16)
        out_ref[g, side(2, heads, size), :] = padded(
            [out_values[t * heads : (t + 1) * heads] * later_by for t in range(3)]
        )


def in_order(packets, held):
    _, chip = position()
    for g in range(CHIPS):
        held[chip ^ g] = packets[g][...]


def chip_fixes(held, b, edges, heads, size):
    return edge_states(held[b, side(2, heads, size), :], edges, heads)


def last_edge_kernel(heads, size, *refs):
    packets, out_ref, held = refs[:CHIPS], refs[CHIPS], refs[CHIPS + 1]
    in_order(packets, held)
    out_ref[...] = held[CHIPS - 1, side(0, heads, size), :]


def span_kernel(heads, size, *refs):
    packets, before, (out_ref, held) = refs[:CHIPS], refs[CHIPS:-2], refs[-2:]
    in_order(packets, held)
    decays = [get_decay(held.at[b], heads, size) for b in range(CHIPS)]
    fixes = [
        chip_fixes(held, b, held[b - 1, side(0, heads, size), :], heads, size)
        for b in range(1, CHIPS)
    ]
    fixes.insert(0, chip_fixes(held, 0, before[0][...], heads, size) if before else None)
    for j in range(heads):
        rows = slice(j * size, (j + 1) * size)
        acc = held[0, rows, :].astype(F32)
        if before:
            acc = acc + fixes[0][j]
        for b in range(1, CHIPS):
            acc = acc * decays[b][j : j + 1] + (held[b, rows, :].astype(F32) + fixes[b][j])
        out_ref[rows, :] = acc.astype(BF16)
    whole = decays[0]
    for b in range(1, CHIPS):
        whole = whole * decays[b]
    out_ref[side(0, heads, size), :] = held[CHIPS - 1, side(0, heads, size), :]
    if before:
        put_decay(out_ref, whole, heads, size)


def spread_kernel(heads, size, *refs):
    packets, before, known, (out_ref, held) = refs[:CHIPS], refs[CHIPS], refs[CHIPS + 1 : -2], refs[-2:]
    _, chip = position()
    later = lax.axis_index("ctx") >= SPAN
    in_order(packets, held)
    decays = [get_decay(held.at[b], heads, size) for b in range(CHIPS)]
    edges = known[0][...] if known else before[side(0, heads, size), :]
    edges = [jnp.where(later, edges.astype(F32), 0.0).astype(BF16)]
    edges += [held[b, side(0, heads, size), :] for b in range(CHIPS - 1)]
    fixes = [chip_fixes(held, b, edges[b], heads, size) for b in range(CHIPS - 1)]
    for j in range(heads):
        rows = slice(j * size, (j + 1) * size)
        acc = jnp.where(later, before[rows, :].astype(F32), 0.0)
        out_ref[chip, rows, :] = acc.astype(BF16)
        for b in range(1, CHIPS):
            acc = acc * decays[b - 1][j : j + 1] + (
                held[b - 1, rows, :].astype(F32) + fixes[b - 1][j]
            )
            out_ref[chip ^ b, rows, :] = acc.astype(BF16)
    for b in range(CHIPS):
        out_ref[chip ^ b, heads * size : heads * size + PARTS, :] = edges[b]


def out_kernel(items, heads, size, *refs):
    q_ref, cum_ref, gain_ref = refs[:3]
    per_item = [refs[3 + 3 * i : 6 + 3 * i] for i in range(len(items))]
    out_ref, inter_ref, score_ref, done_ref, sems = refs[-5:]
    rows = q_ref.shape[0]
    core, _ = position()
    second = core == 1
    row = lax.broadcasted_iota(jnp.int32, (rows, 2 * PARTS), 0)
    column = lax.broadcasted_iota(jnp.int32, (rows, 2 * PARTS), 1)
    edge = lax.rem(column, PARTS)
    causal = (lax.div(edge, heads) <= row) & (edge < 3 * heads)
    ahead = column < PARTS
    kept = ((ahead & (core == 1)) | causal) & (ahead | (core == 1))
    kept = [kept & (lax.rem(edge, heads) == j) for j in range(heads)]
    for i, (mine, g) in enumerate(items):
        prefix_ref, intra_ref, sib_ref = per_item[i]
        b = head_group(mine, g)
        started = jnp.exp(cum_ref[b][0:heads]).T
        by = jnp.where(second, get_decay(sib_ref.at[g], heads, size), 1.0)
        edges = jnp.concatenate(
            [
                prefix_ref[heads * size : heads * size + PARTS, :].astype(F32),
                sib_ref[g, side(0, heads, size), :].astype(F32),
            ],
            0,
        ).astype(BF16)
        for j in range(heads):
            cols = columns(b * heads * size, j * size, size)
            these = slice(j * size, (j + 1) * size)
            sib = jnp.where(second, sib_ref[g, these, :].astype(F32), 0.0)
            prefix = (prefix_ref[these, :].astype(F32) * by[j : j + 1] + sib).astype(BF16)
            both = lax.dot_general(
                q_ref[:, cols],
                jnp.concatenate([prefix, edges], 0),
                (((1,), (1,)), ((), ())),
                preferred_element_type=F32,
            )
            both = both * started[:, j : j + 1]
            inter_ref[i * heads + j] = both[:, 0:size] + intra_ref[g * heads + j]
            score_ref[i * heads + j] = jnp.where(kept[j], both[:, size:], 0.0).astype(BF16)
    copies = []
    for i, (mine, g) in enumerate(items):
        _, intra_ref, sib_ref = per_item[i]
        b = head_group(mine, g)
        values = intra_ref[CHIPS * heads, g * PARTS : (g + 1) * PARTS, :]
        ahead_values = jnp.where(second, sib_ref[g, side(2, heads, size), :].astype(F32), values)
        values = jnp.concatenate([ahead_values, values], 0).astype(BF16)
        for j in range(heads):
            inter_ref[i * heads + j] += jnp.dot(
                score_ref[i * heads + j], values, preferred_element_type=F32
            )
    for i, (mine, g) in enumerate(items):
        b = head_group(mine, g)
        for j in range(heads):
            cols = columns(b * heads * size, j * size, size)
            mixed = inter_ref[i * heads + j]
            scale = lax.rsqrt(jnp.mean(mixed * mixed, axis=1, keepdims=True) + 1e-05)
            done_ref[i, :, j * size : (j + 1) * size] = (
                mixed * scale * gain_ref[:, cols]
            ).astype(BF16)
        wide = columns(b * heads * size, 0, heads * size)
        copies.append(pltpu.make_async_copy(done_ref.at[i], out_ref.at[:, wide], sems.at[i]))
        copies[-1].start()
    for copy in copies:
        copy.wait()


def join_spans(earlier, later, heads, size):
    base = heads * size
    own = side(1, heads, size)

    def decay(x):
        tail = x[own].astype(F32)
        return tail[0:heads] + tail[heads : 2 * heads] + tail[2 * heads : 3 * heads]

    by = decay(later)
    state = (
        by[:, None, :] * earlier[:base].astype(F32).reshape(heads, size, -1)
        + later[:base].astype(F32).reshape(heads, size, -1)
    ).reshape(base, -1)
    parts = three_parts(by * decay(earlier))
    return jnp.concatenate([state.astype(BF16), later[base : own.start], *parts, later[own.start + 3 * heads :]], 0)


def on_device(queries, key_input, value_input, log_decay, conv_weight, norm_gain):
    rows, width = queries.shape
    head_count = log_decay.shape[1]
    size = width // head_count
    heads = head_count // SPAN
    taps = conv_weight.shape[0]
    half = CHIPS * heads
    packet = heads * size + 3 * PARTS
    n = lax.axis_size("ctx")

    def swap(x, mask):
        return lax.ppermute(x, "ctx", [(i, i ^ mask) for i in range(n)])

    def shift(x, by):
        return lax.ppermute(x, "ctx", [(i, i + by) for i in range(n - by)])

    gain = norm_gain.reshape(1, width)
    ext = pltpu.VMEM((heads, rows + HALO, size), F32)
    held = pltpu.VMEM((half, rows, size), BF16)

    def states(mine):
        return call(
            functools.partial(state_kernel, mine, heads, size),
            "states_mine" if mine else "states_other",
            pltpu.VMEM((CHIPS, packet, size), BF16),
            key_input, value_input, conv_weight, log_decay.T,
            in_specs=[HBM] * 4,
            scratch=[
                pltpu.VMEM((CHIPS, rows, heads * size), BF16),
                pltpu.VMEM((CHIPS, rows, heads * size), BF16),
                pltpu.VMEM((CHIPS, taps, heads * size), F32),
                pltpu.VMEM((head_count, rows), F32),
                pltpu.VMEM((SPAN, 2 * heads, rows), F32),
                ext,
                held,
                pltpu.SemaphoreType.DMA((3 * CHIPS + 1,)),
            ],
        )

    def intra_part(mine, q):
        return call(
            functools.partial(intra_kernel, mine, heads, size),
            "intra_mine" if mine else "intra_other",
            pltpu.VMEM((half + 1, rows, size), F32),
            q, key_input, value_input, conv_weight, cum,
            scratch=[ext, held],
        )

    theirs = states(False)
    got = swap(theirs, 1)
    mine = states(True)
    got_late = swap(mine, 1)

    chip_states = call(
        functools.partial(chip_kernel, heads, size),
        "chip_states",
        pltpu.VMEM((CHIPS, packet, size), BF16),
        mine, got,
    )
    packets = {0: chip_states[0]}
    for g in EXCHANGE:
        packets[g] = swap(chip_states[g], 2 * g)
    q_after, decay_after, chip_states = lax.optimization_barrier(
        (queries, log_decay, chip_states)
    )
    cum = call(
        functools.partial(cum_kernel, heads),
        "cum",
        pltpu.VMEM((SPAN, 2 * heads, rows), F32),
        decay_after.T,
    )
    intra_mine = intra_part(True, q_after)
    *late, intra_mine = lax.optimization_barrier((*[packets[g] for g in EXCHANGE], intra_mine))
    packets.update(zip(EXCHANGE, late))
    packets = [packets[g] for g in range(CHIPS)]

    order = pltpu.VMEM((CHIPS, packet, size), BF16)
    known = []
    if n > 2 * SPAN:
        edge = call(
            functools.partial(last_edge_kernel, heads, size),
            "last_edge",
            pltpu.VMEM((PARTS, size), BF16),
            *packets,
            scratch=[order],
        )
        known = [shift(edge, SPAN)]
    span = call(
        functools.partial(span_kernel, heads, size),
        "span_state",
        pltpu.VMEM((heads * size + (2 if known else 1) * PARTS, size), BF16),
        *packets, *known,
        scratch=[order],
    )
    before = swap(span, SPAN) if n == 2 * SPAN else shift(span, SPAN)
    reach = 1
    while reach < n // SPAN - 1:
        before = join_spans(shift(before, SPAN * reach), before, heads, size)
        reach *= 2
    q_after, span = lax.optimization_barrier((queries, span))
    intra_other = intra_part(False, q_after)
    before, intra_other = lax.optimization_barrier((before, intra_other))

    chip_prefix = call(
        functools.partial(spread_kernel, heads, size),
        "chip_prefix",
        pltpu.VMEM((CHIPS, heads * size + PARTS, size), BF16),
        *packets, before, *known,
        scratch=[order],
    )
    own = {0: chip_prefix[0]}
    for g in EXCHANGE:
        own[g] = swap(chip_prefix[g], 2 * g)
    other = {0: swap(own[0], 1)}

    def output(items, result):
        args = [queries, cum, gain]
        for mine, g in items:
            args += [own[g], intra_mine, got] if mine else [other[g], intra_other, got_late]
        count = len(args)
        extra = [] if result is None else [result]
        return call(
            functools.partial(out_kernel, items, heads, size),
            "out_" + "_".join(("m" if mine else "o") + str(g) for mine, g in items),
            jax.ShapeDtypeStruct((rows, width), BF16),
            *args, *extra,
            in_specs=[VMEM] * count + [HBM] * len(extra),
            out_specs=HBM,
            input_output_aliases={count: 0} if extra else {},
            cost_estimate=pl.CostEstimate(flops=1, transcendentals=0, bytes_accessed=1),
            scratch=[
                pltpu.VMEM((len(items) * heads, rows, size), F32),
                pltpu.VMEM((len(items) * heads, rows, 2 * PARTS), BF16),
                pltpu.VMEM((len(items), rows, heads * size), BF16),
                pltpu.SemaphoreType.DMA((len(items),)),
            ],
        )

    result = output([(True, 0), (False, 0)], None)
    *late, result = lax.optimization_barrier((*[own[g] for g in EXCHANGE], result))
    own.update(zip(EXCHANGE, late))
    other.update({g: swap(own[g], 1) for g in EXCHANGE})
    result = output([(True, g) for g in EXCHANGE], result)
    return output([(False, g) for g in EXCHANGE], result)


def solution(mesh):
    rows = P(("groups", "ctx"), None)
    return jax.shard_map(
        on_device,
        mesh=mesh,
        in_specs=(rows, rows, rows, rows, P(), P()),
        out_specs=rows,
        check_vma=False,
    )
```

```python
import functools

import jax
import jax.numpy as jnp
from jax import lax
from jax.experimental import pallas as pl
from jax.experimental.pallas import tpu as pltpu
from jax.sharding import PartitionSpec as P

F32 = jnp.float32
BF16 = jnp.bfloat16
CHIPS = 4
SPAN = 2 * CHIPS
HALO = 8
EXCHANGE = (2, 3, 1)
PARTS = 16
VMEM = pl.BlockSpec(memory_space=pltpu.VMEM)
HBM = pl.BlockSpec(memory_space=pltpu.HBM)


def position():
    me = lax.axis_index("ctx")
    return me & 1, (me >> 1) & (CHIPS - 1)


def head_group(mine, g):
    core, chip = position()
    return (core if mine else 1 - core) * CHIPS + (chip ^ g)


def columns(block, offset, size):
    return pl.ds(pl.multiple_of(block + offset, size), size)


def call(kernel, name, out_shape, *args, scratch=(), in_specs=None, out_specs=VMEM, **options):
    if in_specs is None:
        in_specs = [VMEM] * len(args)
    args = [
        pltpu.with_memory_space_constraint(x, pltpu.VMEM if s is VMEM else pltpu.HBM)
        for x, s in zip(args, in_specs)
    ]
    return pl.pallas_call(
        kernel,
        out_shape=out_shape,
        in_specs=in_specs,
        out_specs=out_specs,
        scratch_shapes=list(scratch),
        name=name,
        compiler_params=pltpu.CompilerParams(vmem_limit_bytes=6 << 20),
        **options,
    )(*args)


def cum_kernel(heads, decay_ref, out_ref):
    x = decay_ref[...]
    count, rows = x.shape
    upto = lax.broadcasted_iota(jnp.int32, (rows, rows), 0) <= lax.broadcasted_iota(
        jnp.int32, (rows, rows), 1
    )
    parts = jnp.concatenate([p.astype(F32) for p in three_parts(x)], 0).astype(BF16)
    sums = jnp.dot(parts, upto.astype(F32).astype(BF16), preferred_element_type=F32)
    sums = sums[0:count] + (sums[count : 2 * count] + sums[2 * count :])
    total = jnp.broadcast_to(sums[:, rows - 1 : rows], sums.shape)
    for b in range(out_ref.shape[0]):
        these = slice(b * heads, (b + 1) * heads)
        out_ref[b, 0:heads, :] = sums[these]
        out_ref[b, heads : 2 * heads, :] = total[these]


def three_parts(x):
    hi = x.astype(BF16)
    rest = x - hi.astype(F32)
    mid = rest.astype(BF16)
    low = (rest - mid.astype(F32)).astype(BF16)
    return hi, mid, low


def side(part, heads, size):
    base = heads * size + part * PARTS
    return slice(base, base + PARTS)


def padded(rows):
    rows = jnp.concatenate(rows, 0)
    spare = jnp.zeros((PARTS - rows.shape[0], rows.shape[1]), F32)
    return jnp.concatenate([rows, spare], 0).astype(BF16)


def put_decay(out, decays, heads, size):
    out[side(1, heads, size), :] = padded([p.astype(F32) for p in three_parts(decays)])


def get_decay(packet, heads, size):
    tail = packet[side(1, heads, size), :].astype(F32)
    return tail[0:heads] + tail[heads : 2 * heads] + tail[2 * heads : 3 * heads]


def edge_states(values, edges, heads):
    row = lax.broadcasted_iota(jnp.int32, values.shape, 0)
    out = []
    for j in range(heads):
        picked = jnp.where(lax.rem(row, heads) == j, values.astype(F32), 0.0).astype(BF16)
        out.append(
            lax.dot_general(picked, edges, (((0,), (0,)), ((), ())), preferred_element_type=F32)
        )
    return out


def conv_keys(k_ref, halo, w_ref, ext, cols):
    rows = k_ref.shape[0]
    ext[0:HALO, :] = halo
    ext[HALO : HALO + rows, :] = k_ref[:, cols].astype(F32)
    total = None
    for j in range(w_ref.shape[0]):
        term = w_ref[j : j + 1, cols] * ext[HALO - j : HALO - j + rows, :]
        total = term if total is None else total + term
    return total.astype(BF16)


def fetched_state_kernel(
    mine, heads, size, k_hbm, v_hbm, w_hbm, decay_hbm, out_ref,
    k_buf, v_buf, w_buf, decay_buf, cum_ref, ext, held, sems,
):
    wide = heads * size
    copies = [pltpu.make_async_copy(decay_hbm, decay_buf, sems.at[3 * CHIPS])]
    copies[0].start()
    for g in range(CHIPS):
        cols = columns(head_group(mine, g) * wide, 0, wide)
        for i, (source, buf) in enumerate(((k_hbm, k_buf), (w_hbm, w_buf), (v_hbm, v_buf))):
            copies.append(
                pltpu.make_async_copy(source.at[:, cols], buf.at[g], sems.at[3 * g + i])
            )
            copies[-1].start()
    copies[0].wait()
    groups = [(k_buf.at[g], v_buf.at[g], w_buf.at[g]) for g in range(CHIPS)]
    waits = [copies[1 + 3 * g : 4 + 3 * g] for g in range(CHIPS)]
    states_of(mine, heads, size, groups, waits, decay_buf, out_ref, cum_ref, ext, held)


def state_kernel(
    mine, heads, size, k_ref, v_ref, w_ref, decay_ref, out_ref, cum_ref, ext, held
):
    groups = []
    for g in range(CHIPS):
        cols = columns(head_group(mine, g) * heads * size, 0, heads * size)
        groups.append((k_ref.at[:, cols], v_ref.at[:, cols], w_ref.at[:, cols]))
    waits = [[]] * CHIPS
    states_of(mine, heads, size, groups, waits, decay_ref, out_ref, cum_ref, ext, held)


def states_of(mine, heads, size, groups, waits, decay_ref, out_ref, cum_ref, ext, held):
    rows = groups[0][0].shape[0]
    taps = groups[0][2].shape[0]
    cum_kernel(heads, decay_ref, cum_ref)
    none = jnp.zeros((HALO, size), F32)
    for g in range(CHIPS):
        k_ref, v_ref, w_ref = groups[g]
        for copy in waits[g]:
            copy.wait()
        cum = cum_ref[head_group(mine, g)]
        ending = jnp.exp(cum[heads : 2 * heads] - cum[0:heads]).T
        edges, values = [], []
        for j in range(heads):
            cols = slice(j * size, (j + 1) * size)
            key_conv = conv_keys(k_ref, none, w_ref, ext.at[j], cols)
            held[g * heads + j] = (key_conv.astype(F32) * ending[:, j : j + 1]).astype(BF16)
            last = k_ref[rows - HALO : rows, cols].astype(F32)
            head_edges = []
            for t in range(taps - 1):
                terms = [
                    w_ref[i : i + 1, cols] * last[HALO + t - i : HALO + t - i + 1]
                    for i in range(t + 1, taps)
                ]
                head_edges.append(sum(terms[1:], terms[0]))
            edges.append(head_edges)
            values.append(v_ref[0:HALO, cols].astype(F32) * ending[0:HALO, j : j + 1])
        put_decay(out_ref.at[g], jnp.exp(cum[heads : 2 * heads]), heads, size)
        out_ref[g, side(0, heads, size), :] = padded(
            [edges[j][t] for t in range(taps - 1) for j in range(heads)]
        )
        out_ref[g, side(2, heads, size), :] = padded(
            [values[j][t : t + 1] for t in range(taps - 1) for j in range(heads)]
        )
    for g in range(CHIPS):
        for j in range(heads):
            cols = slice(j * size, (j + 1) * size)
            state = lax.dot_general(
                groups[g][1][:, cols], held[g * heads + j], (((0,), (0,)), ((), ())),
                preferred_element_type=F32,
            )
            out_ref[g, cols, :] = state.astype(BF16)


def intra_kernel(mine, heads, size, q_ref, k_ref, v_ref, w_ref, cum_ref, out_ref, ext, held):
    rows = q_ref.shape[0]
    causal = lax.broadcasted_iota(jnp.int32, (rows, rows), 0) >= lax.broadcasted_iota(
        jnp.int32, (rows, rows), 1
    )
    none = jnp.zeros((HALO, size), F32)
    for g in range(CHIPS):
        b = head_group(mine, g)
        cum = cum_ref[b][0:heads]
        cum_col = cum.T
        growth = jnp.exp(-cum_col[0:HALO])
        values = []
        for j in range(heads):
            cols = columns(b * heads * size, j * size, size)
            key_conv = conv_keys(k_ref, none, w_ref, ext.at[j], cols)
            scores = lax.dot_general(
                q_ref[:, cols], key_conv, (((1,), (1,)), ((), ())), preferred_element_type=F32
            )
            spread = cum_col[:, j : j + 1] - cum[j : j + 1]
            weights = jnp.where(causal, scores * jnp.exp(jnp.where(causal, spread, 0.0)), 0.0)
            held[g * heads + j] = weights.astype(BF16)
            values.append(v_ref[0:HALO, cols].astype(F32) * growth[:, j : j + 1])
        out_ref[CHIPS * heads, g * PARTS : (g + 1) * PARTS, :] = padded(
            [values[j][t : t + 1] for t in range(3) for j in range(heads)]
        ).astype(F32)
    for g in range(CHIPS):
        b = head_group(mine, g)
        for j in range(heads):
            cols = columns(b * heads * size, j * size, size)
            out_ref[g * heads + j] = jnp.dot(
                held[g * heads + j], v_ref[:, cols], preferred_element_type=F32
            )


def chip_kernel(heads, size, own_ref, got_ref, out_ref):
    core, _ = position()
    first = core == 0
    for g in range(CHIPS):
        own_decay = get_decay(own_ref.at[g], heads, size)
        got_decay = get_decay(got_ref.at[g], heads, size)
        own_by = jnp.where(first, got_decay, 1.0)
        got_by = jnp.where(first, 1.0, own_decay)

        def earlier_later(part):
            own = own_ref[g, side(part, heads, size), :].astype(F32)
            got = got_ref[g, side(part, heads, size), :].astype(F32)
            return jnp.where(first, own, got), jnp.where(first, got, own)

        edges, out_edges = earlier_later(0)
        out_values, values = earlier_later(2)
        fixes = edge_states(values.astype(BF16), edges.astype(BF16), heads)
        for j in range(heads):
            rows = slice(j * size, (j + 1) * size)
            out_ref[g, rows, :] = (
                own_ref[g, rows, :].astype(F32) * own_by[j : j + 1]
                + got_ref[g, rows, :].astype(F32) * got_by[j : j + 1]
                + fixes[j]
            ).astype(BF16)
        put_decay(out_ref.at[g], own_decay * got_decay, heads, size)
        later_by = jnp.where(first, got_decay, own_decay)
        out_ref[g, side(0, heads, size), :] = out_edges.astype(BF16)
        out_ref[g, side(2, heads, size), :] = padded(
            [out_values[t * heads : (t + 1) * heads] * later_by for t in range(3)]
        )


def in_order(packets, held):
    _, chip = position()
    for g in range(CHIPS):
        held[chip ^ g] = packets[g][...]


def chip_fixes(held, b, edges, heads, size):
    return edge_states(held[b, side(2, heads, size), :], edges, heads)


def last_edge_kernel(heads, size, *refs):
    packets, out_ref, held = refs[:CHIPS], refs[CHIPS], refs[CHIPS + 1]
    in_order(packets, held)
    out_ref[...] = held[CHIPS - 1, side(0, heads, size), :]


def span_kernel(heads, size, *refs):
    packets, before, (out_ref, held) = refs[:CHIPS], refs[CHIPS:-2], refs[-2:]
    in_order(packets, held)
    decays = [get_decay(held.at[b], heads, size) for b in range(CHIPS)]
    fixes = [
        chip_fixes(held, b, held[b - 1, side(0, heads, size), :], heads, size)
        for b in range(1, CHIPS)
    ]
    fixes.insert(0, chip_fixes(held, 0, before[0][...], heads, size) if before else None)
    for j in range(heads):
        rows = slice(j * size, (j + 1) * size)
        acc = held[0, rows, :].astype(F32)
        if before:
            acc = acc + fixes[0][j]
        for b in range(1, CHIPS):
            acc = acc * decays[b][j : j + 1] + (held[b, rows, :].astype(F32) + fixes[b][j])
        out_ref[rows, :] = acc.astype(BF16)
    whole = decays[0]
    for b in range(1, CHIPS):
        whole = whole * decays[b]
    out_ref[side(0, heads, size), :] = held[CHIPS - 1, side(0, heads, size), :]
    if before:
        put_decay(out_ref, whole, heads, size)


def spread_kernel(heads, size, *refs):
    packets, before, known, (out_ref, held) = refs[:CHIPS], refs[CHIPS], refs[CHIPS + 1 : -2], refs[-2:]
    _, chip = position()
    later = lax.axis_index("ctx") >= SPAN
    in_order(packets, held)
    decays = [get_decay(held.at[b], heads, size) for b in range(CHIPS)]
    edges = known[0][...] if known else before[side(0, heads, size), :]
    edges = [jnp.where(later, edges.astype(F32), 0.0).astype(BF16)]
    edges += [held[b, side(0, heads, size), :] for b in range(CHIPS - 1)]
    fixes = [chip_fixes(held, b, edges[b], heads, size) for b in range(CHIPS - 1)]
    for j in range(heads):
        rows = slice(j * size, (j + 1) * size)
        acc = jnp.where(later, before[rows, :].astype(F32), 0.0)
        out_ref[chip, rows, :] = acc.astype(BF16)
        for b in range(1, CHIPS):
            acc = acc * decays[b - 1][j : j + 1] + (
                held[b - 1, rows, :].astype(F32) + fixes[b - 1][j]
            )
            out_ref[chip ^ b, rows, :] = acc.astype(BF16)
    for b in range(CHIPS):
        out_ref[chip ^ b, heads * size : heads * size + PARTS, :] = edges[b]


def out_kernel(items, heads, size, *refs):
    q_ref, cum_ref, gain_ref = refs[:3]
    per_item = [refs[3 + 3 * i : 6 + 3 * i] for i in range(len(items))]
    out_ref, inter_ref, score_ref, done_ref, sems = refs[-5:]
    rows = q_ref.shape[0]
    core, _ = position()
    second = core == 1
    row = lax.broadcasted_iota(jnp.int32, (rows, 2 * PARTS), 0)
    column = lax.broadcasted_iota(jnp.int32, (rows, 2 * PARTS), 1)
    edge = lax.rem(column, PARTS)
    causal = (lax.div(edge, heads) <= row) & (edge < 3 * heads)
    ahead = column < PARTS
    kept = ((ahead & (core == 1)) | causal) & (ahead | (core == 1))
    kept = [kept & (lax.rem(edge, heads) == j) for j in range(heads)]
    for i, (mine, g) in enumerate(items):
        prefix_ref, intra_ref, sib_ref = per_item[i]
        b = head_group(mine, g)
        started = jnp.exp(cum_ref[b][0:heads]).T
        by = jnp.where(second, get_decay(sib_ref.at[g], heads, size), 1.0)
        edges = jnp.concatenate(
            [
                prefix_ref[heads * size : heads * size + PARTS, :].astype(F32),
                sib_ref[g, side(0, heads, size), :].astype(F32),
            ],
            0,
        ).astype(BF16)
        for j in range(heads):
            cols = columns(b * heads * size, j * size, size)
            these = slice(j * size, (j + 1) * size)
            sib = jnp.where(second, sib_ref[g, these, :].astype(F32), 0.0)
            prefix = (prefix_ref[these, :].astype(F32) * by[j : j + 1] + sib).astype(BF16)
            both = lax.dot_general(
                q_ref[:, cols],
                jnp.concatenate([prefix, edges], 0),
                (((1,), (1,)), ((), ())),
                preferred_element_type=F32,
            )
            both = both * started[:, j : j + 1]
            inter_ref[i * heads + j] = both[:, 0:size] + intra_ref[g * heads + j]
            score_ref[i * heads + j] = jnp.where(kept[j], both[:, size:], 0.0).astype(BF16)
    copies = []
    for i, (mine, g) in enumerate(items):
        _, intra_ref, sib_ref = per_item[i]
        b = head_group(mine, g)
        values = intra_ref[CHIPS * heads, g * PARTS : (g + 1) * PARTS, :]
        ahead_values = jnp.where(second, sib_ref[g, side(2, heads, size), :].astype(F32), values)
        values = jnp.concatenate([ahead_values, values], 0).astype(BF16)
        for j in range(heads):
            inter_ref[i * heads + j] += jnp.dot(
                score_ref[i * heads + j], values, preferred_element_type=F32
            )
    for i, (mine, g) in enumerate(items):
        b = head_group(mine, g)
        for j in range(heads):
            cols = columns(b * heads * size, j * size, size)
            mixed = inter_ref[i * heads + j]
            scale = lax.rsqrt(jnp.mean(mixed * mixed, axis=1, keepdims=True) + 1e-05)
            done_ref[i, :, j * size : (j + 1) * size] = (
                mixed * scale * gain_ref[:, cols]
            ).astype(BF16)
        wide = columns(b * heads * size, 0, heads * size)
        copies.append(pltpu.make_async_copy(done_ref.at[i], out_ref.at[:, wide], sems.at[i]))
        copies[-1].start()
    for copy in copies:
        copy.wait()


def join_spans(earlier, later, heads, size):
    base = heads * size
    own = side(1, heads, size)

    def decay(x):
        tail = x[own].astype(F32)
        return tail[0:heads] + tail[heads : 2 * heads] + tail[2 * heads : 3 * heads]

    by = decay(later)
    state = (
        by[:, None, :] * earlier[:base].astype(F32).reshape(heads, size, -1)
        + later[:base].astype(F32).reshape(heads, size, -1)
    ).reshape(base, -1)
    parts = three_parts(by * decay(earlier))
    return jnp.concatenate([state.astype(BF16), later[base : own.start], *parts, later[own.start + 3 * heads :]], 0)


def on_device(queries, key_input, value_input, log_decay, conv_weight, norm_gain):
    rows, width = queries.shape
    head_count = log_decay.shape[1]
    size = width // head_count
    heads = head_count // SPAN
    taps = conv_weight.shape[0]
    half = CHIPS * heads
    packet = heads * size + 3 * PARTS
    n = lax.axis_size("ctx")

    def swap(x, mask):
        return lax.ppermute(x, "ctx", [(i, i ^ mask) for i in range(n)])

    def shift(x, by):
        return lax.ppermute(x, "ctx", [(i, i + by) for i in range(n - by)])

    gain = norm_gain.reshape(1, width)
    ext = pltpu.VMEM((heads, rows + HALO, size), F32)
    held = pltpu.VMEM((half, rows, size), BF16)

    cum_shape = pltpu.VMEM((SPAN, 2 * heads, rows), F32)

    def states(mine):
        scratch = [cum_shape, ext, held]
        if not mine:
            buf = pltpu.VMEM((CHIPS, rows, heads * size), BF16)
            scratch = [
                buf,
                buf,
                pltpu.VMEM((CHIPS, taps, heads * size), F32),
                pltpu.VMEM((head_count, rows), F32),
                *scratch,
                pltpu.SemaphoreType.DMA((3 * CHIPS + 1,)),
            ]
        return call(
            functools.partial(state_kernel if mine else fetched_state_kernel, mine, heads, size),
            "states_mine" if mine else "states_other",
            pltpu.VMEM((CHIPS, packet, size), BF16),
            key_input, value_input, conv_weight, log_decay.T,
            in_specs=[VMEM if mine else HBM] * 4,
            scratch=scratch,
        )

    def intra_part(mine, q):
        return call(
            functools.partial(intra_kernel, mine, heads, size),
            "intra_mine" if mine else "intra_other",
            pltpu.VMEM((half + 1, rows, size), F32),
            q, key_input, value_input, conv_weight, cum,
            scratch=[ext, held],
        )

    theirs = states(False)
    got = swap(theirs, 1)
    mine = states(True)
    got_late = swap(mine, 1)

    chip_states = call(
        functools.partial(chip_kernel, heads, size),
        "chip_states",
        pltpu.VMEM((CHIPS, packet, size), BF16),
        mine, got,
    )
    packets = {0: chip_states[0]}
    for g in EXCHANGE:
        packets[g] = swap(chip_states[g], 2 * g)
    q_after, decay_after, chip_states = lax.optimization_barrier(
        (queries, log_decay, chip_states)
    )
    cum = call(
        functools.partial(cum_kernel, heads),
        "cum",
        cum_shape,
        decay_after.T,
    )
    intra_mine = intra_part(True, q_after)
    *late, intra_mine = lax.optimization_barrier((*[packets[g] for g in EXCHANGE], intra_mine))
    packets.update(zip(EXCHANGE, late))
    packets = [packets[g] for g in range(CHIPS)]

    order = pltpu.VMEM((CHIPS, packet, size), BF16)
    known = []
    if n > 2 * SPAN:
        edge = call(
            functools.partial(last_edge_kernel, heads, size),
            "last_edge",
            pltpu.VMEM((PARTS, size), BF16),
            *packets,
            scratch=[order],
        )
        known = [shift(edge, SPAN)]
    span = call(
        functools.partial(span_kernel, heads, size),
        "span_state",
        pltpu.VMEM((heads * size + (2 if known else 1) * PARTS, size), BF16),
        *packets, *known,
        scratch=[order],
    )
    before = swap(span, SPAN) if n == 2 * SPAN else shift(span, SPAN)
    reach = 1
    while reach < n // SPAN - 1:
        before = join_spans(shift(before, SPAN * reach), before, heads, size)
        reach *= 2
    q_after, span = lax.optimization_barrier((queries, span))
    intra_other = intra_part(False, q_after)
    before, intra_other = lax.optimization_barrier((before, intra_other))

    chip_prefix = call(
        functools.partial(spread_kernel, heads, size),
        "chip_prefix",
        pltpu.VMEM((CHIPS, heads * size + PARTS, size), BF16),
        *packets, before, *known,
        scratch=[order],
    )
    own = {0: chip_prefix[0]}
    for g in EXCHANGE:
        own[g] = swap(chip_prefix[g], 2 * g)
    other = {0: swap(own[0], 1)}

    def output(items, result):
        args = [queries, cum, gain]
        for mine, g in items:
            args += [own[g], intra_mine, got] if mine else [other[g], intra_other, got_late]
        count = len(args)
        extra = [] if result is None else [result]
        return call(
            functools.partial(out_kernel, items, heads, size),
            "out_" + "_".join(("m" if mine else "o") + str(g) for mine, g in items),
            jax.ShapeDtypeStruct((rows, width), BF16),
            *args, *extra,
            in_specs=[VMEM] * count + [HBM] * len(extra),
            out_specs=HBM,
            input_output_aliases={count: 0} if extra else {},
            cost_estimate=pl.CostEstimate(flops=1, transcendentals=0, bytes_accessed=1),
            scratch=[
                pltpu.VMEM((len(items) * heads, rows, size), F32),
                pltpu.VMEM((len(items) * heads, rows, 2 * PARTS), BF16),
                pltpu.VMEM((len(items), rows, heads * size), BF16),
                pltpu.SemaphoreType.DMA((len(items),)),
            ],
        )

    result = output([(True, 0), (False, 0)], None)
    *early, final = EXCHANGE[::-1]
    *late, result = lax.optimization_barrier((*[own[g] for g in early], result))
    own.update(zip(early, late))
    other.update({g: swap(own[g], 1) for g in early})
    result = output([(True, g) for g in early], result)
    own[final], result = lax.optimization_barrier((own[final], result))
    other[final] = swap(own[final], 1)
    result = output([(True, final)] + [(False, g) for g in early], result)
    return output([(False, final)], result)


def solution(mesh):
    rows = P(("groups", "ctx"), None)
    return jax.shard_map(
        on_device,
        mesh=mesh,
        in_specs=(rows, rows, rows, rows, P(), P()),
        out_specs=rows,
        check_vma=False,
    )
```

```python
import functools

import jax
import jax.numpy as jnp
from jax import lax
from jax.experimental import pallas as pl
from jax.experimental.pallas import tpu as pltpu
from jax.sharding import PartitionSpec as P

F32 = jnp.float32
BF16 = jnp.bfloat16
CHIPS = 4
SPAN = 2 * CHIPS
HALO = 8
EXCHANGE = (2, 3, 1)
CHUNKS = 2
UNITS = CHUNKS * CHIPS
PARTS = 8
VMEM = pl.BlockSpec(memory_space=pltpu.VMEM)
HBM = pl.BlockSpec(memory_space=pltpu.HBM)


def position():
    me = lax.axis_index("ctx")
    return me & 1, (me >> 1) & (CHIPS - 1)


def head_group(mine, unit):
    core, chip = position()
    group = (core if mine else 1 - core) * CHIPS + (chip ^ (unit % CHIPS))
    return group * CHUNKS + unit // CHIPS


def columns(block, offset, size):
    return pl.ds(pl.multiple_of(block + offset, size), size)


def call(kernel, name, out_shape, *args, scratch=(), in_specs=None, out_specs=VMEM, **options):
    if in_specs is None:
        in_specs = [VMEM] * len(args)
    args = [
        pltpu.with_memory_space_constraint(x, pltpu.VMEM if s is VMEM else pltpu.HBM)
        for x, s in zip(args, in_specs)
    ]
    return pl.pallas_call(
        kernel,
        out_shape=out_shape,
        in_specs=in_specs,
        out_specs=out_specs,
        scratch_shapes=list(scratch),
        name=name,
        compiler_params=pltpu.CompilerParams(vmem_limit_bytes=6 << 20),
        **options,
    )(*args)


def cum_kernel(heads, decay_ref, out_ref):
    x = decay_ref[...]
    count, rows = x.shape
    upto = lax.broadcasted_iota(jnp.int32, (rows, rows), 0) <= lax.broadcasted_iota(
        jnp.int32, (rows, rows), 1
    )
    parts = jnp.concatenate([p.astype(F32) for p in three_parts(x)], 0).astype(BF16)
    sums = jnp.dot(parts, upto.astype(F32).astype(BF16), preferred_element_type=F32)
    sums = sums[0:count] + (sums[count : 2 * count] + sums[2 * count :])
    total = jnp.broadcast_to(sums[:, rows - 1 : rows], sums.shape)
    for b in range(out_ref.shape[0]):
        these = slice(b * heads, (b + 1) * heads)
        out_ref[b, 0:heads, :] = sums[these]
        out_ref[b, heads : 2 * heads, :] = total[these]


def three_parts(x):
    hi = x.astype(BF16)
    rest = x - hi.astype(F32)
    mid = rest.astype(BF16)
    low = (rest - mid.astype(F32)).astype(BF16)
    return hi, mid, low


def side(part, heads, size):
    base = heads * size + part * PARTS
    return slice(base, base + PARTS)


def padded(rows):
    rows = jnp.concatenate(rows, 0)
    spare = jnp.zeros((PARTS - rows.shape[0], rows.shape[1]), F32)
    return jnp.concatenate([rows, spare], 0).astype(BF16)


def put_decay(out, decays, heads, size):
    out[side(1, heads, size), :] = padded([p.astype(F32) for p in three_parts(decays)])


def get_decay(packet, heads, size):
    tail = packet[side(1, heads, size), :].astype(F32)
    return tail[0:heads] + tail[heads : 2 * heads] + tail[2 * heads : 3 * heads]


def edge_states(values, edges, heads):
    row = lax.broadcasted_iota(jnp.int32, values.shape, 0)
    out = []
    for j in range(heads):
        picked = jnp.where(lax.rem(row, heads) == j, values.astype(F32), 0.0).astype(BF16)
        out.append(
            lax.dot_general(picked, edges, (((0,), (0,)), ((), ())), preferred_element_type=F32)
        )
    return out


def conv_keys(k_ref, halo, w_ref, ext, cols):
    rows = k_ref.shape[0]
    ext[0:HALO, :] = halo
    ext[HALO : HALO + rows, :] = k_ref[:, cols].astype(F32)
    total = None
    for j in range(w_ref.shape[0]):
        term = w_ref[j : j + 1, cols] * ext[HALO - j : HALO - j + rows, :]
        total = term if total is None else total + term
    return total.astype(BF16)


def fetched_state_kernel(
    mine, heads, size, k_hbm, v_hbm, w_hbm, decay_hbm, out_ref,
    k_buf, v_buf, w_buf, decay_buf, cum_ref, ext, held, sems,
):
    wide = CHUNKS * heads * size
    copies = [pltpu.make_async_copy(decay_hbm, decay_buf, sems.at[3 * CHIPS])]
    copies[0].start()
    for g in range(CHIPS):
        cols = columns(head_group(mine, g) * heads * size, 0, wide)
        for i, (source, buf) in enumerate(((k_hbm, k_buf), (w_hbm, w_buf), (v_hbm, v_buf))):
            copies.append(
                pltpu.make_async_copy(source.at[:, cols], buf.at[g], sems.at[3 * g + i])
            )
            copies[-1].start()
    copies[0].wait()
    groups, waits = [], []
    for u in range(UNITS):
        g, part = u % CHIPS, u // CHIPS
        cols = slice(part * heads * size, (part + 1) * heads * size)
        groups.append(tuple(buf.at[g, :, cols] for buf in (k_buf, v_buf, w_buf)))
        waits.append(copies[1 + 3 * g : 4 + 3 * g] if part == 0 else [])
    states_of(mine, heads, size, groups, waits, decay_buf, out_ref, cum_ref, ext, held)


def state_kernel(
    mine, heads, size, k_ref, v_ref, w_ref, decay_ref, out_ref, cum_ref, ext, held
):
    groups = []
    for u in range(UNITS):
        cols = columns(head_group(mine, u) * heads * size, 0, heads * size)
        groups.append((k_ref.at[:, cols], v_ref.at[:, cols], w_ref.at[:, cols]))
    waits = [[]] * UNITS
    states_of(mine, heads, size, groups, waits, decay_ref, out_ref, cum_ref, ext, held)


def states_of(mine, heads, size, groups, waits, decay_ref, out_ref, cum_ref, ext, held):
    rows = groups[0][0].shape[0]
    taps = groups[0][2].shape[0]
    cum_kernel(heads, decay_ref, cum_ref)
    none = jnp.zeros((HALO, size), F32)
    for g in range(UNITS):
        k_ref, v_ref, w_ref = groups[g]
        for copy in waits[g]:
            copy.wait()
        cum = cum_ref[head_group(mine, g)]
        ending = jnp.exp(cum[heads : 2 * heads] - cum[0:heads]).T
        edges, values = [], []
        for j in range(heads):
            cols = slice(j * size, (j + 1) * size)
            key_conv = conv_keys(k_ref, none, w_ref, ext.at[g % 2 * heads + j], cols)
            held[g * heads + j] = (key_conv.astype(F32) * ending[:, j : j + 1]).astype(BF16)
            last = k_ref[rows - HALO : rows, cols].astype(F32)
            head_edges = []
            for t in range(taps - 1):
                terms = [
                    w_ref[i : i + 1, cols] * last[HALO + t - i : HALO + t - i + 1]
                    for i in range(t + 1, taps)
                ]
                head_edges.append(sum(terms[1:], terms[0]))
            edges.append(head_edges)
            values.append(v_ref[0:HALO, cols].astype(F32) * ending[0:HALO, j : j + 1])
        put_decay(out_ref.at[g], jnp.exp(cum[heads : 2 * heads]), heads, size)
        out_ref[g, side(0, heads, size), :] = padded(
            [edges[j][t] for t in range(taps - 1) for j in range(heads)]
        )
        out_ref[g, side(2, heads, size), :] = padded(
            [values[j][t : t + 1] for t in range(taps - 1) for j in range(heads)]
        )
    for g in range(UNITS):
        for j in range(heads):
            cols = slice(j * size, (j + 1) * size)
            state = lax.dot_general(
                groups[g][1][:, cols], held[g * heads + j], (((0,), (0,)), ((), ())),
                preferred_element_type=F32,
            )
            out_ref[g, cols, :] = state.astype(BF16)


def intra_kernel(mine, heads, size, q_ref, k_ref, v_ref, w_ref, cum_ref, out_ref, ext, held):
    rows = q_ref.shape[0]
    causal = lax.broadcasted_iota(jnp.int32, (rows, rows), 0) >= lax.broadcasted_iota(
        jnp.int32, (rows, rows), 1
    )
    none = jnp.zeros((HALO, size), F32)
    for g in range(UNITS):
        b = head_group(mine, g)
        cum = cum_ref[b][0:heads]
        cum_col = cum.T
        growth = jnp.exp(-cum_col[0:HALO])
        values = []
        for j in range(heads):
            cols = columns(b * heads * size, j * size, size)
            key_conv = conv_keys(k_ref, none, w_ref, ext.at[g % 2 * heads + j], cols)
            scores = lax.dot_general(
                q_ref[:, cols], key_conv, (((1,), (1,)), ((), ())), preferred_element_type=F32
            )
            spread = cum_col[:, j : j + 1] - cum[j : j + 1]
            weights = jnp.where(causal, scores * jnp.exp(jnp.where(causal, spread, 0.0)), 0.0)
            held[g * heads + j] = weights.astype(BF16)
            values.append(v_ref[0:HALO, cols].astype(F32) * growth[:, j : j + 1])
        out_ref[UNITS * heads, g * PARTS : (g + 1) * PARTS, :] = padded(
            [values[j][t : t + 1] for t in range(3) for j in range(heads)]
        ).astype(F32)
    for g in range(UNITS):
        b = head_group(mine, g)
        for j in range(heads):
            cols = columns(b * heads * size, j * size, size)
            out_ref[g * heads + j] = jnp.dot(
                held[g * heads + j], v_ref[:, cols], preferred_element_type=F32
            )


def chip_kernel(heads, size, own_ref, got_ref, out_ref):
    core, _ = position()
    first = core == 0
    for g in range(UNITS):
        own_decay = get_decay(own_ref.at[g], heads, size)
        got_decay = get_decay(got_ref.at[g], heads, size)
        own_by = jnp.where(first, got_decay, 1.0)
        got_by = jnp.where(first, 1.0, own_decay)

        def earlier_later(part):
            own = own_ref[g, side(part, heads, size), :].astype(F32)
            got = got_ref[g, side(part, heads, size), :].astype(F32)
            return jnp.where(first, own, got), jnp.where(first, got, own)

        edges, out_edges = earlier_later(0)
        out_values, values = earlier_later(2)
        fixes = edge_states(values.astype(BF16), edges.astype(BF16), heads)
        for j in range(heads):
            rows = slice(j * size, (j + 1) * size)
            out_ref[g, rows, :] = (
                own_ref[g, rows, :].astype(F32) * own_by[j : j + 1]
                + got_ref[g, rows, :].astype(F32) * got_by[j : j + 1]
                + fixes[j]
            ).astype(BF16)
        put_decay(out_ref.at[g], own_decay * got_decay, heads, size)
        later_by = jnp.where(first, got_decay, own_decay)
        out_ref[g, side(0, heads, size), :] = out_edges.astype(BF16)
        out_ref[g, side(2, heads, size), :] = padded(
            [out_values[t * heads : (t + 1) * heads] * later_by for t in range(3)]
        )


def in_order(packets, held):
    _, chip = position()
    for g in range(CHIPS):
        held[chip ^ g] = packets[g][...]


def chip_fixes(held, b, edges, heads, size):
    return edge_states(held[b, side(2, heads, size), :], edges, heads)


def last_edge_kernel(heads, size, *refs):
    packets, out_ref, held = refs[:CHIPS], refs[CHIPS], refs[CHIPS + 1]
    in_order(packets, held)
    out_ref[...] = held[CHIPS - 1, side(0, heads, size), :]


def span_kernel(heads, size, *refs):
    packets, before, (out_ref, held) = refs[:CHIPS], refs[CHIPS:-2], refs[-2:]
    in_order(packets, held)
    decays = [get_decay(held.at[b], heads, size) for b in range(CHIPS)]
    fixes = [
        chip_fixes(held, b, held[b - 1, side(0, heads, size), :], heads, size)
        for b in range(1, CHIPS)
    ]
    fixes.insert(0, chip_fixes(held, 0, before[0][...], heads, size) if before else None)
    for j in range(heads):
        rows = slice(j * size, (j + 1) * size)
        acc = held[0, rows, :].astype(F32)
        if before:
            acc = acc + fixes[0][j]
        for b in range(1, CHIPS):
            acc = acc * decays[b][j : j + 1] + (held[b, rows, :].astype(F32) + fixes[b][j])
        out_ref[rows, :] = acc.astype(BF16)
    whole = decays[0]
    for b in range(1, CHIPS):
        whole = whole * decays[b]
    out_ref[side(0, heads, size), :] = held[CHIPS - 1, side(0, heads, size), :]
    if before:
        put_decay(out_ref, whole, heads, size)


def spread_kernel(heads, size, *refs):
    packets, before, known, (out_ref, held) = refs[:CHIPS], refs[CHIPS], refs[CHIPS + 1 : -2], refs[-2:]
    _, chip = position()
    later = lax.axis_index("ctx") >= SPAN
    in_order(packets, held)
    decays = [get_decay(held.at[b], heads, size) for b in range(CHIPS)]
    edges = known[0][...] if known else before[side(0, heads, size), :]
    edges = [jnp.where(later, edges.astype(F32), 0.0).astype(BF16)]
    edges += [held[b, side(0, heads, size), :] for b in range(CHIPS - 1)]
    fixes = [chip_fixes(held, b, edges[b], heads, size) for b in range(CHIPS - 1)]
    for j in range(heads):
        rows = slice(j * size, (j + 1) * size)
        acc = jnp.where(later, before[rows, :].astype(F32), 0.0)
        out_ref[chip, rows, :] = acc.astype(BF16)
        for b in range(1, CHIPS):
            acc = acc * decays[b - 1][j : j + 1] + (
                held[b - 1, rows, :].astype(F32) + fixes[b - 1][j]
            )
            out_ref[chip ^ b, rows, :] = acc.astype(BF16)
    for b in range(CHIPS):
        out_ref[chip ^ b, heads * size : heads * size + PARTS, :] = edges[b]


def out_kernel(items, heads, size, *refs):
    q_ref, cum_ref, gain_ref = refs[:3]
    per_item = [refs[3 + 3 * i : 6 + 3 * i] for i in range(len(items))]
    out_ref, inter_ref, score_ref, done_ref, sems = refs[-5:]
    rows = q_ref.shape[0]
    core, _ = position()
    second = core == 1
    row = lax.broadcasted_iota(jnp.int32, (rows, 2 * PARTS), 0)
    column = lax.broadcasted_iota(jnp.int32, (rows, 2 * PARTS), 1)
    edge = lax.rem(column, PARTS)
    causal = (lax.div(edge, heads) <= row) & (edge < 3 * heads)
    ahead = column < PARTS
    kept = ((ahead & (core == 1)) | causal) & (ahead | (core == 1))
    kept = [kept & (lax.rem(edge, heads) == j) for j in range(heads)]
    for i, (mine, g) in enumerate(items):
        prefix_ref, intra_ref, sib_ref = per_item[i]
        b = head_group(mine, g)
        started = jnp.exp(cum_ref[b][0:heads]).T
        by = jnp.where(second, get_decay(sib_ref.at[g], heads, size), 1.0)
        edges = jnp.concatenate(
            [
                prefix_ref[heads * size : heads * size + PARTS, :].astype(F32),
                sib_ref[g, side(0, heads, size), :].astype(F32),
            ],
            0,
        ).astype(BF16)
        for j in range(heads):
            cols = columns(b * heads * size, j * size, size)
            these = slice(j * size, (j + 1) * size)
            sib = jnp.where(second, sib_ref[g, these, :].astype(F32), 0.0)
            prefix = (prefix_ref[these, :].astype(F32) * by[j : j + 1] + sib).astype(BF16)
            both = lax.dot_general(
                q_ref[:, cols],
                jnp.concatenate([prefix, edges], 0),
                (((1,), (1,)), ((), ())),
                preferred_element_type=F32,
            )
            both = both * started[:, j : j + 1]
            inter_ref[i * heads + j] = both[:, 0:size] + intra_ref[g * heads + j]
            score_ref[i * heads + j] = jnp.where(kept[j], both[:, size:], 0.0).astype(BF16)
    copies = []
    for i, (mine, g) in enumerate(items):
        _, intra_ref, sib_ref = per_item[i]
        b = head_group(mine, g)
        values = intra_ref[UNITS * heads, g * PARTS : (g + 1) * PARTS, :]
        ahead_values = jnp.where(second, sib_ref[g, side(2, heads, size), :].astype(F32), values)
        values = jnp.concatenate([ahead_values, values], 0).astype(BF16)
        for j in range(heads):
            inter_ref[i * heads + j] += jnp.dot(
                score_ref[i * heads + j], values, preferred_element_type=F32
            )
    for i, (mine, g) in enumerate(items):
        b = head_group(mine, g)
        for j in range(heads):
            cols = columns(b * heads * size, j * size, size)
            mixed = inter_ref[i * heads + j]
            scale = lax.rsqrt(jnp.mean(mixed * mixed, axis=1, keepdims=True) + 1e-05)
            done_ref[i, :, j * size : (j + 1) * size] = (
                mixed * scale * gain_ref[:, cols]
            ).astype(BF16)
        wide = columns(b * heads * size, 0, heads * size)
        copies.append(pltpu.make_async_copy(done_ref.at[i], out_ref.at[:, wide], sems.at[i]))
        copies[-1].start()
    for copy in copies:
        copy.wait()


def join_spans(earlier, later, heads, size):
    base = heads * size
    own = side(1, heads, size)

    def decay(x):
        tail = x[own].astype(F32)
        return tail[0:heads] + tail[heads : 2 * heads] + tail[2 * heads : 3 * heads]

    by = decay(later)
    state = (
        by[:, None, :] * earlier[:base].astype(F32).reshape(heads, size, -1)
        + later[:base].astype(F32).reshape(heads, size, -1)
    ).reshape(base, -1)
    parts = three_parts(by * decay(earlier))
    return jnp.concatenate([state.astype(BF16), later[base : own.start], *parts, later[own.start + 3 * heads :]], 0)


def on_device(queries, key_input, value_input, log_decay, conv_weight, norm_gain):
    rows, width = queries.shape
    head_count = log_decay.shape[1]
    size = width // head_count
    heads = head_count // (SPAN * CHUNKS)
    taps = conv_weight.shape[0]
    half = UNITS * heads
    packet = heads * size + 3 * PARTS
    n = lax.axis_size("ctx")

    def swap(x, mask):
        return lax.ppermute(x, "ctx", [(i, i ^ mask) for i in range(n)])

    def shift(x, by):
        return lax.ppermute(x, "ctx", [(i, i + by) for i in range(n - by)])

    gain = norm_gain.reshape(1, width)
    ext = pltpu.VMEM((2 * heads, rows + HALO, size), F32)
    held = pltpu.VMEM((half, rows, size), BF16)

    cum_shape = pltpu.VMEM((SPAN * CHUNKS, 2 * heads, rows), F32)

    def states(mine):
        scratch = [cum_shape, ext, held]
        if not mine:
            buf = pltpu.VMEM((CHIPS, rows, CHUNKS * heads * size), BF16)
            scratch = [
                buf,
                buf,
                pltpu.VMEM((CHIPS, taps, CHUNKS * heads * size), F32),
                pltpu.VMEM((head_count, rows), F32),
                *scratch,
                pltpu.SemaphoreType.DMA((3 * CHIPS + 1,)),
            ]
        return call(
            functools.partial(state_kernel if mine else fetched_state_kernel, mine, heads, size),
            "states_mine" if mine else "states_other",
            pltpu.VMEM((UNITS, packet, size), BF16),
            key_input, value_input, conv_weight, log_decay.T,
            in_specs=[VMEM if mine else HBM] * 4,
            scratch=scratch,
        )

    def intra_part(mine, q):
        return call(
            functools.partial(intra_kernel, mine, heads, size),
            "intra_mine" if mine else "intra_other",
            pltpu.VMEM((half + 1, rows, size), F32),
            q, key_input, value_input, conv_weight, cum,
            scratch=[ext, held],
        )

    theirs = states(False)
    got = swap(theirs, 1)
    mine = states(True)
    got_late = swap(mine, 1)

    chip_states = call(
        functools.partial(chip_kernel, heads, size),
        "chip_states",
        pltpu.VMEM((UNITS, packet, size), BF16),
        mine, got,
    )
    order = pltpu.VMEM((CHIPS, packet, size), BF16)

    def joined(packets):
        known = []
        if n > 2 * SPAN:
            edge = call(
                functools.partial(last_edge_kernel, heads, size),
                "last_edge",
                pltpu.VMEM((PARTS, size), BF16),
                *packets,
                scratch=[order],
            )
            known = [shift(edge, SPAN)]
        span = call(
            functools.partial(span_kernel, heads, size),
            "span_state",
            pltpu.VMEM((heads * size + (2 if known else 1) * PARTS, size), BF16),
            *packets, *known,
            scratch=[order],
        )
        before = swap(span, SPAN) if n == 2 * SPAN else shift(span, SPAN)
        reach = 1
        while reach < n // SPAN - 1:
            before = join_spans(shift(before, SPAN * reach), before, heads, size)
            reach *= 2
        return span, before, known

    packets = []
    for part in range(CHUNKS):
        these = {0: chip_states[part * CHIPS]}
        for g in EXCHANGE:
            these[g] = swap(chip_states[part * CHIPS + g], 2 * g)
        packets.append([these[g] for g in range(CHIPS)])
    q_after, decay_after, chip_states = lax.optimization_barrier(
        (queries, log_decay, chip_states)
    )
    cum = call(
        functools.partial(cum_kernel, heads),
        "cum",
        cum_shape,
        decay_after.T,
    )
    intra_mine = intra_part(True, q_after)
    last = packets[-1]
    *late, intra_mine = lax.optimization_barrier((*[last[g] for g in EXCHANGE], intra_mine))
    for g, x in zip(EXCHANGE, late):
        last[g] = x

    spans, befores, knowns = zip(*[joined(p) for p in packets])
    q_after, _ = lax.optimization_barrier((queries, spans[-1]))
    intra_other = intra_part(False, q_after)
    before, intra_other = lax.optimization_barrier((befores[-1], intra_other))
    befores = [*befores[:-1], before]

    own, other = {}, {}
    for part in range(CHUNKS):
        chip_prefix = call(
            functools.partial(spread_kernel, heads, size),
            "chip_prefix",
            pltpu.VMEM((CHIPS, heads * size + PARTS, size), BF16),
            *packets[part], befores[part], *knowns[part],
            scratch=[order],
        )
        first = part * CHIPS
        own[first] = chip_prefix[0]
        for g in EXCHANGE:
            own[first + g] = swap(chip_prefix[g], 2 * g)
        other[first] = swap(own[first], 1)

    def output(items, result):
        args = [queries, cum, gain]
        for mine, g in items:
            args += [own[g], intra_mine, got] if mine else [other[g], intra_other, got_late]
        count = len(args)
        extra = [] if result is None else [result]
        return call(
            functools.partial(out_kernel, items, heads, size),
            "out_" + "_".join(("m" if mine else "o") + str(g) for mine, g in items),
            jax.ShapeDtypeStruct((rows, width), BF16),
            *args, *extra,
            in_specs=[VMEM] * count + [HBM] * len(extra),
            out_specs=HBM,
            input_output_aliases={count: 0} if extra else {},
            cost_estimate=pl.CostEstimate(flops=1, transcendentals=0, bytes_accessed=1),
            scratch=[
                pltpu.VMEM((len(items) * heads, rows, size), F32),
                pltpu.VMEM((len(items) * heads, rows, 2 * PARTS), BF16),
                pltpu.VMEM((len(items), rows, heads * size), BF16),
                pltpu.SemaphoreType.DMA((len(items),)),
            ],
        )

    result = None
    for part in range(CHUNKS):
        first = part * CHIPS
        units = [first + g for g in EXCHANGE]
        result = output([(True, first), (False, first)], result)
        *late, result = lax.optimization_barrier((*[own[u] for u in units], result))
        own.update(zip(units, late))
        other.update({u: swap(own[u], 1) for u in units})
        result = output([(True, u) for u in units], result)
        result = output([(False, u) for u in units], result)
    return result


def solution(mesh):
    rows = P(("groups", "ctx"), None)
    return jax.shard_map(
        on_device,
        mesh=mesh,
        in_specs=(rows, rows, rows, rows, P(), P()),
        out_specs=rows,
        check_vma=False,
    )
```

```python
import functools

import jax
import jax.numpy as jnp
from jax import lax
from jax.experimental import pallas as pl
from jax.experimental.pallas import tpu as pltpu
from jax.sharding import PartitionSpec as P

F32 = jnp.float32
BF16 = jnp.bfloat16
CHIPS = 4
SPAN = 2 * CHIPS
HALO = 8
EXCHANGE = (2, 3, 1)
CHUNKS = 2
UNITS = CHUNKS * CHIPS
PARTS = 8
VMEM = pl.BlockSpec(memory_space=pltpu.VMEM)
HBM = pl.BlockSpec(memory_space=pltpu.HBM)


def position():
    me = lax.axis_index("ctx")
    return me & 1, (me >> 1) & (CHIPS - 1)


def head_group(mine, unit):
    core, chip = position()
    group = (core if mine else 1 - core) * CHIPS + (chip ^ (unit % CHIPS))
    return group * CHUNKS + unit // CHIPS


def columns(block, offset, size):
    return pl.ds(pl.multiple_of(block + offset, size), size)


def call(kernel, name, out_shape, *args, scratch=(), in_specs=None, out_specs=VMEM, **options):
    if in_specs is None:
        in_specs = [VMEM] * len(args)
    args = [
        pltpu.with_memory_space_constraint(x, pltpu.VMEM if s is VMEM else pltpu.HBM)
        for x, s in zip(args, in_specs)
    ]
    return pl.pallas_call(
        kernel,
        out_shape=out_shape,
        in_specs=in_specs,
        out_specs=out_specs,
        scratch_shapes=list(scratch),
        name=name,
        compiler_params=pltpu.CompilerParams(vmem_limit_bytes=6 << 20),
        **options,
    )(*args)


def cum_kernel(heads, decay_ref, out_ref):
    x = decay_ref[...]
    count, rows = x.shape
    upto = lax.broadcasted_iota(jnp.int32, (rows, rows), 0) <= lax.broadcasted_iota(
        jnp.int32, (rows, rows), 1
    )
    parts = jnp.concatenate([p.astype(F32) for p in three_parts(x)], 0).astype(BF16)
    sums = jnp.dot(parts, upto.astype(F32).astype(BF16), preferred_element_type=F32)
    sums = sums[0:count] + (sums[count : 2 * count] + sums[2 * count :])
    total = jnp.broadcast_to(sums[:, rows - 1 : rows], sums.shape)
    for b in range(out_ref.shape[0]):
        these = slice(b * heads, (b + 1) * heads)
        out_ref[b, 0:heads, :] = sums[these]
        out_ref[b, heads : 2 * heads, :] = total[these]


def three_parts(x):
    hi = x.astype(BF16)
    rest = x - hi.astype(F32)
    mid = rest.astype(BF16)
    low = (rest - mid.astype(F32)).astype(BF16)
    return hi, mid, low


def side(part, heads, size):
    base = heads * size + part * PARTS
    return slice(base, base + PARTS)


def padded(rows):
    rows = jnp.concatenate(rows, 0)
    spare = jnp.zeros((PARTS - rows.shape[0], rows.shape[1]), F32)
    return jnp.concatenate([rows, spare], 0).astype(BF16)


def put_decay(out, decays, heads, size):
    out[side(1, heads, size), :] = padded([p.astype(F32) for p in three_parts(decays)])


def get_decay(packet, heads, size):
    tail = packet[side(1, heads, size), :].astype(F32)
    return tail[0:heads] + tail[heads : 2 * heads] + tail[2 * heads : 3 * heads]


def edge_states(values, edges, heads):
    row = lax.broadcasted_iota(jnp.int32, values.shape, 0)
    out = []
    for j in range(heads):
        picked = jnp.where(lax.rem(row, heads) == j, values.astype(F32), 0.0).astype(BF16)
        out.append(
            lax.dot_general(picked, edges, (((0,), (0,)), ((), ())), preferred_element_type=F32)
        )
    return out


def conv_keys(k_ref, halo, w_ref, ext, cols):
    rows = k_ref.shape[0]
    ext[0:HALO, :] = halo
    ext[HALO : HALO + rows, :] = k_ref[:, cols].astype(F32)
    total = None
    for j in range(w_ref.shape[0]):
        term = w_ref[j : j + 1, cols] * ext[HALO - j : HALO - j + rows, :]
        total = term if total is None else total + term
    return total.astype(BF16)


def fetched_state_kernel(
    mine, heads, size, k_hbm, v_hbm, w_hbm, decay_hbm, out_ref,
    k_buf, v_buf, w_buf, decay_buf, cum_ref, ext, held, sems,
):
    wide = CHUNKS * heads * size
    copies = [pltpu.make_async_copy(decay_hbm, decay_buf, sems.at[3 * CHIPS])]
    copies[0].start()
    for g in range(CHIPS):
        cols = columns(head_group(mine, g) * heads * size, 0, wide)
        for i, (source, buf) in enumerate(((k_hbm, k_buf), (w_hbm, w_buf), (v_hbm, v_buf))):
            copies.append(
                pltpu.make_async_copy(source.at[:, cols], buf.at[g], sems.at[3 * g + i])
            )
            copies[-1].start()
    copies[0].wait()
    groups, waits = [], []
    for u in range(UNITS):
        g, part = u % CHIPS, u // CHIPS
        cols = slice(part * heads * size, (part + 1) * heads * size)
        groups.append(tuple(buf.at[g, :, cols] for buf in (k_buf, v_buf, w_buf)))
        waits.append(copies[1 + 3 * g : 4 + 3 * g] if part == 0 else [])
    states_of(mine, heads, size, groups, waits, decay_buf, out_ref, cum_ref, ext, held)


def state_kernel(
    mine, heads, size, k_ref, v_ref, w_ref, decay_ref, out_ref, cum_ref, ext, held
):
    groups = []
    for u in range(UNITS):
        cols = columns(head_group(mine, u) * heads * size, 0, heads * size)
        groups.append((k_ref.at[:, cols], v_ref.at[:, cols], w_ref.at[:, cols]))
    waits = [[]] * UNITS
    states_of(mine, heads, size, groups, waits, decay_ref, out_ref, cum_ref, ext, held)


def states_of(mine, heads, size, groups, waits, decay_ref, out_ref, cum_ref, ext, held):
    rows = groups[0][0].shape[0]
    taps = groups[0][2].shape[0]
    cum_kernel(heads, decay_ref, cum_ref)
    none = jnp.zeros((HALO, size), F32)
    for g in range(UNITS):
        k_ref, v_ref, w_ref = groups[g]
        for copy in waits[g]:
            copy.wait()
        cum = cum_ref[head_group(mine, g)]
        ending = jnp.exp(cum[heads : 2 * heads] - cum[0:heads]).T
        edges, values = [], []
        for j in range(heads):
            cols = slice(j * size, (j + 1) * size)
            key_conv = conv_keys(k_ref, none, w_ref, ext.at[g % 2 * heads + j], cols)
            held[g * heads + j] = (key_conv.astype(F32) * ending[:, j : j + 1]).astype(BF16)
            last = k_ref[rows - HALO : rows, cols].astype(F32)
            head_edges = []
            for t in range(taps - 1):
                terms = [
                    w_ref[i : i + 1, cols] * last[HALO + t - i : HALO + t - i + 1]
                    for i in range(t + 1, taps)
                ]
                head_edges.append(sum(terms[1:], terms[0]))
            edges.append(head_edges)
            values.append(v_ref[0:HALO, cols].astype(F32) * ending[0:HALO, j : j + 1])
        put_decay(out_ref.at[g], jnp.exp(cum[heads : 2 * heads]), heads, size)
        out_ref[g, side(0, heads, size), :] = padded(
            [edges[j][t] for t in range(taps - 1) for j in range(heads)]
        )
        out_ref[g, side(2, heads, size), :] = padded(
            [values[j][t : t + 1] for t in range(taps - 1) for j in range(heads)]
        )
    for g in range(UNITS):
        for j in range(heads):
            cols = slice(j * size, (j + 1) * size)
            state = lax.dot_general(
                groups[g][1][:, cols], held[g * heads + j], (((0,), (0,)), ((), ())),
                preferred_element_type=F32,
            )
            out_ref[g, cols, :] = state.astype(BF16)


def intra_kernel(mine, heads, size, q_ref, k_ref, v_ref, w_ref, cum_ref, out_ref, ext, held):
    rows = q_ref.shape[0]
    causal = lax.broadcasted_iota(jnp.int32, (rows, rows), 0) >= lax.broadcasted_iota(
        jnp.int32, (rows, rows), 1
    )
    none = jnp.zeros((HALO, size), F32)
    for g in range(UNITS):
        b = head_group(mine, g)
        cum = cum_ref[b][0:heads]
        cum_col = cum.T
        growth = jnp.exp(-cum_col[0:HALO])
        values = []
        for j in range(heads):
            cols = columns(b * heads * size, j * size, size)
            key_conv = conv_keys(k_ref, none, w_ref, ext.at[g % 2 * heads + j], cols)
            scores = lax.dot_general(
                q_ref[:, cols], key_conv, (((1,), (1,)), ((), ())), preferred_element_type=F32
            )
            spread = cum_col[:, j : j + 1] - cum[j : j + 1]
            weights = jnp.where(causal, scores * jnp.exp(jnp.where(causal, spread, 0.0)), 0.0)
            held[g * heads + j] = weights.astype(BF16)
            values.append(v_ref[0:HALO, cols].astype(F32) * growth[:, j : j + 1])
        out_ref[UNITS * heads, g * PARTS : (g + 1) * PARTS, :] = padded(
            [values[j][t : t + 1] for t in range(3) for j in range(heads)]
        ).astype(F32)
    for g in range(UNITS):
        b = head_group(mine, g)
        for j in range(heads):
            cols = columns(b * heads * size, j * size, size)
            out_ref[g * heads + j] = jnp.dot(
                held[g * heads + j], v_ref[:, cols], preferred_element_type=F32
            )


def chip_kernel(heads, size, own_ref, got_ref, out_ref):
    core, _ = position()
    first = core == 0
    for g in range(UNITS):
        own_decay = get_decay(own_ref.at[g], heads, size)
        got_decay = get_decay(got_ref.at[g], heads, size)
        own_by = jnp.where(first, got_decay, 1.0)
        got_by = jnp.where(first, 1.0, own_decay)

        def earlier_later(part):
            own = own_ref[g, side(part, heads, size), :].astype(F32)
            got = got_ref[g, side(part, heads, size), :].astype(F32)
            return jnp.where(first, own, got), jnp.where(first, got, own)

        edges, out_edges = earlier_later(0)
        out_values, values = earlier_later(2)
        fixes = edge_states(values.astype(BF16), edges.astype(BF16), heads)
        for j in range(heads):
            rows = slice(j * size, (j + 1) * size)
            out_ref[g, rows, :] = (
                own_ref[g, rows, :].astype(F32) * own_by[j : j + 1]
                + got_ref[g, rows, :].astype(F32) * got_by[j : j + 1]
                + fixes[j]
            ).astype(BF16)
        put_decay(out_ref.at[g], own_decay * got_decay, heads, size)
        later_by = jnp.where(first, got_decay, own_decay)
        out_ref[g, side(0, heads, size), :] = out_edges.astype(BF16)
        out_ref[g, side(2, heads, size), :] = padded(
            [out_values[t * heads : (t + 1) * heads] * later_by for t in range(3)]
        )


def in_order(packets, held):
    _, chip = position()
    for g in range(CHIPS):
        held[chip ^ g] = packets[g][...]


def chip_fixes(held, b, edges, heads, size):
    return edge_states(held[b, side(2, heads, size), :], edges, heads)


def last_edge_kernel(heads, size, *refs):
    packets, out_ref, held = refs[:CHIPS], refs[CHIPS], refs[CHIPS + 1]
    in_order(packets, held)
    out_ref[...] = held[CHIPS - 1, side(0, heads, size), :]


def span_kernel(heads, size, *refs):
    packets, before, (out_ref, held) = refs[:CHIPS], refs[CHIPS:-2], refs[-2:]
    in_order(packets, held)
    decays = [get_decay(held.at[b], heads, size) for b in range(CHIPS)]
    fixes = [
        chip_fixes(held, b, held[b - 1, side(0, heads, size), :], heads, size)
        for b in range(1, CHIPS)
    ]
    fixes.insert(0, chip_fixes(held, 0, before[0][...], heads, size) if before else None)
    for j in range(heads):
        rows = slice(j * size, (j + 1) * size)
        acc = held[0, rows, :].astype(F32)
        if before:
            acc = acc + fixes[0][j]
        for b in range(1, CHIPS):
            acc = acc * decays[b][j : j + 1] + (held[b, rows, :].astype(F32) + fixes[b][j])
        out_ref[rows, :] = acc.astype(BF16)
    whole = decays[0]
    for b in range(1, CHIPS):
        whole = whole * decays[b]
    out_ref[side(0, heads, size), :] = held[CHIPS - 1, side(0, heads, size), :]
    if before:
        put_decay(out_ref, whole, heads, size)


def spread_kernel(heads, size, *refs):
    packets, before, known, (out_ref, held) = refs[:CHIPS], refs[CHIPS], refs[CHIPS + 1 : -2], refs[-2:]
    _, chip = position()
    later = lax.axis_index("ctx") >= SPAN
    in_order(packets, held)
    decays = [get_decay(held.at[b], heads, size) for b in range(CHIPS)]
    edges = known[0][...] if known else before[side(0, heads, size), :]
    edges = [jnp.where(later, edges.astype(F32), 0.0).astype(BF16)]
    edges += [held[b, side(0, heads, size), :] for b in range(CHIPS - 1)]
    fixes = [chip_fixes(held, b, edges[b], heads, size) for b in range(CHIPS - 1)]
    for j in range(heads):
        rows = slice(j * size, (j + 1) * size)
        acc = jnp.where(later, before[rows, :].astype(F32), 0.0)
        out_ref[chip, rows, :] = acc.astype(BF16)
        for b in range(1, CHIPS):
            acc = acc * decays[b - 1][j : j + 1] + (
                held[b - 1, rows, :].astype(F32) + fixes[b - 1][j]
            )
            out_ref[chip ^ b, rows, :] = acc.astype(BF16)
    for b in range(CHIPS):
        out_ref[chip ^ b, heads * size : heads * size + PARTS, :] = edges[b]


def last_out_kernel(items, earlier, heads, size, *refs):
    count = 3 + 3 * len(items)
    made = refs[count : count + len(earlier)]
    out_ref, inter_ref, score_ref, done_ref, sems = refs[-5:]
    copies = []

    def write(item, source):
        cols = columns(head_group(*item) * heads * size, 0, heads * size)
        copies.append(
            pltpu.make_async_copy(source, out_ref.at[:, cols], sems.at[len(copies)])
        )
        copies[-1].start()

    for there, ref in zip(earlier, made):
        for i, item in enumerate(there):
            write(item, ref.at[i])
    out_kernel(items, heads, size, *refs[:count], done_ref, inter_ref, score_ref, write=write)
    for copy in copies:
        copy.wait()


def out_kernel(items, heads, size, *refs, write=None):
    q_ref, cum_ref, gain_ref = refs[:3]
    per_item = [refs[3 + 3 * i : 6 + 3 * i] for i in range(len(items))]
    done_ref, inter_ref, score_ref = refs[-3:]
    rows = q_ref.shape[0]
    core, _ = position()
    second = core == 1
    row = lax.broadcasted_iota(jnp.int32, (rows, 2 * PARTS), 0)
    column = lax.broadcasted_iota(jnp.int32, (rows, 2 * PARTS), 1)
    edge = lax.rem(column, PARTS)
    causal = (lax.div(edge, heads) <= row) & (edge < 3 * heads)
    ahead = column < PARTS
    kept = ((ahead & (core == 1)) | causal) & (ahead | (core == 1))
    kept = [kept & (lax.rem(edge, heads) == j) for j in range(heads)]
    for i, (mine, g) in enumerate(items):
        prefix_ref, intra_ref, sib_ref = per_item[i]
        b = head_group(mine, g)
        started = jnp.exp(cum_ref[b][0:heads]).T
        by = jnp.where(second, get_decay(sib_ref.at[g], heads, size), 1.0)
        edges = jnp.concatenate(
            [
                prefix_ref[heads * size : heads * size + PARTS, :].astype(F32),
                sib_ref[g, side(0, heads, size), :].astype(F32),
            ],
            0,
        ).astype(BF16)
        for j in range(heads):
            cols = columns(b * heads * size, j * size, size)
            these = slice(j * size, (j + 1) * size)
            sib = jnp.where(second, sib_ref[g, these, :].astype(F32), 0.0)
            prefix = (prefix_ref[these, :].astype(F32) * by[j : j + 1] + sib).astype(BF16)
            both = lax.dot_general(
                q_ref[:, cols],
                jnp.concatenate([prefix, edges], 0),
                (((1,), (1,)), ((), ())),
                preferred_element_type=F32,
            )
            both = both * started[:, j : j + 1]
            inter_ref[i * heads + j] = both[:, 0:size] + intra_ref[g * heads + j]
            score_ref[i * heads + j] = jnp.where(kept[j], both[:, size:], 0.0).astype(BF16)
    for i, (mine, g) in enumerate(items):
        _, intra_ref, sib_ref = per_item[i]
        b = head_group(mine, g)
        values = intra_ref[UNITS * heads, g * PARTS : (g + 1) * PARTS, :]
        ahead_values = jnp.where(second, sib_ref[g, side(2, heads, size), :].astype(F32), values)
        values = jnp.concatenate([ahead_values, values], 0).astype(BF16)
        for j in range(heads):
            inter_ref[i * heads + j] += jnp.dot(
                score_ref[i * heads + j], values, preferred_element_type=F32
            )
    for i, (mine, g) in enumerate(items):
        b = head_group(mine, g)
        for j in range(heads):
            cols = columns(b * heads * size, j * size, size)
            mixed = inter_ref[i * heads + j]
            scale = lax.rsqrt(jnp.mean(mixed * mixed, axis=1, keepdims=True) + 1e-05)
            done_ref[i, :, j * size : (j + 1) * size] = (
                mixed * scale * gain_ref[:, cols]
            ).astype(BF16)
        if write is not None:
            write((mine, g), done_ref.at[i])


def join_spans(earlier, later, heads, size):
    base = heads * size
    own = side(1, heads, size)

    def decay(x):
        tail = x[own].astype(F32)
        return tail[0:heads] + tail[heads : 2 * heads] + tail[2 * heads : 3 * heads]

    by = decay(later)
    state = (
        by[:, None, :] * earlier[:base].astype(F32).reshape(heads, size, -1)
        + later[:base].astype(F32).reshape(heads, size, -1)
    ).reshape(base, -1)
    parts = three_parts(by * decay(earlier))
    return jnp.concatenate([state.astype(BF16), later[base : own.start], *parts, later[own.start + 3 * heads :]], 0)


def on_device(queries, key_input, value_input, log_decay, conv_weight, norm_gain):
    rows, width = queries.shape
    head_count = log_decay.shape[1]
    size = width // head_count
    heads = head_count // (SPAN * CHUNKS)
    taps = conv_weight.shape[0]
    half = UNITS * heads
    packet = heads * size + 3 * PARTS
    n = lax.axis_size("ctx")

    def swap(x, mask):
        return lax.ppermute(x, "ctx", [(i, i ^ mask) for i in range(n)])

    def shift(x, by):
        return lax.ppermute(x, "ctx", [(i, i + by) for i in range(n - by)])

    gain = norm_gain.reshape(1, width)
    ext = pltpu.VMEM((2 * heads, rows + HALO, size), F32)
    held = pltpu.VMEM((half, rows, size), BF16)

    cum_shape = pltpu.VMEM((SPAN * CHUNKS, 2 * heads, rows), F32)

    def states(mine):
        scratch = [cum_shape, ext, held]
        if not mine:
            buf = pltpu.VMEM((CHIPS, rows, CHUNKS * heads * size), BF16)
            scratch = [
                buf,
                buf,
                pltpu.VMEM((CHIPS, taps, CHUNKS * heads * size), F32),
                pltpu.VMEM((head_count, rows), F32),
                *scratch,
                pltpu.SemaphoreType.DMA((3 * CHIPS + 1,)),
            ]
        return call(
            functools.partial(state_kernel if mine else fetched_state_kernel, mine, heads, size),
            "states_mine" if mine else "states_other",
            pltpu.VMEM((UNITS, packet, size), BF16),
            key_input, value_input, conv_weight, log_decay.T,
            in_specs=[VMEM if mine else HBM] * 4,
            scratch=scratch,
        )

    def intra_part(mine, q):
        return call(
            functools.partial(intra_kernel, mine, heads, size),
            "intra_mine" if mine else "intra_other",
            pltpu.VMEM((half + 1, rows, size), F32),
            q, key_input, value_input, conv_weight, cum,
            scratch=[ext, held],
        )

    theirs = states(False)
    got = swap(theirs, 1)
    mine = states(True)
    got_late = swap(mine, 1)

    chip_states = call(
        functools.partial(chip_kernel, heads, size),
        "chip_states",
        pltpu.VMEM((UNITS, packet, size), BF16),
        mine, got,
    )
    order = pltpu.VMEM((CHIPS, packet, size), BF16)

    def joined(packets):
        known = []
        if n > 2 * SPAN:
            edge = call(
                functools.partial(last_edge_kernel, heads, size),
                "last_edge",
                pltpu.VMEM((PARTS, size), BF16),
                *packets,
                scratch=[order],
            )
            known = [shift(edge, SPAN)]
        span = call(
            functools.partial(span_kernel, heads, size),
            "span_state",
            pltpu.VMEM((heads * size + (2 if known else 1) * PARTS, size), BF16),
            *packets, *known,
            scratch=[order],
        )
        before = swap(span, SPAN) if n == 2 * SPAN else shift(span, SPAN)
        reach = 1
        while reach < n // SPAN - 1:
            before = join_spans(shift(before, SPAN * reach), before, heads, size)
            reach *= 2
        return span, before, known

    packets = []
    for part in range(CHUNKS):
        these = {0: chip_states[part * CHIPS]}
        for g in EXCHANGE:
            these[g] = swap(chip_states[part * CHIPS + g], 2 * g)
        packets.append([these[g] for g in range(CHIPS)])
    q_after, decay_after, chip_states = lax.optimization_barrier(
        (queries, log_decay, chip_states)
    )
    cum = call(
        functools.partial(cum_kernel, heads),
        "cum",
        cum_shape,
        decay_after.T,
    )
    intra_mine = intra_part(True, q_after)
    last = packets[-1]
    *late, intra_mine = lax.optimization_barrier((*[last[g] for g in EXCHANGE], intra_mine))
    for g, x in zip(EXCHANGE, late):
        last[g] = x

    spans, befores, knowns = zip(*[joined(p) for p in packets])
    q_after, _ = lax.optimization_barrier((queries, spans[-1]))
    intra_other = intra_part(False, q_after)
    before, intra_other = lax.optimization_barrier((befores[-1], intra_other))
    befores = [*befores[:-1], before]

    own, other = {}, {}
    for part in range(CHUNKS):
        chip_prefix = call(
            functools.partial(spread_kernel, heads, size),
            "chip_prefix",
            pltpu.VMEM((CHIPS, heads * size + PARTS, size), BF16),
            *packets[part], befores[part], *knowns[part],
            scratch=[order],
        )
        first = part * CHIPS
        own[first] = chip_prefix[0]
        for g in EXCHANGE:
            own[first + g] = swap(chip_prefix[g], 2 * g)
        other[first] = swap(own[first], 1)

    def output(items, earlier=None):
        args = [queries, cum, gain]
        for mine, u in items:
            args += [own[u], intra_mine, got] if mine else [other[u], intra_other, got_late]
        done = pltpu.VMEM((len(items), rows, heads * size), BF16)
        scratch = [
            pltpu.VMEM((len(items) * heads, rows, size), F32),
            pltpu.VMEM((len(items) * heads, rows, 2 * PARTS), BF16),
        ]
        kernel = functools.partial(out_kernel, items, heads, size)
        hints = {
            "cost_estimate": pl.CostEstimate(flops=1, transcendentals=0, bytes_accessed=1),
        }
        name = "out_" + "_".join(("m" if mine else "o") + str(u) for mine, u in items)
        if earlier is None:
            return call(kernel, name, done, *args, scratch=scratch, **hints)
        there, made = zip(*earlier)
        return call(
            functools.partial(last_out_kernel, items, there, heads, size),
            name,
            jax.ShapeDtypeStruct((rows, width), BF16),
            *args, *made,
            out_specs=HBM,
            scratch=[*scratch, done, pltpu.SemaphoreType.DMA((2 * UNITS,))],
            **hints,
        )

    earlier = []
    for part in range(CHUNKS):
        first = part * CHIPS
        units = [first + g for g in EXCHANGE]
        items = [(True, first), (False, first)]
        made = [output(items)] + [x for _, x in earlier[-1:]]
        late, made = lax.optimization_barrier(([own[u] for u in units], made))
        earlier = earlier[:-1] + [(there, x) for (there, _), x in zip(earlier[-1:], made[1:])]
        earlier.append((items, made[0]))
        own.update(zip(units, late))
        other.update({u: swap(own[u], 1) for u in units})
        items = [(True, u) for u in units]
        if part < CHUNKS - 1:
            others = [(False, u) for u in units]
            earlier += [(others, output(others)), (items, output(items))]
        else:
            earlier.append((items, output(items)))
    return output([(False, u) for u in units], earlier)


def solution(mesh):
    rows = P(("groups", "ctx"), None)
    return jax.shard_map(
        on_device,
        mesh=mesh,
        in_specs=(rows, rows, rows, rows, P(), P()),
        out_specs=rows,
        check_vma=False,
    )
```

```python
import functools

import jax
import jax.numpy as jnp
from jax import lax
from jax.experimental import pallas as pl
from jax.experimental.pallas import tpu as pltpu
from jax.sharding import PartitionSpec as P

F32 = jnp.float32
BF16 = jnp.bfloat16
CHIPS = 4
SPAN = 2 * CHIPS
HALO = 8
EXCHANGE = (2, 3, 1)
CHUNKS = 2
UNITS = CHUNKS * CHIPS
SHIFTS = ((0,), (1,))
PARTS = 8
VMEM = pl.BlockSpec(memory_space=pltpu.VMEM)
HBM = pl.BlockSpec(memory_space=pltpu.HBM)


def position():
    me = lax.axis_index("ctx")
    return me & 1, (me >> 1) & (CHIPS - 1)


def head_group(mine, unit):
    core, chip = position()
    group = (core if mine else 1 - core) * CHIPS + (chip ^ (unit % CHIPS))
    return group * CHUNKS + unit // CHIPS


def columns(block, offset, size):
    return pl.ds(pl.multiple_of(block + offset, size), size)


def call(kernel, name, out_shape, *args, scratch=(), in_specs=None, out_specs=VMEM, **options):
    if in_specs is None:
        in_specs = [VMEM] * len(args)
    args = [
        pltpu.with_memory_space_constraint(x, pltpu.VMEM if s is VMEM else pltpu.HBM)
        for x, s in zip(args, in_specs)
    ]
    return pl.pallas_call(
        kernel,
        out_shape=out_shape,
        in_specs=in_specs,
        out_specs=out_specs,
        scratch_shapes=list(scratch),
        name=name,
        compiler_params=pltpu.CompilerParams(vmem_limit_bytes=6 << 20),
        **options,
    )(*args)


def cum_kernel(heads, decay_ref, out_ref):
    x = decay_ref[...]
    count, rows = x.shape
    upto = lax.broadcasted_iota(jnp.int32, (rows, rows), 0) <= lax.broadcasted_iota(
        jnp.int32, (rows, rows), 1
    )
    parts = jnp.concatenate([p.astype(F32) for p in three_parts(x)], 0).astype(BF16)
    sums = jnp.dot(parts, upto.astype(F32).astype(BF16), preferred_element_type=F32)
    sums = sums[0:count] + (sums[count : 2 * count] + sums[2 * count :])
    total = jnp.broadcast_to(sums[:, rows - 1 : rows], sums.shape)
    for b in range(out_ref.shape[0]):
        these = slice(b * heads, (b + 1) * heads)
        out_ref[b, 0:heads, :] = sums[these]
        out_ref[b, heads : 2 * heads, :] = total[these]


def three_parts(x):
    hi = x.astype(BF16)
    rest = x - hi.astype(F32)
    mid = rest.astype(BF16)
    low = (rest - mid.astype(F32)).astype(BF16)
    return hi, mid, low


def side(part, heads, size):
    base = heads * size + part * PARTS
    return slice(base, base + PARTS)


def padded(rows):
    rows = jnp.concatenate(rows, 0)
    spare = jnp.zeros((PARTS - rows.shape[0], rows.shape[1]), F32)
    return jnp.concatenate([rows, spare], 0).astype(BF16)


def put_decay(out, decays, heads, size):
    out[side(1, heads, size), :] = padded([p.astype(F32) for p in three_parts(decays)])


def get_decay(packet, heads, size):
    tail = packet[side(1, heads, size), :].astype(F32)
    return tail[0:heads] + tail[heads : 2 * heads] + tail[2 * heads : 3 * heads]


def edge_states(values, edges, heads):
    row = lax.broadcasted_iota(jnp.int32, values.shape, 0)
    out = []
    for j in range(heads):
        picked = jnp.where(lax.rem(row, heads) == j, values.astype(F32), 0.0).astype(BF16)
        out.append(
            lax.dot_general(picked, edges, (((0,), (0,)), ((), ())), preferred_element_type=F32)
        )
    return out


def conv_keys(k_ref, halo, w_ref, ext, cols):
    rows = k_ref.shape[0]
    ext[0:HALO, :] = halo
    ext[HALO : HALO + rows, :] = k_ref[:, cols].astype(F32)
    total = None
    for j in range(w_ref.shape[0]):
        term = w_ref[j : j + 1, cols] * ext[HALO - j : HALO - j + rows, :]
        total = term if total is None else total + term
    return total.astype(BF16)


def fetched_state_kernel(
    mine, heads, size, k_hbm, v_hbm, w_hbm, decay_hbm, out_ref,
    k_buf, v_buf, w_buf, decay_buf, cum_ref, ext, held, sems,
):
    wide = CHUNKS * heads * size
    copies = [pltpu.make_async_copy(decay_hbm, decay_buf, sems.at[3 * CHIPS])]
    copies[0].start()
    for g in range(CHIPS):
        cols = columns(head_group(mine, g) * heads * size, 0, wide)
        for i, (source, buf) in enumerate(((k_hbm, k_buf), (w_hbm, w_buf), (v_hbm, v_buf))):
            copies.append(
                pltpu.make_async_copy(source.at[:, cols], buf.at[g], sems.at[3 * g + i])
            )
            copies[-1].start()
    copies[0].wait()
    groups, waits = [], []
    for u in range(UNITS):
        g, part = u % CHIPS, u // CHIPS
        cols = slice(part * heads * size, (part + 1) * heads * size)
        groups.append(tuple(buf.at[g, :, cols] for buf in (k_buf, v_buf, w_buf)))
        waits.append(copies[1 + 3 * g : 4 + 3 * g] if part == 0 else [])
    states_of(mine, heads, size, groups, waits, decay_buf, out_ref, cum_ref, ext, held)


def state_kernel(
    mine, heads, size, k_ref, v_ref, w_ref, decay_ref, out_ref, cum_ref, ext, held
):
    groups = []
    for u in range(UNITS):
        cols = columns(head_group(mine, u) * heads * size, 0, heads * size)
        groups.append((k_ref.at[:, cols], v_ref.at[:, cols], w_ref.at[:, cols]))
    waits = [[]] * UNITS
    states_of(mine, heads, size, groups, waits, decay_ref, out_ref, cum_ref, ext, held)


def states_of(mine, heads, size, groups, waits, decay_ref, out_ref, cum_ref, ext, held):
    rows = groups[0][0].shape[0]
    taps = groups[0][2].shape[0]
    cum_kernel(heads, decay_ref, cum_ref)
    none = jnp.zeros((HALO, size), F32)
    for g in range(UNITS):
        k_ref, v_ref, w_ref = groups[g]
        for copy in waits[g]:
            copy.wait()
        cum = cum_ref[head_group(mine, g)]
        ending = jnp.exp(cum[heads : 2 * heads] - cum[0:heads]).T
        edges, values = [], []
        for j in range(heads):
            cols = slice(j * size, (j + 1) * size)
            key_conv = conv_keys(k_ref, none, w_ref, ext.at[g % 2 * heads + j], cols)
            held[g * heads + j] = (key_conv.astype(F32) * ending[:, j : j + 1]).astype(BF16)
            last = k_ref[rows - HALO : rows, cols].astype(F32)
            head_edges = []
            for t in range(taps - 1):
                terms = [
                    w_ref[i : i + 1, cols] * last[HALO + t - i : HALO + t - i + 1]
                    for i in range(t + 1, taps)
                ]
                head_edges.append(sum(terms[1:], terms[0]))
            edges.append(head_edges)
            values.append(v_ref[0:HALO, cols].astype(F32) * ending[0:HALO, j : j + 1])
        put_decay(out_ref.at[g], jnp.exp(cum[heads : 2 * heads]), heads, size)
        out_ref[g, side(0, heads, size), :] = padded(
            [edges[j][t] for t in range(taps - 1) for j in range(heads)]
        )
        out_ref[g, side(2, heads, size), :] = padded(
            [values[j][t : t + 1] for t in range(taps - 1) for j in range(heads)]
        )
    for g in range(UNITS):
        for j in range(heads):
            cols = slice(j * size, (j + 1) * size)
            state = lax.dot_general(
                groups[g][1][:, cols], held[g * heads + j], (((0,), (0,)), ((), ())),
                preferred_element_type=F32,
            )
            out_ref[g, cols, :] = state.astype(BF16)


def intra_kernel(mine, heads, size, q_ref, k_ref, v_ref, w_ref, cum_ref, out_ref, ext, held):
    rows = q_ref.shape[0]
    causal = lax.broadcasted_iota(jnp.int32, (rows, rows), 0) >= lax.broadcasted_iota(
        jnp.int32, (rows, rows), 1
    )
    none = jnp.zeros((HALO, size), F32)
    for g in range(UNITS):
        b = head_group(mine, g)
        cum = cum_ref[b][0:heads]
        cum_col = cum.T
        growth = jnp.exp(-cum_col[0:HALO])
        values = []
        for j in range(heads):
            cols = columns(b * heads * size, j * size, size)
            key_conv = conv_keys(k_ref, none, w_ref, ext.at[g % 2 * heads + j], cols)
            scores = lax.dot_general(
                q_ref[:, cols], key_conv, (((1,), (1,)), ((), ())), preferred_element_type=F32
            )
            spread = cum_col[:, j : j + 1] - cum[j : j + 1]
            weights = jnp.where(causal, scores * jnp.exp(jnp.where(causal, spread, 0.0)), 0.0)
            held[g * heads + j] = weights.astype(BF16)
            values.append(v_ref[0:HALO, cols].astype(F32) * growth[:, j : j + 1])
        out_ref[UNITS * heads, g * PARTS : (g + 1) * PARTS, :] = padded(
            [values[j][t : t + 1] for t in range(3) for j in range(heads)]
        ).astype(F32)
    for g in range(UNITS):
        b = head_group(mine, g)
        for j in range(heads):
            cols = columns(b * heads * size, j * size, size)
            out_ref[g * heads + j] = jnp.dot(
                held[g * heads + j], v_ref[:, cols], preferred_element_type=F32
            )


def chip_kernel(heads, size, own_ref, got_ref, out_ref):
    core, _ = position()
    first = core == 0
    for g in range(UNITS):
        to = out_ref.at[g % CHIPS, g // CHIPS]
        own_decay = get_decay(own_ref.at[g], heads, size)
        got_decay = get_decay(got_ref.at[g], heads, size)
        own_by = jnp.where(first, got_decay, 1.0)
        got_by = jnp.where(first, 1.0, own_decay)

        def earlier_later(part):
            own = own_ref[g, side(part, heads, size), :].astype(F32)
            got = got_ref[g, side(part, heads, size), :].astype(F32)
            return jnp.where(first, own, got), jnp.where(first, got, own)

        edges, out_edges = earlier_later(0)
        out_values, values = earlier_later(2)
        fixes = edge_states(values.astype(BF16), edges.astype(BF16), heads)
        for j in range(heads):
            rows = slice(j * size, (j + 1) * size)
            to[rows, :] = (
                own_ref[g, rows, :].astype(F32) * own_by[j : j + 1]
                + got_ref[g, rows, :].astype(F32) * got_by[j : j + 1]
                + fixes[j]
            ).astype(BF16)
        put_decay(to, own_decay * got_decay, heads, size)
        later_by = jnp.where(first, got_decay, own_decay)
        to[side(0, heads, size), :] = out_edges.astype(BF16)
        to[side(2, heads, size), :] = padded(
            [out_values[t * heads : (t + 1) * heads] * later_by for t in range(3)]
        )


def in_order(packets, part, held):
    _, chip = position()
    for g in range(CHIPS):
        held[chip ^ g] = packets[g][part]


def chip_fixes(held, b, edges, heads, size):
    return edge_states(held[b, side(2, heads, size), :], edges, heads)


def last_edge_kernel(heads, size, *refs):
    packets, out_ref, held = refs[:CHIPS], refs[CHIPS], refs[CHIPS + 1]
    for part in range(CHUNKS):
        in_order(packets, part, held)
        out_ref[part] = held[CHIPS - 1, side(0, heads, size), :]


def span_kernel(parts, heads, size, *refs):
    packets, before, (whole_ref, held) = refs[:CHIPS], refs[CHIPS:-2], refs[-2:]
    for i, part in enumerate(parts):
        known = [before[0][part]] if before else []
        span_of(part, known, heads, size, packets, whole_ref.at[i], held)


def span_of(part, before, heads, size, packets, out_ref, held):
    in_order(packets, part, held)
    decays = [get_decay(held.at[b], heads, size) for b in range(CHIPS)]
    fixes = [
        chip_fixes(held, b, held[b - 1, side(0, heads, size), :], heads, size)
        for b in range(1, CHIPS)
    ]
    fixes.insert(0, chip_fixes(held, 0, before[0], heads, size) if before else None)
    for j in range(heads):
        rows = slice(j * size, (j + 1) * size)
        acc = held[0, rows, :].astype(F32)
        if before:
            acc = acc + fixes[0][j]
        for b in range(1, CHIPS):
            acc = acc * decays[b][j : j + 1] + (held[b, rows, :].astype(F32) + fixes[b][j])
        out_ref[rows, :] = acc.astype(BF16)
    whole = decays[0]
    for b in range(1, CHIPS):
        whole = whole * decays[b]
    out_ref[side(0, heads, size), :] = held[CHIPS - 1, side(0, heads, size), :]
    if before:
        put_decay(out_ref, whole, heads, size)


def spread_kernel(part, place, heads, size, *refs):
    packets, before, known, (out_ref, held) = refs[:CHIPS], refs[CHIPS], refs[CHIPS + 1 : -2], refs[-2:]
    _, chip = position()
    later = lax.axis_index("ctx") >= SPAN
    in_order(packets, part, held)
    decays = [get_decay(held.at[b], heads, size) for b in range(CHIPS)]
    edges = known[0][part] if known else before[place, side(0, heads, size), :]
    edges = [jnp.where(later, edges.astype(F32), 0.0).astype(BF16)]
    edges += [held[b, side(0, heads, size), :] for b in range(CHIPS - 1)]
    fixes = [chip_fixes(held, b, edges[b], heads, size) for b in range(CHIPS - 1)]
    for j in range(heads):
        rows = slice(j * size, (j + 1) * size)
        acc = jnp.where(later, before[place, rows, :].astype(F32), 0.0)
        out_ref[chip, rows, :] = acc.astype(BF16)
        for b in range(1, CHIPS):
            acc = acc * decays[b - 1][j : j + 1] + (
                held[b - 1, rows, :].astype(F32) + fixes[b - 1][j]
            )
            out_ref[chip ^ b, rows, :] = acc.astype(BF16)
    for b in range(CHIPS):
        out_ref[chip ^ b, heads * size : heads * size + PARTS, :] = edges[b]


def last_out_kernel(items, earlier, heads, size, *refs):
    count = 3 + 3 * len(items)
    made = refs[count : count + len(earlier)]
    out_ref, inter_ref, score_ref, done_ref, sems = refs[-5:]
    copies = []

    def write(item, source):
        cols = columns(head_group(*item) * heads * size, 0, heads * size)
        copies.append(
            pltpu.make_async_copy(source, out_ref.at[:, cols], sems.at[len(copies)])
        )
        copies[-1].start()

    for there, ref in zip(earlier, made):
        for i, item in enumerate(there):
            write(item, ref.at[i])
    out_kernel(items, heads, size, *refs[:count], done_ref, inter_ref, score_ref, write=write)
    for copy in copies:
        copy.wait()


def out_kernel(items, heads, size, *refs, write=None):
    q_ref, cum_ref, gain_ref = refs[:3]
    per_item = [refs[3 + 3 * i : 6 + 3 * i] for i in range(len(items))]
    done_ref, inter_ref, score_ref = refs[-3:]
    rows = q_ref.shape[0]
    core, _ = position()
    second = core == 1
    row = lax.broadcasted_iota(jnp.int32, (rows, 2 * PARTS), 0)
    column = lax.broadcasted_iota(jnp.int32, (rows, 2 * PARTS), 1)
    edge = lax.rem(column, PARTS)
    causal = (lax.div(edge, heads) <= row) & (edge < 3 * heads)
    ahead = column < PARTS
    kept = ((ahead & (core == 1)) | causal) & (ahead | (core == 1))
    kept = [kept & (lax.rem(edge, heads) == j) for j in range(heads)]
    for i, (mine, g) in enumerate(items):
        prefix_ref, intra_ref, sib_ref = per_item[i]
        b = head_group(mine, g)
        started = jnp.exp(cum_ref[b][0:heads]).T
        by = jnp.where(second, get_decay(sib_ref.at[g], heads, size), 1.0)
        edges = jnp.concatenate(
            [
                prefix_ref[heads * size : heads * size + PARTS, :].astype(F32),
                sib_ref[g, side(0, heads, size), :].astype(F32),
            ],
            0,
        ).astype(BF16)
        for j in range(heads):
            cols = columns(b * heads * size, j * size, size)
            these = slice(j * size, (j + 1) * size)
            sib = jnp.where(second, sib_ref[g, these, :].astype(F32), 0.0)
            prefix = (prefix_ref[these, :].astype(F32) * by[j : j + 1] + sib).astype(BF16)
            both = lax.dot_general(
                q_ref[:, cols],
                jnp.concatenate([prefix, edges], 0),
                (((1,), (1,)), ((), ())),
                preferred_element_type=F32,
            )
            both = both * started[:, j : j + 1]
            inter_ref[i * heads + j] = both[:, 0:size] + intra_ref[g * heads + j]
            score_ref[i * heads + j] = jnp.where(kept[j], both[:, size:], 0.0).astype(BF16)
    for i, (mine, g) in enumerate(items):
        _, intra_ref, sib_ref = per_item[i]
        b = head_group(mine, g)
        values = intra_ref[UNITS * heads, g * PARTS : (g + 1) * PARTS, :]
        ahead_values = jnp.where(second, sib_ref[g, side(2, heads, size), :].astype(F32), values)
        values = jnp.concatenate([ahead_values, values], 0).astype(BF16)
        for j in range(heads):
            inter_ref[i * heads + j] += jnp.dot(
                score_ref[i * heads + j], values, preferred_element_type=F32
            )
    for i, (mine, g) in enumerate(items):
        b = head_group(mine, g)
        for j in range(heads):
            cols = columns(b * heads * size, j * size, size)
            mixed = inter_ref[i * heads + j]
            scale = lax.rsqrt(jnp.mean(mixed * mixed, axis=1, keepdims=True) + 1e-05)
            done_ref[i, :, j * size : (j + 1) * size] = (
                mixed * scale * gain_ref[:, cols]
            ).astype(BF16)
        if write is not None:
            write((mine, g), done_ref.at[i])


def join_spans(earlier, later, heads, size):
    base = heads * size
    own = side(1, heads, size)

    def decay(x):
        tail = x[own].astype(F32)
        return tail[0:heads] + tail[heads : 2 * heads] + tail[2 * heads : 3 * heads]

    by = decay(later)
    state = (
        by[:, None, :] * earlier[:base].astype(F32).reshape(heads, size, -1)
        + later[:base].astype(F32).reshape(heads, size, -1)
    ).reshape(base, -1)
    parts = three_parts(by * decay(earlier))
    return jnp.concatenate([state.astype(BF16), later[base : own.start], *parts, later[own.start + 3 * heads :]], 0)


def on_device(queries, key_input, value_input, log_decay, conv_weight, norm_gain):
    rows, width = queries.shape
    head_count = log_decay.shape[1]
    size = width // head_count
    heads = head_count // (SPAN * CHUNKS)
    taps = conv_weight.shape[0]
    half = UNITS * heads
    packet = heads * size + 3 * PARTS
    n = lax.axis_size("ctx")

    def swap(x, mask):
        return lax.ppermute(x, "ctx", [(i, i ^ mask) for i in range(n)])

    def shift(x, by):
        return lax.ppermute(x, "ctx", [(i, i + by) for i in range(n - by)])

    gain = norm_gain.reshape(1, width)
    ext = pltpu.VMEM((2 * heads, rows + HALO, size), F32)
    held = pltpu.VMEM((half, rows, size), BF16)

    cum_shape = pltpu.VMEM((SPAN * CHUNKS, 2 * heads, rows), F32)

    def states(mine):
        scratch = [cum_shape, ext, held]
        if not mine:
            buf = pltpu.VMEM((CHIPS, rows, CHUNKS * heads * size), BF16)
            scratch = [
                buf,
                buf,
                pltpu.VMEM((CHIPS, taps, CHUNKS * heads * size), F32),
                pltpu.VMEM((head_count, rows), F32),
                *scratch,
                pltpu.SemaphoreType.DMA((3 * CHIPS + 1,)),
            ]
        return call(
            functools.partial(state_kernel if mine else fetched_state_kernel, mine, heads, size),
            "states_mine" if mine else "states_other",
            pltpu.VMEM((UNITS, packet, size), BF16),
            key_input, value_input, conv_weight, log_decay.T,
            in_specs=[VMEM if mine else HBM] * 4,
            scratch=scratch,
        )

    def intra_part(mine, q):
        return call(
            functools.partial(intra_kernel, mine, heads, size),
            "intra_mine" if mine else "intra_other",
            pltpu.VMEM((half + 1, rows, size), F32),
            q, key_input, value_input, conv_weight, cum,
            scratch=[ext, held],
        )

    theirs = states(False)
    got = swap(theirs, 1)
    mine = states(True)
    got_late = swap(mine, 1)

    chip_states = call(
        functools.partial(chip_kernel, heads, size),
        "chip_states",
        pltpu.VMEM((CHIPS, CHUNKS, packet, size), BF16),
        mine, got,
    )
    order = pltpu.VMEM((CHIPS, packet, size), BF16)

    packets = {0: chip_states[0]}
    for g in EXCHANGE:
        packets[g] = swap(chip_states[g], 2 * g)
    q_after, decay_after, chip_states = lax.optimization_barrier(
        (queries, log_decay, chip_states)
    )
    cum = call(
        functools.partial(cum_kernel, heads),
        "cum",
        cum_shape,
        decay_after.T,
    )
    intra_mine = intra_part(True, q_after)
    *late, intra_mine = lax.optimization_barrier((*[packets[g] for g in EXCHANGE], intra_mine))
    packets.update(zip(EXCHANGE, late))
    packets = [packets[g] for g in range(CHIPS)]

    known = []
    if n > 2 * SPAN:
        edge = call(
            functools.partial(last_edge_kernel, heads, size),
            "last_edge",
            pltpu.VMEM((CHUNKS, PARTS, size), BF16),
            *packets,
            scratch=[order],
        )
        known = [shift(edge, SPAN)]

    def joined(parts):
        span = call(
            functools.partial(span_kernel, parts, heads, size),
            "span_state",
            pltpu.VMEM((len(parts), heads * size + (2 if known else 1) * PARTS, size), BF16),
            *packets, *known,
            scratch=[order],
        )
        before = swap(span, SPAN) if n == 2 * SPAN else shift(span, SPAN)
        reach = 1
        while reach < n // SPAN - 1:
            before = jax.vmap(functools.partial(join_spans, heads=heads, size=size))(
                shift(before, SPAN * reach), before
            )
            reach *= 2
        return span, before

    spans, befores = zip(*[joined(parts) for parts in SHIFTS])
    q_after, _ = lax.optimization_barrier((queries, spans[-1]))
    intra_other = intra_part(False, q_after)
    before, intra_other = lax.optimization_barrier((befores[-1], intra_other))
    befores = [*befores[:-1], before]
    ahead = {
        part: (place, before)
        for parts, before in zip(SHIFTS, befores)
        for place, part in enumerate(parts)
    }

    own, other = {}, {}
    for part in range(CHUNKS):
        chip_prefix = call(
            functools.partial(spread_kernel, part, ahead[part][0], heads, size),
            "chip_prefix",
            pltpu.VMEM((CHIPS, heads * size + PARTS, size), BF16),
            *packets, ahead[part][1], *known,
            scratch=[order],
        )
        first = part * CHIPS
        own[first] = chip_prefix[0]
        for g in EXCHANGE:
            own[first + g] = swap(chip_prefix[g], 2 * g)
        other[first] = swap(own[first], 1)

    def output(items, earlier=None):
        args = [queries, cum, gain]
        for mine, u in items:
            args += [own[u], intra_mine, got] if mine else [other[u], intra_other, got_late]
        done = pltpu.VMEM((len(items), rows, heads * size), BF16)
        scratch = [
            pltpu.VMEM((len(items) * heads, rows, size), F32),
            pltpu.VMEM((len(items) * heads, rows, 2 * PARTS), BF16),
        ]
        kernel = functools.partial(out_kernel, items, heads, size)
        hints = {
            "cost_estimate": pl.CostEstimate(flops=1, transcendentals=0, bytes_accessed=1),
        }
        name = "out_" + "_".join(("m" if mine else "o") + str(u) for mine, u in items)
        if earlier is None:
            return call(kernel, name, done, *args, scratch=scratch, **hints)
        there, made = zip(*earlier)
        return call(
            functools.partial(last_out_kernel, items, there, heads, size),
            name,
            jax.ShapeDtypeStruct((rows, width), BF16),
            *args, *made,
            out_specs=HBM,
            scratch=[*scratch, done, pltpu.SemaphoreType.DMA((2 * UNITS,))],
            **hints,
        )

    earlier = []
    for part in range(CHUNKS):
        first = part * CHIPS
        units = [first + g for g in EXCHANGE]
        items = [(True, first), (False, first)]
        made = [output(items)] + [x for _, x in earlier[-1:]]
        late, made = lax.optimization_barrier(([own[u] for u in units], made))
        earlier = earlier[:-1] + [(there, x) for (there, _), x in zip(earlier[-1:], made[1:])]
        earlier.append((items, made[0]))
        own.update(zip(units, late))
        other.update({u: swap(own[u], 1) for u in units})
        items = [(True, u) for u in units]
        if part < CHUNKS - 1:
            others = [(False, u) for u in units]
            earlier += [(others, output(others)), (items, output(items))]
        else:
            earlier.append((items, output(items)))
    return output([(False, u) for u in units], earlier)


def solution(mesh):
    rows = P(("groups", "ctx"), None)
    return jax.shard_map(
        on_device,
        mesh=mesh,
        in_specs=(rows, rows, rows, rows, P(), P()),
        out_specs=rows,
        check_vma=False,
    )
```

```python
import functools

import jax
import jax.numpy as jnp
from jax import lax
from jax.experimental import pallas as pl
from jax.experimental.pallas import tpu as pltpu
from jax.sharding import PartitionSpec as P

F32 = jnp.float32
BF16 = jnp.bfloat16
CHIPS = 4
SPAN = 2 * CHIPS
HALO = 8
EXCHANGE = (2, 3, 1)
CHUNKS = 2
UNITS = CHUNKS * CHIPS
SHIFTS = ((0,), (1,))
PARTS = 8
VMEM = pl.BlockSpec(memory_space=pltpu.VMEM)
HBM = pl.BlockSpec(memory_space=pltpu.HBM)


def position():
    me = lax.axis_index("ctx")
    return me & 1, (me >> 1) & (CHIPS - 1)


def head_group(mine, unit):
    core, chip = position()
    group = (core if mine else 1 - core) * CHIPS + (chip ^ (unit % CHIPS))
    return group * CHUNKS + unit // CHIPS


def columns(block, offset, size):
    return pl.ds(pl.multiple_of(block + offset, size), size)


def call(kernel, name, out_shape, *args, scratch=(), in_specs=None, out_specs=VMEM, **options):
    if in_specs is None:
        in_specs = [VMEM] * len(args)
    args = [
        pltpu.with_memory_space_constraint(x, pltpu.VMEM if s is VMEM else pltpu.HBM)
        for x, s in zip(args, in_specs)
    ]
    return pl.pallas_call(
        kernel,
        out_shape=out_shape,
        in_specs=in_specs,
        out_specs=out_specs,
        scratch_shapes=list(scratch),
        name=name,
        compiler_params=pltpu.CompilerParams(vmem_limit_bytes=6 << 20),
        **options,
    )(*args)


def cum_kernel(heads, decay_ref, out_ref):
    x = decay_ref[...]
    count, rows = x.shape
    upto = lax.broadcasted_iota(jnp.int32, (rows, rows), 0) <= lax.broadcasted_iota(
        jnp.int32, (rows, rows), 1
    )
    parts = jnp.concatenate([p.astype(F32) for p in three_parts(x)], 0).astype(BF16)
    sums = jnp.dot(parts, upto.astype(F32).astype(BF16), preferred_element_type=F32)
    sums = sums[0:count] + (sums[count : 2 * count] + sums[2 * count :])
    total = jnp.broadcast_to(sums[:, rows - 1 : rows], sums.shape)
    for b in range(out_ref.shape[0]):
        these = slice(b * heads, (b + 1) * heads)
        out_ref[b, 0:heads, :] = sums[these]
        out_ref[b, heads : 2 * heads, :] = total[these]


def three_parts(x):
    hi = x.astype(BF16)
    rest = x - hi.astype(F32)
    mid = rest.astype(BF16)
    low = (rest - mid.astype(F32)).astype(BF16)
    return hi, mid, low


def side(part, heads, size):
    base = heads * size + part * PARTS
    return slice(base, base + PARTS)


def padded(rows):
    rows = jnp.concatenate(rows, 0)
    spare = jnp.zeros((PARTS - rows.shape[0], rows.shape[1]), F32)
    return jnp.concatenate([rows, spare], 0).astype(BF16)


def put_decay(out, decays, heads, size):
    out[side(1, heads, size), :] = padded([p.astype(F32) for p in three_parts(decays)])


def get_decay(packet, heads, size):
    tail = packet[side(1, heads, size), :].astype(F32)
    return tail[0:heads] + tail[heads : 2 * heads] + tail[2 * heads : 3 * heads]


def edge_states(values, edges, heads):
    row = lax.broadcasted_iota(jnp.int32, values.shape, 0)
    out = []
    for j in range(heads):
        picked = jnp.where(lax.rem(row, heads) == j, values.astype(F32), 0.0).astype(BF16)
        out.append(
            lax.dot_general(picked, edges, (((0,), (0,)), ((), ())), preferred_element_type=F32)
        )
    return out


def conv_keys(k_ref, halo, w_ref, ext, cols):
    rows = k_ref.shape[0]
    ext[0:HALO, :] = halo
    ext[HALO : HALO + rows, :] = k_ref[:, cols].astype(F32)
    total = None
    for j in range(w_ref.shape[0]):
        term = w_ref[j : j + 1, cols] * ext[HALO - j : HALO - j + rows, :]
        total = term if total is None else total + term
    return total.astype(BF16)


def fetched_state_kernel(
    mine, heads, size, k_hbm, v_hbm, w_hbm, decay_hbm, out_ref,
    k_buf, v_buf, w_buf, decay_buf, cum_ref, ext, held, sems,
):
    wide = CHUNKS * heads * size
    copies = [pltpu.make_async_copy(decay_hbm, decay_buf, sems.at[3 * CHIPS])]
    copies[0].start()
    for g in range(CHIPS):
        cols = columns(head_group(mine, g) * heads * size, 0, wide)
        for i, (source, buf) in enumerate(((k_hbm, k_buf), (w_hbm, w_buf), (v_hbm, v_buf))):
            copies.append(
                pltpu.make_async_copy(source.at[:, cols], buf.at[g], sems.at[3 * g + i])
            )
            copies[-1].start()
    copies[0].wait()
    groups, waits = [], []
    for u in range(UNITS):
        g, part = u % CHIPS, u // CHIPS
        cols = slice(part * heads * size, (part + 1) * heads * size)
        groups.append(tuple(buf.at[g, :, cols] for buf in (k_buf, v_buf, w_buf)))
        waits.append(copies[1 + 3 * g : 4 + 3 * g] if part == 0 else [])
    states_of(mine, heads, size, groups, waits, decay_buf, out_ref, cum_ref, ext, held)


def state_kernel(
    mine, heads, size, k_ref, v_ref, w_ref, decay_ref, out_ref, cum_ref, ext, held
):
    groups = []
    for u in range(UNITS):
        cols = columns(head_group(mine, u) * heads * size, 0, heads * size)
        groups.append((k_ref.at[:, cols], v_ref.at[:, cols], w_ref.at[:, cols]))
    waits = [[]] * UNITS
    states_of(mine, heads, size, groups, waits, decay_ref, out_ref, cum_ref, ext, held)


def states_of(mine, heads, size, groups, waits, decay_ref, out_ref, cum_ref, ext, held):
    rows = groups[0][0].shape[0]
    taps = groups[0][2].shape[0]
    cum_kernel(heads, decay_ref, cum_ref)
    none = jnp.zeros((HALO, size), F32)
    for g in range(UNITS):
        k_ref, v_ref, w_ref = groups[g]
        for copy in waits[g]:
            copy.wait()
        cum = cum_ref[head_group(mine, g)]
        ending = jnp.exp(cum[heads : 2 * heads] - cum[0:heads]).T
        edges, values = [], []
        for j in range(heads):
            cols = slice(j * size, (j + 1) * size)
            key_conv = conv_keys(k_ref, none, w_ref, ext.at[g % 2 * heads + j], cols)
            held[g * heads + j] = (key_conv.astype(F32) * ending[:, j : j + 1]).astype(BF16)
            last = k_ref[rows - HALO : rows, cols].astype(F32)
            head_edges = []
            for t in range(taps - 1):
                terms = [
                    w_ref[i : i + 1, cols] * last[HALO + t - i : HALO + t - i + 1]
                    for i in range(t + 1, taps)
                ]
                head_edges.append(sum(terms[1:], terms[0]))
            edges.append(head_edges)
            values.append(v_ref[0:HALO, cols].astype(F32) * ending[0:HALO, j : j + 1])
        put_decay(out_ref.at[g], jnp.exp(cum[heads : 2 * heads]), heads, size)
        out_ref[g, side(0, heads, size), :] = padded(
            [edges[j][t] for t in range(taps - 1) for j in range(heads)]
        )
        out_ref[g, side(2, heads, size), :] = padded(
            [values[j][t : t + 1] for t in range(taps - 1) for j in range(heads)]
        )
    for g in range(UNITS):
        for j in range(heads):
            cols = slice(j * size, (j + 1) * size)
            state = lax.dot_general(
                groups[g][1][:, cols], held[g * heads + j], (((0,), (0,)), ((), ())),
                preferred_element_type=F32,
            )
            out_ref[g, cols, :] = state.astype(BF16)


def intra_kernel(mine, heads, size, q_ref, k_ref, v_ref, w_ref, cum_ref, out_ref, ext, held):
    rows = q_ref.shape[0]
    causal = lax.broadcasted_iota(jnp.int32, (rows, rows), 0) >= lax.broadcasted_iota(
        jnp.int32, (rows, rows), 1
    )
    none = jnp.zeros((HALO, size), F32)
    for g in range(UNITS):
        b = head_group(mine, g)
        cum = cum_ref[b][0:heads]
        cum_col = cum.T
        growth = jnp.exp(-cum_col[0:HALO])
        values = []
        for j in range(heads):
            cols = columns(b * heads * size, j * size, size)
            key_conv = conv_keys(k_ref, none, w_ref, ext.at[g % 2 * heads + j], cols)
            scores = lax.dot_general(
                q_ref[:, cols], key_conv, (((1,), (1,)), ((), ())), preferred_element_type=F32
            )
            spread = cum_col[:, j : j + 1] - cum[j : j + 1]
            weights = jnp.where(causal, scores * jnp.exp(jnp.where(causal, spread, 0.0)), 0.0)
            held[g * heads + j] = weights.astype(BF16)
            values.append(v_ref[0:HALO, cols].astype(F32) * growth[:, j : j + 1])
        out_ref[UNITS * heads, g * PARTS : (g + 1) * PARTS, :] = padded(
            [values[j][t : t + 1] for t in range(3) for j in range(heads)]
        ).astype(F32)
    for g in range(UNITS):
        b = head_group(mine, g)
        for j in range(heads):
            cols = columns(b * heads * size, j * size, size)
            out_ref[g * heads + j] = jnp.dot(
                held[g * heads + j], v_ref[:, cols], preferred_element_type=F32
            )


def chip_kernel(heads, size, own_ref, got_ref, out_ref):
    core, _ = position()
    first = core == 0
    for g in range(UNITS):
        to = out_ref.at[g % CHIPS, g // CHIPS]
        own_decay = get_decay(own_ref.at[g], heads, size)
        got_decay = get_decay(got_ref.at[g], heads, size)
        own_by = jnp.where(first, got_decay, 1.0)
        got_by = jnp.where(first, 1.0, own_decay)

        def earlier_later(part):
            own = own_ref[g, side(part, heads, size), :].astype(F32)
            got = got_ref[g, side(part, heads, size), :].astype(F32)
            return jnp.where(first, own, got), jnp.where(first, got, own)

        edges, out_edges = earlier_later(0)
        out_values, values = earlier_later(2)
        fixes = edge_states(values.astype(BF16), edges.astype(BF16), heads)
        for j in range(heads):
            rows = slice(j * size, (j + 1) * size)
            to[rows, :] = (
                own_ref[g, rows, :].astype(F32) * own_by[j : j + 1]
                + got_ref[g, rows, :].astype(F32) * got_by[j : j + 1]
                + fixes[j]
            ).astype(BF16)
        put_decay(to, own_decay * got_decay, heads, size)
        later_by = jnp.where(first, got_decay, own_decay)
        to[side(0, heads, size), :] = out_edges.astype(BF16)
        to[side(2, heads, size), :] = padded(
            [out_values[t * heads : (t + 1) * heads] * later_by for t in range(3)]
        )


def in_order(packets, part, held):
    _, chip = position()
    for g in range(CHIPS):
        held[chip ^ g] = packets[g][part]


def chip_fixes(held, b, edges, heads, size):
    return edge_states(held[b, side(2, heads, size), :], edges, heads)


def last_edge_kernel(heads, size, *refs):
    packets, out_ref, held = refs[:CHIPS], refs[CHIPS], refs[CHIPS + 1]
    for part in range(CHUNKS):
        in_order(packets, part, held)
        out_ref[part] = held[CHIPS - 1, side(0, heads, size), :]


def span_kernel(parts, heads, size, *refs):
    packets, before, (whole_ref, held) = refs[:CHIPS], refs[CHIPS:-2], refs[-2:]
    for i, part in enumerate(parts):
        known = [before[0][part]] if before else []
        span_of(part, known, heads, size, packets, whole_ref.at[i], held)


def span_of(part, before, heads, size, packets, out_ref, held):
    in_order(packets, part, held)
    decays = [get_decay(held.at[b], heads, size) for b in range(CHIPS)]
    fixes = [
        chip_fixes(held, b, held[b - 1, side(0, heads, size), :], heads, size)
        for b in range(1, CHIPS)
    ]
    fixes.insert(0, chip_fixes(held, 0, before[0], heads, size) if before else None)
    for j in range(heads):
        rows = slice(j * size, (j + 1) * size)
        acc = held[0, rows, :].astype(F32)
        if before:
            acc = acc + fixes[0][j]
        for b in range(1, CHIPS):
            acc = acc * decays[b][j : j + 1] + (held[b, rows, :].astype(F32) + fixes[b][j])
        out_ref[rows, :] = acc.astype(BF16)
    whole = decays[0]
    for b in range(1, CHIPS):
        whole = whole * decays[b]
    out_ref[side(0, heads, size), :] = held[CHIPS - 1, side(0, heads, size), :]
    if before:
        put_decay(out_ref, whole, heads, size)


def spread_kernel(part, place, heads, size, *refs):
    packets, before, known, (out_ref, held) = refs[:CHIPS], refs[CHIPS], refs[CHIPS + 1 : -2], refs[-2:]
    _, chip = position()
    later = lax.axis_index("ctx") >= SPAN
    in_order(packets, part, held)
    decays = [get_decay(held.at[b], heads, size) for b in range(CHIPS)]
    edges = known[0][part] if known else before[place, side(0, heads, size), :]
    edges = [jnp.where(later, edges.astype(F32), 0.0).astype(BF16)]
    edges += [held[b, side(0, heads, size), :] for b in range(CHIPS - 1)]
    fixes = [chip_fixes(held, b, edges[b], heads, size) for b in range(CHIPS - 1)]
    for j in range(heads):
        rows = slice(j * size, (j + 1) * size)
        acc = jnp.where(later, before[place, rows, :].astype(F32), 0.0)
        out_ref[chip, rows, :] = acc.astype(BF16)
        for b in range(1, CHIPS):
            acc = acc * decays[b - 1][j : j + 1] + (
                held[b - 1, rows, :].astype(F32) + fixes[b - 1][j]
            )
            out_ref[chip ^ b, rows, :] = acc.astype(BF16)
    for b in range(CHIPS):
        out_ref[chip ^ b, heads * size : heads * size + PARTS, :] = edges[b]


def last_out_kernel(items, earlier, heads, size, *refs):
    count = 3 + 3 * len(items)
    made = refs[count : count + len(earlier)]
    out_ref, inter_ref, score_ref, done_ref, sems = refs[-5:]
    copies = []

    def write(item, source):
        cols = columns(head_group(*item) * heads * size, 0, heads * size)
        copies.append(
            pltpu.make_async_copy(source, out_ref.at[:, cols], sems.at[len(copies)])
        )
        copies[-1].start()

    for there, ref in zip(earlier, made):
        for i, item in enumerate(there):
            write(item, ref.at[i])
    out_kernel(items, heads, size, *refs[:count], done_ref, inter_ref, score_ref, write=write)
    for copy in copies:
        copy.wait()


def out_kernel(items, heads, size, *refs, write=None):
    q_ref, cum_ref, gain_ref = refs[:3]
    per_item = [refs[3 + 3 * i : 6 + 3 * i] for i in range(len(items))]
    done_ref, inter_ref, score_ref = refs[-3:]
    rows = q_ref.shape[0]
    core, _ = position()
    second = core == 1
    row = lax.broadcasted_iota(jnp.int32, (rows, 2 * PARTS), 0)
    column = lax.broadcasted_iota(jnp.int32, (rows, 2 * PARTS), 1)
    edge = lax.rem(column, PARTS)
    causal = (lax.div(edge, heads) <= row) & (edge < 3 * heads)
    ahead = column < PARTS
    kept = ((ahead & (core == 1)) | causal) & (ahead | (core == 1))
    kept = [kept & (lax.rem(edge, heads) == j) for j in range(heads)]
    for i, (mine, g) in enumerate(items):
        prefix_ref, intra_ref, sib_ref = per_item[i]
        b = head_group(mine, g)
        started = jnp.exp(cum_ref[b][0:heads]).T
        by = jnp.where(second, get_decay(sib_ref.at[g], heads, size), 1.0)
        edges = jnp.concatenate(
            [
                prefix_ref[heads * size : heads * size + PARTS, :].astype(F32),
                sib_ref[g, side(0, heads, size), :].astype(F32),
            ],
            0,
        ).astype(BF16)
        for j in range(heads):
            cols = columns(b * heads * size, j * size, size)
            these = slice(j * size, (j + 1) * size)
            sib = jnp.where(second, sib_ref[g, these, :].astype(F32), 0.0)
            prefix = (prefix_ref[these, :].astype(F32) * by[j : j + 1] + sib).astype(BF16)
            both = lax.dot_general(
                q_ref[:, cols],
                jnp.concatenate([prefix, edges], 0),
                (((1,), (1,)), ((), ())),
                preferred_element_type=F32,
            )
            both = both * started[:, j : j + 1]
            inter_ref[i * heads + j] = both[:, 0:size] + intra_ref[g * heads + j]
            score_ref[i * heads + j] = jnp.where(kept[j], both[:, size:], 0.0).astype(BF16)
    for i, (mine, g) in enumerate(items):
        _, intra_ref, sib_ref = per_item[i]
        b = head_group(mine, g)
        values = intra_ref[UNITS * heads, g * PARTS : (g + 1) * PARTS, :]
        ahead_values = jnp.where(second, sib_ref[g, side(2, heads, size), :].astype(F32), values)
        values = jnp.concatenate([ahead_values, values], 0).astype(BF16)
        for j in range(heads):
            inter_ref[i * heads + j] += jnp.dot(
                score_ref[i * heads + j], values, preferred_element_type=F32
            )
    for i, (mine, g) in enumerate(items):
        b = head_group(mine, g)
        for j in range(heads):
            cols = columns(b * heads * size, j * size, size)
            mixed = inter_ref[i * heads + j]
            scale = lax.rsqrt(jnp.mean(mixed * mixed, axis=1, keepdims=True) + 1e-05)
            done_ref[i, :, j * size : (j + 1) * size] = (
                mixed * scale * gain_ref[:, cols]
            ).astype(BF16)
        if write is not None:
            write((mine, g), done_ref.at[i])


def join_spans(earlier, later, heads, size):
    base = heads * size
    own = side(1, heads, size)

    def decay(x):
        tail = x[own].astype(F32)
        return tail[0:heads] + tail[heads : 2 * heads] + tail[2 * heads : 3 * heads]

    by = decay(later)
    state = (
        by[:, None, :] * earlier[:base].astype(F32).reshape(heads, size, -1)
        + later[:base].astype(F32).reshape(heads, size, -1)
    ).reshape(base, -1)
    parts = three_parts(by * decay(earlier))
    return jnp.concatenate([state.astype(BF16), later[base : own.start], *parts, later[own.start + 3 * heads :]], 0)


def on_device(queries, key_input, value_input, log_decay, conv_weight, norm_gain):
    rows, width = queries.shape
    head_count = log_decay.shape[1]
    size = width // head_count
    heads = head_count // (SPAN * CHUNKS)
    taps = conv_weight.shape[0]
    half = UNITS * heads
    packet = heads * size + 3 * PARTS
    n = lax.axis_size("ctx")

    def swap(x, mask):
        return lax.ppermute(x, "ctx", [(i, i ^ mask) for i in range(n)])

    def shift(x, by):
        return lax.ppermute(x, "ctx", [(i, i + by) for i in range(n - by)])

    gain = norm_gain.reshape(1, width)
    ext = pltpu.VMEM((2 * heads, rows + HALO, size), F32)
    held = pltpu.VMEM((half, rows, size), BF16)

    cum_shape = pltpu.VMEM((SPAN * CHUNKS, 2 * heads, rows), F32)

    def states(mine):
        scratch = [cum_shape, ext, held]
        if not mine:
            buf = pltpu.VMEM((CHIPS, rows, CHUNKS * heads * size), BF16)
            scratch = [
                buf,
                buf,
                pltpu.VMEM((CHIPS, taps, CHUNKS * heads * size), F32),
                pltpu.VMEM((head_count, rows), F32),
                *scratch,
                pltpu.SemaphoreType.DMA((3 * CHIPS + 1,)),
            ]
        return call(
            functools.partial(state_kernel if mine else fetched_state_kernel, mine, heads, size),
            "states_mine" if mine else "states_other",
            pltpu.VMEM((UNITS, packet, size), BF16),
            key_input, value_input, conv_weight, log_decay.T,
            in_specs=[VMEM if mine else HBM] * 4,
            scratch=scratch,
        )

    def intra_part(mine, q):
        return call(
            functools.partial(intra_kernel, mine, heads, size),
            "intra_mine" if mine else "intra_other",
            pltpu.VMEM((half + 1, rows, size), F32),
            q, key_input, value_input, conv_weight, cum,
            scratch=[ext, held],
        )

    theirs = states(False)
    got = swap(theirs, 1)
    mine = states(True)
    got_late = swap(mine, 1)

    chip_states = call(
        functools.partial(chip_kernel, heads, size),
        "chip_states",
        pltpu.VMEM((CHIPS, CHUNKS, packet, size), BF16),
        mine, got,
    )
    order = pltpu.VMEM((CHIPS, packet, size), BF16)

    packets = {0: chip_states[0]}
    for g in EXCHANGE:
        packets[g] = swap(chip_states[g], 2 * g)
    q_after, decay_after, chip_states = lax.optimization_barrier(
        (queries, log_decay, chip_states)
    )
    cum = call(
        functools.partial(cum_kernel, heads),
        "cum",
        cum_shape,
        decay_after.T,
    )
    intra_mine = intra_part(True, q_after)
    *late, intra_mine = lax.optimization_barrier((*[packets[g] for g in EXCHANGE], intra_mine))
    packets.update(zip(EXCHANGE, late))
    packets = [packets[g] for g in range(CHIPS)]

    known = []
    if n > 2 * SPAN:
        edge = call(
            functools.partial(last_edge_kernel, heads, size),
            "last_edge",
            pltpu.VMEM((CHUNKS, PARTS, size), BF16),
            *packets,
            scratch=[order],
        )
        known = [shift(edge, SPAN)]

    def joined(parts, packets):
        span = call(
            functools.partial(span_kernel, parts, heads, size),
            "span_state",
            pltpu.VMEM((len(parts), heads * size + (2 if known else 1) * PARTS, size), BF16),
            *packets, *known,
            scratch=[order],
        )
        before = swap(span, SPAN) if n == 2 * SPAN else shift(span, SPAN)
        reach = 1
        while reach < n // SPAN - 1:
            before = jax.vmap(functools.partial(join_spans, heads=heads, size=size))(
                shift(before, SPAN * reach), before
            )
            reach *= 2
        return span, before

    span, before = joined(SHIFTS[0], packets)
    q_after, _ = lax.optimization_barrier((queries, span))
    intra_other = intra_part(False, q_after)
    packets_after, intra_other = lax.optimization_barrier((packets, intra_other))
    befores = [before] + [joined(parts, packets_after)[1] for parts in SHIFTS[1:]]
    ahead = {
        part: (place, before)
        for parts, before in zip(SHIFTS, befores)
        for place, part in enumerate(parts)
    }

    own, other = {}, {}
    for part in range(CHUNKS):
        chip_prefix = call(
            functools.partial(spread_kernel, part, ahead[part][0], heads, size),
            "chip_prefix",
            pltpu.VMEM((CHIPS, heads * size + PARTS, size), BF16),
            *packets, ahead[part][1], *known,
            scratch=[order],
        )
        first = part * CHIPS
        own[first] = chip_prefix[0]
        for g in EXCHANGE:
            own[first + g] = swap(chip_prefix[g], 2 * g)
        other[first] = swap(own[first], 1)

    def output(items, earlier=None):
        args = [queries, cum, gain]
        for mine, u in items:
            args += [own[u], intra_mine, got] if mine else [other[u], intra_other, got_late]
        done = pltpu.VMEM((len(items), rows, heads * size), BF16)
        scratch = [
            pltpu.VMEM((len(items) * heads, rows, size), F32),
            pltpu.VMEM((len(items) * heads, rows, 2 * PARTS), BF16),
        ]
        kernel = functools.partial(out_kernel, items, heads, size)
        hints = {
            "cost_estimate": pl.CostEstimate(flops=1, transcendentals=0, bytes_accessed=1),
        }
        name = "out_" + "_".join(("m" if mine else "o") + str(u) for mine, u in items)
        if earlier is None:
            return call(kernel, name, done, *args, scratch=scratch, **hints)
        there, made = zip(*earlier)
        return call(
            functools.partial(last_out_kernel, items, there, heads, size),
            name,
            jax.ShapeDtypeStruct((rows, width), BF16),
            *args, *made,
            out_specs=HBM,
            scratch=[*scratch, done, pltpu.SemaphoreType.DMA((2 * UNITS,))],
            **hints,
        )

    earlier = []
    for part in range(CHUNKS):
        first = part * CHIPS
        units = [first + g for g in EXCHANGE]
        items = [(True, first), (False, first)]
        made = [output(items)] + [x for _, x in earlier[-1:]]
        late, made = lax.optimization_barrier(([own[u] for u in units], made))
        earlier = earlier[:-1] + [(there, x) for (there, _), x in zip(earlier[-1:], made[1:])]
        earlier.append((items, made[0]))
        own.update(zip(units, late))
        other.update({u: swap(own[u], 1) for u in units})
        items = [(True, u) for u in units]
        if part < CHUNKS - 1:
            others = [(False, u) for u in units]
            earlier += [(others, output(others)), (items, output(items))]
        else:
            earlier.append((items, output(items)))
    return output([(False, u) for u in units], earlier)


def solution(mesh):
    rows = P(("groups", "ctx"), None)
    return jax.shard_map(
        on_device,
        mesh=mesh,
        in_specs=(rows, rows, rows, rows, P(), P()),
        out_specs=rows,
        check_vma=False,
    )
```

```python
import functools

import jax
import jax.numpy as jnp
from jax import lax
from jax.experimental import pallas as pl
from jax.experimental.pallas import tpu as pltpu
from jax.sharding import PartitionSpec as P

F32 = jnp.float32
BF16 = jnp.bfloat16
CHIPS = 4
SPAN = 2 * CHIPS
HALO = 8
EXCHANGE = (2, 3, 1)
CHUNKS = 1
UNITS = CHUNKS * CHIPS
SHIFTS = ((0,),)
PARTS = 16
VMEM = pl.BlockSpec(memory_space=pltpu.VMEM)
HBM = pl.BlockSpec(memory_space=pltpu.HBM)


def position():
    me = lax.axis_index("ctx")
    return me & 1, (me >> 1) & (CHIPS - 1)


def head_group(mine, unit):
    core, chip = position()
    group = (core if mine else 1 - core) * CHIPS + (chip ^ (unit % CHIPS))
    return group * CHUNKS + unit // CHIPS


def columns(block, offset, size):
    return pl.ds(pl.multiple_of(block + offset, size), size)


def call(kernel, name, out_shape, *args, scratch=(), in_specs=None, out_specs=VMEM, **options):
    if in_specs is None:
        in_specs = [VMEM] * len(args)
    args = [
        pltpu.with_memory_space_constraint(x, pltpu.VMEM if s is VMEM else pltpu.HBM)
        for x, s in zip(args, in_specs)
    ]
    return pl.pallas_call(
        kernel,
        out_shape=out_shape,
        in_specs=in_specs,
        out_specs=out_specs,
        scratch_shapes=list(scratch),
        name=name,
        compiler_params=pltpu.CompilerParams(vmem_limit_bytes=6 << 20),
        **options,
    )(*args)


def cum_kernel(heads, decay_ref, out_ref):
    x = decay_ref[...]
    count, rows = x.shape
    upto = lax.broadcasted_iota(jnp.int32, (rows, rows), 0) <= lax.broadcasted_iota(
        jnp.int32, (rows, rows), 1
    )
    parts = jnp.concatenate([p.astype(F32) for p in three_parts(x)], 0).astype(BF16)
    sums = jnp.dot(parts, upto.astype(F32).astype(BF16), preferred_element_type=F32)
    sums = sums[0:count] + (sums[count : 2 * count] + sums[2 * count :])
    total = jnp.broadcast_to(sums[:, rows - 1 : rows], sums.shape)
    for b in range(out_ref.shape[0]):
        these = slice(b * heads, (b + 1) * heads)
        out_ref[b, 0:heads, :] = sums[these]
        out_ref[b, heads : 2 * heads, :] = total[these]


def three_parts(x):
    hi = x.astype(BF16)
    rest = x - hi.astype(F32)
    mid = rest.astype(BF16)
    low = (rest - mid.astype(F32)).astype(BF16)
    return hi, mid, low


def side(part, heads, size):
    base = heads * size + part * PARTS
    return slice(base, base + PARTS)


def padded(rows):
    rows = jnp.concatenate(rows, 0)
    spare = jnp.zeros((PARTS - rows.shape[0], rows.shape[1]), F32)
    return jnp.concatenate([rows, spare], 0).astype(BF16)


def put_decay(out, decays, heads, size):
    out[side(1, heads, size), :] = padded([p.astype(F32) for p in three_parts(decays)])


def get_decay(packet, heads, size):
    tail = packet[side(1, heads, size), :].astype(F32)
    return tail[0:heads] + tail[heads : 2 * heads] + tail[2 * heads : 3 * heads]


def edge_states(values, edges, heads):
    row = lax.broadcasted_iota(jnp.int32, values.shape, 0)
    out = []
    for j in range(heads):
        picked = jnp.where(lax.rem(row, heads) == j, values.astype(F32), 0.0).astype(BF16)
        out.append(
            lax.dot_general(picked, edges, (((0,), (0,)), ((), ())), preferred_element_type=F32)
        )
    return out


def conv_keys(k_ref, halo, w_ref, ext, cols):
    rows = k_ref.shape[0]
    ext[0:HALO, :] = halo
    ext[HALO : HALO + rows, :] = k_ref[:, cols].astype(F32)
    total = None
    for j in range(w_ref.shape[0]):
        term = w_ref[j : j + 1, cols] * ext[HALO - j : HALO - j + rows, :]
        total = term if total is None else total + term
    return total.astype(BF16)


def fetched_state_kernel(
    mine, heads, size, k_hbm, v_hbm, w_hbm, decay_hbm, out_ref,
    k_buf, v_buf, w_buf, decay_buf, cum_ref, ext, held, sems,
):
    wide = CHUNKS * heads * size
    copies = [pltpu.make_async_copy(decay_hbm, decay_buf, sems.at[3 * CHIPS])]
    copies[0].start()
    for g in range(CHIPS):
        cols = columns(head_group(mine, g) * heads * size, 0, wide)
        for i, (source, buf) in enumerate(((k_hbm, k_buf), (w_hbm, w_buf), (v_hbm, v_buf))):
            copies.append(
                pltpu.make_async_copy(source.at[:, cols], buf.at[g], sems.at[3 * g + i])
            )
            copies[-1].start()
    copies[0].wait()
    groups, waits = [], []
    for u in range(UNITS):
        g, part = u % CHIPS, u // CHIPS
        cols = slice(part * heads * size, (part + 1) * heads * size)
        groups.append(tuple(buf.at[g, :, cols] for buf in (k_buf, v_buf, w_buf)))
        waits.append(copies[1 + 3 * g : 4 + 3 * g] if part == 0 else [])
    states_of(mine, heads, size, groups, waits, decay_buf, out_ref, cum_ref, ext, held)


def state_kernel(
    mine, heads, size, k_ref, v_ref, w_ref, decay_ref, out_ref, cum_ref, ext, held
):
    groups = []
    for u in range(UNITS):
        cols = columns(head_group(mine, u) * heads * size, 0, heads * size)
        groups.append((k_ref.at[:, cols], v_ref.at[:, cols], w_ref.at[:, cols]))
    waits = [[]] * UNITS
    states_of(mine, heads, size, groups, waits, decay_ref, out_ref, cum_ref, ext, held)


def states_of(mine, heads, size, groups, waits, decay_ref, out_ref, cum_ref, ext, held):
    rows = groups[0][0].shape[0]
    taps = groups[0][2].shape[0]
    cum_kernel(heads, decay_ref, cum_ref)
    none = jnp.zeros((HALO, size), F32)
    for g in range(UNITS):
        k_ref, v_ref, w_ref = groups[g]
        for copy in waits[g]:
            copy.wait()
        cum = cum_ref[head_group(mine, g)]
        ending = jnp.exp(cum[heads : 2 * heads] - cum[0:heads]).T
        edges, values = [], []
        for j in range(heads):
            cols = slice(j * size, (j + 1) * size)
            key_conv = conv_keys(k_ref, none, w_ref, ext.at[g % 2 * heads + j], cols)
            held[g * heads + j] = (key_conv.astype(F32) * ending[:, j : j + 1]).astype(BF16)
            last = k_ref[rows - HALO : rows, cols].astype(F32)
            head_edges = []
            for t in range(taps - 1):
                terms = [
                    w_ref[i : i + 1, cols] * last[HALO + t - i : HALO + t - i + 1]
                    for i in range(t + 1, taps)
                ]
                head_edges.append(sum(terms[1:], terms[0]))
            edges.append(head_edges)
            values.append(v_ref[0:HALO, cols].astype(F32) * ending[0:HALO, j : j + 1])
        put_decay(out_ref.at[g], jnp.exp(cum[heads : 2 * heads]), heads, size)
        out_ref[g, side(0, heads, size), :] = padded(
            [edges[j][t] for t in range(taps - 1) for j in range(heads)]
        )
        out_ref[g, side(2, heads, size), :] = padded(
            [values[j][t : t + 1] for t in range(taps - 1) for j in range(heads)]
        )
    for g in range(UNITS):
        for j in range(heads):
            cols = slice(j * size, (j + 1) * size)
            state = lax.dot_general(
                groups[g][1][:, cols], held[g * heads + j], (((0,), (0,)), ((), ())),
                preferred_element_type=F32,
            )
            out_ref[g, cols, :] = state.astype(BF16)


def intra_kernel(mine, heads, size, q_ref, k_ref, v_ref, w_ref, cum_ref, out_ref, ext, held):
    rows = q_ref.shape[0]
    causal = lax.broadcasted_iota(jnp.int32, (rows, rows), 0) >= lax.broadcasted_iota(
        jnp.int32, (rows, rows), 1
    )
    none = jnp.zeros((HALO, size), F32)
    for g in range(UNITS):
        b = head_group(mine, g)
        cum = cum_ref[b][0:heads]
        cum_col = cum.T
        growth = jnp.exp(-cum_col[0:HALO])
        values = []
        for j in range(heads):
            cols = columns(b * heads * size, j * size, size)
            key_conv = conv_keys(k_ref, none, w_ref, ext.at[g % 2 * heads + j], cols)
            scores = lax.dot_general(
                q_ref[:, cols], key_conv, (((1,), (1,)), ((), ())), preferred_element_type=F32
            )
            spread = cum_col[:, j : j + 1] - cum[j : j + 1]
            weights = jnp.where(causal, scores * jnp.exp(jnp.where(causal, spread, 0.0)), 0.0)
            held[g * heads + j] = weights.astype(BF16)
            values.append(v_ref[0:HALO, cols].astype(F32) * growth[:, j : j + 1])
        out_ref[UNITS * heads, g * PARTS : (g + 1) * PARTS, :] = padded(
            [values[j][t : t + 1] for t in range(3) for j in range(heads)]
        ).astype(F32)
    for g in range(UNITS):
        b = head_group(mine, g)
        for j in range(heads):
            cols = columns(b * heads * size, j * size, size)
            out_ref[g * heads + j] = jnp.dot(
                held[g * heads + j], v_ref[:, cols], preferred_element_type=F32
            )


def chip_kernel(heads, size, own_ref, got_ref, out_ref):
    core, _ = position()
    first = core == 0
    for g in range(UNITS):
        to = out_ref.at[g % CHIPS, g // CHIPS]
        own_decay = get_decay(own_ref.at[g], heads, size)
        got_decay = get_decay(got_ref.at[g], heads, size)
        own_by = jnp.where(first, got_decay, 1.0)
        got_by = jnp.where(first, 1.0, own_decay)

        def earlier_later(part):
            own = own_ref[g, side(part, heads, size), :].astype(F32)
            got = got_ref[g, side(part, heads, size), :].astype(F32)
            return jnp.where(first, own, got), jnp.where(first, got, own)

        edges, out_edges = earlier_later(0)
        out_values, values = earlier_later(2)
        fixes = edge_states(values.astype(BF16), edges.astype(BF16), heads)
        for j in range(heads):
            rows = slice(j * size, (j + 1) * size)
            to[rows, :] = (
                own_ref[g, rows, :].astype(F32) * own_by[j : j + 1]
                + got_ref[g, rows, :].astype(F32) * got_by[j : j + 1]
                + fixes[j]
            ).astype(BF16)
        put_decay(to, own_decay * got_decay, heads, size)
        later_by = jnp.where(first, got_decay, own_decay)
        to[side(0, heads, size), :] = out_edges.astype(BF16)
        to[side(2, heads, size), :] = padded(
            [out_values[t * heads : (t + 1) * heads] * later_by for t in range(3)]
        )


def in_order(packets, part, held):
    _, chip = position()
    for g in range(CHIPS):
        held[chip ^ g] = packets[g][part]


def chip_fixes(held, b, edges, heads, size):
    return edge_states(held[b, side(2, heads, size), :], edges, heads)


def last_edge_kernel(heads, size, *refs):
    packets, out_ref, held = refs[:CHIPS], refs[CHIPS], refs[CHIPS + 1]
    for part in range(CHUNKS):
        in_order(packets, part, held)
        out_ref[part] = held[CHIPS - 1, side(0, heads, size), :]


def span_kernel(parts, heads, size, *refs):
    packets, before, (whole_ref, held) = refs[:CHIPS], refs[CHIPS:-2], refs[-2:]
    for i, part in enumerate(parts):
        known = [before[0][part]] if before else []
        span_of(part, known, heads, size, packets, whole_ref.at[i], held)


def span_of(part, before, heads, size, packets, out_ref, held):
    in_order(packets, part, held)
    decays = [get_decay(held.at[b], heads, size) for b in range(CHIPS)]
    fixes = [
        chip_fixes(held, b, held[b - 1, side(0, heads, size), :], heads, size)
        for b in range(1, CHIPS)
    ]
    fixes.insert(0, chip_fixes(held, 0, before[0], heads, size) if before else None)
    for j in range(heads):
        rows = slice(j * size, (j + 1) * size)
        acc = held[0, rows, :].astype(F32)
        if before:
            acc = acc + fixes[0][j]
        for b in range(1, CHIPS):
            acc = acc * decays[b][j : j + 1] + (held[b, rows, :].astype(F32) + fixes[b][j])
        out_ref[rows, :] = acc.astype(BF16)
    whole = decays[0]
    for b in range(1, CHIPS):
        whole = whole * decays[b]
    out_ref[side(0, heads, size), :] = held[CHIPS - 1, side(0, heads, size), :]
    if before:
        put_decay(out_ref, whole, heads, size)


def spread_kernel(part, place, heads, size, *refs):
    packets, before, known, (out_ref, held) = refs[:CHIPS], refs[CHIPS], refs[CHIPS + 1 : -2], refs[-2:]
    _, chip = position()
    later = lax.axis_index("ctx") >= SPAN
    in_order(packets, part, held)
    decays = [get_decay(held.at[b], heads, size) for b in range(CHIPS)]
    edges = known[0][part] if known else before[place, side(0, heads, size), :]
    edges = [jnp.where(later, edges.astype(F32), 0.0).astype(BF16)]
    edges += [held[b, side(0, heads, size), :] for b in range(CHIPS - 1)]
    fixes = [chip_fixes(held, b, edges[b], heads, size) for b in range(CHIPS - 1)]
    for j in range(heads):
        rows = slice(j * size, (j + 1) * size)
        acc = jnp.where(later, before[place, rows, :].astype(F32), 0.0)
        out_ref[chip, rows, :] = acc.astype(BF16)
        for b in range(1, CHIPS):
            acc = acc * decays[b - 1][j : j + 1] + (
                held[b - 1, rows, :].astype(F32) + fixes[b - 1][j]
            )
            out_ref[chip ^ b, rows, :] = acc.astype(BF16)
    for b in range(CHIPS):
        out_ref[chip ^ b, heads * size : heads * size + PARTS, :] = edges[b]


def last_out_kernel(items, earlier, heads, size, *refs):
    count = 3 + 3 * len(items)
    made = refs[count : count + len(earlier)]
    out_ref, inter_ref, score_ref, done_ref, sems = refs[-5:]
    copies = []

    def write(item, source):
        cols = columns(head_group(*item) * heads * size, 0, heads * size)
        copies.append(
            pltpu.make_async_copy(source, out_ref.at[:, cols], sems.at[len(copies)])
        )
        copies[-1].start()

    for there, ref in zip(earlier, made):
        for i, item in enumerate(there):
            write(item, ref.at[i])
    out_kernel(items, heads, size, *refs[:count], done_ref, inter_ref, score_ref, write=write)
    for copy in copies:
        copy.wait()


def out_kernel(items, heads, size, *refs, write=None):
    q_ref, cum_ref, gain_ref = refs[:3]
    per_item = [refs[3 + 3 * i : 6 + 3 * i] for i in range(len(items))]
    done_ref, inter_ref, score_ref = refs[-3:]
    rows = q_ref.shape[0]
    core, _ = position()
    second = core == 1
    row = lax.broadcasted_iota(jnp.int32, (rows, 2 * PARTS), 0)
    column = lax.broadcasted_iota(jnp.int32, (rows, 2 * PARTS), 1)
    edge = lax.rem(column, PARTS)
    causal = (lax.div(edge, heads) <= row) & (edge < 3 * heads)
    ahead = column < PARTS
    kept = ((ahead & (core == 1)) | causal) & (ahead | (core == 1))
    kept = [kept & (lax.rem(edge, heads) == j) for j in range(heads)]
    for i, (mine, g) in enumerate(items):
        prefix_ref, intra_ref, sib_ref = per_item[i]
        b = head_group(mine, g)
        started = jnp.exp(cum_ref[b][0:heads]).T
        by = jnp.where(second, get_decay(sib_ref.at[g], heads, size), 1.0)
        edges = jnp.concatenate(
            [
                prefix_ref[heads * size : heads * size + PARTS, :].astype(F32),
                sib_ref[g, side(0, heads, size), :].astype(F32),
            ],
            0,
        ).astype(BF16)
        for j in range(heads):
            cols = columns(b * heads * size, j * size, size)
            these = slice(j * size, (j + 1) * size)
            sib = jnp.where(second, sib_ref[g, these, :].astype(F32), 0.0)
            prefix = (prefix_ref[these, :].astype(F32) * by[j : j + 1] + sib).astype(BF16)
            both = lax.dot_general(
                q_ref[:, cols],
                jnp.concatenate([prefix, edges], 0),
                (((1,), (1,)), ((), ())),
                preferred_element_type=F32,
            )
            both = both * started[:, j : j + 1]
            inter_ref[i * heads + j] = both[:, 0:size] + intra_ref[g * heads + j]
            score_ref[i * heads + j] = jnp.where(kept[j], both[:, size:], 0.0).astype(BF16)
    for i, (mine, g) in enumerate(items):
        _, intra_ref, sib_ref = per_item[i]
        b = head_group(mine, g)
        values = intra_ref[UNITS * heads, g * PARTS : (g + 1) * PARTS, :]
        ahead_values = jnp.where(second, sib_ref[g, side(2, heads, size), :].astype(F32), values)
        values = jnp.concatenate([ahead_values, values], 0).astype(BF16)
        for j in range(heads):
            inter_ref[i * heads + j] += jnp.dot(
                score_ref[i * heads + j], values, preferred_element_type=F32
            )
    for i, (mine, g) in enumerate(items):
        b = head_group(mine, g)
        for j in range(heads):
            cols = columns(b * heads * size, j * size, size)
            mixed = inter_ref[i * heads + j]
            scale = lax.rsqrt(jnp.mean(mixed * mixed, axis=1, keepdims=True) + 1e-05)
            done_ref[i, :, j * size : (j + 1) * size] = (
                mixed * scale * gain_ref[:, cols]
            ).astype(BF16)
        if write is not None:
            write((mine, g), done_ref.at[i])


def join_spans(earlier, later, heads, size):
    base = heads * size
    own = side(1, heads, size)

    def decay(x):
        tail = x[own].astype(F32)
        return tail[0:heads] + tail[heads : 2 * heads] + tail[2 * heads : 3 * heads]

    by = decay(later)
    state = (
        by[:, None, :] * earlier[:base].astype(F32).reshape(heads, size, -1)
        + later[:base].astype(F32).reshape(heads, size, -1)
    ).reshape(base, -1)
    parts = three_parts(by * decay(earlier))
    return jnp.concatenate([state.astype(BF16), later[base : own.start], *parts, later[own.start + 3 * heads :]], 0)


def on_device(queries, key_input, value_input, log_decay, conv_weight, norm_gain):
    rows, width = queries.shape
    head_count = log_decay.shape[1]
    size = width // head_count
    heads = head_count // (SPAN * CHUNKS)
    taps = conv_weight.shape[0]
    half = UNITS * heads
    packet = heads * size + 3 * PARTS
    n = lax.axis_size("ctx")

    def swap(x, mask):
        return lax.ppermute(x, "ctx", [(i, i ^ mask) for i in range(n)])

    def shift(x, by):
        return lax.ppermute(x, "ctx", [(i, i + by) for i in range(n - by)])

    gain = norm_gain.reshape(1, width)
    ext = pltpu.VMEM((2 * heads, rows + HALO, size), F32)
    held = pltpu.VMEM((half, rows, size), BF16)

    cum_shape = pltpu.VMEM((SPAN * CHUNKS, 2 * heads, rows), F32)

    def states(mine):
        scratch = [cum_shape, ext, held]
        if not mine:
            buf = pltpu.VMEM((CHIPS, rows, CHUNKS * heads * size), BF16)
            scratch = [
                buf,
                buf,
                pltpu.VMEM((CHIPS, taps, CHUNKS * heads * size), F32),
                pltpu.VMEM((head_count, rows), F32),
                *scratch,
                pltpu.SemaphoreType.DMA((3 * CHIPS + 1,)),
            ]
        return call(
            functools.partial(state_kernel if mine else fetched_state_kernel, mine, heads, size),
            "states_mine" if mine else "states_other",
            pltpu.VMEM((UNITS, packet, size), BF16),
            key_input, value_input, conv_weight, log_decay.T,
            in_specs=[VMEM if mine else HBM] * 4,
            scratch=scratch,
        )

    def intra_part(mine, q):
        return call(
            functools.partial(intra_kernel, mine, heads, size),
            "intra_mine" if mine else "intra_other",
            pltpu.VMEM((half + 1, rows, size), F32),
            q, key_input, value_input, conv_weight, cum,
            scratch=[ext, held],
        )

    theirs = states(False)
    got = swap(theirs, 1)
    mine = states(True)
    got_late = swap(mine, 1)

    chip_states = call(
        functools.partial(chip_kernel, heads, size),
        "chip_states",
        pltpu.VMEM((CHIPS, CHUNKS, packet, size), BF16),
        mine, got,
    )
    order = pltpu.VMEM((CHIPS, packet, size), BF16)

    packets = {0: chip_states[0]}
    for g in EXCHANGE:
        packets[g] = swap(chip_states[g], 2 * g)
    q_after, decay_after, chip_states = lax.optimization_barrier(
        (queries, log_decay, chip_states)
    )
    cum = call(
        functools.partial(cum_kernel, heads),
        "cum",
        cum_shape,
        decay_after.T,
    )
    intra_mine = intra_part(True, q_after)
    *late, intra_mine = lax.optimization_barrier((*[packets[g] for g in EXCHANGE], intra_mine))
    packets.update(zip(EXCHANGE, late))
    packets = [packets[g] for g in range(CHIPS)]

    known = []
    if n > 2 * SPAN:
        edge = call(
            functools.partial(last_edge_kernel, heads, size),
            "last_edge",
            pltpu.VMEM((CHUNKS, PARTS, size), BF16),
            *packets,
            scratch=[order],
        )
        known = [shift(edge, SPAN)]

    def joined(parts):
        span = call(
            functools.partial(span_kernel, parts, heads, size),
            "span_state",
            pltpu.VMEM((len(parts), heads * size + (2 if known else 1) * PARTS, size), BF16),
            *packets, *known,
            scratch=[order],
        )
        before = swap(span, SPAN) if n == 2 * SPAN else shift(span, SPAN)
        reach = 1
        while reach < n // SPAN - 1:
            before = jax.vmap(functools.partial(join_spans, heads=heads, size=size))(
                shift(before, SPAN * reach), before
            )
            reach *= 2
        return span, before

    spans, befores = zip(*[joined(parts) for parts in SHIFTS])
    q_after, _ = lax.optimization_barrier((queries, spans[-1]))
    intra_other = intra_part(False, q_after)
    before, intra_other = lax.optimization_barrier((befores[-1], intra_other))
    befores = [*befores[:-1], before]
    ahead = {
        part: (place, before)
        for parts, before in zip(SHIFTS, befores)
        for place, part in enumerate(parts)
    }

    own, other = {}, {}
    for part in range(CHUNKS):
        chip_prefix = call(
            functools.partial(spread_kernel, part, ahead[part][0], heads, size),
            "chip_prefix",
            pltpu.VMEM((CHIPS, heads * size + PARTS, size), BF16),
            *packets, ahead[part][1], *known,
            scratch=[order],
        )
        first = part * CHIPS
        own[first] = chip_prefix[0]
        for g in EXCHANGE:
            own[first + g] = swap(chip_prefix[g], 2 * g)
        other[first] = swap(own[first], 1)

    def output(items, earlier=None):
        args = [queries, cum, gain]
        for mine, u in items:
            args += [own[u], intra_mine, got] if mine else [other[u], intra_other, got_late]
        done = pltpu.VMEM((len(items), rows, heads * size), BF16)
        scratch = [
            pltpu.VMEM((len(items) * heads, rows, size), F32),
            pltpu.VMEM((len(items) * heads, rows, 2 * PARTS), BF16),
        ]
        kernel = functools.partial(out_kernel, items, heads, size)
        hints = {
            "cost_estimate": pl.CostEstimate(flops=1, transcendentals=0, bytes_accessed=1),
        }
        name = "out_" + "_".join(("m" if mine else "o") + str(u) for mine, u in items)
        if earlier is None:
            return call(kernel, name, done, *args, scratch=scratch, **hints)
        there, made = zip(*earlier)
        return call(
            functools.partial(last_out_kernel, items, there, heads, size),
            name,
            jax.ShapeDtypeStruct((rows, width), BF16),
            *args, *made,
            out_specs=HBM,
            scratch=[*scratch, done, pltpu.SemaphoreType.DMA((2 * UNITS,))],
            **hints,
        )

    final, *early = EXCHANGE
    items = [(True, 0), (False, 0)]
    made = output(items)
    *late, made = lax.optimization_barrier((*[own[u] for u in early], made))
    earlier = [(items, made)]
    own.update(zip(early, late))
    other.update({u: swap(own[u], 1) for u in early})
    items = [(True, u) for u in early]
    made = output(items)
    own[final], made = lax.optimization_barrier((own[final], made))
    earlier.append((items, made))
    other[final] = swap(own[final], 1)
    items = [(True, final)] + [(False, u) for u in early]
    earlier.append((items, output(items)))
    return output([(False, final)], earlier)


def solution(mesh):
    rows = P(("groups", "ctx"), None)
    return jax.shard_map(
        on_device,
        mesh=mesh,
        in_specs=(rows, rows, rows, rows, P(), P()),
        out_specs=rows,
        check_vma=False,
    )
```

```python
import functools

import jax
import jax.numpy as jnp
from jax import lax
from jax.experimental import pallas as pl
from jax.experimental.pallas import tpu as pltpu
from jax.sharding import PartitionSpec as P

F32 = jnp.float32
BF16 = jnp.bfloat16
CHIPS = 4
SPAN = 2 * CHIPS
HALO = 8
EXCHANGE = (2, 3, 1)
CHUNKS = 1
UNITS = CHUNKS * CHIPS
SHIFTS = ((0,),)
PARTS = 16
VMEM = pl.BlockSpec(memory_space=pltpu.VMEM)
HBM = pl.BlockSpec(memory_space=pltpu.HBM)


def position():
    me = lax.axis_index("ctx")
    return me & 1, (me >> 1) & (CHIPS - 1)


def head_group(mine, unit):
    core, chip = position()
    group = (core if mine else 1 - core) * CHIPS + (chip ^ (unit % CHIPS))
    return group * CHUNKS + unit // CHIPS


def columns(block, offset, size):
    return pl.ds(pl.multiple_of(block + offset, size), size)


def call(kernel, name, out_shape, *args, scratch=(), in_specs=None, out_specs=VMEM, **options):
    if in_specs is None:
        in_specs = [VMEM] * len(args)
    args = [
        pltpu.with_memory_space_constraint(x, pltpu.VMEM if s is VMEM else pltpu.HBM)
        for x, s in zip(args, in_specs)
    ]
    return pl.pallas_call(
        kernel,
        out_shape=out_shape,
        in_specs=in_specs,
        out_specs=out_specs,
        scratch_shapes=list(scratch),
        name=name,
        compiler_params=pltpu.CompilerParams(vmem_limit_bytes=6 << 20),
        **options,
    )(*args)


def cum_kernel(heads, decay_ref, out_ref):
    x = decay_ref[...]
    count, rows = x.shape
    upto = lax.broadcasted_iota(jnp.int32, (rows, rows), 0) <= lax.broadcasted_iota(
        jnp.int32, (rows, rows), 1
    )
    parts = jnp.concatenate([p.astype(F32) for p in three_parts(x)], 0).astype(BF16)
    sums = jnp.dot(parts, upto.astype(F32).astype(BF16), preferred_element_type=F32)
    sums = sums[0:count] + (sums[count : 2 * count] + sums[2 * count :])
    total = jnp.broadcast_to(sums[:, rows - 1 : rows], sums.shape)
    for b in range(out_ref.shape[0]):
        these = slice(b * heads, (b + 1) * heads)
        out_ref[b, 0:heads, :] = sums[these]
        out_ref[b, heads : 2 * heads, :] = total[these]


def three_parts(x):
    hi = x.astype(BF16)
    rest = x - hi.astype(F32)
    mid = rest.astype(BF16)
    low = (rest - mid.astype(F32)).astype(BF16)
    return hi, mid, low


def side(part, heads, size):
    base = heads * size + part * PARTS
    return slice(base, base + PARTS)


def padded(rows):
    rows = jnp.concatenate(rows, 0)
    spare = jnp.zeros((PARTS - rows.shape[0], rows.shape[1]), F32)
    return jnp.concatenate([rows, spare], 0).astype(BF16)


def put_decay(out, decays, heads, size):
    out[side(1, heads, size), :] = padded([p.astype(F32) for p in three_parts(decays)])


def get_decay(packet, heads, size):
    tail = packet[side(1, heads, size), :].astype(F32)
    return tail[0:heads] + tail[heads : 2 * heads] + tail[2 * heads : 3 * heads]


def edge_states(values, edges, heads):
    row = lax.broadcasted_iota(jnp.int32, values.shape, 0)
    out = []
    for j in range(heads):
        picked = jnp.where(lax.rem(row, heads) == j, values.astype(F32), 0.0).astype(BF16)
        out.append(
            lax.dot_general(picked, edges, (((0,), (0,)), ((), ())), preferred_element_type=F32)
        )
    return out


def conv_keys(k_ref, halo, w_ref, ext, cols):
    rows = k_ref.shape[0]
    ext[0:HALO, :] = halo
    ext[HALO : HALO + rows, :] = k_ref[:, cols].astype(F32)
    total = None
    for j in range(w_ref.shape[0]):
        term = w_ref[j : j + 1, cols] * ext[HALO - j : HALO - j + rows, :]
        total = term if total is None else total + term
    return total.astype(BF16)


def fetched_state_kernel(
    mine, heads, size, k_hbm, v_hbm, w_hbm, decay_hbm, out_ref,
    k_buf, v_buf, w_buf, decay_buf, cum_ref, ext, held, sems,
):
    wide = CHUNKS * heads * size
    copies = [pltpu.make_async_copy(decay_hbm, decay_buf, sems.at[3 * CHIPS])]
    copies[0].start()
    for g in range(CHIPS):
        cols = columns(head_group(mine, g) * heads * size, 0, wide)
        for i, (source, buf) in enumerate(((k_hbm, k_buf), (w_hbm, w_buf), (v_hbm, v_buf))):
            copies.append(
                pltpu.make_async_copy(source.at[:, cols], buf.at[g], sems.at[3 * g + i])
            )
            copies[-1].start()
    copies[0].wait()
    groups, waits = [], []
    for u in range(UNITS):
        g, part = u % CHIPS, u // CHIPS
        cols = slice(part * heads * size, (part + 1) * heads * size)
        groups.append(tuple(buf.at[g, :, cols] for buf in (k_buf, v_buf, w_buf)))
        waits.append(copies[1 + 3 * g : 4 + 3 * g] if part == 0 else [])
    states_of(mine, heads, size, groups, waits, decay_buf, out_ref, cum_ref, ext, held)


def state_kernel(
    mine, heads, size, k_ref, v_ref, w_ref, decay_ref, out_ref, cum_ref, ext, held
):
    groups = []
    for u in range(UNITS):
        cols = columns(head_group(mine, u) * heads * size, 0, heads * size)
        groups.append((k_ref.at[:, cols], v_ref.at[:, cols], w_ref.at[:, cols]))
    waits = [[]] * UNITS
    states_of(mine, heads, size, groups, waits, decay_ref, out_ref, cum_ref, ext, held)


def states_of(mine, heads, size, groups, waits, decay_ref, out_ref, cum_ref, ext, held):
    rows = groups[0][0].shape[0]
    taps = groups[0][2].shape[0]
    cum_kernel(heads, decay_ref, cum_ref)
    none = jnp.zeros((HALO, size), F32)
    for g in range(UNITS):
        k_ref, v_ref, w_ref = groups[g]
        for copy in waits[g]:
            copy.wait()
        cum = cum_ref[head_group(mine, g)]
        ending = jnp.exp(cum[heads : 2 * heads] - cum[0:heads]).T
        edges, values = [], []
        for j in range(heads):
            cols = slice(j * size, (j + 1) * size)
            key_conv = conv_keys(k_ref, none, w_ref, ext.at[g % 2 * heads + j], cols)
            held[g * heads + j] = (key_conv.astype(F32) * ending[:, j : j + 1]).astype(BF16)
            last = k_ref[rows - HALO : rows, cols].astype(F32)
            head_edges = []
            for t in range(taps - 1):
                terms = [
                    w_ref[i : i + 1, cols] * last[HALO + t - i : HALO + t - i + 1]
                    for i in range(t + 1, taps)
                ]
                head_edges.append(sum(terms[1:], terms[0]))
            edges.append(head_edges)
            values.append(v_ref[0:HALO, cols].astype(F32) * ending[0:HALO, j : j + 1])
        put_decay(out_ref.at[g], jnp.exp(cum[heads : 2 * heads]), heads, size)
        out_ref[g, side(0, heads, size), :] = padded(
            [edges[j][t] for t in range(taps - 1) for j in range(heads)]
        )
        out_ref[g, side(2, heads, size), :] = padded(
            [values[j][t : t + 1] for t in range(taps - 1) for j in range(heads)]
        )
    for g in range(UNITS):
        for j in range(heads):
            cols = slice(j * size, (j + 1) * size)
            state = lax.dot_general(
                groups[g][1][:, cols], held[g * heads + j], (((0,), (0,)), ((), ())),
                preferred_element_type=F32,
            )
            out_ref[g, cols, :] = state.astype(BF16)


def intra_kernel(mine, heads, size, q_ref, k_ref, v_ref, w_ref, cum_ref, out_ref, ext, held):
    rows = q_ref.shape[0]
    causal = lax.broadcasted_iota(jnp.int32, (rows, rows), 0) >= lax.broadcasted_iota(
        jnp.int32, (rows, rows), 1
    )
    none = jnp.zeros((HALO, size), F32)
    for g in range(UNITS):
        b = head_group(mine, g)
        cum = cum_ref[b][0:heads]
        cum_col = cum.T
        growth = jnp.exp(-cum_col[0:HALO])
        values = []
        for j in range(heads):
            cols = columns(b * heads * size, j * size, size)
            key_conv = conv_keys(k_ref, none, w_ref, ext.at[g % 2 * heads + j], cols)
            scores = lax.dot_general(
                q_ref[:, cols], key_conv, (((1,), (1,)), ((), ())), preferred_element_type=F32
            )
            spread = cum_col[:, j : j + 1] - cum[j : j + 1]
            weights = jnp.where(causal, scores * jnp.exp(jnp.where(causal, spread, 0.0)), 0.0)
            held[g * heads + j] = weights.astype(BF16)
            values.append(v_ref[0:HALO, cols].astype(F32) * growth[:, j : j + 1])
        out_ref[UNITS * heads, g * PARTS : (g + 1) * PARTS, :] = padded(
            [values[j][t : t + 1] for t in range(3) for j in range(heads)]
        ).astype(F32)
    for g in range(UNITS):
        b = head_group(mine, g)
        for j in range(heads):
            cols = columns(b * heads * size, j * size, size)
            out_ref[g * heads + j] = jnp.dot(
                held[g * heads + j], v_ref[:, cols], preferred_element_type=F32
            )


def chip_kernel(heads, size, own_ref, got_ref, out_ref):
    core, _ = position()
    first = core == 0
    for g in range(UNITS):
        to = out_ref.at[g % CHIPS, g // CHIPS]
        own_decay = get_decay(own_ref.at[g], heads, size)
        got_decay = get_decay(got_ref.at[g], heads, size)
        own_by = jnp.where(first, got_decay, 1.0)
        got_by = jnp.where(first, 1.0, own_decay)

        def earlier_later(part):
            own = own_ref[g, side(part, heads, size), :].astype(F32)
            got = got_ref[g, side(part, heads, size), :].astype(F32)
            return jnp.where(first, own, got), jnp.where(first, got, own)

        edges, out_edges = earlier_later(0)
        out_values, values = earlier_later(2)
        fixes = edge_states(values.astype(BF16), edges.astype(BF16), heads)
        for j in range(heads):
            rows = slice(j * size, (j + 1) * size)
            to[rows, :] = (
                own_ref[g, rows, :].astype(F32) * own_by[j : j + 1]
                + got_ref[g, rows, :].astype(F32) * got_by[j : j + 1]
                + fixes[j]
            ).astype(BF16)
        put_decay(to, own_decay * got_decay, heads, size)
        later_by = jnp.where(first, got_decay, own_decay)
        to[side(0, heads, size), :] = out_edges.astype(BF16)
        to[side(2, heads, size), :] = padded(
            [out_values[t * heads : (t + 1) * heads] * later_by for t in range(3)]
        )


def in_order(packets, part, held):
    _, chip = position()
    for g in range(CHIPS):
        held[chip ^ g] = packets[g][part]


def chip_fixes(held, b, edges, heads, size):
    return edge_states(held[b, side(2, heads, size), :], edges, heads)


def last_edge_kernel(heads, size, *refs):
    packets, out_ref, held = refs[:CHIPS], refs[CHIPS], refs[CHIPS + 1]
    for part in range(CHUNKS):
        in_order(packets, part, held)
        out_ref[part] = held[CHIPS - 1, side(0, heads, size), :]


def span_kernel(parts, heads, size, *refs):
    packets, before, (whole_ref, held) = refs[:CHIPS], refs[CHIPS:-2], refs[-2:]
    for i, part in enumerate(parts):
        known = [before[0][part]] if before else []
        span_of(part, known, heads, size, packets, whole_ref.at[i], held)


def span_of(part, before, heads, size, packets, out_ref, held):
    in_order(packets, part, held)
    decays = [get_decay(held.at[b], heads, size) for b in range(CHIPS)]
    fixes = [
        chip_fixes(held, b, held[b - 1, side(0, heads, size), :], heads, size)
        for b in range(1, CHIPS)
    ]
    fixes.insert(0, chip_fixes(held, 0, before[0], heads, size) if before else None)
    for j in range(heads):
        rows = slice(j * size, (j + 1) * size)
        acc = held[0, rows, :].astype(F32)
        if before:
            acc = acc + fixes[0][j]
        for b in range(1, CHIPS):
            acc = acc * decays[b][j : j + 1] + (held[b, rows, :].astype(F32) + fixes[b][j])
        out_ref[rows, :] = acc.astype(BF16)
    whole = decays[0]
    for b in range(1, CHIPS):
        whole = whole * decays[b]
    out_ref[side(0, heads, size), :] = held[CHIPS - 1, side(0, heads, size), :]
    if before:
        put_decay(out_ref, whole, heads, size)


def spread_kernel(part, place, heads, size, *refs):
    packets, before, known, (out_ref, held) = refs[:CHIPS], refs[CHIPS], refs[CHIPS + 1 : -2], refs[-2:]
    _, chip = position()
    later = lax.axis_index("ctx") >= SPAN
    in_order(packets, part, held)
    decays = [get_decay(held.at[b], heads, size) for b in range(CHIPS)]
    edges = known[0][part] if known else before[place, side(0, heads, size), :]
    edges = [jnp.where(later, edges.astype(F32), 0.0).astype(BF16)]
    edges += [held[b, side(0, heads, size), :] for b in range(CHIPS - 1)]
    fixes = [chip_fixes(held, b, edges[b], heads, size) for b in range(CHIPS - 1)]
    for j in range(heads):
        rows = slice(j * size, (j + 1) * size)
        acc = jnp.where(later, before[place, rows, :].astype(F32), 0.0)
        out_ref[chip, rows, :] = acc.astype(BF16)
        for b in range(1, CHIPS):
            acc = acc * decays[b - 1][j : j + 1] + (
                held[b - 1, rows, :].astype(F32) + fixes[b - 1][j]
            )
            out_ref[chip ^ b, rows, :] = acc.astype(BF16)
    for b in range(CHIPS):
        out_ref[chip ^ b, heads * size : heads * size + PARTS, :] = edges[b]


def last_out_kernel(items, earlier, heads, size, *refs):
    count = 3 + 3 * len(items)
    made = refs[count : count + len(earlier)]
    out_ref, inter_ref, score_ref, done_ref, sems = refs[-5:]
    copies = []

    def write(item, source):
        cols = columns(head_group(*item) * heads * size, 0, heads * size)
        copies.append(
            pltpu.make_async_copy(source, out_ref.at[:, cols], sems.at[len(copies)])
        )
        copies[-1].start()

    for there, ref in zip(earlier, made):
        for i, item in enumerate(there):
            write(item, ref.at[i])
    out_kernel(items, heads, size, *refs[:count], done_ref, inter_ref, score_ref, write=write)
    for copy in copies:
        copy.wait()


def out_kernel(items, heads, size, *refs, write=None):
    q_ref, cum_ref, gain_ref = refs[:3]
    per_item = [refs[3 + 3 * i : 6 + 3 * i] for i in range(len(items))]
    done_ref, inter_ref, score_ref = refs[-3:]
    rows = q_ref.shape[0]
    core, _ = position()
    second = core == 1
    row = lax.broadcasted_iota(jnp.int32, (rows, 2 * PARTS), 0)
    column = lax.broadcasted_iota(jnp.int32, (rows, 2 * PARTS), 1)
    edge = lax.rem(column, PARTS)
    causal = (lax.div(edge, heads) <= row) & (edge < 3 * heads)
    ahead = column < PARTS
    kept = ((ahead & (core == 1)) | causal) & (ahead | (core == 1))
    kept = [kept & (lax.rem(edge, heads) == j) for j in range(heads)]
    for i, (mine, g) in enumerate(items):
        prefix_ref, intra_ref, sib_ref = per_item[i]
        b = head_group(mine, g)
        started = jnp.exp(cum_ref[b][0:heads]).T
        by = jnp.where(second, get_decay(sib_ref.at[g], heads, size), 1.0)
        edges = jnp.concatenate(
            [
                prefix_ref[heads * size : heads * size + PARTS, :].astype(F32),
                sib_ref[g, side(0, heads, size), :].astype(F32),
            ],
            0,
        ).astype(BF16)
        for j in range(heads):
            cols = columns(b * heads * size, j * size, size)
            these = slice(j * size, (j + 1) * size)
            sib = jnp.where(second, sib_ref[g, these, :].astype(F32), 0.0)
            prefix = (prefix_ref[these, :].astype(F32) * by[j : j + 1] + sib).astype(BF16)
            both = lax.dot_general(
                q_ref[:, cols],
                jnp.concatenate([prefix, edges], 0),
                (((1,), (1,)), ((), ())),
                preferred_element_type=F32,
            )
            both = both * started[:, j : j + 1]
            inter_ref[i * heads + j] = both[:, 0:size] + intra_ref[g * heads + j]
            score_ref[i * heads + j] = jnp.where(kept[j], both[:, size:], 0.0).astype(BF16)
    for i, (mine, g) in enumerate(items):
        _, intra_ref, sib_ref = per_item[i]
        b = head_group(mine, g)
        values = intra_ref[UNITS * heads, g * PARTS : (g + 1) * PARTS, :]
        ahead_values = jnp.where(second, sib_ref[g, side(2, heads, size), :].astype(F32), values)
        values = jnp.concatenate([ahead_values, values], 0).astype(BF16)
        for j in range(heads):
            inter_ref[i * heads + j] += jnp.dot(
                score_ref[i * heads + j], values, preferred_element_type=F32
            )
    for i, (mine, g) in enumerate(items):
        b = head_group(mine, g)
        for j in range(heads):
            cols = columns(b * heads * size, j * size, size)
            mixed = inter_ref[i * heads + j]
            scale = lax.rsqrt(jnp.mean(mixed * mixed, axis=1, keepdims=True) + 1e-05)
            done_ref[i, :, j * size : (j + 1) * size] = (
                mixed * scale * gain_ref[:, cols]
            ).astype(BF16)
        if write is not None:
            write((mine, g), done_ref.at[i])


def join_spans(earlier, later, heads, size):
    base = heads * size
    own = side(1, heads, size)

    def decay(x):
        tail = x[own].astype(F32)
        return tail[0:heads] + tail[heads : 2 * heads] + tail[2 * heads : 3 * heads]

    by = decay(later)
    state = (
        by[:, None, :] * earlier[:base].astype(F32).reshape(heads, size, -1)
        + later[:base].astype(F32).reshape(heads, size, -1)
    ).reshape(base, -1)
    parts = three_parts(by * decay(earlier))
    return jnp.concatenate([state.astype(BF16), later[base : own.start], *parts, later[own.start + 3 * heads :]], 0)


def on_device(queries, key_input, value_input, log_decay, conv_weight, norm_gain):
    rows, width = queries.shape
    head_count = log_decay.shape[1]
    size = width // head_count
    heads = head_count // (SPAN * CHUNKS)
    taps = conv_weight.shape[0]
    half = UNITS * heads
    packet = heads * size + 3 * PARTS
    n = lax.axis_size("ctx")

    def swap(x, mask):
        return lax.ppermute(x, "ctx", [(i, i ^ mask) for i in range(n)])

    def shift(x, by):
        return lax.ppermute(x, "ctx", [(i, i + by) for i in range(n - by)])

    gain = norm_gain.reshape(1, width)
    ext = pltpu.VMEM((2 * heads, rows + HALO, size), F32)
    held = pltpu.VMEM((half, rows, size), BF16)

    cum_shape = pltpu.VMEM((SPAN * CHUNKS, 2 * heads, rows), F32)

    def states(mine):
        scratch = [cum_shape, ext, held]
        if not mine:
            buf = pltpu.VMEM((CHIPS, rows, CHUNKS * heads * size), BF16)
            scratch = [
                buf,
                buf,
                pltpu.VMEM((CHIPS, taps, CHUNKS * heads * size), F32),
                pltpu.VMEM((head_count, rows), F32),
                *scratch,
                pltpu.SemaphoreType.DMA((3 * CHIPS + 1,)),
            ]
        return call(
            functools.partial(state_kernel if mine else fetched_state_kernel, mine, heads, size),
            "states_mine" if mine else "states_other",
            pltpu.VMEM((UNITS, packet, size), BF16),
            key_input, value_input, conv_weight, log_decay.T,
            in_specs=[VMEM if mine else HBM] * 4,
            scratch=scratch,
        )

    def intra_part(mine, q):
        return call(
            functools.partial(intra_kernel, mine, heads, size),
            "intra_mine" if mine else "intra_other",
            pltpu.VMEM((half + 1, rows, size), F32),
            q, key_input, value_input, conv_weight, cum,
            scratch=[ext, held],
        )

    theirs = states(False)
    got = swap(theirs, 1)
    mine = states(True)
    got_late = swap(mine, 1)

    chip_states = call(
        functools.partial(chip_kernel, heads, size),
        "chip_states",
        pltpu.VMEM((CHIPS, CHUNKS, packet, size), BF16),
        mine, got,
    )
    order = pltpu.VMEM((CHIPS, packet, size), BF16)

    packets = {0: chip_states[0]}
    for g in EXCHANGE:
        packets[g] = swap(chip_states[g], 2 * g)
    q_after, decay_after, chip_states = lax.optimization_barrier(
        (queries, log_decay, chip_states)
    )
    cum = call(
        functools.partial(cum_kernel, heads),
        "cum",
        cum_shape,
        decay_after.T,
    )
    intra_mine = intra_part(True, q_after)
    *late, intra_mine = lax.optimization_barrier((*[packets[g] for g in EXCHANGE], intra_mine))
    packets.update(zip(EXCHANGE, late))
    packets = [packets[g] for g in range(CHIPS)]

    known = []
    if n > 2 * SPAN:
        edge = call(
            functools.partial(last_edge_kernel, heads, size),
            "last_edge",
            pltpu.VMEM((CHUNKS, PARTS, size), BF16),
            *packets,
            scratch=[order],
        )
        known = [shift(edge, SPAN)]

    def joined(parts):
        span = call(
            functools.partial(span_kernel, parts, heads, size),
            "span_state",
            pltpu.VMEM((len(parts), heads * size + (2 if known else 1) * PARTS, size), BF16),
            *packets, *known,
            scratch=[order],
        )
        before = swap(span, SPAN) if n == 2 * SPAN else shift(span, SPAN)
        reach = 1
        while reach < n // SPAN - 1:
            before = jax.vmap(functools.partial(join_spans, heads=heads, size=size))(
                shift(before, SPAN * reach), before
            )
            reach *= 2
        return span, before

    spans, befores = zip(*[joined(parts) for parts in SHIFTS])
    q_after, _ = lax.optimization_barrier((queries, spans[-1]))
    intra_other = intra_part(False, q_after)
    before, intra_other = lax.optimization_barrier((befores[-1], intra_other))
    befores = [*befores[:-1], before]
    ahead = {
        part: (place, before)
        for parts, before in zip(SHIFTS, befores)
        for place, part in enumerate(parts)
    }

    own, other = {}, {}
    for part in range(CHUNKS):
        chip_prefix = call(
            functools.partial(spread_kernel, part, ahead[part][0], heads, size),
            "chip_prefix",
            pltpu.VMEM((CHIPS, heads * size + PARTS, size), BF16),
            *packets, ahead[part][1], *known,
            scratch=[order],
        )
        first = part * CHIPS
        own[first] = chip_prefix[0]
        for g in EXCHANGE:
            own[first + g] = swap(chip_prefix[g], 2 * g)
        other[first] = swap(own[first], 1)

    def output(items, earlier=None):
        args = [queries, cum, gain]
        for mine, u in items:
            args += [own[u], intra_mine, got] if mine else [other[u], intra_other, got_late]
        done = pltpu.VMEM((len(items), rows, heads * size), BF16)
        scratch = [
            pltpu.VMEM((len(items) * heads, rows, size), F32),
            pltpu.VMEM((len(items) * heads, rows, 2 * PARTS), BF16),
        ]
        kernel = functools.partial(out_kernel, items, heads, size)
        hints = {
            "cost_estimate": pl.CostEstimate(flops=1, transcendentals=0, bytes_accessed=1),
        }
        name = "out_" + "_".join(("m" if mine else "o") + str(u) for mine, u in items)
        if earlier is None:
            return call(kernel, name, done, *args, scratch=scratch, **hints)
        there, made = zip(*earlier)
        return call(
            functools.partial(last_out_kernel, items, there, heads, size),
            name,
            jax.ShapeDtypeStruct((rows, width), BF16),
            *args, *made,
            out_specs=HBM,
            scratch=[*scratch, done, pltpu.SemaphoreType.DMA((2 * UNITS,))],
            **hints,
        )

    items = [(True, 0), (False, 0)]
    made = output(items)
    *late, made = lax.optimization_barrier((*[own[u] for u in EXCHANGE], made))
    earlier = [(items, made)]
    own.update(zip(EXCHANGE, late))
    other.update({u: swap(own[u], 1) for u in EXCHANGE})
    items = [(True, u) for u in EXCHANGE]
    earlier.append((items, output(items)))
    return output([(False, u) for u in EXCHANGE], earlier)


def solution(mesh):
    rows = P(("groups", "ctx"), None)
    return jax.shard_map(
        on_device,
        mesh=mesh,
        in_specs=(rows, rows, rows, rows, P(), P()),
        out_specs=rows,
        check_vma=False,
    )
```

```python
import functools

import jax
import jax.numpy as jnp
from jax import lax
from jax.experimental import pallas as pl
from jax.experimental.pallas import tpu as pltpu
from jax.sharding import PartitionSpec as P

F32 = jnp.float32
BF16 = jnp.bfloat16
CHIPS = 4
SPAN = 2 * CHIPS
HALO = 8
EXCHANGE = (2, 3, 1)
CHUNKS = 1
UNITS = CHUNKS * CHIPS
SHIFTS = ((0,),)
PARTS = 16
VMEM = pl.BlockSpec(memory_space=pltpu.VMEM)
HBM = pl.BlockSpec(memory_space=pltpu.HBM)


def position():
    me = lax.axis_index("ctx")
    return me & 1, (me >> 1) & (CHIPS - 1)


def head_group(mine, unit):
    core, chip = position()
    core = core if mine else 1 - core
    group = core * CHIPS + (chip ^ distance(unit % CHIPS, core))
    return group * CHUNKS + unit // CHIPS


def distance(slot, core):
    turned = ((slot & 1) << 1) | (slot >> 1)
    return slot + core * (turned - slot)


def columns(block, offset, size):
    return pl.ds(pl.multiple_of(block + offset, size), size)


def call(kernel, name, out_shape, *args, scratch=(), in_specs=None, out_specs=VMEM, **options):
    if in_specs is None:
        in_specs = [VMEM] * len(args)
    args = [
        pltpu.with_memory_space_constraint(x, pltpu.VMEM if s is VMEM else pltpu.HBM)
        for x, s in zip(args, in_specs)
    ]
    return pl.pallas_call(
        kernel,
        out_shape=out_shape,
        in_specs=in_specs,
        out_specs=out_specs,
        scratch_shapes=list(scratch),
        name=name,
        compiler_params=pltpu.CompilerParams(vmem_limit_bytes=6 << 20),
        **options,
    )(*args)


def cum_kernel(heads, decay_ref, out_ref):
    x = decay_ref[...]
    count, rows = x.shape
    upto = lax.broadcasted_iota(jnp.int32, (rows, rows), 0) <= lax.broadcasted_iota(
        jnp.int32, (rows, rows), 1
    )
    parts = jnp.concatenate([p.astype(F32) for p in three_parts(x)], 0).astype(BF16)
    sums = jnp.dot(parts, upto.astype(F32).astype(BF16), preferred_element_type=F32)
    sums = sums[0:count] + (sums[count : 2 * count] + sums[2 * count :])
    total = jnp.broadcast_to(sums[:, rows - 1 : rows], sums.shape)
    for b in range(out_ref.shape[0]):
        these = slice(b * heads, (b + 1) * heads)
        out_ref[b, 0:heads, :] = sums[these]
        out_ref[b, heads : 2 * heads, :] = total[these]


def three_parts(x):
    hi = x.astype(BF16)
    rest = x - hi.astype(F32)
    mid = rest.astype(BF16)
    low = (rest - mid.astype(F32)).astype(BF16)
    return hi, mid, low


def side(part, heads, size):
    base = heads * size + part * PARTS
    return slice(base, base + PARTS)


def padded(rows):
    rows = jnp.concatenate(rows, 0)
    spare = jnp.zeros((PARTS - rows.shape[0], rows.shape[1]), F32)
    return jnp.concatenate([rows, spare], 0).astype(BF16)


def put_decay(out, decays, heads, size):
    out[side(1, heads, size), :] = padded([p.astype(F32) for p in three_parts(decays)])


def get_decay(packet, heads, size):
    tail = packet[side(1, heads, size), :].astype(F32)
    return tail[0:heads] + tail[heads : 2 * heads] + tail[2 * heads : 3 * heads]


def edge_states(values, edges, heads):
    row = lax.broadcasted_iota(jnp.int32, values.shape, 0)
    out = []
    for j in range(heads):
        picked = jnp.where(lax.rem(row, heads) == j, values.astype(F32), 0.0).astype(BF16)
        out.append(
            lax.dot_general(picked, edges, (((0,), (0,)), ((), ())), preferred_element_type=F32)
        )
    return out


def conv_keys(k_ref, halo, w_ref, ext, cols):
    rows = k_ref.shape[0]
    ext[0:HALO, :] = halo
    ext[HALO : HALO + rows, :] = k_ref[:, cols].astype(F32)
    total = None
    for j in range(w_ref.shape[0]):
        term = w_ref[j : j + 1, cols] * ext[HALO - j : HALO - j + rows, :]
        total = term if total is None else total + term
    return total.astype(BF16)


def fetched_state_kernel(
    mine, heads, size, k_hbm, v_hbm, w_hbm, decay_hbm, out_ref,
    k_buf, v_buf, w_buf, decay_buf, cum_ref, ext, held, sems,
):
    wide = CHUNKS * heads * size
    copies = [pltpu.make_async_copy(decay_hbm, decay_buf, sems.at[3 * CHIPS])]
    copies[0].start()
    for g in range(CHIPS):
        cols = columns(head_group(mine, g) * heads * size, 0, wide)
        for i, (source, buf) in enumerate(((k_hbm, k_buf), (w_hbm, w_buf), (v_hbm, v_buf))):
            copies.append(
                pltpu.make_async_copy(source.at[:, cols], buf.at[g], sems.at[3 * g + i])
            )
            copies[-1].start()
    copies[0].wait()
    groups, waits = [], []
    for u in range(UNITS):
        g, part = u % CHIPS, u // CHIPS
        cols = slice(part * heads * size, (part + 1) * heads * size)
        groups.append(tuple(buf.at[g, :, cols] for buf in (k_buf, v_buf, w_buf)))
        waits.append(copies[1 + 3 * g : 4 + 3 * g] if part == 0 else [])
    states_of(mine, heads, size, groups, waits, decay_buf, out_ref, cum_ref, ext, held)


def state_kernel(
    mine, heads, size, k_ref, v_ref, w_ref, decay_ref, out_ref, cum_ref, ext, held
):
    groups = []
    for u in range(UNITS):
        cols = columns(head_group(mine, u) * heads * size, 0, heads * size)
        groups.append((k_ref.at[:, cols], v_ref.at[:, cols], w_ref.at[:, cols]))
    waits = [[]] * UNITS
    states_of(mine, heads, size, groups, waits, decay_ref, out_ref, cum_ref, ext, held)


def states_of(mine, heads, size, groups, waits, decay_ref, out_ref, cum_ref, ext, held):
    rows = groups[0][0].shape[0]
    taps = groups[0][2].shape[0]
    cum_kernel(heads, decay_ref, cum_ref)
    none = jnp.zeros((HALO, size), F32)
    for g in range(UNITS):
        k_ref, v_ref, w_ref = groups[g]
        for copy in waits[g]:
            copy.wait()
        cum = cum_ref[head_group(mine, g)]
        ending = jnp.exp(cum[heads : 2 * heads] - cum[0:heads]).T
        edges, values = [], []
        for j in range(heads):
            cols = slice(j * size, (j + 1) * size)
            key_conv = conv_keys(k_ref, none, w_ref, ext.at[g % 2 * heads + j], cols)
            held[g * heads + j] = (key_conv.astype(F32) * ending[:, j : j + 1]).astype(BF16)
            last = k_ref[rows - HALO : rows, cols].astype(F32)
            head_edges = []
            for t in range(taps - 1):
                terms = [
                    w_ref[i : i + 1, cols] * last[HALO + t - i : HALO + t - i + 1]
                    for i in range(t + 1, taps)
                ]
                head_edges.append(sum(terms[1:], terms[0]))
            edges.append(head_edges)
            values.append(v_ref[0:HALO, cols].astype(F32) * ending[0:HALO, j : j + 1])
        put_decay(out_ref.at[g], jnp.exp(cum[heads : 2 * heads]), heads, size)
        out_ref[g, side(0, heads, size), :] = padded(
            [edges[j][t] for t in range(taps - 1) for j in range(heads)]
        )
        out_ref[g, side(2, heads, size), :] = padded(
            [values[j][t : t + 1] for t in range(taps - 1) for j in range(heads)]
        )
    for g in range(UNITS):
        for j in range(heads):
            cols = slice(j * size, (j + 1) * size)
            state = lax.dot_general(
                groups[g][1][:, cols], held[g * heads + j], (((0,), (0,)), ((), ())),
                preferred_element_type=F32,
            )
            out_ref[g, cols, :] = state.astype(BF16)


def intra_kernel(mine, heads, size, q_ref, k_ref, v_ref, w_ref, cum_ref, out_ref, ext, held):
    rows = q_ref.shape[0]
    causal = lax.broadcasted_iota(jnp.int32, (rows, rows), 0) >= lax.broadcasted_iota(
        jnp.int32, (rows, rows), 1
    )
    none = jnp.zeros((HALO, size), F32)
    for g in range(UNITS):
        b = head_group(mine, g)
        cum = cum_ref[b][0:heads]
        cum_col = cum.T
        growth = jnp.exp(-cum_col[0:HALO])
        values = []
        for j in range(heads):
            cols = columns(b * heads * size, j * size, size)
            key_conv = conv_keys(k_ref, none, w_ref, ext.at[g % 2 * heads + j], cols)
            scores = lax.dot_general(
                q_ref[:, cols], key_conv, (((1,), (1,)), ((), ())), preferred_element_type=F32
            )
            spread = cum_col[:, j : j + 1] - cum[j : j + 1]
            weights = jnp.where(causal, scores * jnp.exp(jnp.where(causal, spread, 0.0)), 0.0)
            held[g * heads + j] = weights.astype(BF16)
            values.append(v_ref[0:HALO, cols].astype(F32) * growth[:, j : j + 1])
        out_ref[UNITS * heads, g * PARTS : (g + 1) * PARTS, :] = padded(
            [values[j][t : t + 1] for t in range(3) for j in range(heads)]
        ).astype(F32)
    for g in range(UNITS):
        b = head_group(mine, g)
        for j in range(heads):
            cols = columns(b * heads * size, j * size, size)
            out_ref[g * heads + j] = jnp.dot(
                held[g * heads + j], v_ref[:, cols], preferred_element_type=F32
            )


def chip_kernel(heads, size, own_ref, got_ref, out_ref):
    core, _ = position()
    first = core == 0
    for g in range(UNITS):
        to = out_ref.at[g % CHIPS, g // CHIPS]
        own_decay = get_decay(own_ref.at[g], heads, size)
        got_decay = get_decay(got_ref.at[g], heads, size)
        own_by = jnp.where(first, got_decay, 1.0)
        got_by = jnp.where(first, 1.0, own_decay)

        def earlier_later(part):
            own = own_ref[g, side(part, heads, size), :].astype(F32)
            got = got_ref[g, side(part, heads, size), :].astype(F32)
            return jnp.where(first, own, got), jnp.where(first, got, own)

        edges, out_edges = earlier_later(0)
        out_values, values = earlier_later(2)
        fixes = edge_states(values.astype(BF16), edges.astype(BF16), heads)
        for j in range(heads):
            rows = slice(j * size, (j + 1) * size)
            to[rows, :] = (
                own_ref[g, rows, :].astype(F32) * own_by[j : j + 1]
                + got_ref[g, rows, :].astype(F32) * got_by[j : j + 1]
                + fixes[j]
            ).astype(BF16)
        put_decay(to, own_decay * got_decay, heads, size)
        later_by = jnp.where(first, got_decay, own_decay)
        to[side(0, heads, size), :] = out_edges.astype(BF16)
        to[side(2, heads, size), :] = padded(
            [out_values[t * heads : (t + 1) * heads] * later_by for t in range(3)]
        )


def in_order(packets, part, held):
    core, chip = position()
    for g in range(CHIPS):
        held[chip ^ distance(g, core)] = packets[g][part]


def chip_fixes(held, b, edges, heads, size):
    return edge_states(held[b, side(2, heads, size), :], edges, heads)


def last_edge_kernel(heads, size, *refs):
    packets, out_ref, held = refs[:CHIPS], refs[CHIPS], refs[CHIPS + 1]
    for part in range(CHUNKS):
        in_order(packets, part, held)
        out_ref[part] = held[CHIPS - 1, side(0, heads, size), :]


def span_kernel(parts, heads, size, *refs):
    packets, before, (whole_ref, held) = refs[:CHIPS], refs[CHIPS:-2], refs[-2:]
    for i, part in enumerate(parts):
        known = [before[0][part]] if before else []
        span_of(part, known, heads, size, packets, whole_ref.at[i], held)


def span_of(part, before, heads, size, packets, out_ref, held):
    in_order(packets, part, held)
    decays = [get_decay(held.at[b], heads, size) for b in range(CHIPS)]
    fixes = [
        chip_fixes(held, b, held[b - 1, side(0, heads, size), :], heads, size)
        for b in range(1, CHIPS)
    ]
    fixes.insert(0, chip_fixes(held, 0, before[0], heads, size) if before else None)
    for j in range(heads):
        rows = slice(j * size, (j + 1) * size)
        acc = held[0, rows, :].astype(F32)
        if before:
            acc = acc + fixes[0][j]
        for b in range(1, CHIPS):
            acc = acc * decays[b][j : j + 1] + (held[b, rows, :].astype(F32) + fixes[b][j])
        out_ref[rows, :] = acc.astype(BF16)
    whole = decays[0]
    for b in range(1, CHIPS):
        whole = whole * decays[b]
    out_ref[side(0, heads, size), :] = held[CHIPS - 1, side(0, heads, size), :]
    if before:
        put_decay(out_ref, whole, heads, size)


def spread_kernel(part, place, heads, size, *refs):
    packets, before, known, (out_ref, held) = refs[:CHIPS], refs[CHIPS], refs[CHIPS + 1 : -2], refs[-2:]
    core, chip = position()
    slots = [distance(chip ^ b, core) for b in range(CHIPS)]
    later = lax.axis_index("ctx") >= SPAN
    in_order(packets, part, held)
    decays = [get_decay(held.at[b], heads, size) for b in range(CHIPS)]
    edges = known[0][part] if known else before[place, side(0, heads, size), :]
    edges = [jnp.where(later, edges.astype(F32), 0.0).astype(BF16)]
    edges += [held[b, side(0, heads, size), :] for b in range(CHIPS - 1)]
    fixes = [chip_fixes(held, b, edges[b], heads, size) for b in range(CHIPS - 1)]
    for j in range(heads):
        rows = slice(j * size, (j + 1) * size)
        acc = jnp.where(later, before[place, rows, :].astype(F32), 0.0)
        out_ref[slots[0], rows, :] = acc.astype(BF16)
        for b in range(1, CHIPS):
            acc = acc * decays[b - 1][j : j + 1] + (
                held[b - 1, rows, :].astype(F32) + fixes[b - 1][j]
            )
            out_ref[slots[b], rows, :] = acc.astype(BF16)
    for b in range(CHIPS):
        out_ref[slots[b], heads * size : heads * size + PARTS, :] = edges[b]


def last_out_kernel(items, earlier, heads, size, *refs):
    count = 3 + 3 * len(items)
    made = refs[count : count + len(earlier)]
    out_ref, inter_ref, score_ref, done_ref, sems = refs[-5:]
    copies = []

    def write(item, source):
        cols = columns(head_group(*item) * heads * size, 0, heads * size)
        copies.append(
            pltpu.make_async_copy(source, out_ref.at[:, cols], sems.at[len(copies)])
        )
        copies[-1].start()

    for there, ref in zip(earlier, made):
        for i, item in enumerate(there):
            write(item, ref.at[i])
    out_kernel(items, heads, size, *refs[:count], done_ref, inter_ref, score_ref, write=write)
    for copy in copies:
        copy.wait()


def out_kernel(items, heads, size, *refs, write=None):
    q_ref, cum_ref, gain_ref = refs[:3]
    per_item = [refs[3 + 3 * i : 6 + 3 * i] for i in range(len(items))]
    done_ref, inter_ref, score_ref = refs[-3:]
    rows = q_ref.shape[0]
    core, _ = position()
    second = core == 1
    row = lax.broadcasted_iota(jnp.int32, (rows, 2 * PARTS), 0)
    column = lax.broadcasted_iota(jnp.int32, (rows, 2 * PARTS), 1)
    edge = lax.rem(column, PARTS)
    causal = (lax.div(edge, heads) <= row) & (edge < 3 * heads)
    ahead = column < PARTS
    kept = ((ahead & (core == 1)) | causal) & (ahead | (core == 1))
    kept = [kept & (lax.rem(edge, heads) == j) for j in range(heads)]
    for i, (mine, g) in enumerate(items):
        prefix_ref, intra_ref, sib_ref = per_item[i]
        b = head_group(mine, g)
        started = jnp.exp(cum_ref[b][0:heads]).T
        by = jnp.where(second, get_decay(sib_ref.at[g], heads, size), 1.0)
        edges = jnp.concatenate(
            [
                prefix_ref[heads * size : heads * size + PARTS, :].astype(F32),
                sib_ref[g, side(0, heads, size), :].astype(F32),
            ],
            0,
        ).astype(BF16)
        for j in range(heads):
            cols = columns(b * heads * size, j * size, size)
            these = slice(j * size, (j + 1) * size)
            sib = jnp.where(second, sib_ref[g, these, :].astype(F32), 0.0)
            prefix = (prefix_ref[these, :].astype(F32) * by[j : j + 1] + sib).astype(BF16)
            both = lax.dot_general(
                q_ref[:, cols],
                jnp.concatenate([prefix, edges], 0),
                (((1,), (1,)), ((), ())),
                preferred_element_type=F32,
            )
            both = both * started[:, j : j + 1]
            inter_ref[i * heads + j] = both[:, 0:size] + intra_ref[g * heads + j]
            score_ref[i * heads + j] = jnp.where(kept[j], both[:, size:], 0.0).astype(BF16)
    for i, (mine, g) in enumerate(items):
        _, intra_ref, sib_ref = per_item[i]
        b = head_group(mine, g)
        values = intra_ref[UNITS * heads, g * PARTS : (g + 1) * PARTS, :]
        ahead_values = jnp.where(second, sib_ref[g, side(2, heads, size), :].astype(F32), values)
        values = jnp.concatenate([ahead_values, values], 0).astype(BF16)
        for j in range(heads):
            inter_ref[i * heads + j] += jnp.dot(
                score_ref[i * heads + j], values, preferred_element_type=F32
            )
    for i, (mine, g) in enumerate(items):
        b = head_group(mine, g)
        for j in range(heads):
            cols = columns(b * heads * size, j * size, size)
            mixed = inter_ref[i * heads + j]
            scale = lax.rsqrt(jnp.mean(mixed * mixed, axis=1, keepdims=True) + 1e-05)
            done_ref[i, :, j * size : (j + 1) * size] = (
                mixed * scale * gain_ref[:, cols]
            ).astype(BF16)
        if write is not None:
            write((mine, g), done_ref.at[i])


def join_spans(earlier, later, heads, size):
    base = heads * size
    own = side(1, heads, size)

    def decay(x):
        tail = x[own].astype(F32)
        return tail[0:heads] + tail[heads : 2 * heads] + tail[2 * heads : 3 * heads]

    by = decay(later)
    state = (
        by[:, None, :] * earlier[:base].astype(F32).reshape(heads, size, -1)
        + later[:base].astype(F32).reshape(heads, size, -1)
    ).reshape(base, -1)
    parts = three_parts(by * decay(earlier))
    return jnp.concatenate([state.astype(BF16), later[base : own.start], *parts, later[own.start + 3 * heads :]], 0)


def on_device(queries, key_input, value_input, log_decay, conv_weight, norm_gain):
    rows, width = queries.shape
    head_count = log_decay.shape[1]
    size = width // head_count
    heads = head_count // (SPAN * CHUNKS)
    taps = conv_weight.shape[0]
    half = UNITS * heads
    packet = heads * size + 3 * PARTS
    n = lax.axis_size("ctx")

    def swap(x, mask):
        return lax.ppermute(x, "ctx", [(i, i ^ mask) for i in range(n)])

    def exchange(x, slot):
        return lax.ppermute(x, "ctx", [(i, i ^ (2 * distance(slot, i & 1))) for i in range(n)])

    def shift(x, by):
        return lax.ppermute(x, "ctx", [(i, i + by) for i in range(n - by)])

    gain = norm_gain.reshape(1, width)
    ext = pltpu.VMEM((2 * heads, rows + HALO, size), F32)
    held = pltpu.VMEM((half, rows, size), BF16)

    cum_shape = pltpu.VMEM((SPAN * CHUNKS, 2 * heads, rows), F32)

    def states(mine):
        scratch = [cum_shape, ext, held]
        if not mine:
            buf = pltpu.VMEM((CHIPS, rows, CHUNKS * heads * size), BF16)
            scratch = [
                buf,
                buf,
                pltpu.VMEM((CHIPS, taps, CHUNKS * heads * size), F32),
                pltpu.VMEM((head_count, rows), F32),
                *scratch,
                pltpu.SemaphoreType.DMA((3 * CHIPS + 1,)),
            ]
        return call(
            functools.partial(state_kernel if mine else fetched_state_kernel, mine, heads, size),
            "states_mine" if mine else "states_other",
            pltpu.VMEM((UNITS, packet, size), BF16),
            key_input, value_input, conv_weight, log_decay.T,
            in_specs=[VMEM if mine else HBM] * 4,
            scratch=scratch,
        )

    def intra_part(mine, q):
        return call(
            functools.partial(intra_kernel, mine, heads, size),
            "intra_mine" if mine else "intra_other",
            pltpu.VMEM((half + 1, rows, size), F32),
            q, key_input, value_input, conv_weight, cum,
            scratch=[ext, held],
        )

    theirs = states(False)
    got = swap(theirs, 1)
    mine = states(True)
    got_late = swap(mine, 1)

    chip_states = call(
        functools.partial(chip_kernel, heads, size),
        "chip_states",
        pltpu.VMEM((CHIPS, CHUNKS, packet, size), BF16),
        mine, got,
    )
    order = pltpu.VMEM((CHIPS, packet, size), BF16)

    packets = {0: chip_states[0]}
    for g in EXCHANGE:
        packets[g] = exchange(chip_states[g], g)
    q_after, decay_after, chip_states = lax.optimization_barrier(
        (queries, log_decay, chip_states)
    )
    cum = call(
        functools.partial(cum_kernel, heads),
        "cum",
        cum_shape,
        decay_after.T,
    )
    intra_mine = intra_part(True, q_after)
    *late, intra_mine = lax.optimization_barrier((*[packets[g] for g in EXCHANGE], intra_mine))
    packets.update(zip(EXCHANGE, late))
    packets = [packets[g] for g in range(CHIPS)]

    known = []
    if n > 2 * SPAN:
        edge = call(
            functools.partial(last_edge_kernel, heads, size),
            "last_edge",
            pltpu.VMEM((CHUNKS, PARTS, size), BF16),
            *packets,
            scratch=[order],
        )
        known = [shift(edge, SPAN)]

    def joined(parts):
        span = call(
            functools.partial(span_kernel, parts, heads, size),
            "span_state",
            pltpu.VMEM((len(parts), heads * size + (2 if known else 1) * PARTS, size), BF16),
            *packets, *known,
            scratch=[order],
        )
        before = swap(span, SPAN) if n == 2 * SPAN else shift(span, SPAN)
        reach = 1
        while reach < n // SPAN - 1:
            before = jax.vmap(functools.partial(join_spans, heads=heads, size=size))(
                shift(before, SPAN * reach), before
            )
            reach *= 2
        return span, before

    spans, befores = zip(*[joined(parts) for parts in SHIFTS])
    q_after, _ = lax.optimization_barrier((queries, spans[-1]))
    intra_other = intra_part(False, q_after)
    before, intra_other = lax.optimization_barrier((befores[-1], intra_other))
    befores = [*befores[:-1], before]
    ahead = {
        part: (place, before)
        for parts, before in zip(SHIFTS, befores)
        for place, part in enumerate(parts)
    }

    own, other = {}, {}
    for part in range(CHUNKS):
        chip_prefix = call(
            functools.partial(spread_kernel, part, ahead[part][0], heads, size),
            "chip_prefix",
            pltpu.VMEM((CHIPS, heads * size + PARTS, size), BF16),
            *packets, ahead[part][1], *known,
            scratch=[order],
        )
        first = part * CHIPS
        own[first] = chip_prefix[0]
        for g in EXCHANGE:
            own[first + g] = exchange(chip_prefix[g], g)
        other[first] = swap(own[first], 1)

    def output(items, earlier=None):
        args = [queries, cum, gain]
        for mine, u in items:
            args += [own[u], intra_mine, got] if mine else [other[u], intra_other, got_late]
        done = pltpu.VMEM((len(items), rows, heads * size), BF16)
        scratch = [
            pltpu.VMEM((len(items) * heads, rows, size), F32),
            pltpu.VMEM((len(items) * heads, rows, 2 * PARTS), BF16),
        ]
        kernel = functools.partial(out_kernel, items, heads, size)
        hints = {
            "cost_estimate": pl.CostEstimate(flops=1, transcendentals=0, bytes_accessed=1),
        }
        name = "out_" + "_".join(("m" if mine else "o") + str(u) for mine, u in items)
        if earlier is None:
            return call(kernel, name, done, *args, scratch=scratch, **hints)
        there, made = zip(*earlier)
        return call(
            functools.partial(last_out_kernel, items, there, heads, size),
            name,
            jax.ShapeDtypeStruct((rows, width), BF16),
            *args, *made,
            out_specs=HBM,
            scratch=[*scratch, done, pltpu.SemaphoreType.DMA((2 * UNITS,))],
            **hints,
        )

    final, *early = EXCHANGE
    items = [(True, 0), (False, 0)]
    made = output(items)
    *late, made = lax.optimization_barrier((*[own[u] for u in early], made))
    earlier = [(items, made)]
    own.update(zip(early, late))
    other.update({u: swap(own[u], 1) for u in early})
    items = [(True, u) for u in early]
    made = output(items)
    own[final], made = lax.optimization_barrier((own[final], made))
    earlier.append((items, made))
    other[final] = swap(own[final], 1)
    items = [(True, final)] + [(False, u) for u in early]
    earlier.append((items, output(items)))
    return output([(False, final)], earlier)


def solution(mesh):
    rows = P(("groups", "ctx"), None)
    return jax.shard_map(
        on_device,
        mesh=mesh,
        in_specs=(rows, rows, rows, rows, P(), P()),
        out_specs=rows,
        check_vma=False,
    )
```

```python
import functools

import jax
import jax.numpy as jnp
from jax import lax
from jax.experimental import pallas as pl
from jax.experimental.pallas import tpu as pltpu
from jax.sharding import PartitionSpec as P

F32 = jnp.float32
BF16 = jnp.bfloat16
CHIPS = 4
SPAN = 2 * CHIPS
HALO = 8
EXCHANGE = (2, 3, 1)
CHUNKS = 1
UNITS = CHUNKS * CHIPS
SHIFTS = ((0,),)
PARTS = 16
VMEM = pl.BlockSpec(memory_space=pltpu.VMEM)
HBM = pl.BlockSpec(memory_space=pltpu.HBM)


def position():
    me = lax.axis_index("ctx")
    return me & 1, (me >> 1) & (CHIPS - 1)


def head_group(mine, unit):
    core, chip = position()
    core = core if mine else 1 - core
    group = core * CHIPS + (chip ^ distance(unit % CHIPS, core))
    return group * CHUNKS + unit // CHIPS


def distance(slot, core):
    turned = ((slot & 1) << 1) | (slot >> 1)
    return slot + core * (turned - slot)


def columns(block, offset, size):
    return pl.ds(pl.multiple_of(block + offset, size), size)


def call(kernel, name, out_shape, *args, scratch=(), in_specs=None, out_specs=VMEM, **options):
    if in_specs is None:
        in_specs = [VMEM] * len(args)
    args = [
        pltpu.with_memory_space_constraint(x, pltpu.VMEM if s is VMEM else pltpu.HBM)
        for x, s in zip(args, in_specs)
    ]
    return pl.pallas_call(
        kernel,
        out_shape=out_shape,
        in_specs=in_specs,
        out_specs=out_specs,
        scratch_shapes=list(scratch),
        name=name,
        compiler_params=pltpu.CompilerParams(vmem_limit_bytes=6 << 20),
        **options,
    )(*args)


def cum_kernel(heads, decay_ref, out_ref):
    x = decay_ref[...]
    count, rows = x.shape
    upto = lax.broadcasted_iota(jnp.int32, (rows, rows), 0) <= lax.broadcasted_iota(
        jnp.int32, (rows, rows), 1
    )
    parts = jnp.concatenate([p.astype(F32) for p in three_parts(x)], 0).astype(BF16)
    sums = jnp.dot(parts, upto.astype(F32).astype(BF16), preferred_element_type=F32)
    sums = sums[0:count] + (sums[count : 2 * count] + sums[2 * count :])
    total = jnp.broadcast_to(sums[:, rows - 1 : rows], sums.shape)
    for b in range(out_ref.shape[0]):
        these = slice(b * heads, (b + 1) * heads)
        out_ref[b, 0:heads, :] = sums[these]
        out_ref[b, heads : 2 * heads, :] = total[these]


def three_parts(x):
    hi = x.astype(BF16)
    rest = x - hi.astype(F32)
    mid = rest.astype(BF16)
    low = (rest - mid.astype(F32)).astype(BF16)
    return hi, mid, low


def side(part, heads, size):
    base = heads * size + part * PARTS
    return slice(base, base + PARTS)


def padded(rows):
    rows = jnp.concatenate(rows, 0)
    spare = jnp.zeros((PARTS - rows.shape[0], rows.shape[1]), F32)
    return jnp.concatenate([rows, spare], 0).astype(BF16)


def put_decay(out, decays, heads, size):
    out[side(1, heads, size), :] = padded([p.astype(F32) for p in three_parts(decays)])


def get_decay(packet, heads, size):
    tail = packet[side(1, heads, size), :].astype(F32)
    return tail[0:heads] + tail[heads : 2 * heads] + tail[2 * heads : 3 * heads]


def edge_states(values, edges, heads):
    row = lax.broadcasted_iota(jnp.int32, values.shape, 0)
    out = []
    for j in range(heads):
        picked = jnp.where(lax.rem(row, heads) == j, values.astype(F32), 0.0).astype(BF16)
        out.append(
            lax.dot_general(picked, edges, (((0,), (0,)), ((), ())), preferred_element_type=F32)
        )
    return out


def conv_keys(k_ref, halo, w_ref, ext, cols):
    rows = k_ref.shape[0]
    ext[0:HALO, :] = halo
    ext[HALO : HALO + rows, :] = k_ref[:, cols].astype(F32)
    total = None
    for j in range(w_ref.shape[0]):
        term = w_ref[j : j + 1, cols] * ext[HALO - j : HALO - j + rows, :]
        total = term if total is None else total + term
    return total.astype(BF16)


def fetched_state_kernel(
    mine, heads, size, k_hbm, v_hbm, w_hbm, decay_hbm, out_ref,
    k_buf, v_buf, w_buf, decay_buf, cum_ref, ext, held, sems,
):
    wide = CHUNKS * heads * size
    copies = [pltpu.make_async_copy(decay_hbm, decay_buf, sems.at[3 * CHIPS])]
    copies[0].start()
    for g in range(CHIPS):
        cols = columns(head_group(mine, g) * heads * size, 0, wide)
        for i, (source, buf) in enumerate(((k_hbm, k_buf), (w_hbm, w_buf), (v_hbm, v_buf))):
            copies.append(
                pltpu.make_async_copy(source.at[:, cols], buf.at[g], sems.at[3 * g + i])
            )
            copies[-1].start()
    copies[0].wait()
    groups, waits = [], []
    for u in range(UNITS):
        g, part = u % CHIPS, u // CHIPS
        cols = slice(part * heads * size, (part + 1) * heads * size)
        groups.append(tuple(buf.at[g, :, cols] for buf in (k_buf, v_buf, w_buf)))
        waits.append(copies[1 + 3 * g : 4 + 3 * g] if part == 0 else [])
    states_of(mine, heads, size, groups, waits, decay_buf, out_ref, cum_ref, ext, held)


def state_kernel(
    mine, heads, size, k_ref, v_ref, w_ref, decay_ref, out_ref, cum_ref, ext, held
):
    groups = []
    for u in range(UNITS):
        cols = columns(head_group(mine, u) * heads * size, 0, heads * size)
        groups.append((k_ref.at[:, cols], v_ref.at[:, cols], w_ref.at[:, cols]))
    waits = [[]] * UNITS
    states_of(mine, heads, size, groups, waits, decay_ref, out_ref, cum_ref, ext, held)


def states_of(mine, heads, size, groups, waits, decay_ref, out_ref, cum_ref, ext, held):
    rows = groups[0][0].shape[0]
    taps = groups[0][2].shape[0]
    cum_kernel(heads, decay_ref, cum_ref)
    none = jnp.zeros((HALO, size), F32)
    for g in range(UNITS):
        k_ref, v_ref, w_ref = groups[g]
        for copy in waits[g]:
            copy.wait()
        cum = cum_ref[head_group(mine, g)]
        ending = jnp.exp(cum[heads : 2 * heads] - cum[0:heads]).T
        edges, values = [], []
        for j in range(heads):
            cols = slice(j * size, (j + 1) * size)
            key_conv = conv_keys(k_ref, none, w_ref, ext.at[g % 2 * heads + j], cols)
            held[g * heads + j] = (key_conv.astype(F32) * ending[:, j : j + 1]).astype(BF16)
            last = k_ref[rows - HALO : rows, cols].astype(F32)
            head_edges = []
            for t in range(taps - 1):
                terms = [
                    w_ref[i : i + 1, cols] * last[HALO + t - i : HALO + t - i + 1]
                    for i in range(t + 1, taps)
                ]
                head_edges.append(sum(terms[1:], terms[0]))
            edges.append(head_edges)
            values.append(v_ref[0:HALO, cols].astype(F32) * ending[0:HALO, j : j + 1])
        put_decay(out_ref.at[g], jnp.exp(cum[heads : 2 * heads]), heads, size)
        out_ref[g, side(0, heads, size), :] = padded(
            [edges[j][t] for t in range(taps - 1) for j in range(heads)]
        )
        out_ref[g, side(2, heads, size), :] = padded(
            [values[j][t : t + 1] for t in range(taps - 1) for j in range(heads)]
        )
    for g in range(UNITS):
        for j in range(heads):
            cols = slice(j * size, (j + 1) * size)
            state = lax.dot_general(
                groups[g][1][:, cols], held[g * heads + j], (((0,), (0,)), ((), ())),
                preferred_element_type=F32,
            )
            out_ref[g, cols, :] = state.astype(BF16)


def intra_kernel(mine, heads, size, q_ref, k_ref, v_ref, w_ref, cum_ref, out_ref, ext, held):
    rows = q_ref.shape[0]
    causal = lax.broadcasted_iota(jnp.int32, (rows, rows), 0) >= lax.broadcasted_iota(
        jnp.int32, (rows, rows), 1
    )
    none = jnp.zeros((HALO, size), F32)
    for g in range(UNITS):
        b = head_group(mine, g)
        cum = cum_ref[b][0:heads]
        cum_col = cum.T
        growth = jnp.exp(-cum_col[0:HALO])
        values = []
        for j in range(heads):
            cols = columns(b * heads * size, j * size, size)
            key_conv = conv_keys(k_ref, none, w_ref, ext.at[g % 2 * heads + j], cols)
            scores = lax.dot_general(
                q_ref[:, cols], key_conv, (((1,), (1,)), ((), ())), preferred_element_type=F32
            )
            spread = cum_col[:, j : j + 1] - cum[j : j + 1]
            weights = jnp.where(causal, scores * jnp.exp(jnp.where(causal, spread, 0.0)), 0.0)
            held[g * heads + j] = weights.astype(BF16)
            values.append(v_ref[0:HALO, cols].astype(F32) * growth[:, j : j + 1])
        out_ref[UNITS * heads, g * PARTS : (g + 1) * PARTS, :] = padded(
            [values[j][t : t + 1] for t in range(3) for j in range(heads)]
        ).astype(F32)
    for g in range(UNITS):
        b = head_group(mine, g)
        for j in range(heads):
            cols = columns(b * heads * size, j * size, size)
            out_ref[g * heads + j] = jnp.dot(
                held[g * heads + j], v_ref[:, cols], preferred_element_type=F32
            )


def chip_kernel(heads, size, own_ref, got_ref, out_ref):
    core, _ = position()
    first = core == 0
    for g in range(UNITS):
        to = out_ref.at[g % CHIPS, g // CHIPS]
        own_decay = get_decay(own_ref.at[g], heads, size)
        got_decay = get_decay(got_ref.at[g], heads, size)
        own_by = jnp.where(first, got_decay, 1.0)
        got_by = jnp.where(first, 1.0, own_decay)

        def earlier_later(part):
            own = own_ref[g, side(part, heads, size), :].astype(F32)
            got = got_ref[g, side(part, heads, size), :].astype(F32)
            return jnp.where(first, own, got), jnp.where(first, got, own)

        edges, out_edges = earlier_later(0)
        out_values, values = earlier_later(2)
        fixes = edge_states(values.astype(BF16), edges.astype(BF16), heads)
        for j in range(heads):
            rows = slice(j * size, (j + 1) * size)
            to[rows, :] = (
                own_ref[g, rows, :].astype(F32) * own_by[j : j + 1]
                + got_ref[g, rows, :].astype(F32) * got_by[j : j + 1]
                + fixes[j]
            ).astype(BF16)
        put_decay(to, own_decay * got_decay, heads, size)
        later_by = jnp.where(first, got_decay, own_decay)
        to[side(0, heads, size), :] = out_edges.astype(BF16)
        to[side(2, heads, size), :] = padded(
            [out_values[t * heads : (t + 1) * heads] * later_by for t in range(3)]
        )


def in_order(packets, part, held):
    core, chip = position()
    for g in range(CHIPS):
        held[chip ^ distance(g, core)] = packets[g][part]


def chip_fixes(held, b, edges, heads, size):
    return edge_states(held[b, side(2, heads, size), :], edges, heads)


def last_edge_kernel(heads, size, *refs):
    packets, out_ref, held = refs[:CHIPS], refs[CHIPS], refs[CHIPS + 1]
    for part in range(CHUNKS):
        in_order(packets, part, held)
        out_ref[part] = held[CHIPS - 1, side(0, heads, size), :]


def span_kernel(parts, heads, size, *refs):
    packets, before, (whole_ref, held) = refs[:CHIPS], refs[CHIPS:-2], refs[-2:]
    for i, part in enumerate(parts):
        known = [before[0][part]] if before else []
        span_of(part, known, heads, size, packets, whole_ref.at[i], held)


def span_of(part, before, heads, size, packets, out_ref, held):
    in_order(packets, part, held)
    decays = [get_decay(held.at[b], heads, size) for b in range(CHIPS)]
    fixes = [
        chip_fixes(held, b, held[b - 1, side(0, heads, size), :], heads, size)
        for b in range(1, CHIPS)
    ]
    fixes.insert(0, chip_fixes(held, 0, before[0], heads, size) if before else None)
    for j in range(heads):
        rows = slice(j * size, (j + 1) * size)
        acc = held[0, rows, :].astype(F32)
        if before:
            acc = acc + fixes[0][j]
        for b in range(1, CHIPS):
            acc = acc * decays[b][j : j + 1] + (held[b, rows, :].astype(F32) + fixes[b][j])
        out_ref[rows, :] = acc.astype(BF16)
    whole = decays[0]
    for b in range(1, CHIPS):
        whole = whole * decays[b]
    out_ref[side(0, heads, size), :] = held[CHIPS - 1, side(0, heads, size), :]
    if before:
        put_decay(out_ref, whole, heads, size)


def spread_kernel(part, place, heads, size, *refs):
    packets, before, known, (out_ref, held) = refs[:CHIPS], refs[CHIPS], refs[CHIPS + 1 : -2], refs[-2:]
    core, chip = position()
    slots = [distance(chip ^ b, core) for b in range(CHIPS)]
    later = lax.axis_index("ctx") >= SPAN
    in_order(packets, part, held)
    decays = [get_decay(held.at[b], heads, size) for b in range(CHIPS)]
    edges = known[0][part] if known else before[place, side(0, heads, size), :]
    edges = [jnp.where(later, edges.astype(F32), 0.0).astype(BF16)]
    edges += [held[b, side(0, heads, size), :] for b in range(CHIPS - 1)]
    fixes = [chip_fixes(held, b, edges[b], heads, size) for b in range(CHIPS - 1)]
    for j in range(heads):
        rows = slice(j * size, (j + 1) * size)
        acc = jnp.where(later, before[place, rows, :].astype(F32), 0.0)
        out_ref[slots[0], rows, :] = acc.astype(BF16)
        for b in range(1, CHIPS):
            acc = acc * decays[b - 1][j : j + 1] + (
                held[b - 1, rows, :].astype(F32) + fixes[b - 1][j]
            )
            out_ref[slots[b], rows, :] = acc.astype(BF16)
    for b in range(CHIPS):
        out_ref[slots[b], heads * size : heads * size + PARTS, :] = edges[b]


def last_out_kernel(items, earlier, heads, size, *refs):
    count = 3 + 3 * len(items)
    made = refs[count : count + len(earlier)]
    out_ref, inter_ref, score_ref, done_ref, sems = refs[-5:]
    copies = []

    def write(item, source):
        cols = columns(head_group(*item) * heads * size, 0, heads * size)
        copies.append(
            pltpu.make_async_copy(source, out_ref.at[:, cols], sems.at[len(copies)])
        )
        copies[-1].start()

    for there, ref in zip(earlier, made):
        for i, item in enumerate(there):
            write(item, ref.at[i])
    out_kernel(items, heads, size, *refs[:count], done_ref, inter_ref, score_ref, write=write)
    for copy in copies:
        copy.wait()


def out_kernel(items, heads, size, *refs, write=None):
    q_ref, cum_ref, gain_ref = refs[:3]
    per_item = [refs[3 + 3 * i : 6 + 3 * i] for i in range(len(items))]
    done_ref, inter_ref, score_ref = refs[-3:]
    rows = q_ref.shape[0]
    core, _ = position()
    second = core == 1
    row = lax.broadcasted_iota(jnp.int32, (rows, 2 * PARTS), 0)
    column = lax.broadcasted_iota(jnp.int32, (rows, 2 * PARTS), 1)
    edge = lax.rem(column, PARTS)
    causal = (lax.div(edge, heads) <= row) & (edge < 3 * heads)
    ahead = column < PARTS
    kept = ((ahead & (core == 1)) | causal) & (ahead | (core == 1))
    kept = [kept & (lax.rem(edge, heads) == j) for j in range(heads)]
    for i, (mine, g) in enumerate(items):
        prefix_ref, intra_ref, sib_ref = per_item[i]
        b = head_group(mine, g)
        started = jnp.exp(cum_ref[b][0:heads]).T
        by = jnp.where(second, get_decay(sib_ref.at[g], heads, size), 1.0)
        edges = jnp.concatenate(
            [
                prefix_ref[heads * size : heads * size + PARTS, :].astype(F32),
                sib_ref[g, side(0, heads, size), :].astype(F32),
            ],
            0,
        ).astype(BF16)
        for j in range(heads):
            cols = columns(b * heads * size, j * size, size)
            these = slice(j * size, (j + 1) * size)
            sib = jnp.where(second, sib_ref[g, these, :].astype(F32), 0.0)
            prefix = (prefix_ref[these, :].astype(F32) * by[j : j + 1] + sib).astype(BF16)
            both = lax.dot_general(
                q_ref[:, cols],
                jnp.concatenate([prefix, edges], 0),
                (((1,), (1,)), ((), ())),
                preferred_element_type=F32,
            )
            both = both * started[:, j : j + 1]
            inter_ref[i * heads + j] = both[:, 0:size] + intra_ref[g * heads + j]
            score_ref[i * heads + j] = jnp.where(kept[j], both[:, size:], 0.0).astype(BF16)
    for i, (mine, g) in enumerate(items):
        _, intra_ref, sib_ref = per_item[i]
        b = head_group(mine, g)
        values = intra_ref[UNITS * heads, g * PARTS : (g + 1) * PARTS, :]
        ahead_values = jnp.where(second, sib_ref[g, side(2, heads, size), :].astype(F32), values)
        values = jnp.concatenate([ahead_values, values], 0).astype(BF16)
        for j in range(heads):
            inter_ref[i * heads + j] += jnp.dot(
                score_ref[i * heads + j], values, preferred_element_type=F32
            )
    for i, (mine, g) in enumerate(items):
        b = head_group(mine, g)
        for j in range(heads):
            cols = columns(b * heads * size, j * size, size)
            mixed = inter_ref[i * heads + j]
            scale = lax.rsqrt(jnp.mean(mixed * mixed, axis=1, keepdims=True) + 1e-05)
            done_ref[i, :, j * size : (j + 1) * size] = (
                mixed * scale * gain_ref[:, cols]
            ).astype(BF16)
        if write is not None:
            write((mine, g), done_ref.at[i])


def join_spans(earlier, later, heads, size):
    base = heads * size
    own = side(1, heads, size)

    def decay(x):
        tail = x[own].astype(F32)
        return tail[0:heads] + tail[heads : 2 * heads] + tail[2 * heads : 3 * heads]

    by = decay(later)
    state = (
        by[:, None, :] * earlier[:base].astype(F32).reshape(heads, size, -1)
        + later[:base].astype(F32).reshape(heads, size, -1)
    ).reshape(base, -1)
    parts = three_parts(by * decay(earlier))
    return jnp.concatenate([state.astype(BF16), later[base : own.start], *parts, later[own.start + 3 * heads :]], 0)


def on_device(queries, key_input, value_input, log_decay, conv_weight, norm_gain):
    rows, width = queries.shape
    head_count = log_decay.shape[1]
    size = width // head_count
    heads = head_count // (SPAN * CHUNKS)
    taps = conv_weight.shape[0]
    half = UNITS * heads
    packet = heads * size + 3 * PARTS
    n = lax.axis_size("ctx")

    def swap(x, mask):
        return lax.ppermute(x, "ctx", [(i, i ^ mask) for i in range(n)])

    def exchange(x, slot):
        return lax.ppermute(x, "ctx", [(i, i ^ (2 * distance(slot, i & 1))) for i in range(n)])

    def shift(x, by):
        return lax.ppermute(x, "ctx", [(i, i + by) for i in range(n - by)])

    gain = norm_gain.reshape(1, width)
    ext = pltpu.VMEM((2 * heads, rows + HALO, size), F32)
    held = pltpu.VMEM((half, rows, size), BF16)

    cum_shape = pltpu.VMEM((SPAN * CHUNKS, 2 * heads, rows), F32)

    def states(mine):
        scratch = [cum_shape, ext, held]
        if not mine:
            buf = pltpu.VMEM((CHIPS, rows, CHUNKS * heads * size), BF16)
            scratch = [
                buf,
                buf,
                pltpu.VMEM((CHIPS, taps, CHUNKS * heads * size), F32),
                pltpu.VMEM((head_count, rows), F32),
                *scratch,
                pltpu.SemaphoreType.DMA((3 * CHIPS + 1,)),
            ]
        return call(
            functools.partial(state_kernel if mine else fetched_state_kernel, mine, heads, size),
            "states_mine" if mine else "states_other",
            pltpu.VMEM((UNITS, packet, size), BF16),
            key_input, value_input, conv_weight, log_decay.T,
            in_specs=[VMEM if mine else HBM] * 4,
            scratch=scratch,
        )

    def intra_part(mine, q):
        return call(
            functools.partial(intra_kernel, mine, heads, size),
            "intra_mine" if mine else "intra_other",
            pltpu.VMEM((half + 1, rows, size), F32),
            q, key_input, value_input, conv_weight, cum,
            scratch=[ext, held],
        )

    theirs = states(False)
    got = swap(theirs, 1)
    mine = states(True)
    got_late = swap(mine, 1)

    chip_states = call(
        functools.partial(chip_kernel, heads, size),
        "chip_states",
        pltpu.VMEM((CHIPS, CHUNKS, packet, size), BF16),
        mine, got,
    )
    order = pltpu.VMEM((CHIPS, packet, size), BF16)

    packets = {0: chip_states[0]}
    for g in EXCHANGE:
        packets[g] = exchange(chip_states[g], g)
    q_after, decay_after, chip_states = lax.optimization_barrier(
        (queries, log_decay, chip_states)
    )
    cum = call(
        functools.partial(cum_kernel, heads),
        "cum",
        cum_shape,
        decay_after.T,
    )
    intra_mine = intra_part(True, q_after)
    *late, intra_mine = lax.optimization_barrier((*[packets[g] for g in EXCHANGE], intra_mine))
    packets.update(zip(EXCHANGE, late))
    packets = [packets[g] for g in range(CHIPS)]

    known = []
    if n > 2 * SPAN:
        edge = call(
            functools.partial(last_edge_kernel, heads, size),
            "last_edge",
            pltpu.VMEM((CHUNKS, PARTS, size), BF16),
            *packets,
            scratch=[order],
        )
        known = [shift(edge, SPAN)]

    def joined(parts):
        span = call(
            functools.partial(span_kernel, parts, heads, size),
            "span_state",
            pltpu.VMEM((len(parts), heads * size + (2 if known else 1) * PARTS, size), BF16),
            *packets, *known,
            scratch=[order],
        )
        before = swap(span, SPAN) if n == 2 * SPAN else shift(span, SPAN)
        reach = 1
        while reach < n // SPAN - 1:
            before = jax.vmap(functools.partial(join_spans, heads=heads, size=size))(
                shift(before, SPAN * reach), before
            )
            reach *= 2
        return span, before

    spans, befores = zip(*[joined(parts) for parts in SHIFTS])
    q_after, _ = lax.optimization_barrier((queries, spans[-1]))
    intra_other = intra_part(False, q_after)
    before, intra_other = lax.optimization_barrier((befores[-1], intra_other))
    befores = [*befores[:-1], before]
    ahead = {
        part: (place, before)
        for parts, before in zip(SHIFTS, befores)
        for place, part in enumerate(parts)
    }

    own, other = {}, {}
    for part in range(CHUNKS):
        chip_prefix = call(
            functools.partial(spread_kernel, part, ahead[part][0], heads, size),
            "chip_prefix",
            pltpu.VMEM((CHIPS, heads * size + PARTS, size), BF16),
            *packets, ahead[part][1], *known,
            scratch=[order],
        )
        first = part * CHIPS
        own[first] = chip_prefix[0]
        for g in EXCHANGE:
            own[first + g] = exchange(chip_prefix[g], g)
        other[first] = swap(own[first], 1)

    def output(items, earlier=None):
        args = [queries, cum, gain]
        for mine, u in items:
            args += [own[u], intra_mine, got] if mine else [other[u], intra_other, got_late]
        done = pltpu.VMEM((len(items), rows, heads * size), BF16)
        scratch = [
            pltpu.VMEM((len(items) * heads, rows, size), F32),
            pltpu.VMEM((len(items) * heads, rows, 2 * PARTS), BF16),
        ]
        kernel = functools.partial(out_kernel, items, heads, size)
        hints = {
            "cost_estimate": pl.CostEstimate(flops=1, transcendentals=0, bytes_accessed=1),
        }
        name = "out_" + "_".join(("m" if mine else "o") + str(u) for mine, u in items)
        if earlier is None:
            return call(kernel, name, done, *args, scratch=scratch, **hints)
        there, made = zip(*earlier)
        return call(
            functools.partial(last_out_kernel, items, there, heads, size),
            name,
            jax.ShapeDtypeStruct((rows, width), BF16),
            *args, *made,
            out_specs=HBM,
            scratch=[*scratch, done, pltpu.SemaphoreType.DMA((2 * UNITS,))],
            **hints,
        )

    *late, soon = EXCHANGE[1], EXCHANGE[0], EXCHANGE[2]
    items = [(True, 0), (False, 0)]
    made = output(items)
    own[soon], made = lax.optimization_barrier((own[soon], made))
    earlier = [(items, made)]
    other[soon] = swap(own[soon], 1)
    items = [(True, soon)]
    made = output(items)
    *arrived, made = lax.optimization_barrier((*[own[u] for u in late], made))
    earlier.append((items, made))
    own.update(zip(late, arrived))
    other.update({u: swap(own[u], 1) for u in late})
    items = [(True, u) for u in late] + [(False, soon)]
    earlier.append((items, output(items)))
    return output([(False, u) for u in late], earlier)


def solution(mesh):
    rows = P(("groups", "ctx"), None)
    return jax.shard_map(
        on_device,
        mesh=mesh,
        in_specs=(rows, rows, rows, rows, P(), P()),
        out_specs=rows,
        check_vma=False,
    )
```

```python
import functools

import jax
import jax.numpy as jnp
from jax import lax
from jax.experimental import pallas as pl
from jax.experimental.pallas import tpu as pltpu
from jax.sharding import PartitionSpec as P

F32 = jnp.float32
BF16 = jnp.bfloat16
CHIPS = 4
SPAN = 2 * CHIPS
HALO = 8
EXCHANGE = (2, 3, 1)
CHUNKS = 1
UNITS = CHUNKS * CHIPS
SHIFTS = ((0,),)
PARTS = 16
VMEM = pl.BlockSpec(memory_space=pltpu.VMEM)
HBM = pl.BlockSpec(memory_space=pltpu.HBM)


def position():
    me = lax.axis_index("ctx")
    return me & 1, (me >> 1) & (CHIPS - 1)


def head_group(mine, unit):
    core, chip = position()
    core = core if mine else 1 - core
    group = core * CHIPS + (chip ^ distance(unit % CHIPS, core))
    return group * CHUNKS + unit // CHIPS


def distance(slot, core):
    turned = ((slot & 1) << 1) | (slot >> 1)
    return slot + core * (turned - slot)


def columns(block, offset, size):
    return pl.ds(pl.multiple_of(block + offset, size), size)


def call(kernel, name, out_shape, *args, scratch=(), in_specs=None, out_specs=VMEM, **options):
    if in_specs is None:
        in_specs = [VMEM] * len(args)
    args = [
        pltpu.with_memory_space_constraint(x, pltpu.VMEM if s is VMEM else pltpu.HBM)
        for x, s in zip(args, in_specs)
    ]
    return pl.pallas_call(
        kernel,
        out_shape=out_shape,
        in_specs=in_specs,
        out_specs=out_specs,
        scratch_shapes=list(scratch),
        name=name,
        compiler_params=pltpu.CompilerParams(vmem_limit_bytes=6 << 20),
        **options,
    )(*args)


def cum_kernel(heads, decay_ref, out_ref):
    x = decay_ref[...]
    count, rows = x.shape
    upto = lax.broadcasted_iota(jnp.int32, (rows, rows), 0) <= lax.broadcasted_iota(
        jnp.int32, (rows, rows), 1
    )
    parts = jnp.concatenate([p.astype(F32) for p in three_parts(x)], 0).astype(BF16)
    sums = jnp.dot(parts, upto.astype(F32).astype(BF16), preferred_element_type=F32)
    sums = sums[0:count] + (sums[count : 2 * count] + sums[2 * count :])
    total = jnp.broadcast_to(sums[:, rows - 1 : rows], sums.shape)
    for b in range(out_ref.shape[0]):
        these = slice(b * heads, (b + 1) * heads)
        out_ref[b, 0:heads, :] = sums[these]
        out_ref[b, heads : 2 * heads, :] = total[these]


def three_parts(x):
    hi = x.astype(BF16)
    rest = x - hi.astype(F32)
    mid = rest.astype(BF16)
    low = (rest - mid.astype(F32)).astype(BF16)
    return hi, mid, low


def side(part, heads, size):
    base = heads * size + part * PARTS
    return slice(base, base + PARTS)


def padded(rows):
    rows = jnp.concatenate(rows, 0)
    spare = jnp.zeros((PARTS - rows.shape[0], rows.shape[1]), F32)
    return jnp.concatenate([rows, spare], 0).astype(BF16)


def put_decay(out, decays, heads, size):
    out[side(1, heads, size), :] = padded([p.astype(F32) for p in three_parts(decays)])


def get_decay(packet, heads, size):
    tail = packet[side(1, heads, size), :].astype(F32)
    return tail[0:heads] + tail[heads : 2 * heads] + tail[2 * heads : 3 * heads]


def edge_states(values, edges, heads):
    row = lax.broadcasted_iota(jnp.int32, values.shape, 0)
    out = []
    for j in range(heads):
        picked = jnp.where(lax.rem(row, heads) == j, values.astype(F32), 0.0).astype(BF16)
        out.append(
            lax.dot_general(picked, edges, (((0,), (0,)), ((), ())), preferred_element_type=F32)
        )
    return out


def conv_keys(k_ref, halo, w_ref, ext, cols):
    rows = k_ref.shape[0]
    ext[0:HALO, :] = halo
    ext[HALO : HALO + rows, :] = k_ref[:, cols].astype(F32)
    total = None
    for j in range(w_ref.shape[0]):
        term = w_ref[j : j + 1, cols] * ext[HALO - j : HALO - j + rows, :]
        total = term if total is None else total + term
    return total.astype(BF16)


def fetched_state_kernel(
    mine, heads, size, k_hbm, v_hbm, w_hbm, decay_hbm, out_ref,
    k_buf, v_buf, w_buf, decay_buf, cum_ref, ext, held, sems,
):
    wide = CHUNKS * heads * size
    copies = [pltpu.make_async_copy(decay_hbm, decay_buf, sems.at[3 * CHIPS])]
    copies[0].start()
    for g in range(CHIPS):
        cols = columns(head_group(mine, g) * heads * size, 0, wide)
        for i, (source, buf) in enumerate(((k_hbm, k_buf), (w_hbm, w_buf), (v_hbm, v_buf))):
            copies.append(
                pltpu.make_async_copy(source.at[:, cols], buf.at[g], sems.at[3 * g + i])
            )
            copies[-1].start()
    copies[0].wait()
    groups, waits = [], []
    for u in range(UNITS):
        g, part = u % CHIPS, u // CHIPS
        cols = slice(part * heads * size, (part + 1) * heads * size)
        groups.append(tuple(buf.at[g, :, cols] for buf in (k_buf, v_buf, w_buf)))
        waits.append(copies[1 + 3 * g : 4 + 3 * g] if part == 0 else [])
    states_of(mine, heads, size, groups, waits, decay_buf, out_ref, cum_ref, ext, held)


def state_kernel(
    mine, heads, size, k_ref, v_ref, w_ref, decay_ref, out_ref, cum_ref, ext, held
):
    groups = []
    for u in range(UNITS):
        cols = columns(head_group(mine, u) * heads * size, 0, heads * size)
        groups.append((k_ref.at[:, cols], v_ref.at[:, cols], w_ref.at[:, cols]))
    waits = [[]] * UNITS
    states_of(mine, heads, size, groups, waits, decay_ref, out_ref, cum_ref, ext, held)


def states_of(mine, heads, size, groups, waits, decay_ref, out_ref, cum_ref, ext, held):
    rows = groups[0][0].shape[0]
    taps = groups[0][2].shape[0]
    cum_kernel(heads, decay_ref, cum_ref)
    none = jnp.zeros((HALO, size), F32)
    for g in range(UNITS):
        k_ref, v_ref, w_ref = groups[g]
        for copy in waits[g]:
            copy.wait()
        cum = cum_ref[head_group(mine, g)]
        ending = jnp.exp(cum[heads : 2 * heads] - cum[0:heads]).T
        edges, values = [], []
        for j in range(heads):
            cols = slice(j * size, (j + 1) * size)
            key_conv = conv_keys(k_ref, none, w_ref, ext.at[g % 2 * heads + j], cols)
            held[g * heads + j] = (key_conv.astype(F32) * ending[:, j : j + 1]).astype(BF16)
            last = k_ref[rows - HALO : rows, cols].astype(F32)
            head_edges = []
            for t in range(taps - 1):
                terms = [
                    w_ref[i : i + 1, cols] * last[HALO + t - i : HALO + t - i + 1]
                    for i in range(t + 1, taps)
                ]
                head_edges.append(sum(terms[1:], terms[0]))
            edges.append(head_edges)
            values.append(v_ref[0:HALO, cols].astype(F32) * ending[0:HALO, j : j + 1])
        put_decay(out_ref.at[g], jnp.exp(cum[heads : 2 * heads]), heads, size)
        out_ref[g, side(0, heads, size), :] = padded(
            [edges[j][t] for t in range(taps - 1) for j in range(heads)]
        )
        out_ref[g, side(2, heads, size), :] = padded(
            [values[j][t : t + 1] for t in range(taps - 1) for j in range(heads)]
        )
    for g in range(UNITS):
        for j in range(heads):
            cols = slice(j * size, (j + 1) * size)
            state = lax.dot_general(
                groups[g][1][:, cols], held[g * heads + j], (((0,), (0,)), ((), ())),
                preferred_element_type=F32,
            )
            out_ref[g, cols, :] = state.astype(BF16)


def intra_kernel(mine, heads, size, q_ref, k_ref, v_ref, w_ref, cum_ref, out_ref, ext, held):
    rows = q_ref.shape[0]
    causal = lax.broadcasted_iota(jnp.int32, (rows, rows), 0) >= lax.broadcasted_iota(
        jnp.int32, (rows, rows), 1
    )
    none = jnp.zeros((HALO, size), F32)
    for g in range(UNITS):
        b = head_group(mine, g)
        cum = cum_ref[b][0:heads]
        cum_col = cum.T
        growth = jnp.exp(-cum_col[0:HALO])
        values = []
        for j in range(heads):
            cols = columns(b * heads * size, j * size, size)
            key_conv = conv_keys(k_ref, none, w_ref, ext.at[g % 2 * heads + j], cols)
            scores = lax.dot_general(
                q_ref[:, cols], key_conv, (((1,), (1,)), ((), ())), preferred_element_type=F32
            )
            spread = cum_col[:, j : j + 1] - cum[j : j + 1]
            weights = jnp.where(causal, scores * jnp.exp(jnp.where(causal, spread, 0.0)), 0.0)
            held[g * heads + j] = weights.astype(BF16)
            values.append(v_ref[0:HALO, cols].astype(F32) * growth[:, j : j + 1])
        out_ref[UNITS * heads, g * PARTS : (g + 1) * PARTS, :] = padded(
            [values[j][t : t + 1] for t in range(3) for j in range(heads)]
        ).astype(F32)
    for g in range(UNITS):
        b = head_group(mine, g)
        for j in range(heads):
            cols = columns(b * heads * size, j * size, size)
            out_ref[g * heads + j] = jnp.dot(
                held[g * heads + j], v_ref[:, cols], preferred_element_type=F32
            )


def chip_kernel(heads, size, own_ref, got_ref, out_ref):
    core, _ = position()
    first = core == 0
    for g in range(UNITS):
        to = out_ref.at[g % CHIPS, g // CHIPS]
        own_decay = get_decay(own_ref.at[g], heads, size)
        got_decay = get_decay(got_ref.at[g], heads, size)
        own_by = jnp.where(first, got_decay, 1.0)
        got_by = jnp.where(first, 1.0, own_decay)

        def earlier_later(part):
            own = own_ref[g, side(part, heads, size), :].astype(F32)
            got = got_ref[g, side(part, heads, size), :].astype(F32)
            return jnp.where(first, own, got), jnp.where(first, got, own)

        edges, out_edges = earlier_later(0)
        out_values, values = earlier_later(2)
        fixes = edge_states(values.astype(BF16), edges.astype(BF16), heads)
        for j in range(heads):
            rows = slice(j * size, (j + 1) * size)
            to[rows, :] = (
                own_ref[g, rows, :].astype(F32) * own_by[j : j + 1]
                + got_ref[g, rows, :].astype(F32) * got_by[j : j + 1]
                + fixes[j]
            ).astype(BF16)
        put_decay(to, own_decay * got_decay, heads, size)
        later_by = jnp.where(first, got_decay, own_decay)
        to[side(0, heads, size), :] = out_edges.astype(BF16)
        to[side(2, heads, size), :] = padded(
            [out_values[t * heads : (t + 1) * heads] * later_by for t in range(3)]
        )


def in_order(packets, part, held):
    core, chip = position()
    for g in range(CHIPS):
        held[chip ^ distance(g, core)] = packets[g][part]


def chip_fixes(held, b, edges, heads, size):
    return edge_states(held[b, side(2, heads, size), :], edges, heads)


def last_edge_kernel(heads, size, *refs):
    packets, out_ref, held = refs[:CHIPS], refs[CHIPS], refs[CHIPS + 1]
    for part in range(CHUNKS):
        in_order(packets, part, held)
        out_ref[part] = held[CHIPS - 1, side(0, heads, size), :]


def span_kernel(parts, heads, size, *refs):
    packets, before, (whole_ref, held) = refs[:CHIPS], refs[CHIPS:-2], refs[-2:]
    for i, part in enumerate(parts):
        known = [before[0][part]] if before else []
        span_of(part, known, heads, size, packets, whole_ref.at[i], held)


def span_of(part, before, heads, size, packets, out_ref, held):
    in_order(packets, part, held)
    decays = [get_decay(held.at[b], heads, size) for b in range(CHIPS)]
    fixes = [
        chip_fixes(held, b, held[b - 1, side(0, heads, size), :], heads, size)
        for b in range(1, CHIPS)
    ]
    fixes.insert(0, chip_fixes(held, 0, before[0], heads, size) if before else None)
    for j in range(heads):
        rows = slice(j * size, (j + 1) * size)
        acc = held[0, rows, :].astype(F32)
        if before:
            acc = acc + fixes[0][j]
        for b in range(1, CHIPS):
            acc = acc * decays[b][j : j + 1] + (held[b, rows, :].astype(F32) + fixes[b][j])
        out_ref[rows, :] = acc.astype(BF16)
    whole = decays[0]
    for b in range(1, CHIPS):
        whole = whole * decays[b]
    out_ref[side(0, heads, size), :] = held[CHIPS - 1, side(0, heads, size), :]
    if before:
        put_decay(out_ref, whole, heads, size)


def spread_kernel(part, place, heads, size, *refs):
    packets, before, known, (out_ref, held) = refs[:CHIPS], refs[CHIPS], refs[CHIPS + 1 : -2], refs[-2:]
    core, chip = position()
    slots = [distance(chip ^ b, core) for b in range(CHIPS)]
    later = lax.axis_index("ctx") >= SPAN
    in_order(packets, part, held)
    decays = [get_decay(held.at[b], heads, size) for b in range(CHIPS)]
    edges = known[0][part] if known else before[place, side(0, heads, size), :]
    edges = [jnp.where(later, edges.astype(F32), 0.0).astype(BF16)]
    edges += [held[b, side(0, heads, size), :] for b in range(CHIPS - 1)]
    fixes = [chip_fixes(held, b, edges[b], heads, size) for b in range(CHIPS - 1)]
    for j in range(heads):
        rows = slice(j * size, (j + 1) * size)
        acc = jnp.where(later, before[place, rows, :].astype(F32), 0.0)
        out_ref[slots[0], rows, :] = acc.astype(BF16)
        for b in range(1, CHIPS):
            acc = acc * decays[b - 1][j : j + 1] + (
                held[b - 1, rows, :].astype(F32) + fixes[b - 1][j]
            )
            out_ref[slots[b], rows, :] = acc.astype(BF16)
    for b in range(CHIPS):
        out_ref[slots[b], heads * size : heads * size + PARTS, :] = edges[b]


def last_out_kernel(items, earlier, heads, size, *refs):
    count = 3 + 3 * len(items)
    made = refs[count : count + len(earlier)]
    out_ref, inter_ref, score_ref, done_ref, sems = refs[-5:]
    copies = []

    def write(item, source):
        cols = columns(head_group(*item) * heads * size, 0, heads * size)
        copies.append(
            pltpu.make_async_copy(source, out_ref.at[:, cols], sems.at[len(copies)])
        )
        copies[-1].start()

    for there, ref in zip(earlier, made):
        for i, item in enumerate(there):
            write(item, ref.at[i])
    out_kernel(items, heads, size, *refs[:count], done_ref, inter_ref, score_ref, write=write)
    for copy in copies:
        copy.wait()


def out_kernel(items, heads, size, *refs, write=None):
    q_ref, cum_ref, gain_ref = refs[:3]
    per_item = [refs[3 + 3 * i : 6 + 3 * i] for i in range(len(items))]
    done_ref, inter_ref, score_ref = refs[-3:]
    rows = q_ref.shape[0]
    core, _ = position()
    second = core == 1
    row = lax.broadcasted_iota(jnp.int32, (rows, 2 * PARTS), 0)
    column = lax.broadcasted_iota(jnp.int32, (rows, 2 * PARTS), 1)
    edge = lax.rem(column, PARTS)
    causal = (lax.div(edge, heads) <= row) & (edge < 3 * heads)
    ahead = column < PARTS
    kept = ((ahead & (core == 1)) | causal) & (ahead | (core == 1))
    kept = [kept & (lax.rem(edge, heads) == j) for j in range(heads)]
    for i, (mine, g) in enumerate(items):
        prefix_ref, intra_ref, sib_ref = per_item[i]
        b = head_group(mine, g)
        started = jnp.exp(cum_ref[b][0:heads]).T
        by = jnp.where(second, get_decay(sib_ref.at[g], heads, size), 1.0)
        edges = jnp.concatenate(
            [
                prefix_ref[heads * size : heads * size + PARTS, :].astype(F32),
                sib_ref[g, side(0, heads, size), :].astype(F32),
            ],
            0,
        ).astype(BF16)
        for j in range(heads):
            cols = columns(b * heads * size, j * size, size)
            these = slice(j * size, (j + 1) * size)
            sib = jnp.where(second, sib_ref[g, these, :].astype(F32), 0.0)
            prefix = (prefix_ref[these, :].astype(F32) * by[j : j + 1] + sib).astype(BF16)
            both = lax.dot_general(
                q_ref[:, cols],
                jnp.concatenate([prefix, edges], 0),
                (((1,), (1,)), ((), ())),
                preferred_element_type=F32,
            )
            both = both * started[:, j : j + 1]
            inter_ref[i * heads + j] = both[:, 0:size] + intra_ref[g * heads + j]
            score_ref[i * heads + j] = jnp.where(kept[j], both[:, size:], 0.0).astype(BF16)
    for i, (mine, g) in enumerate(items):
        _, intra_ref, sib_ref = per_item[i]
        b = head_group(mine, g)
        values = intra_ref[UNITS * heads, g * PARTS : (g + 1) * PARTS, :]
        ahead_values = jnp.where(second, sib_ref[g, side(2, heads, size), :].astype(F32), values)
        values = jnp.concatenate([ahead_values, values], 0).astype(BF16)
        for j in range(heads):
            inter_ref[i * heads + j] += jnp.dot(
                score_ref[i * heads + j], values, preferred_element_type=F32
            )
    for i, (mine, g) in enumerate(items):
        b = head_group(mine, g)
        for j in range(heads):
            cols = columns(b * heads * size, j * size, size)
            mixed = inter_ref[i * heads + j]
            scale = lax.rsqrt(jnp.mean(mixed * mixed, axis=1, keepdims=True) + 1e-05)
            done_ref[i, :, j * size : (j + 1) * size] = (
                mixed * scale * gain_ref[:, cols]
            ).astype(BF16)
        if write is not None:
            write((mine, g), done_ref.at[i])


def join_spans(earlier, later, heads, size):
    base = heads * size
    own = side(1, heads, size)

    def decay(x):
        tail = x[own].astype(F32)
        return tail[0:heads] + tail[heads : 2 * heads] + tail[2 * heads : 3 * heads]

    by = decay(later)
    state = (
        by[:, None, :] * earlier[:base].astype(F32).reshape(heads, size, -1)
        + later[:base].astype(F32).reshape(heads, size, -1)
    ).reshape(base, -1)
    parts = three_parts(by * decay(earlier))
    return jnp.concatenate([state.astype(BF16), later[base : own.start], *parts, later[own.start + 3 * heads :]], 0)


def on_device(queries, key_input, value_input, log_decay, conv_weight, norm_gain):
    rows, width = queries.shape
    head_count = log_decay.shape[1]
    size = width // head_count
    heads = head_count // (SPAN * CHUNKS)
    taps = conv_weight.shape[0]
    half = UNITS * heads
    packet = heads * size + 3 * PARTS
    n = lax.axis_size("ctx")

    def swap(x, mask):
        return lax.ppermute(x, "ctx", [(i, i ^ mask) for i in range(n)])

    def exchange(x, slot):
        return lax.ppermute(x, "ctx", [(i, i ^ (2 * distance(slot, i & 1))) for i in range(n)])

    def shift(x, by):
        return lax.ppermute(x, "ctx", [(i, i + by) for i in range(n - by)])

    gain = norm_gain.reshape(1, width)
    ext = pltpu.VMEM((2 * heads, rows + HALO, size), F32)
    held = pltpu.VMEM((half, rows, size), BF16)

    cum_shape = pltpu.VMEM((SPAN * CHUNKS, 2 * heads, rows), F32)

    def states(mine):
        scratch = [cum_shape, ext, held]
        if not mine:
            buf = pltpu.VMEM((CHIPS, rows, CHUNKS * heads * size), BF16)
            scratch = [
                buf,
                buf,
                pltpu.VMEM((CHIPS, taps, CHUNKS * heads * size), F32),
                pltpu.VMEM((head_count, rows), F32),
                *scratch,
                pltpu.SemaphoreType.DMA((3 * CHIPS + 1,)),
            ]
        return call(
            functools.partial(state_kernel if mine else fetched_state_kernel, mine, heads, size),
            "states_mine" if mine else "states_other",
            pltpu.VMEM((UNITS, packet, size), BF16),
            key_input, value_input, conv_weight, log_decay.T,
            in_specs=[VMEM if mine else HBM] * 4,
            scratch=scratch,
        )

    def intra_part(mine, q):
        return call(
            functools.partial(intra_kernel, mine, heads, size),
            "intra_mine" if mine else "intra_other",
            pltpu.VMEM((half + 1, rows, size), F32),
            q, key_input, value_input, conv_weight, cum,
            scratch=[ext, held],
        )

    theirs = states(False)
    got = swap(theirs, 1)
    mine = states(True)
    got_late = swap(mine, 1)

    chip_states = call(
        functools.partial(chip_kernel, heads, size),
        "chip_states",
        pltpu.VMEM((CHIPS, CHUNKS, packet, size), BF16),
        mine, got,
    )
    order = pltpu.VMEM((CHIPS, packet, size), BF16)

    packets = {0: chip_states[0]}
    for g in EXCHANGE[::-1]:
        packets[g] = exchange(chip_states[g], g)
    q_after, decay_after, chip_states = lax.optimization_barrier(
        (queries, log_decay, chip_states)
    )
    cum = call(
        functools.partial(cum_kernel, heads),
        "cum",
        cum_shape,
        decay_after.T,
    )
    intra_mine = intra_part(True, q_after)
    *late, intra_mine = lax.optimization_barrier(
        (*[packets[g] for g in EXCHANGE[::-1]], intra_mine)
    )
    packets.update(zip(EXCHANGE[::-1], late))
    packets = [packets[g] for g in range(CHIPS)]

    known = []
    if n > 2 * SPAN:
        edge = call(
            functools.partial(last_edge_kernel, heads, size),
            "last_edge",
            pltpu.VMEM((CHUNKS, PARTS, size), BF16),
            *packets,
            scratch=[order],
        )
        known = [shift(edge, SPAN)]

    def joined(parts):
        span = call(
            functools.partial(span_kernel, parts, heads, size),
            "span_state",
            pltpu.VMEM((len(parts), heads * size + (2 if known else 1) * PARTS, size), BF16),
            *packets, *known,
            scratch=[order],
        )
        before = swap(span, SPAN) if n == 2 * SPAN else shift(span, SPAN)
        reach = 1
        while reach < n // SPAN - 1:
            before = jax.vmap(functools.partial(join_spans, heads=heads, size=size))(
                shift(before, SPAN * reach), before
            )
            reach *= 2
        return span, before

    spans, befores = zip(*[joined(parts) for parts in SHIFTS])
    q_after, _ = lax.optimization_barrier((queries, spans[-1]))
    intra_other = intra_part(False, q_after)
    before, intra_other = lax.optimization_barrier((befores[-1], intra_other))
    befores = [*befores[:-1], before]
    ahead = {
        part: (place, before)
        for parts, before in zip(SHIFTS, befores)
        for place, part in enumerate(parts)
    }

    own, other = {}, {}
    for part in range(CHUNKS):
        chip_prefix = call(
            functools.partial(spread_kernel, part, ahead[part][0], heads, size),
            "chip_prefix",
            pltpu.VMEM((CHIPS, heads * size + PARTS, size), BF16),
            *packets, ahead[part][1], *known,
            scratch=[order],
        )
        first = part * CHIPS
        own[first] = chip_prefix[0]
        for g in EXCHANGE:
            own[first + g] = exchange(chip_prefix[g], g)
        other[first] = swap(own[first], 1)

    def output(items, earlier=None):
        args = [queries, cum, gain]
        for mine, u in items:
            args += [own[u], intra_mine, got] if mine else [other[u], intra_other, got_late]
        done = pltpu.VMEM((len(items), rows, heads * size), BF16)
        scratch = [
            pltpu.VMEM((len(items) * heads, rows, size), F32),
            pltpu.VMEM((len(items) * heads, rows, 2 * PARTS), BF16),
        ]
        kernel = functools.partial(out_kernel, items, heads, size)
        hints = {
            "cost_estimate": pl.CostEstimate(flops=1, transcendentals=0, bytes_accessed=1),
        }
        name = "out_" + "_".join(("m" if mine else "o") + str(u) for mine, u in items)
        if earlier is None:
            return call(kernel, name, done, *args, scratch=scratch, **hints)
        there, made = zip(*earlier)
        return call(
            functools.partial(last_out_kernel, items, there, heads, size),
            name,
            jax.ShapeDtypeStruct((rows, width), BF16),
            *args, *made,
            out_specs=HBM,
            scratch=[*scratch, done, pltpu.SemaphoreType.DMA((2 * UNITS,))],
            **hints,
        )

    *late, soon = EXCHANGE[1], EXCHANGE[0], EXCHANGE[2]
    items = [(True, 0), (False, 0)]
    made = output(items)
    own[soon], made = lax.optimization_barrier((own[soon], made))
    earlier = [(items, made)]
    other[soon] = swap(own[soon], 1)
    items = [(True, soon)]
    made = output(items)
    *arrived, made = lax.optimization_barrier((*[own[u] for u in late], made))
    earlier.append((items, made))
    own.update(zip(late, arrived))
    other.update({u: swap(own[u], 1) for u in late})
    items = [(True, u) for u in late] + [(False, soon)]
    earlier.append((items, output(items)))
    return output([(False, u) for u in late], earlier)


def solution(mesh):
    rows = P(("groups", "ctx"), None)
    return jax.shard_map(
        on_device,
        mesh=mesh,
        in_specs=(rows, rows, rows, rows, P(), P()),
        out_specs=rows,
        check_vma=False,
    )
```

```python
import functools

import jax
import jax.numpy as jnp
from jax import lax
from jax.experimental import pallas as pl
from jax.experimental.pallas import tpu as pltpu
from jax.sharding import PartitionSpec as P

F32 = jnp.float32
BF16 = jnp.bfloat16
CHIPS = 4
SPAN = 2 * CHIPS
HALO = 8
EXCHANGE = (2, 3, 1)
CHUNKS = 1
UNITS = CHUNKS * CHIPS
SHIFTS = ((0,),)
PARTS = 16
VMEM = pl.BlockSpec(memory_space=pltpu.VMEM)
HBM = pl.BlockSpec(memory_space=pltpu.HBM)


def position():
    me = lax.axis_index("ctx")
    return me & 1, (me >> 1) & (CHIPS - 1)


def head_group(mine, unit):
    core, chip = position()
    core = core if mine else 1 - core
    group = core * CHIPS + (chip ^ distance(unit % CHIPS, core))
    return group * CHUNKS + unit // CHIPS


def distance(slot, core):
    turned = ((slot & 1) << 1) | (slot >> 1)
    return slot + core * (turned - slot)


def columns(block, offset, size):
    return pl.ds(pl.multiple_of(block + offset, size), size)


def call(kernel, name, out_shape, *args, scratch=(), in_specs=None, out_specs=VMEM, **options):
    if in_specs is None:
        in_specs = [VMEM] * len(args)
    args = [
        pltpu.with_memory_space_constraint(x, pltpu.VMEM if s is VMEM else pltpu.HBM)
        for x, s in zip(args, in_specs)
    ]
    return pl.pallas_call(
        kernel,
        out_shape=out_shape,
        in_specs=in_specs,
        out_specs=out_specs,
        scratch_shapes=list(scratch),
        name=name,
        compiler_params=pltpu.CompilerParams(vmem_limit_bytes=6 << 20),
        **options,
    )(*args)


def cum_kernel(heads, decay_ref, out_ref):
    x = decay_ref[...]
    count, rows = x.shape
    upto = lax.broadcasted_iota(jnp.int32, (rows, rows), 0) <= lax.broadcasted_iota(
        jnp.int32, (rows, rows), 1
    )
    parts = jnp.concatenate([p.astype(F32) for p in three_parts(x)], 0).astype(BF16)
    sums = jnp.dot(parts, upto.astype(F32).astype(BF16), preferred_element_type=F32)
    sums = sums[0:count] + (sums[count : 2 * count] + sums[2 * count :])
    total = jnp.broadcast_to(sums[:, rows - 1 : rows], sums.shape)
    for b in range(out_ref.shape[0]):
        these = slice(b * heads, (b + 1) * heads)
        out_ref[b, 0:heads, :] = sums[these]
        out_ref[b, heads : 2 * heads, :] = total[these]


def three_parts(x):
    hi = x.astype(BF16)
    rest = x - hi.astype(F32)
    mid = rest.astype(BF16)
    low = (rest - mid.astype(F32)).astype(BF16)
    return hi, mid, low


def side(part, heads, size):
    base = heads * size + part * PARTS
    return slice(base, base + PARTS)


def padded(rows):
    rows = jnp.concatenate(rows, 0)
    spare = jnp.zeros((PARTS - rows.shape[0], rows.shape[1]), F32)
    return jnp.concatenate([rows, spare], 0).astype(BF16)


def put_decay(out, decays, heads, size):
    out[side(1, heads, size), :] = padded([p.astype(F32) for p in three_parts(decays)])


def get_decay(packet, heads, size):
    tail = packet[side(1, heads, size), :].astype(F32)
    return tail[0:heads] + tail[heads : 2 * heads] + tail[2 * heads : 3 * heads]


def edge_states(values, edges, heads):
    row = lax.broadcasted_iota(jnp.int32, values.shape, 0)
    out = []
    for j in range(heads):
        picked = jnp.where(lax.rem(row, heads) == j, values.astype(F32), 0.0).astype(BF16)
        out.append(
            lax.dot_general(picked, edges, (((0,), (0,)), ((), ())), preferred_element_type=F32)
        )
    return out


def conv_keys(k_ref, halo, w_ref, ext, cols):
    rows = k_ref.shape[0]
    ext[0:HALO, :] = halo
    ext[HALO : HALO + rows, :] = k_ref[:, cols].astype(F32)
    total = None
    for j in range(w_ref.shape[0]):
        term = w_ref[j : j + 1, cols] * ext[HALO - j : HALO - j + rows, :]
        total = term if total is None else total + term
    return total.astype(BF16)


def fetched_state_kernel(
    mine, heads, size, k_hbm, v_hbm, w_hbm, decay_hbm, out_ref,
    k_buf, v_buf, w_buf, decay_buf, cum_ref, ext, held, sems,
):
    wide = CHUNKS * heads * size
    copies = [pltpu.make_async_copy(decay_hbm, decay_buf, sems.at[3 * CHIPS])]
    copies[0].start()
    for g in range(CHIPS):
        cols = columns(head_group(mine, g) * heads * size, 0, wide)
        for i, (source, buf) in enumerate(((k_hbm, k_buf), (w_hbm, w_buf), (v_hbm, v_buf))):
            copies.append(
                pltpu.make_async_copy(source.at[:, cols], buf.at[g], sems.at[3 * g + i])
            )
            copies[-1].start()
    copies[0].wait()
    groups, waits = [], []
    for u in range(UNITS):
        g, part = u % CHIPS, u // CHIPS
        cols = slice(part * heads * size, (part + 1) * heads * size)
        groups.append(tuple(buf.at[g, :, cols] for buf in (k_buf, v_buf, w_buf)))
        waits.append(copies[1 + 3 * g : 4 + 3 * g] if part == 0 else [])
    states_of(mine, heads, size, groups, waits, decay_buf, out_ref, cum_ref, ext, held)


def state_kernel(
    mine, heads, size, k_ref, v_ref, w_ref, decay_ref, out_ref, cum_ref, ext, held
):
    groups = []
    for u in range(UNITS):
        cols = columns(head_group(mine, u) * heads * size, 0, heads * size)
        groups.append((k_ref.at[:, cols], v_ref.at[:, cols], w_ref.at[:, cols]))
    waits = [[]] * UNITS
    states_of(mine, heads, size, groups, waits, decay_ref, out_ref, cum_ref, ext, held)


def states_of(mine, heads, size, groups, waits, decay_ref, out_ref, cum_ref, ext, held):
    rows = groups[0][0].shape[0]
    taps = groups[0][2].shape[0]
    cum_kernel(heads, decay_ref, cum_ref)
    none = jnp.zeros((HALO, size), F32)
    for g in range(UNITS):
        k_ref, v_ref, w_ref = groups[g]
        for copy in waits[g]:
            copy.wait()
        cum = cum_ref[head_group(mine, g)]
        ending = jnp.exp(cum[heads : 2 * heads] - cum[0:heads]).T
        edges, values = [], []
        for j in range(heads):
            cols = slice(j * size, (j + 1) * size)
            key_conv = conv_keys(k_ref, none, w_ref, ext.at[g % 2 * heads + j], cols)
            held[g * heads + j] = (key_conv.astype(F32) * ending[:, j : j + 1]).astype(BF16)
            last = k_ref[rows - HALO : rows, cols].astype(F32)
            head_edges = []
            for t in range(taps - 1):
                terms = [
                    w_ref[i : i + 1, cols] * last[HALO + t - i : HALO + t - i + 1]
                    for i in range(t + 1, taps)
                ]
                head_edges.append(sum(terms[1:], terms[0]))
            edges.append(head_edges)
            values.append(v_ref[0:HALO, cols].astype(F32) * ending[0:HALO, j : j + 1])
        put_decay(out_ref.at[g], jnp.exp(cum[heads : 2 * heads]), heads, size)
        out_ref[g, side(0, heads, size), :] = padded(
            [edges[j][t] for t in range(taps - 1) for j in range(heads)]
        )
        out_ref[g, side(2, heads, size), :] = padded(
            [values[j][t : t + 1] for t in range(taps - 1) for j in range(heads)]
        )
    for g in range(UNITS):
        for j in range(heads):
            cols = slice(j * size, (j + 1) * size)
            state = lax.dot_general(
                groups[g][1][:, cols], held[g * heads + j], (((0,), (0,)), ((), ())),
                preferred_element_type=F32,
            )
            out_ref[g, cols, :] = state.astype(BF16)


def intra_kernel(mine, heads, size, q_ref, k_ref, v_ref, w_ref, cum_ref, out_ref, ext, held):
    rows = q_ref.shape[0]
    causal = lax.broadcasted_iota(jnp.int32, (rows, rows), 0) >= lax.broadcasted_iota(
        jnp.int32, (rows, rows), 1
    )
    none = jnp.zeros((HALO, size), F32)
    for g in range(UNITS):
        b = head_group(mine, g)
        cum = cum_ref[b][0:heads]
        cum_col = cum.T
        growth = jnp.exp(-cum_col[0:HALO])
        values = []
        for j in range(heads):
            cols = columns(b * heads * size, j * size, size)
            key_conv = conv_keys(k_ref, none, w_ref, ext.at[g % 2 * heads + j], cols)
            scores = lax.dot_general(
                q_ref[:, cols], key_conv, (((1,), (1,)), ((), ())), preferred_element_type=F32
            )
            spread = cum_col[:, j : j + 1] - cum[j : j + 1]
            weights = jnp.where(causal, scores * jnp.exp(jnp.where(causal, spread, 0.0)), 0.0)
            held[g * heads + j] = weights.astype(BF16)
            values.append(v_ref[0:HALO, cols].astype(F32) * growth[:, j : j + 1])
        out_ref[UNITS * heads, g * PARTS : (g + 1) * PARTS, :] = padded(
            [values[j][t : t + 1] for t in range(3) for j in range(heads)]
        ).astype(F32)
    for g in range(UNITS):
        b = head_group(mine, g)
        for j in range(heads):
            cols = columns(b * heads * size, j * size, size)
            out_ref[g * heads + j] = jnp.dot(
                held[g * heads + j], v_ref[:, cols], preferred_element_type=F32
            )


def chip_kernel(heads, size, own_ref, got_ref, out_ref):
    core, _ = position()
    first = core == 0
    for g in range(UNITS):
        to = out_ref.at[g % CHIPS, g // CHIPS]
        own_decay = get_decay(own_ref.at[g], heads, size)
        got_decay = get_decay(got_ref.at[g], heads, size)
        own_by = jnp.where(first, got_decay, 1.0)
        got_by = jnp.where(first, 1.0, own_decay)

        def earlier_later(part):
            own = own_ref[g, side(part, heads, size), :].astype(F32)
            got = got_ref[g, side(part, heads, size), :].astype(F32)
            return jnp.where(first, own, got), jnp.where(first, got, own)

        edges, out_edges = earlier_later(0)
        out_values, values = earlier_later(2)
        fixes = edge_states(values.astype(BF16), edges.astype(BF16), heads)
        for j in range(heads):
            rows = slice(j * size, (j + 1) * size)
            to[rows, :] = (
                own_ref[g, rows, :].astype(F32) * own_by[j : j + 1]
                + got_ref[g, rows, :].astype(F32) * got_by[j : j + 1]
                + fixes[j]
            ).astype(BF16)
        put_decay(to, own_decay * got_decay, heads, size)
        later_by = jnp.where(first, got_decay, own_decay)
        to[side(0, heads, size), :] = out_edges.astype(BF16)
        to[side(2, heads, size), :] = padded(
            [out_values[t * heads : (t + 1) * heads] * later_by for t in range(3)]
        )


def in_order(packets, part, held):
    core, chip = position()
    for g in range(CHIPS):
        held[chip ^ distance(g, core)] = packets[g][part]


def chip_fixes(held, b, edges, heads, size):
    return edge_states(held[b, side(2, heads, size), :], edges, heads)


def last_edge_kernel(heads, size, *refs):
    packets, out_ref, held = refs[:CHIPS], refs[CHIPS], refs[CHIPS + 1]
    for part in range(CHUNKS):
        in_order(packets, part, held)
        out_ref[part] = held[CHIPS - 1, side(0, heads, size), :]


def span_kernel(parts, heads, size, *refs):
    packets, before, (whole_ref, held) = refs[:CHIPS], refs[CHIPS:-2], refs[-2:]
    for i, part in enumerate(parts):
        known = [before[0][part]] if before else []
        span_of(part, known, heads, size, packets, whole_ref.at[i], held)


def span_of(part, before, heads, size, packets, out_ref, held):
    in_order(packets, part, held)
    decays = [get_decay(held.at[b], heads, size) for b in range(CHIPS)]
    fixes = [
        chip_fixes(held, b, held[b - 1, side(0, heads, size), :], heads, size)
        for b in range(1, CHIPS)
    ]
    fixes.insert(0, chip_fixes(held, 0, before[0], heads, size) if before else None)
    for j in range(heads):
        rows = slice(j * size, (j + 1) * size)
        acc = held[0, rows, :].astype(F32)
        if before:
            acc = acc + fixes[0][j]
        for b in range(1, CHIPS):
            acc = acc * decays[b][j : j + 1] + (held[b, rows, :].astype(F32) + fixes[b][j])
        out_ref[rows, :] = acc.astype(BF16)
    whole = decays[0]
    for b in range(1, CHIPS):
        whole = whole * decays[b]
    out_ref[side(0, heads, size), :] = held[CHIPS - 1, side(0, heads, size), :]
    if before:
        put_decay(out_ref, whole, heads, size)


def spread_kernel(part, place, heads, size, *refs):
    packets, before, known, (out_ref, held) = refs[:CHIPS], refs[CHIPS], refs[CHIPS + 1 : -2], refs[-2:]
    core, chip = position()
    slots = [distance(chip ^ b, core) for b in range(CHIPS)]
    later = lax.axis_index("ctx") >= SPAN
    in_order(packets, part, held)
    decays = [get_decay(held.at[b], heads, size) for b in range(CHIPS)]
    edges = known[0][part] if known else before[place, side(0, heads, size), :]
    edges = [jnp.where(later, edges.astype(F32), 0.0).astype(BF16)]
    edges += [held[b, side(0, heads, size), :] for b in range(CHIPS - 1)]
    fixes = [chip_fixes(held, b, edges[b], heads, size) for b in range(CHIPS - 1)]
    for j in range(heads):
        rows = slice(j * size, (j + 1) * size)
        acc = jnp.where(later, before[place, rows, :].astype(F32), 0.0)
        out_ref[slots[0], rows, :] = acc.astype(BF16)
        for b in range(1, CHIPS):
            acc = acc * decays[b - 1][j : j + 1] + (
                held[b - 1, rows, :].astype(F32) + fixes[b - 1][j]
            )
            out_ref[slots[b], rows, :] = acc.astype(BF16)
    for b in range(CHIPS):
        out_ref[slots[b], heads * size : heads * size + PARTS, :] = edges[b]


def last_out_kernel(items, earlier, heads, size, *refs):
    count = 3 + 3 * len(items)
    made = refs[count : count + len(earlier)]
    out_ref, inter_ref, score_ref, done_ref, sems = refs[-5:]
    copies = []

    def write(item, source):
        cols = columns(head_group(*item) * heads * size, 0, heads * size)
        copies.append(
            pltpu.make_async_copy(source, out_ref.at[:, cols], sems.at[len(copies)])
        )
        copies[-1].start()

    for there, ref in zip(earlier, made):
        for i, item in enumerate(there):
            write(item, ref.at[i])
    out_kernel(items, heads, size, *refs[:count], done_ref, inter_ref, score_ref, write=write)
    for copy in copies:
        copy.wait()


def out_kernel(items, heads, size, *refs, write=None):
    q_ref, cum_ref, gain_ref = refs[:3]
    per_item = [refs[3 + 3 * i : 6 + 3 * i] for i in range(len(items))]
    done_ref, inter_ref, score_ref = refs[-3:]
    rows = q_ref.shape[0]
    core, _ = position()
    second = core == 1
    row = lax.broadcasted_iota(jnp.int32, (rows, 2 * PARTS), 0)
    column = lax.broadcasted_iota(jnp.int32, (rows, 2 * PARTS), 1)
    edge = lax.rem(column, PARTS)
    causal = (lax.div(edge, heads) <= row) & (edge < 3 * heads)
    ahead = column < PARTS
    kept = ((ahead & (core == 1)) | causal) & (ahead | (core == 1))
    kept = [kept & (lax.rem(edge, heads) == j) for j in range(heads)]
    for i, (mine, g) in enumerate(items):
        prefix_ref, intra_ref, sib_ref = per_item[i]
        b = head_group(mine, g)
        started = jnp.exp(cum_ref[b][0:heads]).T
        by = jnp.where(second, get_decay(sib_ref.at[g], heads, size), 1.0)
        edges = jnp.concatenate(
            [
                prefix_ref[heads * size : heads * size + PARTS, :].astype(F32),
                sib_ref[g, side(0, heads, size), :].astype(F32),
            ],
            0,
        ).astype(BF16)
        for j in range(heads):
            cols = columns(b * heads * size, j * size, size)
            these = slice(j * size, (j + 1) * size)
            sib = jnp.where(second, sib_ref[g, these, :].astype(F32), 0.0)
            prefix = (prefix_ref[these, :].astype(F32) * by[j : j + 1] + sib).astype(BF16)
            both = lax.dot_general(
                q_ref[:, cols],
                jnp.concatenate([prefix, edges], 0),
                (((1,), (1,)), ((), ())),
                preferred_element_type=F32,
            )
            both = both * started[:, j : j + 1]
            inter_ref[i * heads + j] = both[:, 0:size] + intra_ref[g * heads + j]
            score_ref[i * heads + j] = jnp.where(kept[j], both[:, size:], 0.0).astype(BF16)
    for i, (mine, g) in enumerate(items):
        _, intra_ref, sib_ref = per_item[i]
        b = head_group(mine, g)
        values = intra_ref[UNITS * heads, g * PARTS : (g + 1) * PARTS, :]
        ahead_values = jnp.where(second, sib_ref[g, side(2, heads, size), :].astype(F32), values)
        values = jnp.concatenate([ahead_values, values], 0).astype(BF16)
        for j in range(heads):
            inter_ref[i * heads + j] += jnp.dot(
                score_ref[i * heads + j], values, preferred_element_type=F32
            )
    for i, (mine, g) in enumerate(items):
        b = head_group(mine, g)
        for j in range(heads):
            cols = columns(b * heads * size, j * size, size)
            mixed = inter_ref[i * heads + j]
            scale = lax.rsqrt(jnp.mean(mixed * mixed, axis=1, keepdims=True) + 1e-05)
            done_ref[i, :, j * size : (j + 1) * size] = (
                mixed * scale * gain_ref[:, cols]
            ).astype(BF16)
        if write is not None:
            write((mine, g), done_ref.at[i])


def join_spans(earlier, later, heads, size):
    base = heads * size
    own = side(1, heads, size)

    def decay(x):
        tail = x[own].astype(F32)
        return tail[0:heads] + tail[heads : 2 * heads] + tail[2 * heads : 3 * heads]

    by = decay(later)
    state = (
        by[:, None, :] * earlier[:base].astype(F32).reshape(heads, size, -1)
        + later[:base].astype(F32).reshape(heads, size, -1)
    ).reshape(base, -1)
    parts = three_parts(by * decay(earlier))
    return jnp.concatenate([state.astype(BF16), later[base : own.start], *parts, later[own.start + 3 * heads :]], 0)


def on_device(queries, key_input, value_input, log_decay, conv_weight, norm_gain):
    rows, width = queries.shape
    head_count = log_decay.shape[1]
    size = width // head_count
    heads = head_count // (SPAN * CHUNKS)
    taps = conv_weight.shape[0]
    half = UNITS * heads
    packet = heads * size + 3 * PARTS
    n = lax.axis_size("ctx")

    def swap(x, mask):
        return lax.ppermute(x, "ctx", [(i, i ^ mask) for i in range(n)])

    def exchange(x, slot):
        return lax.ppermute(x, "ctx", [(i, i ^ (2 * distance(slot, i & 1))) for i in range(n)])

    def shift(x, by):
        return lax.ppermute(x, "ctx", [(i, i + by) for i in range(n - by)])

    gain = norm_gain.reshape(1, width)
    ext = pltpu.VMEM((2 * heads, rows + HALO, size), F32)
    held = pltpu.VMEM((half, rows, size), BF16)

    cum_shape = pltpu.VMEM((SPAN * CHUNKS, 2 * heads, rows), F32)

    def states(mine):
        scratch = [cum_shape, ext, held]
        if not mine:
            buf = pltpu.VMEM((CHIPS, rows, CHUNKS * heads * size), BF16)
            scratch = [
                buf,
                buf,
                pltpu.VMEM((CHIPS, taps, CHUNKS * heads * size), F32),
                pltpu.VMEM((head_count, rows), F32),
                *scratch,
                pltpu.SemaphoreType.DMA((3 * CHIPS + 1,)),
            ]
        return call(
            functools.partial(state_kernel if mine else fetched_state_kernel, mine, heads, size),
            "states_mine" if mine else "states_other",
            pltpu.VMEM((UNITS, packet, size), BF16),
            key_input, value_input, conv_weight, log_decay.T,
            in_specs=[VMEM if mine else HBM] * 4,
            scratch=scratch,
        )

    def intra_part(mine, q):
        return call(
            functools.partial(intra_kernel, mine, heads, size),
            "intra_mine" if mine else "intra_other",
            pltpu.VMEM((half + 1, rows, size), F32),
            q, key_input, value_input, conv_weight, cum,
            scratch=[ext, held],
        )

    theirs = states(False)
    got = swap(theirs, 1)
    mine = states(True)
    got_late = swap(mine, 1)

    chip_states = call(
        functools.partial(chip_kernel, heads, size),
        "chip_states",
        pltpu.VMEM((CHIPS, CHUNKS, packet, size), BF16),
        mine, got,
    )
    order = pltpu.VMEM((CHIPS, packet, size), BF16)

    packets = {0: chip_states[0]}
    for g in EXCHANGE[::-1]:
        packets[g] = exchange(chip_states[g], g)
    q_after, decay_after, chip_states = lax.optimization_barrier(
        (queries, log_decay, chip_states)
    )
    cum = call(
        functools.partial(cum_kernel, heads),
        "cum",
        cum_shape,
        decay_after.T,
    )
    intra_mine = intra_part(True, q_after)
    *late, intra_mine = lax.optimization_barrier(
        (*[packets[g] for g in EXCHANGE[::-1]], intra_mine)
    )
    packets.update(zip(EXCHANGE[::-1], late))
    packets = [packets[g] for g in range(CHIPS)]

    known = []
    if n > 2 * SPAN:
        edge = call(
            functools.partial(last_edge_kernel, heads, size),
            "last_edge",
            pltpu.VMEM((CHUNKS, PARTS, size), BF16),
            *packets,
            scratch=[order],
        )
        known = [shift(edge, SPAN)]

    def joined(parts):
        span = call(
            functools.partial(span_kernel, parts, heads, size),
            "span_state",
            pltpu.VMEM((len(parts), heads * size + (2 if known else 1) * PARTS, size), BF16),
            *packets, *known,
            scratch=[order],
        )
        before = swap(span, SPAN) if n == 2 * SPAN else shift(span, SPAN)
        reach = 1
        while reach < n // SPAN - 1:
            before = jax.vmap(functools.partial(join_spans, heads=heads, size=size))(
                shift(before, SPAN * reach), before
            )
            reach *= 2
        return span, before

    spans, befores = zip(*[joined(parts) for parts in SHIFTS])
    q_after, _ = lax.optimization_barrier((queries, spans[-1]))
    intra_other = intra_part(False, q_after)
    before, intra_other = lax.optimization_barrier((befores[-1], intra_other))
    befores = [*befores[:-1], before]
    ahead = {
        part: (place, before)
        for parts, before in zip(SHIFTS, befores)
        for place, part in enumerate(parts)
    }

    own, other = {}, {}
    for part in range(CHUNKS):
        chip_prefix = call(
            functools.partial(spread_kernel, part, ahead[part][0], heads, size),
            "chip_prefix",
            pltpu.VMEM((CHIPS, heads * size + PARTS, size), BF16),
            *packets, ahead[part][1], *known,
            scratch=[order],
        )
        first = part * CHIPS
        own[first] = chip_prefix[0]
        for g in EXCHANGE:
            own[first + g] = exchange(chip_prefix[g], g)

    def output(items, earlier=None):
        args = [queries, cum, gain]
        for mine, u in items:
            args += [own[u], intra_mine, got] if mine else [other[u], intra_other, got_late]
        done = pltpu.VMEM((len(items), rows, heads * size), BF16)
        scratch = [
            pltpu.VMEM((len(items) * heads, rows, size), F32),
            pltpu.VMEM((len(items) * heads, rows, 2 * PARTS), BF16),
        ]
        kernel = functools.partial(out_kernel, items, heads, size)
        hints = {
            "cost_estimate": pl.CostEstimate(flops=1, transcendentals=0, bytes_accessed=1),
        }
        name = "out_" + "_".join(("m" if mine else "o") + str(u) for mine, u in items)
        if earlier is None:
            return call(kernel, name, done, *args, scratch=scratch, **hints)
        there, made = zip(*earlier)
        return call(
            functools.partial(last_out_kernel, items, there, heads, size),
            name,
            jax.ShapeDtypeStruct((rows, width), BF16),
            *args, *made,
            out_specs=HBM,
            scratch=[*scratch, done, pltpu.SemaphoreType.DMA((2 * UNITS,))],
            **hints,
        )

    *late, soon = EXCHANGE[1], EXCHANGE[0], EXCHANGE[2]
    own[0], own[soon] = lax.optimization_barrier((own[0], own[soon]))
    other.update({u: swap(own[u], 1) for u in (0, soon)})
    earlier = []
    items = [(True, 0), (True, soon)]
    made = output(items)
    *arrived, made = lax.optimization_barrier((*[own[u] for u in late], made))
    earlier.append((items, made))
    own.update(zip(late, arrived))
    other.update({u: swap(own[u], 1) for u in late})
    items = [(True, u) for u in late] + [(False, 0), (False, soon)]
    earlier.append((items, output(items)))
    return output([(False, u) for u in late], earlier)


def solution(mesh):
    rows = P(("groups", "ctx"), None)
    return jax.shard_map(
        on_device,
        mesh=mesh,
        in_specs=(rows, rows, rows, rows, P(), P()),
        out_specs=rows,
        check_vma=False,
    )
```
